32 devices in a mesh: dp: 8 (over z, y), tensor: 4 (over x, core).
Axes of the slice: x: 2, y: 2, z: 4, core: 2. Of those that a mesh axis runs over, the one named last changes fastest.
Arguments:
- layer_input: bfloat16 [16, 512, 1024], P('dp'), may hold values from -6 to 6
- seq_lengths: int32 [16], P('dp'), may hold values from 128 to 512, as said below
- attn_gain: float32 [2, 1024], replicated, may hold values from 0.5 to 1.5
- query_proj: bfloat16 [2, 1024, 512], P(None, None, 'tensor'), as said below
- key_proj: bfloat16 [2, 1024, 512], P(None, None, 'tensor'), as said below
- value_proj: bfloat16 [2, 1024, 1024], P(None, None, 'tensor'), may hold values from -0.1875 to 0.1875
- gate_proj: bfloat16 [2, 1024, 1024], P(None, None, 'tensor'), may hold values from -0.1875 to 0.1875
- decay_down: bfloat16 [2, 1024, 16], replicated, may hold values from -0.1875 to 0.1875
- decay_up: bfloat16 [2, 16, 512], P(None, None, 'tensor'), may hold values from -1.5 to 1.5
- decay_bias: float32 [2, 512], P(None, 'tensor'), may hold values from -4 to 4
- group_gain: float32 [2, 256], replicated, may hold values from 0.5 to 1.5
- output_proj: bfloat16 [2, 1024, 1024], P(None, 'tensor'), may hold values from -0.375 to 0.375
- ffn_gain: float32 [2, 1024], replicated, may hold values from 0.5 to 1.5
- ffn_gate: bfloat16 [2, 1024, 2816], P(None, None, 'tensor'), may hold values from -0.1875 to 0.1875
- ffn_up: bfloat16 [2, 1024, 2816], P(None, None, 'tensor'), may hold values from -0.1875 to 0.1875
- ffn_down: bfloat16 [2, 2816, 1024], P(None, 'tensor'), may hold values from -0.109375 to 0.109375
- cotangent: bfloat16 [16, 512, 1024], P('dp'), may hold values from -6 to 6
Outputs:
- layer_output: bfloat16 [16, 512, 1024], P('dp')
- input_grad: float32 [16, 512, 1024], P('dp')
- grad_attn_gain: float32 [2, 1024], replicated
- grad_query: float32 [2, 1024, 512], P(None, None, 'tensor')
- grad_key: float32 [2, 1024, 512], P(None, None, 'tensor')
- grad_value: float32 [2, 1024, 1024], P(None, None, 'tensor')
- grad_gate: float32 [2, 1024, 1024], P(None, None, 'tensor')
- grad_decay_down: float32 [2, 1024, 16], replicated
- grad_decay_up: float32 [2, 16, 512], P(None, None, 'tensor')
- grad_decay_bias: float32 [2, 512], P(None, 'tensor')
- grad_group_gain: float32 [2, 256], replicated
- grad_output: float32 [2, 1024, 1024], P(None, 'tensor')
- grad_ffn_gain: float32 [2, 1024], replicated
- grad_ffn_gate: float32 [2, 1024, 2816], P(None, None, 'tensor')
- grad_ffn_up: float32 [2, 1024, 2816], P(None, None, 'tensor')
- grad_ffn_down: float32 [2, 2816, 1024], P(None, 'tensor')
The draws below stay inside these ranges and needn't reach their ends.
Inputs may be any that keep to these rules, and one draw needn't show every extreme that they name: seq_lengths[s] real tokens fill the first slots of sequence slot s; the rest are padding; some entry equals 512. `query_proj`: entries of order 1024^-0.5. `key_proj`: entries of order 1024^-0.5.
All inputs are finite; a program needn't handle non-finite values.
Results may differ from the reference program's by a relative error of at most 0.018.
Values sent between devices are 32-bit elements; how exact they have to be, the bound alone decides.
A program may use at most 256 MiB of HBM per device.

```python
import jax
import jax.numpy as jnp
from jax import lax

D = 1024
HK = 128
HV = 256
RANK = 16
FF = 2816
SPAN = 64
LAYERS = 2
SLOT = 512
KEY = 512
VAL = 1024
SEQS = 16


def draw_seq_lengths(key, part):
    picks = jax.random.randint(key, (SEQS,), SLOT // 4, SLOT + 1, dtype=jnp.int32)
    return picks.at[0].set(SLOT).astype(jnp.int32)


def projection_base(key):
    base_key = jax.random.fold_in(key, 7101)
    return jax.random.truncated_normal(base_key, -4.0, 4.0, (LAYERS, D, KEY), jnp.float32)


def draw_query_proj(key, part):
    base = projection_base(key)
    return (base * D ** (-0.5)).astype(jnp.bfloat16)


def draw_key_proj(key, part):
    base = projection_base(key)
    extra_key = jax.random.fold_in(key, 7202)
    extra = jax.random.truncated_normal(extra_key, -4.0, 4.0, (LAYERS, D, KEY), jnp.float32)
    return ((0.8 * base + 0.6 * extra) * D ** (-0.5)).astype(jnp.bfloat16)


def block_scale(rng, dims, cuts, smallest, high):
    factor_of, own = 1.0, jax.random.fold_in(rng, 6)
    for position, shards_of in cuts:
        draws = jnp.exp(jax.random.uniform(jax.random.fold_in(own, position), (shards_of,), jnp.float32, smallest / len(cuts), high / len(cuts)))
        factor_of = factor_of * jnp.repeat(draws, dims[position] // shards_of).reshape([-1 if axis == position else 1 for axis in range(len(dims))])
    return factor_of


def scatter_about(rng, extent, scale, most, split=(), kind=jnp.bfloat16):
    entries = scale * jax.random.normal(rng, extent, jnp.float32)
    if split:
        entries = entries * block_scale(rng, extent, split, -0.22, 0.18)
    return jnp.clip(entries, -most, most).astype(kind)


def setup_inputs(seed: int = 0) -> dict:
    splits = jax.random.split(jax.random.key(seed), 18)
    return {
        "layer_input": scatter_about(splits[0], (SEQS, SLOT, D), 1.0, 6.0, ((0, 8),)),
        "seq_lengths": draw_seq_lengths(jax.random.fold_in(splits[17], 71), 0),
        "attn_gain": jnp.clip(1.0 + 0.1 * jax.random.normal(splits[2], (LAYERS, D), jnp.float32), 0.5, 1.5),
        "query_proj": draw_query_proj(jax.random.fold_in(splits[17], 71), 0),
        "key_proj": draw_key_proj(jax.random.fold_in(splits[17], 71), 0),
        "value_proj": scatter_about(splits[5], (LAYERS, D, VAL), D ** -0.5, 0.1875, ((2, 4),)),
        "gate_proj": scatter_about(splits[6], (LAYERS, D, VAL), D ** -0.5, 0.1875, ((2, 4),)),
        "decay_down": scatter_about(splits[7], (LAYERS, D, RANK), D ** -0.5, 0.1875),
        "decay_up": scatter_about(splits[8], (LAYERS, RANK, KEY), RANK ** -0.5, 1.5, ((2, 4),)),
        "decay_bias": scatter_about(splits[9], (LAYERS, KEY), 1.0, 4.0, ((1, 4),), jnp.float32),
        "group_gain": jnp.clip(1.0 + 0.1 * jax.random.normal(splits[10], (LAYERS, HV), jnp.float32), 0.5, 1.5),
        "output_proj": scatter_about(splits[11], (LAYERS, VAL, D), HV ** -0.5, 0.375, ((1, 4),)),
        "ffn_gain": jnp.clip(1.0 + 0.1 * jax.random.normal(splits[12], (LAYERS, D), jnp.float32), 0.5, 1.5),
        "ffn_gate": scatter_about(splits[13], (LAYERS, D, FF), D ** -0.5, 0.1875, ((2, 4),)),
        "ffn_up": scatter_about(splits[14], (LAYERS, D, FF), D ** -0.5, 0.1875, ((2, 4),)),
        "ffn_down": scatter_about(splits[15], (LAYERS, FF, D), FF ** -0.5, 0.109375, ((1, 4),)),
        "cotangent": scatter_about(splits[16], (SEQS, SLOT, D), 1.0, 6.0, ((0, 8),)),
    }


@jax.custom_vjp
def low(v):
    return lax.optimization_barrier(v.astype(jnp.bfloat16)).astype(jnp.float32)

@jax.custom_vjp
def low_back(v):
    return v

def low_keep(v):
    return (low(v), None)

def low_pass(kept, grad):
    return (grad,)

def back_keep(v):
    return (v, None)

def back_low(kept, grad):
    return (low(grad),)
low.defvjp(low_keep, low_pass)
low_back.defvjp(back_keep, back_low)
HIGHEST = lax.Precision.HIGHEST
norm_epsilon = 1e-06
group_epsilon = 1e-05

def matmul_high(left, right):
    return jnp.dot(left, right, precision=HIGHEST)

def rms_scale(hidden, norm_weight):
    return hidden * lax.rsqrt(lax.optimization_barrier(jnp.mean(hidden * hidden, axis=-1, keepdims=True)) + norm_epsilon) * norm_weight

def gated_linear(queries, key_rows, values, log_decay):
    length = queries.shape[0]
    blocks = length // SPAN
    queries = queries.reshape(blocks, SPAN, queries.shape[1])
    key_rows = key_rows.reshape(blocks, SPAN, key_rows.shape[1])
    values = values.reshape(blocks, SPAN, values.shape[1])
    cumulative = jnp.cumsum(log_decay.reshape(blocks, SPAN, log_decay.shape[1]), axis=1)
    causal = (jnp.arange(SPAN, dtype=jnp.int32)[:, None] >= jnp.arange(SPAN, dtype=jnp.int32)[None, :])[None, :, :, None]
    differ = cumulative[:, :, None, :] - cumulative[:, None, :, :]
    nothing = jnp.zeros((), dtype=differ.dtype)
    spread = jnp.where(causal, differ, nothing)
    factors = jnp.where(causal, jnp.exp(spread), nothing)
    scores = lax.optimization_barrier(jnp.sum(queries[:, :, None, :] * key_rows[:, None, :, :] * factors, axis=-1))
    inside = jnp.einsum('cij,cjv->civ', scores, values, precision=HIGHEST)
    last_decay = cumulative[:, -1, :]
    carried = key_rows * jnp.exp(last_decay[:, None, :] - cumulative)
    updates = jnp.einsum('cjd,cjv->cdv', carried, values, precision=HIGHEST)

    def advance(state, pieces):
        fading, update = pieces
        return (jnp.exp(fading)[:, None] * state + update, state)
    start_state = jnp.zeros((key_rows.shape[2], values.shape[2]), dtype=updates.dtype)
    final_state, before = lax.scan(advance, start_state, (last_decay, updates))
    outside = jnp.einsum('cid,cdv->civ', queries * jnp.exp(cumulative), before, precision=HIGHEST)
    return (inside + outside).reshape(length, values.shape[2])

def token_mixer(queries, key_rows, values, out_gate, low_rank, decay_map, decay_shift, group_weight):
    length, head_count, key_width = queries.shape
    logits = jnp.dot(low_rank, decay_map, precision=HIGHEST) + decay_shift
    log_decay = (jax.nn.log_sigmoid(logits) / 16.0).reshape(length, head_count, key_width)
    scaled = queries * key_width ** (-0.5)
    mixed_rows = jax.vmap(gated_linear, in_axes=1, out_axes=1)(scaled, key_rows, values, log_decay)
    normed = mixed_rows * lax.rsqrt(lax.optimization_barrier(jnp.mean(mixed_rows * mixed_rows, axis=-1, keepdims=True)) + group_epsilon) * group_weight
    return normed * out_gate * jax.nn.sigmoid(out_gate)

def mixer_flat(queries, key_rows, values, out_gate, low_rank, decay_map, decay_shift, group_weight):
    length = queries.shape[0]
    head_count = queries.shape[1] // HK
    mixed_rows = token_mixer(queries.reshape(length, head_count, HK), key_rows.reshape(length, head_count, HK), values.reshape(length, head_count, HV), out_gate.reshape(length, head_count, HV), low_rank, decay_map, decay_shift, group_weight)
    return mixed_rows.reshape(length, head_count * HV)

def residual_block(hidden, weights):
    attn_norm, query_map, key_map, value_map, gate_map, down_map, up_map, shift_vec, group_weight, output_map, ffn_norm, ffn_gate_map, ffn_up_map, ffn_down_map = weights
    normed = low(rms_scale(hidden, attn_norm))
    queries = low_back(low(matmul_high(normed, query_map)))
    key_rows = low_back(low(matmul_high(normed, key_map)))
    values = low_back(low(matmul_high(normed, value_map)))
    out_gate = low_back(matmul_high(normed, gate_map))
    low_rank = low_back(matmul_high(normed, down_map))
    gated = low(mixer_flat(queries, key_rows, values, out_gate, low_rank, up_map, shift_vec, group_weight))
    middle = hidden + low_back(matmul_high(gated, output_map))
    normed_ffn = low(rms_scale(middle, ffn_norm))
    gate_act = low_back(matmul_high(normed_ffn, ffn_gate_map))
    up_act = low_back(matmul_high(normed_ffn, ffn_up_map))
    inner = low(jax.nn.silu(gate_act) * up_act)
    return middle + low_back(matmul_high(inner, ffn_down_map))

def reference(layer_input, seq_lengths, attn_gain, query_proj, key_proj, value_proj, gate_proj, decay_down, decay_up, decay_bias, group_gain, output_proj, ffn_gain, ffn_gate, ffn_up, ffn_down, cotangent):
    weights = tuple((weight_item.astype(jnp.float32) for weight_item in (attn_gain, query_proj, key_proj, value_proj, gate_proj, decay_down, decay_up, decay_bias, group_gain, output_proj, ffn_gain, ffn_gate, ffn_up, ffn_down)))
    work_type = weights[1].dtype

    def network(row_block, params):
        for layer_index in range(LAYERS):
            row_block = residual_block(row_block, tuple((weight_item[layer_index] for weight_item in params)))
        return row_block

    def one_sequence(totals, pieces):
        row_block, length_now, upstream = pieces
        slots = jnp.arange(SLOT, dtype=jnp.int32)
        keep_mask = (slots < length_now.astype(jnp.int32)).astype(work_type)[:, None]

        def masked(rows_in, params):
            return network(rows_in, params) * keep_mask
        output, pullback = jax.vjp(masked, row_block.astype(work_type), weights)
        grad_rows, grad_params = pullback(upstream.astype(work_type))
        new_totals = tuple((total_item + grad_item.astype(total_item.dtype) for total_item, grad_item in zip(totals, grad_params)))
        return (new_totals, (output.astype(work_type), grad_rows.astype(work_type)))
    zero_grads = tuple((jnp.zeros(weight_item.shape, dtype=weight_item.dtype) for weight_item in weights))
    totals, (outputs, grad_inputs) = lax.scan(one_sequence, zero_grads, (layer_input, seq_lengths.astype(jnp.int32), cotangent))
    outputs = outputs.astype(jnp.bfloat16)
    return (outputs, grad_inputs, totals[0], totals[1], totals[2], totals[3], totals[4], totals[5], totals[6], totals[7], totals[8], totals[9], totals[10], totals[11], totals[12], totals[13])
```

```python
import functools
import jax, jax.numpy as jnp
from jax import lax
from jax.experimental import pallas as pl
from jax.experimental.pallas import tpu as pltpu
from jax.sharding import PartitionSpec as P
HK, HV, CH = 128, 256, 128
group_epsilon = 1e-05
bf, f32 = jnp.bfloat16, jnp.float32
SCALE = HK ** -0.5

def nn(a, b):
    return lax.dot_general(a, b, (((1,), (0,)), ((), ())), preferred_element_type=f32)
def nt(a, b):
    return lax.dot_general(a, b, (((1,), (1,)), ((), ())), preferred_element_type=f32)
def tn(a, b):
    return lax.dot_general(a, b, (((0,), (0,)), ((), ())), preferred_element_type=f32)

def halves(a):
    top = a.astype(bf)
    return top, (a - top.astype(f32)).astype(bf)

def thirds(a):
    top = a.astype(bf)
    return (top,) + halves(a - top.astype(f32))

def sigmoid(a):
    return 1.0 / (1.0 + jnp.exp(-a))

def log_sigmoid(a):
    return jnp.minimum(a, 0.0) - jnp.log1p(jnp.exp(-jnp.abs(a)))

def steps_below(n):
    out, h = [], 1
    while h < n:
        out.append(h)
        h *= 2
    return out

def decay_sums(ld):
    n = ld.shape[0]
    rows = lax.broadcasted_iota(jnp.int32, ld.shape, 0)
    total, pre, suf = ld, ld, jnp.zeros_like(ld)
    levels = []
    for h in steps_below(n):
        upper = (rows & h) != 0
        levels.append((h, upper, jnp.exp(jnp.where(upper, pre, suf))))
        below, above = pltpu.roll(total, h, 0), pltpu.roll(total, n - h, 0)
        pre = jnp.where(upper, pre + below, pre)
        suf = jnp.where(upper, suf, suf + above)
        total = total + jnp.where(upper, below, above)
    return levels, pre, suf, total

def tile_rows(c):
    return pl.ds(c * CH, CH)

def logits_of(z, up_ref, bias_ref):
    return sum(nn(piece, up_ref[...]) for piece in thirds(z[:, 2 * HK + 2 * HV:])) + bias_ref[...]

def wide_levels(chunks):
    out, h = [], 1
    while h < chunks:
        for base in range(0, chunks, 2 * h):
            out.append((tuple(range(base, base + h)), tuple(range(base + h, base + 2 * h))))
        h *= 2
    return out

def wide_factor(c, group, is_upper, pre, suf, tot):
    arg = pre[tile_rows(c), :] if is_upper else suf[tile_rows(c), :]
    for o in group:
        if (o < c) if is_upper else (o > c):
            arg = arg + tot[pl.ds(o * 8, 1), :]
    return jnp.exp(arg)

def mixer_forward(z_ref, up_ref, bias_ref, gain_ref, gated_ref, mixed_ref, scores_ref, pre, suf, tot):
    chunks = z_ref.shape[0] // CH
    i = lax.broadcasted_iota(jnp.int32, (CH, CH), 0)
    j = lax.broadcasted_iota(jnp.int32, (CH, CH), 1)
    apart = i ^ j
    scores_ref[...] = jnp.zeros_like(scores_ref)
    for c in range(chunks):
        z = z_ref[tile_rows(c), :]
        q, k = z[:, :HK].astype(bf), z[:, HK:2 * HK].astype(bf)
        ld = log_sigmoid(logits_of(z, up_ref, bias_ref)) / 16.0
        levels, p, s, t = decay_sums(ld)
        pre[tile_rows(c), :], suf[tile_rows(c), :], tot[pl.ds(c * 8, 8), :] = p, s, t[:8]
        tile = nt(q, k)
        qf, kf = q.astype(f32), k.astype(f32)
        for h, upper, factor in levels:
            rows = (jnp.where(upper, qf, kf) * factor).astype(bf)
            tile = jnp.where(apart >= h, nt(rows, rows), tile)
        scores_ref[tile_rows(c), tile_rows(c)] = jnp.where(i >= j, tile * SCALE, 0.0).astype(bf)
    for low_group, up_group in wide_levels(chunks):
        q_rows = [(z_ref[tile_rows(c), :HK].astype(bf).astype(f32) * wide_factor(c, up_group, True, pre, suf, tot)).astype(bf) for c in up_group]
        k_rows = [(z_ref[tile_rows(c), HK:2 * HK].astype(bf).astype(f32) * wide_factor(c, low_group, False, pre, suf, tot)).astype(bf) for c in low_group]
        for a, c in enumerate(up_group):
            for b, o in enumerate(low_group):
                scores_ref[tile_rows(c), tile_rows(o)] = (nt(q_rows[a], k_rows[b]) * SCALE).astype(bf)
    for c in range(chunks):
        width = (c + 1) * CH
        mixed = nn(scores_ref[tile_rows(c), :width], z_ref[:width, 2 * HK:2 * HK + HV].astype(bf))
        mixed_ref[tile_rows(c), :] = mixed
        out_gate = z_ref[tile_rows(c), 2 * HK + HV:2 * HK + 2 * HV]
        normed = mixed * lax.rsqrt(jnp.mean(mixed * mixed, axis=-1, keepdims=True) + group_epsilon) * gain_ref[...]
        gated_ref[tile_rows(c), :] = (normed * out_gate * sigmoid(out_gate)).astype(bf)

def mixer_backward(z_ref, up_ref, bias_ref, gain_ref, mixed_ref, scores_ref, grad_ref,
                   out_ref, up_out, bias_out, gain_out, pre, suf, tot, dm_ref, dq_ref, dk_ref, flow):
    chunks = z_ref.shape[0] // CH
    i = lax.broadcasted_iota(jnp.int32, (CH, CH), 0)
    j = lax.broadcasted_iota(jnp.int32, (CH, CH), 1)
    apart = i ^ j
    rows_in = lax.broadcasted_iota(jnp.int32, (CH, HK), 0)

    @pl.when(pl.program_id(0) == 0)
    def _():
        up_out[...] = jnp.zeros_like(up_out)
        bias_out[...] = jnp.zeros_like(bias_out)
        gain_out[...] = jnp.zeros_like(gain_out)

    for c in range(chunks):
        mixed, e = mixed_ref[tile_rows(c), :], grad_ref[tile_rows(c), :]
        g = z_ref[tile_rows(c), 2 * HK + HV:2 * HK + 2 * HV]
        r = lax.rsqrt(jnp.mean(mixed * mixed, axis=-1, keepdims=True) + group_epsilon)
        sig = sigmoid(g)
        unit = mixed * r
        out_ref[tile_rows(c), 2 * HK + HV:2 * HK + 2 * HV] = (e * unit * gain_ref[...] * (sig + g * sig * (1.0 - sig))).astype(bf)
        upstream = e * g * sig
        gain_out[...] += jnp.sum(upstream * unit, axis=0, keepdims=True)
        weighted = upstream * gain_ref[...]
        dm_ref[tile_rows(c), :] = (r * (weighted - unit * jnp.mean(unit * weighted, axis=-1, keepdims=True))).astype(bf)

    def score_grad(c, o):
        return nt(dm_ref[tile_rows(c), :], z_ref[tile_rows(o), 2 * HK:2 * HK + HV].astype(bf)) * SCALE

    for c in range(chunks):
        z = z_ref[tile_rows(c), :]
        q, k = z[:, :HK].astype(bf).astype(f32), z[:, HK:2 * HK].astype(bf).astype(f32)
        ld = log_sigmoid(logits_of(z, up_ref, bias_ref)) / 16.0
        levels, p, s, t = decay_sums(ld)
        pre[tile_rows(c), :], suf[tile_rows(c), :], tot[pl.ds(c * 8, 8), :] = p, s, t[:8]
        ds = score_grad(c, c)
        diagonal = jnp.sum(jnp.where(i == j, ds, 0.0), axis=-1, keepdims=True)
        ds = jnp.where(i > j, ds, 0.0)
        both = ds + ds.T
        dq, dk = diagonal * k, diagonal * q
        fl = jnp.zeros_like(dq)
        for h, upper, factor in levels:
            rows = (jnp.where(upper, q, k) * factor).astype(bf)
            near = jnp.where((apart >= h) & (apart < 2 * h), both, 0.0).astype(bf)
            back = nn(near, rows)
            part = back * factor
            dq, dk = dq + jnp.where(upper, part, 0.0), dk + jnp.where(upper, 0.0, part)
            moved = back * rows.astype(f32)
            fl = fl + jnp.where(upper, moved, -moved)
        dq_ref[tile_rows(c), :], dk_ref[tile_rows(c), :], flow[tile_rows(c), :] = dq, dk, fl
    for low_group, up_group in wide_levels(chunks):
        q_fac = [wide_factor(c, up_group, True, pre, suf, tot) for c in up_group]
        k_fac = [wide_factor(c, low_group, False, pre, suf, tot) for c in low_group]
        q_rows = [(z_ref[tile_rows(c), :HK].astype(bf).astype(f32) * f).astype(bf) for c, f in zip(up_group, q_fac)]
        k_rows = [(z_ref[tile_rows(c), HK:2 * HK].astype(bf).astype(f32) * f).astype(bf) for c, f in zip(low_group, k_fac)]
        grads = [[score_grad(c, o).astype(bf) for o in low_group] for c in up_group]
        for a, c in enumerate(up_group):
            back = sum(nn(grads[a][b], k_rows[b]) for b in range(len(low_group)))
            dq_ref[tile_rows(c), :] += back * q_fac[a]
            flow[tile_rows(c), :] += back * q_rows[a].astype(f32)
        for b, o in enumerate(low_group):
            back = sum(tn(grads[a][b], q_rows[a]) for a in range(len(up_group)))
            dk_ref[tile_rows(o), :] += back * k_fac[b]
            flow[tile_rows(o), :] -= back * k_rows[b].astype(f32)
    later = jnp.zeros((1, HK), f32)
    for c in reversed(range(chunks)):
        out_ref[tile_rows(c), :HK] = dq_ref[tile_rows(c), :].astype(bf)
        out_ref[tile_rows(c), HK:2 * HK] = dk_ref[tile_rows(c), :].astype(bf)
        out_ref[tile_rows(c), 2 * HK:2 * HK + HV] = tn(scores_ref[pl.ds(c * CH, (chunks - c) * CH), tile_rows(c)], dm_ref[pl.ds(c * CH, (chunks - c) * CH), :]).astype(bf)
        fl = flow[tile_rows(c), :]
        for h in steps_below(CH):
            fl = fl + jnp.where(rows_in < CH - h, pltpu.roll(fl, CH - h, 0), 0.0)
        fl = fl + later
        later = fl[:1]
        z = z_ref[tile_rows(c), :]
        logits = logits_of(z, up_ref, bias_ref)
        d_logit = fl * sigmoid(-logits) / 16.0
        bias_out[...] += jnp.sum(d_logit, axis=0, keepdims=True)
        d1, d2 = halves(d_logit)
        l1, l2 = halves(z[:, 2 * HK + 2 * HV:])
        up_out[...] += tn(l1, d1) + tn(l1, d2) + tn(l2, d1)
        out_ref[tile_rows(c), 2 * HK + 2 * HV:] = (nt(d1, up_ref[...]) + nt(d2, up_ref[...])).astype(bf)

def run_forward(z, up, bias, gain, seqs):
    rows, width = z.shape
    length = rows // seqs
    whole = lambda s: (0, 0)
    mine = lambda s: (s, 0)
    return pl.pallas_call(
        mixer_forward, name="mixer_forward", grid=(seqs,),
        in_specs=[pl.BlockSpec((length, width), mine), pl.BlockSpec(up.shape, whole), pl.BlockSpec(bias.shape, whole), pl.BlockSpec(gain.shape, whole)],
        out_specs=[pl.BlockSpec((length, HV), mine), pl.BlockSpec((length, HV), mine), pl.BlockSpec((length, length), mine)],
        out_shape=[jax.ShapeDtypeStruct((rows, HV), bf), jax.ShapeDtypeStruct((rows, HV), f32), jax.ShapeDtypeStruct((rows, length), bf)],
        scratch_shapes=[pltpu.VMEM((length, HK), f32), pltpu.VMEM((length, HK), f32), pltpu.VMEM((length // CH * 8, HK), f32)],
        compiler_params=pltpu.CompilerParams(vmem_limit_bytes=40 << 20),
        cost_estimate=pl.CostEstimate(flops=rows * length * (HK + HV) * 2, bytes_accessed=rows * width * 4 + rows * HV * 6 + rows * length * 2, transcendentals=rows * HK * 10),
    )(z, up, bias, gain)

def run_backward(z, up, bias, gain, mixed, scores, grad, seqs):
    rows, width = z.shape
    length = rows // seqs
    whole = lambda s: (0, 0)
    mine = lambda s: (s, 0)
    return pl.pallas_call(
        mixer_backward, name="mixer_backward", grid=(seqs,),
        in_specs=[pl.BlockSpec((length, width), mine), pl.BlockSpec(up.shape, whole), pl.BlockSpec(bias.shape, whole), pl.BlockSpec(gain.shape, whole),
                  pl.BlockSpec((length, HV), mine), pl.BlockSpec((length, length), mine), pl.BlockSpec((length, HV), mine)],
        out_specs=[pl.BlockSpec((length, width), mine), pl.BlockSpec(up.shape, whole), pl.BlockSpec(bias.shape, whole), pl.BlockSpec(gain.shape, whole)],
        out_shape=[jax.ShapeDtypeStruct((rows, width), bf), jax.ShapeDtypeStruct(up.shape, f32), jax.ShapeDtypeStruct(bias.shape, f32), jax.ShapeDtypeStruct(gain.shape, f32)],
        scratch_shapes=[pltpu.VMEM((length, HK), f32), pltpu.VMEM((length, HK), f32), pltpu.VMEM((length // CH * 8, HK), f32), pltpu.VMEM((length, HV), bf),
                        pltpu.VMEM((length, HK), f32), pltpu.VMEM((length, HK), f32), pltpu.VMEM((length, HK), f32)],
        compiler_params=pltpu.CompilerParams(vmem_limit_bytes=40 << 20),
        cost_estimate=pl.CostEstimate(flops=rows * length * (HK + HV) * 4, bytes_accessed=rows * width * 6 + rows * HV * 8 + rows * length * 2, transcendentals=rows * HK * 10),
    )(z, up, bias, gain, mixed, scores, grad)


norm_epsilon = 1e-06
MESH = pl.DeviceIdType.MESH
SMALL_COLS = 384


def peer_of(index, bit):
    return jnp.where((index // bit) % 2 == 0, index + bit, index - bit)


def greet(peers):
    barrier = pltpu.get_barrier_semaphore()
    for peer in peers:
        pl.semaphore_signal(barrier, inc=1, device_id=peer, device_id_type=MESH)
    pl.semaphore_wait(barrier, len(peers))


def rms_unit(h):
    return lax.rsqrt(jnp.mean(h * h, axis=-1, keepdims=True) + norm_epsilon)


def exchange_kernel(kind, seqs, *refs):
    if kind == "norm":
        partial, resid, gain, full_out, resid_out = refs[:5]
        scratch = refs[5:]
    elif kind == "last":
        partial, resid, keep, full_out = refs[:4]
        scratch = refs[4:]
    else:
        partial, resid, gain, entry, full_out, resid_out, gain_out = refs[:7]
        scratch = refs[7:]
    first, second, passed, kept, gathered, send, recv = scratch
    me = lax.axis_index("tensor")
    core, cross = me % 2, me // 2
    core_peer, cross_peer = {"tensor": peer_of(me, 1)}, {"tensor": peer_of(me, 2)}
    length = partial.shape[0] // seqs
    half, own = length // 2, length // 4
    greet((core_peer, cross_peer))

    def copy(src, dst, stage, s, peer):
        return pltpu.make_async_remote_copy(
            src_ref=src, dst_ref=dst, send_sem=send.at[stage, s], recv_sem=recv.at[stage, s],
            device_id=peer, device_id_type=MESH,
        )

    def rows(s, c, x, size):
        return pl.ds(pl.multiple_of(s * length + c * half + x * own, own), size)

    def piece(x):
        return pl.ds(pl.multiple_of(x * own, own), own)

    copies = []
    for s in range(seqs):
        step = copy(partial.at[rows(s, 1 - core, 0, half)], first.at[s], 0, s, core_peer)
        step.start()
        copies.append(step)
    crossing = []
    for s in range(seqs):
        copies[s].wait_recv()
        passed[s] = partial[rows(s, core, 1 - cross, own), :] + first[s, piece(1 - cross), :]
        step = copy(passed.at[s], second.at[s], 1, s, cross_peer)
        step.start()
        crossing.append(step)
        kept[s] = partial[rows(s, core, cross, own), :] + first[s, piece(cross), :]
    if kind in ("back", "back_last"):
        gain_out[...] = jnp.zeros_like(gain_out)
    over, near = [], []
    for s in range(seqs):
        crossing[s].wait_recv()
        total = kept[s] + second[s]
        mine = pl.ds(s * own, own)
        if kind == "norm":
            new = resid[mine, :] + total
            resid_out[mine, :] = new
            sent = (new * rms_unit(new) * gain[...]).astype(bf).astype(f32)
        elif kind == "last":
            sent = ((resid[mine, :] + total) * keep[mine, :1]).astype(bf).astype(f32)
        else:
            h = entry[mine, :]
            r = rms_unit(h)
            unit = h * r
            gain_out[...] += jnp.sum(total * unit, axis=0, keepdims=True)
            weighted = total * gain[...]
            new = resid[mine, :] + r * (weighted - unit * jnp.mean(unit * weighted, axis=-1, keepdims=True))
            if kind == "back":
                resid_out[mine, :] = new
                sent = new.astype(bf).astype(f32)
            else:
                resid_out[pl.ds(0, 8), :] = new[:8]
                sent = new
        gathered[rows(s, core, cross, own), :] = sent
        block = gathered.at[rows(s, core, cross, own)]
        step = copy(block, block, 2, s, cross_peer)
        step.start()
        over.append(step)
        step = copy(block, block, 3, s, core_peer)
        step.start()
        near.append(step)
    last = []
    for s in range(seqs):
        over[s].wait_recv()
        block = gathered.at[rows(s, core, 1 - cross, own)]
        step = copy(block, block, 4, s, core_peer)
        step.start()
        last.append(step)
        full_out[rows(s, core, 0, half), :] = gathered[rows(s, core, 0, half), :].astype(full_out.dtype)
    for s in range(seqs):
        near[s].wait_recv()
        last[s].wait_recv()
        full_out[rows(s, 1 - core, 0, half), :] = gathered[rows(s, 1 - core, 0, half), :].astype(full_out.dtype)
    for step in copies + crossing + over + near + last:
        step.wait_send()


EXCHANGE_IDS = {"norm": 1, "last": 2, "back": 3, "back_last": 4}


def exchange(kind, seqs, partial, resid, *extra):
    rows, width = partial.shape
    length = rows // seqs
    full = jax.ShapeDtypeStruct((rows, width), f32 if kind == "back_last" else bf)
    outs = [full]
    if kind == "norm" or kind == "back":
        outs.append(jax.ShapeDtypeStruct(resid.shape, f32))
    if kind == "back_last":
        outs.append(jax.ShapeDtypeStruct((8, width), f32))
    if kind in ("back", "back_last"):
        outs.append(jax.ShapeDtypeStruct((1, width), f32))
    vmem = pl.BlockSpec(memory_space=pltpu.VMEM)
    return pl.pallas_call(
        functools.partial(exchange_kernel, kind, seqs), name="exchange_" + kind,
        in_specs=[vmem] * (2 + len(extra)), out_specs=[vmem] * len(outs), out_shape=outs,
        scratch_shapes=[
            pltpu.VMEM((seqs, length // 2, width), f32), pltpu.VMEM((seqs, length // 4, width), f32),
            pltpu.VMEM((seqs, length // 4, width), f32), pltpu.VMEM((seqs, length // 4, width), f32),
            pltpu.VMEM((rows, width), f32),
            pltpu.SemaphoreType.DMA((5, seqs)), pltpu.SemaphoreType.DMA((5, seqs)),
        ],
        compiler_params=pltpu.CompilerParams(collective_id=EXCHANGE_IDS[kind], has_side_effects=True, vmem_limit_bytes=48 << 20),
        cost_estimate=pl.CostEstimate(flops=rows * width * 4, bytes_accessed=rows * width * 40, transcendentals=0),
    )(partial, resid, *extra)


def ring_place(index, n):
    return jnp.where(index % 2 == 0, index // 2, n - 1 - index // 2)


def ring_index(place, n):
    return jnp.where(place < n // 2, 2 * place, 2 * (n - 1 - place) + 1)


def ring_cut(shape, n):
    rows, cols = shape
    if rows % (16 * n) == 0:
        return rows // (2 * n), cols, True
    if rows % (8 * n) == 0 and cols % 256 == 0:
        return rows // n, cols // 2, False
    return None


def ring_kernel(n, tensor, shapes, *refs):
    count = len(shapes)
    ins, outs = refs[:count], refs[count:2 * count]
    rest = refs[2 * count:]
    own, slots = rest[:count], rest[count:2 * count]
    shared, load, rs_send, rs_recv, ag_send, ag_recv, store, peer_send, peer_recv = rest[2 * count:]
    place = ring_place(lax.axis_index("dp"), n)
    me = lax.axis_index("tensor")
    spots = (place, n - 1 - place)
    others = [{"tensor": lax.rem(me + hop, tensor)} for hop in range(1, tensor)]
    after = {"dp": ring_index(lax.rem(place + 1, n), n)}
    before = {"dp": ring_index(lax.rem(place + n - 1, n), n)}
    ahead = (after, before)
    greet([after, before] + others)
    cuts = [ring_cut(shape, n) for shape in shapes]
    last = count - 1

    def seg(a, way, index):
        rows, cols, by_rows = cuts[a]
        if by_rows:
            return (pl.ds(pl.multiple_of((index * 2 + way) * rows, rows), rows), pl.ds(0, cols))
        return (pl.ds(pl.multiple_of(index * rows, rows), rows), pl.ds(way * cols, cols))

    def local(a):
        return pltpu.make_async_copy(ins[a].at[:, pl.ds(0, shapes[a][1])], own[a], load.at[a])

    def remote(src, dst, send, recv, peer):
        return pltpu.make_async_remote_copy(src_ref=src, dst_ref=dst, send_sem=send, recv_sem=recv, device_id=peer, device_id_type=MESH)

    def rs(a, way, step, src):
        return remote(src, slots[a].at[way, step], rs_send.at[step, a, way], rs_recv.at[step, a, way], ahead[way])

    def ag(a, way, step, src, index):
        return remote(src, outs[a].at[seg(a, way, index)], ag_send.at[step, a, way], ag_recv.at[step, a, way], ahead[way])

    def add_own(a, way, step, index):
        rows, cols, _ = cuts[a]
        row_ds, col_ds = seg(a, way, index)

        @pl.loop(0, rows // 8)
        def _(block):
            here = pl.ds(pl.multiple_of(block * 8, 8), 8)
            there = pl.ds(pl.multiple_of(row_ds.start + block * 8, 8), 8)
            slots[a][way, step, here, :] += own[a][there, col_ds]

    peers = [remote(ins[last], shared.at[hop], peer_send.at[hop], peer_recv.at[hop], other) for hop, other in enumerate(others)]
    for a in range(last):
        for way in range(2):
            rs(a, way, 0, ins[a].at[seg(a, way, spots[way])]).start()
    for step in peers:
        step.start()
    for a in range(count):
        local(a).start()
    for a in range(count):
        local(a).wait()
    for step in peers:
        step.wait()
    own[last][...] += sum(shared[hop] for hop in range(len(others)))
    for way in range(2):
        rs(last, way, 0, own[last].at[seg(last, way, spots[way])]).start()

    @pl.loop(0, n - 2)
    def _(step):
        for a in range(count):
            for way in range(2):
                index = lax.rem(spots[way] + (2 * n - 1) - step, n)
                rs(a, way, step, slots[a].at[way, step]).wait_recv()
                add_own(a, way, step, index)
                rs(a, way, step + 1, slots[a].at[way, step]).start()

    for a in range(count):
        for way in range(2):
            index = lax.rem(spots[way] + 1, n)
            slot = slots[a].at[way, n - 2]
            rs(a, way, n - 2, slot).wait_recv()
            add_own(a, way, n - 2, index)
            ag(a, way, 0, slot, index).start()
            pltpu.make_async_copy(slot, outs[a].at[seg(a, way, index)], store.at[a, way]).start()

    @pl.loop(0, n - 2)
    def _(step):
        for a in range(count):
            for way in range(2):
                index = lax.rem(spots[way] + n - step, n)
                piece = outs[a].at[seg(a, way, index)]
                ag(a, way, step, piece, index).wait_recv()
                ag(a, way, step + 1, piece, index).start()

    for a in range(count):
        for way in range(2):
            index = lax.rem(spots[way] + 2, n)
            piece = outs[a].at[seg(a, way, index)]
            ag(a, way, n - 2, piece, index).wait_recv()
            slot = slots[a].at[way, n - 2]
            pltpu.make_async_copy(slot, piece, store.at[a, way]).wait()

    @pl.loop(0, n - 1)
    def _(step):
        for a in range(count):
            for way in range(2):
                slot = slots[a].at[way, 0]
                rs(a, way, step, slot).wait_send()
                ag(a, way, step, slot, 0).wait_send()


def ring_sum(n, tensor, arrays, widths):
    shapes = [(a.shape[0], width) for a, width in zip(arrays, widths)]
    cuts = [ring_cut(shape, n) for shape in shapes]
    count = len(arrays)
    anywhere = pl.BlockSpec(memory_space=pl.ANY)
    dma = pltpu.SemaphoreType.DMA
    return pl.pallas_call(
        functools.partial(ring_kernel, n, tensor, shapes), name="ring_sum",
        in_specs=[anywhere] * count, out_specs=[anywhere] * count,
        out_shape=[jax.ShapeDtypeStruct(shape, f32) for shape in shapes],
        scratch_shapes=[pltpu.VMEM(shape, f32) for shape in shapes]
        + [pltpu.VMEM((2, n - 1, rows, cols), f32) for rows, cols, _ in cuts]
        + [pltpu.VMEM((tensor - 1,) + shapes[-1], f32), dma((count,)),
           dma((n - 1, count, 2)), dma((n - 1, count, 2)), dma((n - 1, count, 2)), dma((n - 1, count, 2)),
           dma((count, 2)), dma((tensor - 1,)), dma((tensor - 1,))],
        compiler_params=pltpu.CompilerParams(collective_id=5, has_side_effects=True, vmem_limit_bytes=58 << 20),
        cost_estimate=pl.CostEstimate(flops=10**6, bytes_accessed=10**9, transcendentals=0),
    )(*arrays)


def sum_over_groups(n, tensor, arrays, widths):
    if tensor == 4 and all(ring_cut((a.shape[0], width), n) for a, width in zip(arrays, widths)):
        return ring_sum(n, tensor, arrays, widths)
    summed = lax.psum(tuple(a[:, :width] for a, width in zip(arrays[:-1], widths)), "dp")
    return list(summed) + [lax.psum(arrays[-1], ("dp", "tensor"))]


def shards(
    groups, tensor, layer_input, seq_lengths, attn_gain, query_proj, key_proj, value_proj, gate_proj,
    decay_down, decay_up, decay_bias, group_gain, output_proj, ffn_gain, ffn_gate, ffn_up, ffn_down, cotangent,
):
    seqs, length, width = layer_input.shape
    depth = attn_gain.shape[0]
    rank = decay_down.shape[2]
    rows = seqs * length
    own = length // 4
    me = lax.axis_index("tensor")
    core, cross = me % 2, me // 2

    def mine(full):
        parts = full.reshape(seqs, 4, own, full.shape[-1])
        return lax.dynamic_slice_in_dim(parts, core * 2 + cross, 1, axis=1).reshape(seqs * own, full.shape[-1])

    keep = (jnp.arange(length, dtype=jnp.int32)[None, :] < seq_lengths[:, None]).astype(f32).reshape(rows, 1)
    cat = [
        jnp.concatenate([query_proj[l], key_proj[l], value_proj[l], gate_proj[l], jnp.pad(decay_down[l], ((0, 0), (0, 128 - rank)))], axis=1)
        for l in range(depth)
    ]
    ups = [jnp.pad(decay_up[l], ((0, 128 - rank), (0, 0))) for l in range(depth)]
    hidden = layer_input.reshape(rows, width).astype(f32)
    normed = (hidden * rms_unit(hidden) * attn_gain[0]).astype(bf)
    resid = mine(hidden)
    saved = []
    for l in range(depth):
        z = nn(normed, cat[l])
        gated, mixed, scores = run_forward(z, ups[l], decay_bias[l:l + 1], group_gain[l:l + 1], seqs)
        entry = resid
        normed_ffn, middle = exchange("norm", seqs, nn(gated, output_proj[l]), resid, ffn_gain[l:l + 1])
        gate_act, up_act = nn(normed_ffn, ffn_gate[l]), nn(normed_ffn, ffn_up[l])
        inner = (gate_act * sigmoid(gate_act) * up_act).astype(bf)
        out = nn(inner, ffn_down[l])
        saved.append((entry, normed, z, gated, mixed, scores, middle, normed_ffn, gate_act, up_act, inner))
        if l + 1 < depth:
            normed, resid = exchange("norm", seqs, out, middle, attn_gain[l + 1:l + 2])
        else:
            layer_output, = exchange("last", seqs, out, middle, jnp.broadcast_to(mine(keep), (seqs * own, 128)))
    upstream = cotangent.reshape(rows, width).astype(f32) * keep
    resid = mine(upstream)
    ffn_grad = upstream.astype(bf)
    gains, ring, ffn_sums = [None] * depth, [None] * depth, [None] * depth
    for l in reversed(range(depth)):
        entry, normed, z, gated, mixed, scores, middle, normed_ffn, gate_act, up_act, inner = saved[l]
        inner_grad = nt(ffn_grad, ffn_down[l])
        sig = sigmoid(gate_act)
        gate_low = (inner_grad * up_act * sig * (1.0 + gate_act * (1.0 - sig))).astype(bf)
        up_low = (inner_grad * gate_act * sig).astype(bf)
        grad_down = tn(inner, ffn_grad)
        grad_gate = tn(normed_ffn, gate_low)
        grad_up = tn(normed_ffn, up_low)
        if l > 0:
            ffn_sums[l] = lax.psum((grad_gate, grad_up, grad_down), "dp")
        mix_grad, resid, ffn_gain_grad = exchange(
            "back", seqs, nt(gate_low, ffn_gate[l]) + nt(up_low, ffn_up[l]), resid, ffn_gain[l:l + 1], middle)
        gated_grad = nt(mix_grad, output_proj[l])
        low, up_grad, bias_grad, group_grad = run_backward(z, ups[l], decay_bias[l:l + 1], group_gain[l:l + 1], mixed, scores, gated_grad, seqs)
        grad_output = tn(gated, mix_grad)
        grad_cat = tn(normed, low)
        back = nt(low, cat[l])
        if l > 0:
            ffn_grad, resid, attn_gain_grad = exchange("back", seqs, back, resid, attn_gain[l:l + 1], entry)
        else:
            input_grad, _, attn_gain_grad = exchange("back_last", seqs, back, resid, attn_gain[l:l + 1], entry)
        ring[l] = [grad_cat, grad_output] + ([] if l > 0 else [grad_gate, grad_up, grad_down])
        gains[l] = (attn_gain_grad, ffn_gain_grad, group_grad, grad_cat[:, 2 * HK + 2 * HV:2 * HK + 2 * HV + rank], up_grad[:rank], bias_grad)
    local = jnp.concatenate([part.reshape(-1) for l in range(depth) for part in gains[l][4:]])
    local_size = local.shape[0]
    local = jnp.pad(local, (0, -local_size % (128 * 128))).reshape(-1, 128)
    shared = jnp.concatenate([part.reshape(-1) for l in range(depth) for part in gains[l][:4]])
    shared = jnp.pad(shared, (0, -shared.shape[0] % (128 * 128))).reshape(128, -1)
    arrays, widths = [], []
    for l in reversed(range(depth)):
        arrays += ring[l]
        widths += [2 * HK + 2 * HV] + [a.shape[1] for a in ring[l][1:]]
    arrays += [local, shared]
    widths += [local.shape[1], shared.shape[1]]
    sums = sum_over_groups(groups, tensor, arrays, widths)
    shared, local = sums[-1].reshape(-1), sums[-2].reshape(-1)
    cats, outs_, ffns = [None] * depth, [None] * depth, [None] * depth
    at = 0
    for l in reversed(range(depth)):
        cats[l], outs_[l] = sums[at], sums[at + 1]
        at += 2
        if l > 0:
            ffns[l] = ffn_sums[l]
        else:
            ffns[l] = sums[at:at + 3]
            at += 3

    def take(flat, shapes):
        found, start = [], 0
        for l in range(depth):
            row = []
            for shape in shapes:
                size = 1
                for extent in shape:
                    size *= extent
                row.append(flat[start:start + size].reshape(shape))
                start += size
            found.append(row)
        return [jnp.stack([found[l][k] for l in range(depth)]) for k in range(len(shapes))]

    g_attn, g_ffn, g_group, g_decay_down = take(shared, [(width,), (width,), (HV,), (width, rank)])
    g_up, g_bias = take(local, [(rank, HK), (HK,)])
    cut = lambda a, b: jnp.stack([cats[l][:, a:b] for l in range(depth)])
    return (
        layer_output.reshape(seqs, length, width),
        input_grad.reshape(seqs, length, width),
        g_attn,
        cut(0, HK),
        cut(HK, 2 * HK),
        cut(2 * HK, 2 * HK + HV),
        cut(2 * HK + HV, 2 * HK + 2 * HV),
        g_decay_down,
        g_up,
        g_bias,
        g_group,
        jnp.stack(outs_),
        g_ffn,
        jnp.stack([ffns[l][0] for l in range(depth)]),
        jnp.stack([ffns[l][1] for l in range(depth)]),
        jnp.stack([ffns[l][2] for l in range(depth)]),
    )


def solution(mesh):
    over, across = P("dp", None, None), P(None, None, "tensor")
    deep = P(None, "tensor", None)
    return jax.shard_map(
        functools.partial(shards, mesh.shape["dp"], mesh.shape["tensor"]),
        mesh=mesh,
        in_specs=(over, P("dp"), P(), across, across, across, across, P(), across, P(None, "tensor"), P(), deep, P(), across, across, deep, over),
        out_specs=(over, over, P(), across, across, across, across, P(), across, P(None, "tensor"), P(), deep, P(), across, across, deep),
        check_vma=False,
    )
```

```python
import functools
import jax, jax.numpy as jnp
from jax import lax
from jax.experimental import pallas as pl
from jax.experimental.pallas import tpu as pltpu
from jax.sharding import PartitionSpec as P
HK, HV, CH = 128, 256, 128
group_epsilon = 1e-05
bf, f32 = jnp.bfloat16, jnp.float32
SCALE = HK ** -0.5

def nn(a, b):
    return lax.dot_general(a, b, (((1,), (0,)), ((), ())), preferred_element_type=f32)
def nt(a, b):
    return lax.dot_general(a, b, (((1,), (1,)), ((), ())), preferred_element_type=f32)
def tn(a, b):
    return lax.dot_general(a, b, (((0,), (0,)), ((), ())), preferred_element_type=f32)

def halves(a):
    top = a.astype(bf)
    return top, (a - top.astype(f32)).astype(bf)

def thirds(a):
    top = a.astype(bf)
    return (top,) + halves(a - top.astype(f32))

def sigmoid(a):
    return 1.0 / (1.0 + jnp.exp(-a))

def log_sigmoid(a):
    return jnp.minimum(a, 0.0) - jnp.log1p(jnp.exp(-jnp.abs(a)))

def steps_below(n):
    out, h = [], 1
    while h < n:
        out.append(h)
        h *= 2
    return out

def decay_sums(ld):
    n = ld.shape[0]
    rows = lax.broadcasted_iota(jnp.int32, ld.shape, 0)
    total, pre, suf = ld, ld, jnp.zeros_like(ld)
    levels = []
    for h in steps_below(n):
        upper = (rows & h) != 0
        levels.append((h, upper, jnp.exp(jnp.where(upper, pre, suf))))
        below, above = pltpu.roll(total, h, 0), pltpu.roll(total, n - h, 0)
        pre = jnp.where(upper, pre + below, pre)
        suf = jnp.where(upper, suf, suf + above)
        total = total + jnp.where(upper, below, above)
    return levels, pre, suf, total

def tile_rows(c):
    return pl.ds(c * CH, CH)

def logits_of(z, up_ref, bias_ref):
    return sum(nn(piece, up_ref[...]) for piece in thirds(z[:, 2 * HK + 2 * HV:])) + bias_ref[...]

def wide_levels(chunks):
    out, h = [], 1
    while h < chunks:
        for base in range(0, chunks, 2 * h):
            out.append((tuple(range(base, base + h)), tuple(range(base + h, base + 2 * h))))
        h *= 2
    return out

def wide_factor(c, group, is_upper, pre, suf, tot):
    arg = pre[tile_rows(c), :] if is_upper else suf[tile_rows(c), :]
    for o in group:
        if (o < c) if is_upper else (o > c):
            arg = arg + tot[pl.ds(o * 8, 1), :]
    return jnp.exp(arg)

def mixer_forward(z_ref, up_ref, bias_ref, gain_ref, gated_ref, mixed_ref, scores_ref, pre, suf, tot):
    chunks = z_ref.shape[0] // CH
    i = lax.broadcasted_iota(jnp.int32, (CH, CH), 0)
    j = lax.broadcasted_iota(jnp.int32, (CH, CH), 1)
    apart = i ^ j
    scores_ref[...] = jnp.zeros_like(scores_ref)
    for c in range(chunks):
        z = z_ref[tile_rows(c), :]
        q, k = z[:, :HK].astype(bf), z[:, HK:2 * HK].astype(bf)
        ld = log_sigmoid(logits_of(z, up_ref, bias_ref)) / 16.0
        levels, p, s, t = decay_sums(ld)
        pre[tile_rows(c), :], suf[tile_rows(c), :], tot[pl.ds(c * 8, 8), :] = p, s, t[:8]
        tile = nt(q, k)
        qf, kf = q.astype(f32), k.astype(f32)
        for h, upper, factor in levels:
            rows = (jnp.where(upper, qf, kf) * factor).astype(bf)
            tile = jnp.where(apart >= h, nt(rows, rows), tile)
        scores_ref[tile_rows(c), tile_rows(c)] = jnp.where(i >= j, tile * SCALE, 0.0).astype(bf)
    for low_group, up_group in wide_levels(chunks):
        q_rows = [(z_ref[tile_rows(c), :HK].astype(bf).astype(f32) * wide_factor(c, up_group, True, pre, suf, tot)).astype(bf) for c in up_group]
        k_rows = [(z_ref[tile_rows(c), HK:2 * HK].astype(bf).astype(f32) * wide_factor(c, low_group, False, pre, suf, tot)).astype(bf) for c in low_group]
        for a, c in enumerate(up_group):
            for b, o in enumerate(low_group):
                scores_ref[tile_rows(c), tile_rows(o)] = (nt(q_rows[a], k_rows[b]) * SCALE).astype(bf)
    for c in range(chunks):
        width = (c + 1) * CH
        mixed = nn(scores_ref[tile_rows(c), :width], z_ref[:width, 2 * HK:2 * HK + HV].astype(bf))
        mixed_ref[tile_rows(c), :] = mixed
        out_gate = z_ref[tile_rows(c), 2 * HK + HV:2 * HK + 2 * HV]
        normed = mixed * lax.rsqrt(jnp.mean(mixed * mixed, axis=-1, keepdims=True) + group_epsilon) * gain_ref[...]
        gated_ref[tile_rows(c), :] = (normed * out_gate * sigmoid(out_gate)).astype(bf)

def mixer_backward(z_ref, up_ref, bias_ref, gain_ref, mixed_ref, scores_ref, grad_ref,
                   out_ref, up_out, bias_out, gain_out, pre, suf, tot, dm_ref, dq_ref, dk_ref, flow):
    chunks = z_ref.shape[0] // CH
    i = lax.broadcasted_iota(jnp.int32, (CH, CH), 0)
    j = lax.broadcasted_iota(jnp.int32, (CH, CH), 1)
    apart = i ^ j
    rows_in = lax.broadcasted_iota(jnp.int32, (CH, HK), 0)

    @pl.when(pl.program_id(0) == 0)
    def _():
        up_out[...] = jnp.zeros_like(up_out)
        bias_out[...] = jnp.zeros_like(bias_out)
        gain_out[...] = jnp.zeros_like(gain_out)

    for c in range(chunks):
        mixed, e = mixed_ref[tile_rows(c), :], grad_ref[tile_rows(c), :]
        g = z_ref[tile_rows(c), 2 * HK + HV:2 * HK + 2 * HV]
        r = lax.rsqrt(jnp.mean(mixed * mixed, axis=-1, keepdims=True) + group_epsilon)
        sig = sigmoid(g)
        unit = mixed * r
        out_ref[tile_rows(c), 2 * HK + HV:2 * HK + 2 * HV] = (e * unit * gain_ref[...] * (sig + g * sig * (1.0 - sig))).astype(bf)
        upstream = e * g * sig
        gain_out[...] += jnp.sum(upstream * unit, axis=0, keepdims=True)
        weighted = upstream * gain_ref[...]
        dm_ref[tile_rows(c), :] = (r * (weighted - unit * jnp.mean(unit * weighted, axis=-1, keepdims=True))).astype(bf)

    def score_grad(c, o):
        return nt(dm_ref[tile_rows(c), :], z_ref[tile_rows(o), 2 * HK:2 * HK + HV].astype(bf)) * SCALE

    for c in range(chunks):
        z = z_ref[tile_rows(c), :]
        q, k = z[:, :HK].astype(bf).astype(f32), z[:, HK:2 * HK].astype(bf).astype(f32)
        ld = log_sigmoid(logits_of(z, up_ref, bias_ref)) / 16.0
        levels, p, s, t = decay_sums(ld)
        pre[tile_rows(c), :], suf[tile_rows(c), :], tot[pl.ds(c * 8, 8), :] = p, s, t[:8]
        ds = score_grad(c, c)
        diagonal = jnp.sum(jnp.where(i == j, ds, 0.0), axis=-1, keepdims=True)
        ds = jnp.where(i > j, ds, 0.0)
        both = ds + ds.T
        dq, dk = diagonal * k, diagonal * q
        fl = jnp.zeros_like(dq)
        for h, upper, factor in levels:
            rows = (jnp.where(upper, q, k) * factor).astype(bf)
            near = jnp.where((apart >= h) & (apart < 2 * h), both, 0.0).astype(bf)
            back = nn(near, rows)
            part = back * factor
            dq, dk = dq + jnp.where(upper, part, 0.0), dk + jnp.where(upper, 0.0, part)
            moved = back * rows.astype(f32)
            fl = fl + jnp.where(upper, moved, -moved)
        dq_ref[tile_rows(c), :], dk_ref[tile_rows(c), :], flow[tile_rows(c), :] = dq, dk, fl
    for low_group, up_group in wide_levels(chunks):
        q_fac = [wide_factor(c, up_group, True, pre, suf, tot) for c in up_group]
        k_fac = [wide_factor(c, low_group, False, pre, suf, tot) for c in low_group]
        q_rows = [(z_ref[tile_rows(c), :HK].astype(bf).astype(f32) * f).astype(bf) for c, f in zip(up_group, q_fac)]
        k_rows = [(z_ref[tile_rows(c), HK:2 * HK].astype(bf).astype(f32) * f).astype(bf) for c, f in zip(low_group, k_fac)]
        grads = [[score_grad(c, o).astype(bf) for o in low_group] for c in up_group]
        for a, c in enumerate(up_group):
            back = sum(nn(grads[a][b], k_rows[b]) for b in range(len(low_group)))
            dq_ref[tile_rows(c), :] += back * q_fac[a]
            flow[tile_rows(c), :] += back * q_rows[a].astype(f32)
        for b, o in enumerate(low_group):
            back = sum(tn(grads[a][b], q_rows[a]) for a in range(len(up_group)))
            dk_ref[tile_rows(o), :] += back * k_fac[b]
            flow[tile_rows(o), :] -= back * k_rows[b].astype(f32)
    later = jnp.zeros((1, HK), f32)
    for c in reversed(range(chunks)):
        out_ref[tile_rows(c), :HK] = dq_ref[tile_rows(c), :].astype(bf)
        out_ref[tile_rows(c), HK:2 * HK] = dk_ref[tile_rows(c), :].astype(bf)
        out_ref[tile_rows(c), 2 * HK:2 * HK + HV] = tn(scores_ref[pl.ds(c * CH, (chunks - c) * CH), tile_rows(c)], dm_ref[pl.ds(c * CH, (chunks - c) * CH), :]).astype(bf)
        fl = flow[tile_rows(c), :]
        for h in steps_below(CH):
            fl = fl + jnp.where(rows_in < CH - h, pltpu.roll(fl, CH - h, 0), 0.0)
        fl = fl + later
        later = fl[:1]
        z = z_ref[tile_rows(c), :]
        logits = logits_of(z, up_ref, bias_ref)
        d_logit = fl * sigmoid(-logits) / 16.0
        bias_out[...] += jnp.sum(d_logit, axis=0, keepdims=True)
        d1, d2 = halves(d_logit)
        l1, l2 = halves(z[:, 2 * HK + 2 * HV:])
        up_out[...] += tn(l1, d1) + tn(l1, d2) + tn(l2, d1)
        out_ref[tile_rows(c), 2 * HK + 2 * HV:] = (nt(d1, up_ref[...]) + nt(d2, up_ref[...])).astype(bf)

def run_forward(z, up, bias, gain, seqs):
    rows, width = z.shape
    length = rows // seqs
    whole = lambda s: (0, 0)
    mine = lambda s: (s, 0)
    return pl.pallas_call(
        mixer_forward, name="mixer_forward", grid=(seqs,),
        in_specs=[pl.BlockSpec((length, width), mine), pl.BlockSpec(up.shape, whole), pl.BlockSpec(bias.shape, whole), pl.BlockSpec(gain.shape, whole)],
        out_specs=[pl.BlockSpec((length, HV), mine), pl.BlockSpec((length, HV), mine), pl.BlockSpec((length, length), mine)],
        out_shape=[jax.ShapeDtypeStruct((rows, HV), bf), jax.ShapeDtypeStruct((rows, HV), f32), jax.ShapeDtypeStruct((rows, length), bf)],
        scratch_shapes=[pltpu.VMEM((length, HK), f32), pltpu.VMEM((length, HK), f32), pltpu.VMEM((length // CH * 8, HK), f32)],
        compiler_params=pltpu.CompilerParams(vmem_limit_bytes=40 << 20),
        cost_estimate=pl.CostEstimate(flops=rows * length * (HK + HV) * 2, bytes_accessed=rows * width * 4 + rows * HV * 6 + rows * length * 2, transcendentals=rows * HK * 10),
    )(z, up, bias, gain)

def run_backward(z, up, bias, gain, mixed, scores, grad, seqs):
    rows, width = z.shape
    length = rows // seqs
    whole = lambda s: (0, 0)
    mine = lambda s: (s, 0)
    return pl.pallas_call(
        mixer_backward, name="mixer_backward", grid=(seqs,),
        in_specs=[pl.BlockSpec((length, width), mine), pl.BlockSpec(up.shape, whole), pl.BlockSpec(bias.shape, whole), pl.BlockSpec(gain.shape, whole),
                  pl.BlockSpec((length, HV), mine), pl.BlockSpec((length, length), mine), pl.BlockSpec((length, HV), mine)],
        out_specs=[pl.BlockSpec((length, width), mine), pl.BlockSpec(up.shape, whole), pl.BlockSpec(bias.shape, whole), pl.BlockSpec(gain.shape, whole)],
        out_shape=[jax.ShapeDtypeStruct((rows, width), bf), jax.ShapeDtypeStruct(up.shape, f32), jax.ShapeDtypeStruct(bias.shape, f32), jax.ShapeDtypeStruct(gain.shape, f32)],
        scratch_shapes=[pltpu.VMEM((length, HK), f32), pltpu.VMEM((length, HK), f32), pltpu.VMEM((length // CH * 8, HK), f32), pltpu.VMEM((length, HV), bf),
                        pltpu.VMEM((length, HK), f32), pltpu.VMEM((length, HK), f32), pltpu.VMEM((length, HK), f32)],
        compiler_params=pltpu.CompilerParams(vmem_limit_bytes=40 << 20),
        cost_estimate=pl.CostEstimate(flops=rows * length * (HK + HV) * 4, bytes_accessed=rows * width * 6 + rows * HV * 8 + rows * length * 2, transcendentals=rows * HK * 10),
    )(z, up, bias, gain, mixed, scores, grad)


norm_epsilon = 1e-06
MESH = pl.DeviceIdType.MESH
VMEM_SPEC = pl.BlockSpec(memory_space=pltpu.VMEM)
ANY_SPEC = pl.BlockSpec(memory_space=pl.ANY)
DMA = pltpu.SemaphoreType.DMA


def peer_of(index, bit):
    return jnp.where((index // bit) % 2 == 0, index + bit, index - bit)


def rms_unit(h):
    return lax.rsqrt(jnp.mean(h * h, axis=-1, keepdims=True) + norm_epsilon)


def remote(src, dst, send, recv, peer):
    return pltpu.make_async_remote_copy(
        src_ref=src, dst_ref=dst, send_sem=send, recv_sem=recv, device_id=peer, device_id_type=MESH
    )


class Exchange:
    def __init__(self, kind, seqs, rows, width):
        self.kind, self.seqs, self.rows, self.width = kind, seqs, rows, width
        self.own = rows // seqs // 4

    def inputs(self):
        return {"norm": 3, "last": 3, "back": 4, "end": 4}[self.kind]

    def outputs(self):
        shapes = [jax.ShapeDtypeStruct((self.rows, self.width), f32 if self.kind == "end" else bf)]
        if self.kind in ("norm", "back"):
            shapes.append(jax.ShapeDtypeStruct((self.seqs * self.own, self.width), f32))
        if self.kind in ("back", "end"):
            shapes.append(jax.ShapeDtypeStruct((1, self.width), f32))
        return shapes

    def scratch(self):
        seqs, own, width = self.seqs, self.own, self.width
        return [
            pltpu.VMEM((seqs, 2 * own, width), f32), pltpu.VMEM((seqs, own, width), f32), pltpu.VMEM((seqs, own, width), f32),
            pltpu.VMEM((seqs, own, width), f32), pltpu.VMEM((self.rows, width), f32), DMA((5, seqs)), DMA((5, seqs)),
        ]

    def peers(self):
        me = lax.axis_index("tensor")
        return [{"tensor": peer_of(me, 1)}, {"tensor": peer_of(me, 2)}]

    def steps(self, ins, outs, scratch):
        kind, seqs, own = self.kind, self.seqs, self.own
        half, length = 2 * own, 4 * own
        partial, resid, gain = ins[:3]
        full_out = outs[0]
        first, second, passed, kept, gathered, send, recv = scratch
        me = lax.axis_index("tensor")
        core, cross = me % 2, me // 2
        core_peer, cross_peer = self.peers()

        def copy(src, dst, stage, s, peer):
            step = remote(src, dst, send.at[stage, s], recv.at[stage, s], peer)
            step.start()
            return step

        def at(s, c, x, size):
            return pl.ds(pl.multiple_of(s * length + c * half + x * own, own), size)

        def piece(x):
            return pl.ds(pl.multiple_of(x * own, own), own)

        near = [copy(partial.at[at(s, 1 - core, 0, half)], first.at[s], 0, s, core_peer) for s in range(seqs)]
        started = list(near)
        yield
        crossing, over, close, end = [], [], [], []
        for s in range(seqs):
            near[s].wait_recv()
            passed[s] = partial[at(s, core, 1 - cross, own), :] + first[s, piece(1 - cross), :]
            crossing.append(copy(passed.at[s], second.at[s], 1, s, cross_peer))
            kept[s] = partial[at(s, core, cross, own), :] + first[s, piece(cross), :]
        if kind in ("back", "end"):
            outs[-1][...] = jnp.zeros_like(outs[-1])
        for s in range(seqs):
            yield
            crossing[s].wait_recv()
            total = kept[s] + second[s]
            mine = pl.ds(s * own, own)
            if kind == "norm":
                new = resid[mine, :] + total
                outs[1][mine, :] = new
                sent = (new * rms_unit(new) * gain[...]).astype(bf).astype(f32)
            elif kind == "last":
                sent = ((resid[mine, :] + total) * gain[mine, :1]).astype(bf).astype(f32)
            else:
                h = ins[3][mine, :]
                r = rms_unit(h)
                unit = h * r
                outs[-1][...] += jnp.sum(total * unit, axis=0, keepdims=True)
                weighted = total * gain[...]
                new = resid[mine, :] + r * (weighted - unit * jnp.mean(unit * weighted, axis=-1, keepdims=True))
                if kind == "back":
                    outs[1][mine, :] = new
                    sent = new.astype(bf).astype(f32)
                else:
                    sent = new
            gathered[at(s, core, cross, own), :] = sent
            block = gathered.at[at(s, core, cross, own)]
            over.append(copy(block, block, 2, s, cross_peer))
            close.append(copy(block, block, 3, s, core_peer))
        for s in range(seqs):
            yield
            over[s].wait_recv()
            block = gathered.at[at(s, core, 1 - cross, own)]
            end.append(copy(block, block, 4, s, core_peer))
            full_out[at(s, core, 0, half), :] = gathered[at(s, core, 0, half), :].astype(full_out.dtype)
        for s in range(seqs):
            close[s].wait_recv()
            end[s].wait_recv()
            full_out[at(s, 1 - core, 0, half), :] = gathered[at(s, 1 - core, 0, half), :].astype(full_out.dtype)
        for step in started + crossing + over + close + end:
            step.wait_send()


def ring_place(index, n):
    return jnp.where(index % 2 == 0, index // 2, n - 1 - index // 2)


def ring_index(place, n):
    return jnp.where(place < n // 2, 2 * place, 2 * (n - 1 - place) + 1)


def ring_cut(shape, n):
    rows, cols = shape
    if rows % (16 * n) == 0:
        return rows // (2 * n), cols, True
    if rows % (8 * n) == 0 and cols % 256 == 0:
        return rows // n, cols // 2, False
    return None


class Ring:
    def __init__(self, n, shapes, reduce, gather, over_tensor=0):
        self.n, self.shapes, self.reduce, self.gather, self.over_tensor = n, shapes, reduce, gather, over_tensor
        self.cuts = [ring_cut(shape, n) for shape in shapes]
        self.count = len(shapes)

    def inputs(self):
        return self.count

    def in_specs(self):
        return [ANY_SPEC if self.reduce else VMEM_SPEC] * self.count

    def outputs(self):
        if self.gather:
            return [jax.ShapeDtypeStruct(shape, f32) for shape in self.shapes]
        return [jax.ShapeDtypeStruct((2, rows, cols), f32) for rows, cols, _ in self.cuts]

    def out_specs(self):
        return [ANY_SPEC if self.gather else VMEM_SPEC] * self.count

    def scratch(self):
        n, count = self.n, self.count
        found = []
        if self.reduce:
            found += [pltpu.VMEM(shape, f32) for shape in self.shapes]
            found += [pltpu.VMEM((2, n - 1, rows, cols), f32) for rows, cols, _ in self.cuts]
            found += [DMA((count,)), DMA((n - 1, count, 2)), DMA((n - 1, count, 2))]
            if self.over_tensor:
                hops = self.over_tensor - 1
                found += [pltpu.VMEM((hops,) + self.shapes[-1], f32), DMA((hops,)), DMA((hops,))]
        if self.gather:
            found += [DMA((n - 1, count, 2)), DMA((n - 1, count, 2)), DMA((count, 2))]
        return found

    def places(self):
        n = self.n
        place = ring_place(lax.axis_index("dp"), n)
        ahead = ({"dp": ring_index(lax.rem(place + 1, n), n)}, {"dp": ring_index(lax.rem(place + n - 1, n), n)})
        return (place, n - 1 - place), ahead

    def others(self):
        me = lax.axis_index("tensor")
        return [{"tensor": lax.rem(me + hop, self.over_tensor)} for hop in range(1, self.over_tensor)]

    def peers(self):
        return list(self.places()[1])

    def segment(self, a, way, index):
        rows, cols, by_rows = self.cuts[a]
        if by_rows:
            return (pl.ds(pl.multiple_of((index * 2 + way) * rows, rows), rows), pl.ds(0, cols))
        return (pl.ds(pl.multiple_of(index * rows, rows), rows), pl.ds(way * cols, cols))

    def steps(self, ins, outs, scratch):
        n, count = self.n, self.count
        spots, ahead = self.places()
        pairs = [(a, way) for a in range(count) for way in range(2)]
        scratch = list(scratch)
        sends = []
        ends = {}
        if self.reduce:
            own, slots = scratch[:count], scratch[count:2 * count]
            load, rs_send, rs_recv = scratch[2 * count:2 * count + 3]
            scratch = scratch[2 * count + 3:]

            def pass_on(a, way, step, src):
                hop = remote(src, slots[a].at[way, step], rs_send.at[step, a, way], rs_recv.at[step, a, way], ahead[way])
                hop.start()
                sends.append(hop)
                return hop

            late = count - 1 if self.over_tensor else count
            moving = {}
            for a, way in pairs:
                if a < late:
                    moving[a, way] = pass_on(a, way, 0, ins[a].at[self.segment(a, way, spots[way])])
            loads = [pltpu.make_async_copy(ins[a].at[:, pl.ds(0, self.shapes[a][1])], own[a], load.at[a]) for a in range(count)]
            for step in loads:
                step.start()
            if self.over_tensor:
                shared, peer_send, peer_recv = scratch[:3]
                scratch = scratch[3:]
                to_peers = [remote(ins[late], shared.at[hop], peer_send.at[hop], peer_recv.at[hop], other) for hop, other in enumerate(self.others())]
                for step in to_peers:
                    step.start()
            for step in loads:
                step.wait()
            if self.over_tensor:
                for step in to_peers:
                    step.wait()
                own[late][...] += sum(shared[hop] for hop in range(len(to_peers)))
                for way in range(2):
                    moving[late, way] = pass_on(late, way, 0, own[late].at[self.segment(late, way, spots[way])])
            for step in range(n - 1):
                yield
                for a, way in pairs:
                    moving[a, way].wait_recv()
                    self.add(a, way, step, lax.rem(spots[way] + (2 * n - 1) - step, n), slots[a], own[a], None if self.gather or step < n - 2 else outs[a])
                    if step < n - 2:
                        moving[a, way] = pass_on(a, way, step + 1, slots[a].at[way, step])
                    elif self.gather:
                        ends[a, way] = slots[a].at[way, step]
        else:
            for a, way in pairs:
                ends[a, way] = ins[a].at[way]
        if self.gather:
            ag_send, ag_recv, store = scratch[:3]

            def hand_on(a, way, step, src, index):
                hop = remote(src, outs[a].at[self.segment(a, way, index)], ag_send.at[step, a, way], ag_recv.at[step, a, way], ahead[way])
                hop.start()
                sends.append(hop)
                return hop

            stores, moving = [], {}
            for a, way in pairs:
                index = lax.rem(spots[way] + 1, n)
                moving[a, way] = hand_on(a, way, 0, ends[a, way], index)
                kept = pltpu.make_async_copy(ends[a, way], outs[a].at[self.segment(a, way, index)], store.at[a, way])
                kept.start()
                stores.append(kept)
            for step in range(n - 1):
                yield
                for a, way in pairs:
                    index = lax.rem(spots[way] + n - step, n)
                    moving[a, way].wait_recv()
                    if step < n - 2:
                        moving[a, way] = hand_on(a, way, step + 1, outs[a].at[self.segment(a, way, index)], index)
            for kept in stores:
                kept.wait()
        for hop in sends:
            hop.wait_send()

    def add(self, a, way, step, index, slot, own, out):
        rows, cols, _ = self.cuts[a]
        row_ds, col_ds = self.segment(a, way, index)

        @pl.loop(0, rows // 8)
        def _(block):
            here = pl.ds(pl.multiple_of(block * 8, 8), 8)
            there = pl.ds(pl.multiple_of(row_ds.start + block * 8, 8), 8)
            total = slot[way, step, here, :] + own[there, col_ds]
            if out is None:
                slot[way, step, here, :] = total
            else:
                out[way, here, :] = total


def together(parts, order, refs):
    ins, outs, scratch = [], [], []
    at = 0
    for part in parts:
        ins.append(refs[at:at + part.inputs()])
        at += part.inputs()
    for part in parts:
        outs.append(refs[at:at + len(part.outputs())])
        at += len(part.outputs())
    for part in parts:
        scratch.append(refs[at:at + len(part.scratch())])
        at += len(part.scratch())
    barrier = pltpu.get_barrier_semaphore()
    peers = [peer for part in parts for peer in part.peers()]
    for part in parts:
        if isinstance(part, Ring) and part.over_tensor:
            me = lax.axis_index("tensor")
            peers = [peer for peer in peers if "dp" in peer] + part.others()
    for peer in peers:
        pl.semaphore_signal(barrier, inc=1, device_id=peer, device_id_type=MESH)
    pl.semaphore_wait(barrier, len(peers))
    running = [part.steps(i, o, s) for part, i, o, s in zip(parts, ins, outs, scratch)]
    over = object()
    for which in order:
        if which < len(running):
            next(running[which], over)
    for steps in running:
        for _ in steps:
            pass


def run_together(name, collective, parts, order, *arrays):
    in_specs, out_specs, outs, scratch = [], [], [], []
    for part in parts:
        in_specs += part.in_specs() if isinstance(part, Ring) else [VMEM_SPEC] * part.inputs()
        out_specs += part.out_specs() if isinstance(part, Ring) else [VMEM_SPEC] * len(part.outputs())
        outs += part.outputs()
        scratch += part.scratch()

    def kernel(*refs):
        together(parts, order, refs)

    return pl.pallas_call(
        kernel, name=name, in_specs=in_specs, out_specs=out_specs, out_shape=outs, scratch_shapes=scratch,
        compiler_params=pltpu.CompilerParams(collective_id=collective, has_side_effects=True, vmem_limit_bytes=56 << 20),
        cost_estimate=pl.CostEstimate(flops=10**6, bytes_accessed=2 * 10**8, transcendentals=0),
    )(*arrays)


MIXED = (0, 1, 0, 1, 1, 0, 1, 0, 1, 0, 1, 0, 1)


def shards(
    groups, tensor, layer_input, seq_lengths, attn_gain, query_proj, key_proj, value_proj, gate_proj,
    decay_down, decay_up, decay_bias, group_gain, output_proj, ffn_gain, ffn_gate, ffn_up, ffn_down, cotangent,
):
    seqs, length, width = layer_input.shape
    depth = attn_gain.shape[0]
    rank = decay_down.shape[2]
    rows = seqs * length
    own = length // 4
    me = lax.axis_index("tensor")
    core, cross = me % 2, me // 2
    mix_cols = 2 * HK + 2 * HV
    hidden_units = ffn_gate.shape[2]
    ffn_shapes = [(width, hidden_units), (width, hidden_units), (hidden_units, width)]
    mix_shapes = [(width, mix_cols), (output_proj.shape[1], width)]
    small_shapes = [(16 * groups, HK), (8 * groups, width)]
    ringed = all(ring_cut(shape, groups) for shape in ffn_shapes + mix_shapes + small_shapes)

    def mine(full):
        parts = full.reshape(seqs, 4, own, full.shape[-1])
        return lax.dynamic_slice_in_dim(parts, core * 2 + cross, 1, axis=1).reshape(seqs * own, full.shape[-1])

    def exchange(kind, number, arrays, ring=None, ring_arrays=()):
        parts = [Exchange(kind, seqs, rows, width)] + ([ring] if ring is not None else [])
        outs = run_together("exchange_" + kind, number, parts, MIXED, *arrays, *ring_arrays)
        cut = len(parts[0].outputs())
        return outs[:cut], outs[cut:]

    keep = (jnp.arange(length, dtype=jnp.int32)[None, :] < seq_lengths[:, None]).astype(f32).reshape(rows, 1)
    keep_mine = jnp.broadcast_to(mine(keep), (seqs * own, 128))
    cat = [
        jnp.concatenate([query_proj[l], key_proj[l], value_proj[l], gate_proj[l], jnp.pad(decay_down[l], ((0, 0), (0, 128 - rank)))], axis=1)
        for l in range(depth)
    ]
    ups = [jnp.pad(decay_up[l], ((0, 128 - rank), (0, 0))) for l in range(depth)]
    hidden = layer_input.reshape(rows, width).astype(f32)
    normed = (hidden * rms_unit(hidden) * attn_gain[0]).astype(bf)
    resid = mine(hidden)
    saved = []
    for l in range(depth):
        z = nn(normed, cat[l])
        gated, mixed, scores = run_forward(z, ups[l], decay_bias[l:l + 1], group_gain[l:l + 1], seqs)
        entry = resid
        (normed_ffn, middle), _ = exchange("norm", 1, (nn(gated, output_proj[l]), resid, ffn_gain[l:l + 1]))
        gate_act, up_act = nn(normed_ffn, ffn_gate[l]), nn(normed_ffn, ffn_up[l])
        inner = (gate_act * sigmoid(gate_act) * up_act).astype(bf)
        out = nn(inner, ffn_down[l])
        saved.append((entry, normed, z, gated, mixed, scores, middle, normed_ffn, gate_act, up_act, inner))
        if l + 1 < depth:
            (normed, resid), _ = exchange("norm", 1, (out, middle, attn_gain[l + 1:l + 2]))
    final = (out, middle, keep_mine)
    upstream = cotangent.reshape(rows, width).astype(f32) * keep
    resid = mine(upstream)
    ffn_grad = upstream.astype(bf)
    smalls, mix_terms, ffn_sums, mix_sums = [None] * depth, [None] * depth, [None] * depth, [None] * depth
    for l in reversed(range(depth)):
        entry, normed, z, gated, mixed, scores, middle, normed_ffn, gate_act, up_act, inner = saved[l]
        inner_grad = nt(ffn_grad, ffn_down[l])
        sig = sigmoid(gate_act)
        gate_low = (inner_grad * up_act * sig * (1.0 + gate_act * (1.0 - sig))).astype(bf)
        up_low = (inner_grad * gate_act * sig).astype(bf)
        ffn_terms = (tn(normed_ffn, gate_low), tn(normed_ffn, up_low), tn(inner, ffn_grad))
        scatter = Ring(groups, ffn_shapes, True, False) if ringed else None
        (mix_grad, resid, ffn_gain_grad), pieces = exchange(
            "back", 2, (nt(gate_low, ffn_gate[l]) + nt(up_low, ffn_up[l]), resid, ffn_gain[l:l + 1], middle), scatter, ffn_terms if ringed else ())
        gated_grad = nt(mix_grad, output_proj[l])
        low, up_grad, bias_grad, group_grad = run_backward(z, ups[l], decay_bias[l:l + 1], group_gain[l:l + 1], mixed, scores, gated_grad, seqs)
        mix_terms[l] = (tn(normed, low), tn(gated, mix_grad))
        back = nt(low, cat[l])
        collect = Ring(groups, ffn_shapes, False, True) if ringed else None
        if l > 0:
            mix_sums[l] = lax.psum((mix_terms[l][0][:, :mix_cols], mix_terms[l][1]), "dp")
            (ffn_grad, resid, attn_gain_grad), full = exchange("back", 3, (back, resid, attn_gain[l:l + 1], entry), collect, pieces)
        else:
            (input_grad, attn_gain_grad), full = exchange("end", 4, (back, resid, attn_gain[l:l + 1], entry), collect, pieces)
        ffn_sums[l] = full if ringed else lax.psum(ffn_terms, "dp")
        down_grad = tn(low[:, mix_cols:mix_cols + rank], normed)
        smalls[l] = ((up_grad[:rank], bias_grad), (down_grad, attn_gain_grad, ffn_gain_grad, jnp.pad(group_grad, ((0, 0), (0, width - HV)))))
    local = jnp.concatenate([part for l in range(depth) for part in smalls[l][0]])
    local = jnp.pad(local, ((0, 16 * groups - local.shape[0]), (0, 0)))
    shared = jnp.concatenate([part for l in range(depth) for part in smalls[l][1]])
    shared = jnp.pad(shared, ((0, 8 * groups - shared.shape[0]), (0, 0)))
    if ringed:
        parts = [Exchange("last", seqs, rows, width), Ring(groups, mix_shapes + small_shapes, True, True, tensor)]
        layer_output, *mix_sums[0], local, shared = run_together("ring_sum", 5, parts, MIXED, *final, *mix_terms[0], local, shared)
    else:
        (layer_output,), _ = exchange("last", 6, final)
        *mix_sums[0], local = lax.psum((mix_terms[0][0][:, :mix_cols], mix_terms[0][1], local), "dp")
        shared = lax.psum(shared, ("dp", "tensor"))

    def split(flat, heights):
        found, start = [[] for _ in heights], 0
        for l in range(depth):
            for k, height in enumerate(heights):
                found[k].append(flat[start:start + height])
                start += height
        return [jnp.stack(rows_of) for rows_of in found]

    g_up, g_bias = split(local, (rank, 1))
    g_down, g_attn, g_ffn, g_group = split(shared, (rank, 1, 1, 1))
    cut = lambda a, b: jnp.stack([mix_sums[l][0][:, a:b] for l in range(depth)])
    pick = lambda sums, k: jnp.stack([sums[l][k] for l in range(depth)])
    return (
        layer_output.reshape(seqs, length, width),
        input_grad.reshape(seqs, length, width),
        g_attn[:, 0],
        cut(0, HK),
        cut(HK, 2 * HK),
        cut(2 * HK, 2 * HK + HV),
        cut(2 * HK + HV, mix_cols),
        g_down.transpose(0, 2, 1),
        g_up,
        g_bias[:, 0],
        g_group[:, 0, :HV],
        pick(mix_sums, 1),
        g_ffn[:, 0],
        pick(ffn_sums, 0),
        pick(ffn_sums, 1),
        pick(ffn_sums, 2),
    )


def solution(mesh):
    over, across = P("dp", None, None), P(None, None, "tensor")
    deep = P(None, "tensor", None)
    return jax.shard_map(
        functools.partial(shards, mesh.shape["dp"], mesh.shape["tensor"]),
        mesh=mesh,
        in_specs=(over, P("dp"), P(), across, across, across, across, P(), across, P(None, "tensor"), P(), deep, P(), across, across, deep, over),
        out_specs=(over, over, P(), across, across, across, across, P(), across, P(None, "tensor"), P(), deep, P(), across, across, deep),
        check_vma=False,
    )
```

```python
import functools
import jax, jax.numpy as jnp
from jax import lax
from jax.experimental import pallas as pl
from jax.experimental.pallas import tpu as pltpu
from jax.sharding import PartitionSpec as P
HK, HV, CH = 128, 256, 128
group_epsilon = 1e-05
bf, f32 = jnp.bfloat16, jnp.float32
SCALE = HK ** -0.5

def nn(a, b):
    return lax.dot_general(a, b, (((1,), (0,)), ((), ())), preferred_element_type=f32)
def nt(a, b):
    return lax.dot_general(a, b, (((1,), (1,)), ((), ())), preferred_element_type=f32)
def tn(a, b):
    return lax.dot_general(a, b, (((0,), (0,)), ((), ())), preferred_element_type=f32)

def halves(a):
    top = a.astype(bf)
    return top, (a - top.astype(f32)).astype(bf)

def thirds(a):
    top = a.astype(bf)
    return (top,) + halves(a - top.astype(f32))

def sigmoid(a):
    return 1.0 / (1.0 + jnp.exp(-a))

def log_sigmoid(a):
    return jnp.minimum(a, 0.0) - jnp.log1p(jnp.exp(-jnp.abs(a)))

def steps_below(n):
    out, h = [], 1
    while h < n:
        out.append(h)
        h *= 2
    return out

def decay_sums(ld):
    n = ld.shape[0]
    rows = lax.broadcasted_iota(jnp.int32, ld.shape, 0)
    total, pre, suf = ld, ld, jnp.zeros_like(ld)
    levels = []
    for h in steps_below(n):
        upper = (rows & h) != 0
        levels.append((h, upper, jnp.exp(jnp.where(upper, pre, suf))))
        below, above = pltpu.roll(total, h, 0), pltpu.roll(total, n - h, 0)
        pre = jnp.where(upper, pre + below, pre)
        suf = jnp.where(upper, suf, suf + above)
        total = total + jnp.where(upper, below, above)
    return levels, pre, suf, total

def tile_rows(c):
    return pl.ds(c * CH, CH)

def logits_of(z, up_ref, bias_ref):
    return sum(nn(piece, up_ref[...]) for piece in thirds(z[:, 2 * HK + 2 * HV:])) + bias_ref[...]

def wide_levels(chunks):
    out, h = [], 1
    while h < chunks:
        for base in range(0, chunks, 2 * h):
            out.append((tuple(range(base, base + h)), tuple(range(base + h, base + 2 * h))))
        h *= 2
    return out

def wide_factor(c, group, is_upper, pre, suf, tot):
    arg = pre[tile_rows(c), :] if is_upper else suf[tile_rows(c), :]
    for o in group:
        if (o < c) if is_upper else (o > c):
            arg = arg + tot[pl.ds(o * 8, 1), :]
    return jnp.exp(arg)

def mixer_forward(z_ref, up_ref, bias_ref, gain_ref, gated_ref, mixed_ref, scores_ref, pre, suf, tot):
    chunks = z_ref.shape[0] // CH
    i = lax.broadcasted_iota(jnp.int32, (CH, CH), 0)
    j = lax.broadcasted_iota(jnp.int32, (CH, CH), 1)
    apart = i ^ j
    scores_ref[...] = jnp.zeros_like(scores_ref)
    for c in range(chunks):
        z = z_ref[tile_rows(c), :]
        q, k = z[:, :HK].astype(bf), z[:, HK:2 * HK].astype(bf)
        ld = log_sigmoid(logits_of(z, up_ref, bias_ref)) / 16.0
        levels, p, s, t = decay_sums(ld)
        pre[tile_rows(c), :], suf[tile_rows(c), :], tot[pl.ds(c * 8, 8), :] = p, s, t[:8]
        tile = nt(q, k)
        qf, kf = q.astype(f32), k.astype(f32)
        for h, upper, factor in levels:
            rows = (jnp.where(upper, qf, kf) * factor).astype(bf)
            tile = jnp.where(apart >= h, nt(rows, rows), tile)
        scores_ref[tile_rows(c), tile_rows(c)] = jnp.where(i >= j, tile * SCALE, 0.0).astype(bf)
    for low_group, up_group in wide_levels(chunks):
        q_rows = [(z_ref[tile_rows(c), :HK].astype(bf).astype(f32) * wide_factor(c, up_group, True, pre, suf, tot)).astype(bf) for c in up_group]
        k_rows = [(z_ref[tile_rows(c), HK:2 * HK].astype(bf).astype(f32) * wide_factor(c, low_group, False, pre, suf, tot)).astype(bf) for c in low_group]
        for a, c in enumerate(up_group):
            for b, o in enumerate(low_group):
                scores_ref[tile_rows(c), tile_rows(o)] = (nt(q_rows[a], k_rows[b]) * SCALE).astype(bf)
    for c in range(chunks):
        width = (c + 1) * CH
        mixed = nn(scores_ref[tile_rows(c), :width], z_ref[:width, 2 * HK:2 * HK + HV].astype(bf))
        mixed_ref[tile_rows(c), :] = mixed
        out_gate = z_ref[tile_rows(c), 2 * HK + HV:2 * HK + 2 * HV]
        normed = mixed * lax.rsqrt(jnp.mean(mixed * mixed, axis=-1, keepdims=True) + group_epsilon) * gain_ref[...]
        gated_ref[tile_rows(c), :] = (normed * out_gate * sigmoid(out_gate)).astype(bf)

def mixer_backward(z_ref, up_ref, bias_ref, gain_ref, mixed_ref, scores_ref, grad_ref,
                   out_ref, up_out, bias_out, gain_out, pre, suf, tot, dm_ref, dq_ref, dk_ref, flow):
    chunks = z_ref.shape[0] // CH
    i = lax.broadcasted_iota(jnp.int32, (CH, CH), 0)
    j = lax.broadcasted_iota(jnp.int32, (CH, CH), 1)
    apart = i ^ j
    rows_in = lax.broadcasted_iota(jnp.int32, (CH, HK), 0)

    @pl.when(pl.program_id(0) == 0)
    def _():
        up_out[...] = jnp.zeros_like(up_out)
        bias_out[...] = jnp.zeros_like(bias_out)
        gain_out[...] = jnp.zeros_like(gain_out)

    for c in range(chunks):
        mixed, e = mixed_ref[tile_rows(c), :], grad_ref[tile_rows(c), :]
        g = z_ref[tile_rows(c), 2 * HK + HV:2 * HK + 2 * HV]
        r = lax.rsqrt(jnp.mean(mixed * mixed, axis=-1, keepdims=True) + group_epsilon)
        sig = sigmoid(g)
        unit = mixed * r
        out_ref[tile_rows(c), 2 * HK + HV:2 * HK + 2 * HV] = (e * unit * gain_ref[...] * (sig + g * sig * (1.0 - sig))).astype(bf)
        upstream = e * g * sig
        gain_out[...] += jnp.sum(upstream * unit, axis=0, keepdims=True)
        weighted = upstream * gain_ref[...]
        dm_ref[tile_rows(c), :] = (r * (weighted - unit * jnp.mean(unit * weighted, axis=-1, keepdims=True))).astype(bf)

    def score_grad(c, o):
        return nt(dm_ref[tile_rows(c), :], z_ref[tile_rows(o), 2 * HK:2 * HK + HV].astype(bf)) * SCALE

    for c in range(chunks):
        z = z_ref[tile_rows(c), :]
        q, k = z[:, :HK].astype(bf).astype(f32), z[:, HK:2 * HK].astype(bf).astype(f32)
        ld = log_sigmoid(logits_of(z, up_ref, bias_ref)) / 16.0
        levels, p, s, t = decay_sums(ld)
        pre[tile_rows(c), :], suf[tile_rows(c), :], tot[pl.ds(c * 8, 8), :] = p, s, t[:8]
        ds = score_grad(c, c)
        diagonal = jnp.sum(jnp.where(i == j, ds, 0.0), axis=-1, keepdims=True)
        ds = jnp.where(i > j, ds, 0.0)
        both = ds + ds.T
        dq, dk = diagonal * k, diagonal * q
        fl = jnp.zeros_like(dq)
        for h, upper, factor in levels:
            rows = (jnp.where(upper, q, k) * factor).astype(bf)
            near = jnp.where((apart >= h) & (apart < 2 * h), both, 0.0).astype(bf)
            back = nn(near, rows)
            part = back * factor
            dq, dk = dq + jnp.where(upper, part, 0.0), dk + jnp.where(upper, 0.0, part)
            moved = back * rows.astype(f32)
            fl = fl + jnp.where(upper, moved, -moved)
        dq_ref[tile_rows(c), :], dk_ref[tile_rows(c), :], flow[tile_rows(c), :] = dq, dk, fl
    for low_group, up_group in wide_levels(chunks):
        q_fac = [wide_factor(c, up_group, True, pre, suf, tot) for c in up_group]
        k_fac = [wide_factor(c, low_group, False, pre, suf, tot) for c in low_group]
        q_rows = [(z_ref[tile_rows(c), :HK].astype(bf).astype(f32) * f).astype(bf) for c, f in zip(up_group, q_fac)]
        k_rows = [(z_ref[tile_rows(c), HK:2 * HK].astype(bf).astype(f32) * f).astype(bf) for c, f in zip(low_group, k_fac)]
        grads = [[score_grad(c, o).astype(bf) for o in low_group] for c in up_group]
        for a, c in enumerate(up_group):
            back = sum(nn(grads[a][b], k_rows[b]) for b in range(len(low_group)))
            dq_ref[tile_rows(c), :] += back * q_fac[a]
            flow[tile_rows(c), :] += back * q_rows[a].astype(f32)
        for b, o in enumerate(low_group):
            back = sum(tn(grads[a][b], q_rows[a]) for a in range(len(up_group)))
            dk_ref[tile_rows(o), :] += back * k_fac[b]
            flow[tile_rows(o), :] -= back * k_rows[b].astype(f32)
    later = jnp.zeros((1, HK), f32)
    for c in reversed(range(chunks)):
        out_ref[tile_rows(c), :HK] = dq_ref[tile_rows(c), :].astype(bf)
        out_ref[tile_rows(c), HK:2 * HK] = dk_ref[tile_rows(c), :].astype(bf)
        out_ref[tile_rows(c), 2 * HK:2 * HK + HV] = tn(scores_ref[pl.ds(c * CH, (chunks - c) * CH), tile_rows(c)], dm_ref[pl.ds(c * CH, (chunks - c) * CH), :]).astype(bf)
        fl = flow[tile_rows(c), :]
        for h in steps_below(CH):
            fl = fl + jnp.where(rows_in < CH - h, pltpu.roll(fl, CH - h, 0), 0.0)
        fl = fl + later
        later = fl[:1]
        z = z_ref[tile_rows(c), :]
        logits = logits_of(z, up_ref, bias_ref)
        d_logit = fl * sigmoid(-logits) / 16.0
        bias_out[...] += jnp.sum(d_logit, axis=0, keepdims=True)
        d1, d2 = halves(d_logit)
        l1, l2 = halves(z[:, 2 * HK + 2 * HV:])
        up_out[...] += tn(l1, d1) + tn(l1, d2) + tn(l2, d1)
        out_ref[tile_rows(c), 2 * HK + 2 * HV:] = (nt(d1, up_ref[...]) + nt(d2, up_ref[...])).astype(bf)

def run_forward(z, up, bias, gain, seqs):
    rows, width = z.shape
    length = rows // seqs
    whole = lambda s: (0, 0)
    mine = lambda s: (s, 0)
    return pl.pallas_call(
        mixer_forward, name="mixer_forward", grid=(seqs,),
        in_specs=[pl.BlockSpec((length, width), mine), pl.BlockSpec(up.shape, whole), pl.BlockSpec(bias.shape, whole), pl.BlockSpec(gain.shape, whole)],
        out_specs=[pl.BlockSpec((length, HV), mine), pl.BlockSpec((length, HV), mine), pl.BlockSpec((length, length), mine)],
        out_shape=[jax.ShapeDtypeStruct((rows, HV), bf), jax.ShapeDtypeStruct((rows, HV), f32), jax.ShapeDtypeStruct((rows, length), bf)],
        scratch_shapes=[pltpu.VMEM((length, HK), f32), pltpu.VMEM((length, HK), f32), pltpu.VMEM((length // CH * 8, HK), f32)],
        compiler_params=pltpu.CompilerParams(vmem_limit_bytes=40 << 20),
        cost_estimate=pl.CostEstimate(flops=rows * length * (HK + HV) * 2, bytes_accessed=rows * width * 4 + rows * HV * 6 + rows * length * 2, transcendentals=rows * HK * 10),
    )(z, up, bias, gain)

def run_backward(z, up, bias, gain, mixed, scores, grad, seqs):
    rows, width = z.shape
    length = rows // seqs
    whole = lambda s: (0, 0)
    mine = lambda s: (s, 0)
    return pl.pallas_call(
        mixer_backward, name="mixer_backward", grid=(seqs,),
        in_specs=[pl.BlockSpec((length, width), mine), pl.BlockSpec(up.shape, whole), pl.BlockSpec(bias.shape, whole), pl.BlockSpec(gain.shape, whole),
                  pl.BlockSpec((length, HV), mine), pl.BlockSpec((length, length), mine), pl.BlockSpec((length, HV), mine)],
        out_specs=[pl.BlockSpec((length, width), mine), pl.BlockSpec(up.shape, whole), pl.BlockSpec(bias.shape, whole), pl.BlockSpec(gain.shape, whole)],
        out_shape=[jax.ShapeDtypeStruct((rows, width), bf), jax.ShapeDtypeStruct(up.shape, f32), jax.ShapeDtypeStruct(bias.shape, f32), jax.ShapeDtypeStruct(gain.shape, f32)],
        scratch_shapes=[pltpu.VMEM((length, HK), f32), pltpu.VMEM((length, HK), f32), pltpu.VMEM((length // CH * 8, HK), f32), pltpu.VMEM((length, HV), bf),
                        pltpu.VMEM((length, HK), f32), pltpu.VMEM((length, HK), f32), pltpu.VMEM((length, HK), f32)],
        compiler_params=pltpu.CompilerParams(vmem_limit_bytes=40 << 20),
        cost_estimate=pl.CostEstimate(flops=rows * length * (HK + HV) * 4, bytes_accessed=rows * width * 6 + rows * HV * 8 + rows * length * 2, transcendentals=rows * HK * 10),
    )(z, up, bias, gain, mixed, scores, grad)


norm_epsilon = 1e-06
MESH = pl.DeviceIdType.MESH
VMEM_SPEC = pl.BlockSpec(memory_space=pltpu.VMEM)
ANY_SPEC = pl.BlockSpec(memory_space=pl.ANY)
DMA = pltpu.SemaphoreType.DMA


def peer_of(index, bit):
    return jnp.where((index // bit) % 2 == 0, index + bit, index - bit)


def rms_unit(h):
    return lax.rsqrt(jnp.mean(h * h, axis=-1, keepdims=True) + norm_epsilon)


def remote(src, dst, send, recv, peer):
    return pltpu.make_async_remote_copy(
        src_ref=src, dst_ref=dst, send_sem=send, recv_sem=recv, device_id=peer, device_id_type=MESH
    )


class Exchange:
    def __init__(self, kind, seqs, rows, width):
        self.kind, self.seqs, self.rows, self.width = kind, seqs, rows, width
        self.own = rows // seqs // 4

    def inputs(self):
        return {"norm": 3, "last": 3, "back": 4, "end": 4}[self.kind]

    def outputs(self):
        shapes = [jax.ShapeDtypeStruct((self.rows, self.width), f32 if self.kind == "end" else bf)]
        if self.kind in ("norm", "back"):
            shapes.append(jax.ShapeDtypeStruct((self.seqs * self.own, self.width), f32))
        if self.kind in ("back", "end"):
            shapes.append(jax.ShapeDtypeStruct((1, self.width), f32))
        return shapes

    def scratch(self):
        seqs, own, width = self.seqs, self.own, self.width
        return [
            pltpu.VMEM((seqs, 2 * own, width), f32), pltpu.VMEM((seqs, own, width), f32), pltpu.VMEM((seqs, own, width), f32),
            pltpu.VMEM((seqs, own, width), f32), pltpu.VMEM((self.rows, width), f32), DMA((5, seqs)), DMA((5, seqs)),
        ]

    def peers(self):
        me = lax.axis_index("tensor")
        return [{"tensor": peer_of(me, 1)}, {"tensor": peer_of(me, 2)}]

    def steps(self, ins, outs, scratch):
        kind, seqs, own = self.kind, self.seqs, self.own
        half, length = 2 * own, 4 * own
        partial, resid, gain = ins[:3]
        full_out = outs[0]
        first, second, passed, kept, gathered, send, recv = scratch
        me = lax.axis_index("tensor")
        core, cross = me % 2, me // 2
        core_peer, cross_peer = self.peers()

        def copy(src, dst, stage, s, peer):
            step = remote(src, dst, send.at[stage, s], recv.at[stage, s], peer)
            step.start()
            return step

        def at(s, c, x, size):
            return pl.ds(pl.multiple_of(s * length + c * half + x * own, own), size)

        def piece(x):
            return pl.ds(pl.multiple_of(x * own, own), own)

        near = [copy(partial.at[at(s, 1 - core, 0, half)], first.at[s], 0, s, core_peer) for s in range(seqs)]
        started = list(near)
        yield
        crossing, over, close, end = [], [], [], []
        for s in range(seqs):
            near[s].wait_recv()
            passed[s] = partial[at(s, core, 1 - cross, own), :] + first[s, piece(1 - cross), :]
            crossing.append(copy(passed.at[s], second.at[s], 1, s, cross_peer))
            kept[s] = partial[at(s, core, cross, own), :] + first[s, piece(cross), :]
        if kind in ("back", "end"):
            outs[-1][...] = jnp.zeros_like(outs[-1])
        for s in range(seqs):
            yield
            crossing[s].wait_recv()
            total = kept[s] + second[s]
            mine = pl.ds(s * own, own)
            if kind == "norm":
                new = resid[mine, :] + total
                outs[1][mine, :] = new
                sent = (new * rms_unit(new) * gain[...]).astype(bf).astype(f32)
            elif kind == "last":
                sent = ((resid[mine, :] + total) * gain[mine, :1]).astype(bf).astype(f32)
            else:
                h = ins[3][mine, :]
                r = rms_unit(h)
                unit = h * r
                outs[-1][...] += jnp.sum(total * unit, axis=0, keepdims=True)
                weighted = total * gain[...]
                new = resid[mine, :] + r * (weighted - unit * jnp.mean(unit * weighted, axis=-1, keepdims=True))
                if kind == "back":
                    outs[1][mine, :] = new
                    sent = new.astype(bf).astype(f32)
                else:
                    sent = new
            gathered[at(s, core, cross, own), :] = sent
            block = gathered.at[at(s, core, cross, own)]
            over.append(copy(block, block, 2, s, cross_peer))
            close.append(copy(block, block, 3, s, core_peer))
        for s in range(seqs):
            yield
            over[s].wait_recv()
            block = gathered.at[at(s, core, 1 - cross, own)]
            end.append(copy(block, block, 4, s, core_peer))
            full_out[at(s, core, 0, half), :] = gathered[at(s, core, 0, half), :].astype(full_out.dtype)
        for s in range(seqs):
            close[s].wait_recv()
            end[s].wait_recv()
            full_out[at(s, 1 - core, 0, half), :] = gathered[at(s, 1 - core, 0, half), :].astype(full_out.dtype)
        for step in started + crossing + over + close + end:
            step.wait_send()


def ring_place(index, n):
    return jnp.where(index % 2 == 0, index // 2, n - 1 - index // 2)


def ring_index(place, n):
    return jnp.where(place < n // 2, 2 * place, 2 * (n - 1 - place) + 1)


def ring_cut(shape, n):
    rows, cols = shape
    if rows % (16 * n) == 0:
        return rows // (2 * n), cols, True
    if rows % (8 * n) == 0 and cols % 256 == 0:
        return rows // n, cols // 2, False
    return None


class Ring:
    def __init__(self, n, shapes, reduce, gather, over_tensor=0):
        self.n, self.shapes, self.reduce, self.gather, self.over_tensor = n, shapes, reduce, gather, over_tensor
        self.cuts = [ring_cut(shape, n) for shape in shapes]
        self.count = len(shapes)

    def inputs(self):
        return self.count

    def in_specs(self):
        return [ANY_SPEC if self.reduce else VMEM_SPEC] * self.count

    def outputs(self):
        if self.gather:
            return [jax.ShapeDtypeStruct(shape, f32) for shape in self.shapes]
        return [jax.ShapeDtypeStruct((2, rows, cols), f32) for rows, cols, _ in self.cuts]

    def out_specs(self):
        return [ANY_SPEC if self.gather else VMEM_SPEC] * self.count

    def scratch(self):
        n, count = self.n, self.count
        found = []
        if self.reduce:
            found += [pltpu.VMEM(shape, f32) for shape in self.shapes]
            found += [pltpu.VMEM((2, n - 1, rows, cols), f32) for rows, cols, _ in self.cuts]
            found += [DMA((count,)), DMA((n - 1, count, 2)), DMA((n - 1, count, 2))]
            if self.over_tensor:
                hops = self.over_tensor - 1
                found += [pltpu.VMEM((hops,) + self.shapes[-1], f32), DMA((hops,)), DMA((hops,))]
        if self.gather:
            found += [DMA((n - 1, count, 2)), DMA((n - 1, count, 2)), DMA((count, 2))]
        return found

    def places(self):
        n = self.n
        place = ring_place(lax.axis_index("dp"), n)
        ahead = ({"dp": ring_index(lax.rem(place + 1, n), n)}, {"dp": ring_index(lax.rem(place + n - 1, n), n)})
        return (place, n - 1 - place), ahead

    def others(self):
        me = lax.axis_index("tensor")
        return [{"tensor": lax.rem(me + hop, self.over_tensor)} for hop in range(1, self.over_tensor)]

    def peers(self):
        return list(self.places()[1])

    def segment(self, a, way, index):
        rows, cols, by_rows = self.cuts[a]
        if by_rows:
            return (pl.ds(pl.multiple_of((index * 2 + way) * rows, rows), rows), pl.ds(0, cols))
        return (pl.ds(pl.multiple_of(index * rows, rows), rows), pl.ds(way * cols, cols))

    def steps(self, ins, outs, scratch):
        n, count = self.n, self.count
        spots, ahead = self.places()
        pairs = [(a, way) for a in range(count) for way in range(2)]
        scratch = list(scratch)
        sends = []
        ends = {}
        if self.reduce:
            own, slots = scratch[:count], scratch[count:2 * count]
            load, rs_send, rs_recv = scratch[2 * count:2 * count + 3]
            scratch = scratch[2 * count + 3:]

            def pass_on(a, way, step, src):
                hop = remote(src, slots[a].at[way, step], rs_send.at[step, a, way], rs_recv.at[step, a, way], ahead[way])
                hop.start()
                sends.append(hop)
                return hop

            late = count - 1 if self.over_tensor else count
            moving = {}
            for a, way in pairs:
                if a < late:
                    moving[a, way] = pass_on(a, way, 0, ins[a].at[self.segment(a, way, spots[way])])
            loads = [pltpu.make_async_copy(ins[a].at[:, pl.ds(0, self.shapes[a][1])], own[a], load.at[a]) for a in range(count)]
            for step in loads:
                step.start()
            if self.over_tensor:
                shared, peer_send, peer_recv = scratch[:3]
                scratch = scratch[3:]
                to_peers = [remote(ins[late], shared.at[hop], peer_send.at[hop], peer_recv.at[hop], other) for hop, other in enumerate(self.others())]
                for step in to_peers:
                    step.start()
            for step in loads:
                step.wait()
            if self.over_tensor:
                for step in to_peers:
                    step.wait()
                own[late][...] += sum(shared[hop] for hop in range(len(to_peers)))
                for way in range(2):
                    moving[late, way] = pass_on(late, way, 0, own[late].at[self.segment(late, way, spots[way])])
            for step in range(n - 1):
                yield
                for a, way in pairs:
                    moving[a, way].wait_recv()
                    self.add(a, way, step, lax.rem(spots[way] + (2 * n - 1) - step, n), slots[a], own[a], None if self.gather or step < n - 2 else outs[a])
                    if step < n - 2:
                        moving[a, way] = pass_on(a, way, step + 1, slots[a].at[way, step])
                    elif self.gather:
                        ends[a, way] = slots[a].at[way, step]
        else:
            for a, way in pairs:
                ends[a, way] = ins[a].at[way]
        if self.gather:
            ag_send, ag_recv, store = scratch[:3]

            def hand_on(a, way, step, src, index):
                hop = remote(src, outs[a].at[self.segment(a, way, index)], ag_send.at[step, a, way], ag_recv.at[step, a, way], ahead[way])
                hop.start()
                sends.append(hop)
                return hop

            stores, moving = [], {}
            for a, way in pairs:
                index = lax.rem(spots[way] + 1, n)
                moving[a, way] = hand_on(a, way, 0, ends[a, way], index)
                kept = pltpu.make_async_copy(ends[a, way], outs[a].at[self.segment(a, way, index)], store.at[a, way])
                kept.start()
                stores.append(kept)
            for step in range(n - 1):
                yield
                for a, way in pairs:
                    index = lax.rem(spots[way] + n - step, n)
                    moving[a, way].wait_recv()
                    if step < n - 2:
                        moving[a, way] = hand_on(a, way, step + 1, outs[a].at[self.segment(a, way, index)], index)
            for kept in stores:
                kept.wait()
        for hop in sends:
            hop.wait_send()

    def add(self, a, way, step, index, slot, own, out):
        rows, cols, _ = self.cuts[a]
        row_ds, col_ds = self.segment(a, way, index)

        @pl.loop(0, rows // 8)
        def _(block):
            here = pl.ds(pl.multiple_of(block * 8, 8), 8)
            there = pl.ds(pl.multiple_of(row_ds.start + block * 8, 8), 8)
            total = slot[way, step, here, :] + own[there, col_ds]
            if out is None:
                slot[way, step, here, :] = total
            else:
                out[way, here, :] = total


def together(parts, order, refs):
    ins, outs, scratch = [], [], []
    at = 0
    for part in parts:
        ins.append(refs[at:at + part.inputs()])
        at += part.inputs()
    for part in parts:
        outs.append(refs[at:at + len(part.outputs())])
        at += len(part.outputs())
    for part in parts:
        scratch.append(refs[at:at + len(part.scratch())])
        at += len(part.scratch())
    barrier = pltpu.get_barrier_semaphore()
    rings = [part for part in parts if isinstance(part, Ring)]
    wide = [part for part in rings if part.over_tensor]
    peers = rings[0].peers() if rings else []
    peers = peers + (wide[0].others() if wide else parts[0].peers())
    for peer in peers:
        pl.semaphore_signal(barrier, inc=1, device_id=peer, device_id_type=MESH)
    pl.semaphore_wait(barrier, len(peers))
    running = [part.steps(i, o, s) for part, i, o, s in zip(parts, ins, outs, scratch)]
    over = object()
    for which in order:
        if which < len(running):
            next(running[which], over)
    for steps in running:
        for _ in steps:
            pass


def run_together(name, collective, parts, order, *arrays):
    in_specs, out_specs, outs, scratch = [], [], [], []
    for part in parts:
        in_specs += part.in_specs() if isinstance(part, Ring) else [VMEM_SPEC] * part.inputs()
        out_specs += part.out_specs() if isinstance(part, Ring) else [VMEM_SPEC] * len(part.outputs())
        outs += part.outputs()
        scratch += part.scratch()

    def kernel(*refs):
        together(parts, order, refs)

    return pl.pallas_call(
        kernel, name=name, in_specs=in_specs, out_specs=out_specs, out_shape=outs, scratch_shapes=scratch,
        compiler_params=pltpu.CompilerParams(collective_id=collective, has_side_effects=True, vmem_limit_bytes=56 << 20),
        cost_estimate=pl.CostEstimate(flops=10**6, bytes_accessed=2 * 10**8, transcendentals=0),
    )(*arrays)


MIXED = (0, 1, 0, 1, 0, 1, 0, 1, 0, 1, 0, 1)
LAST = (1, 2, 0, 1, 2, 0) * 5 + (1, 2) * 14


def shards(
    groups, tensor, layer_input, seq_lengths, attn_gain, query_proj, key_proj, value_proj, gate_proj,
    decay_down, decay_up, decay_bias, group_gain, output_proj, ffn_gain, ffn_gate, ffn_up, ffn_down, cotangent,
):
    seqs, length, width = layer_input.shape
    depth = attn_gain.shape[0]
    rank = decay_down.shape[2]
    rows = seqs * length
    own = length // 4
    me = lax.axis_index("tensor")
    core, cross = me % 2, me // 2
    mix_cols = 2 * HK + 2 * HV
    hidden_units = ffn_gate.shape[2]
    ffn_shapes = [(hidden_units, width)] * 3
    mix_shapes = [(width, mix_cols), (output_proj.shape[1], width)]
    small_shapes = [(16 * groups, HK), (8 * groups, width)]
    ringed = all(ring_cut(shape, groups) for shape in ffn_shapes + mix_shapes + small_shapes)

    def mine(full):
        parts = full.reshape(seqs, 4, own, full.shape[-1])
        return lax.dynamic_slice_in_dim(parts, core * 2 + cross, 1, axis=1).reshape(seqs * own, full.shape[-1])

    def exchange(kind, number, arrays, ring=None, ring_arrays=()):
        parts = [Exchange(kind, seqs, rows, width)] + ([ring] if ring is not None else [])
        outs = run_together("exchange_" + kind, number, parts, MIXED, *arrays, *ring_arrays)
        cut = len(parts[0].outputs())
        return outs[:cut], outs[cut:]

    keep = (jnp.arange(length, dtype=jnp.int32)[None, :] < seq_lengths[:, None]).astype(f32).reshape(rows, 1)
    keep_mine = jnp.broadcast_to(mine(keep), (seqs * own, 128))
    cat = [
        jnp.concatenate([query_proj[l], key_proj[l], value_proj[l], gate_proj[l], jnp.pad(decay_down[l], ((0, 0), (0, 128 - rank)))], axis=1)
        for l in range(depth)
    ]
    ups = [jnp.pad(decay_up[l], ((0, 128 - rank), (0, 0))) for l in range(depth)]
    hidden = layer_input.reshape(rows, width).astype(f32)
    normed = (hidden * rms_unit(hidden) * attn_gain[0]).astype(bf)
    resid = mine(layer_input.reshape(rows, width)).astype(f32)
    saved = []
    for l in range(depth):
        z = nn(normed, cat[l])
        gated, mixed, scores = run_forward(z, ups[l], decay_bias[l:l + 1], group_gain[l:l + 1], seqs)
        entry = resid
        (normed_ffn, middle), _ = exchange("norm", 1, (nn(gated, output_proj[l]), resid, ffn_gain[l:l + 1]))
        gate_act, up_act = nn(normed_ffn, ffn_gate[l]), nn(normed_ffn, ffn_up[l])
        inner = (gate_act * sigmoid(gate_act) * up_act).astype(bf)
        out = nn(inner, ffn_down[l])
        saved.append((entry, normed, z, gated, mixed, scores, middle, normed_ffn, gate_act, up_act, inner))
        if l + 1 < depth:
            (normed, resid), _ = exchange("norm", 1, (out, middle, attn_gain[l + 1:l + 2]))
    final = (out, middle, keep_mine)
    ffn_grad = cotangent.reshape(rows, width) * keep.astype(bf)
    resid = mine(cotangent.reshape(rows, width)).astype(f32) * keep_mine[:, :1]
    smalls, mix_terms, ffn_sums, mix_sums = [None] * depth, [None] * depth, [None] * depth, [None] * depth
    for l in reversed(range(depth)):
        entry, normed, z, gated, mixed, scores, middle, normed_ffn, gate_act, up_act, inner = saved[l]
        inner_grad = nt(ffn_grad, ffn_down[l])
        sig = sigmoid(gate_act)
        gate_low = (inner_grad * up_act * sig * (1.0 + gate_act * (1.0 - sig))).astype(bf)
        up_low = (inner_grad * gate_act * sig).astype(bf)
        ffn_terms = (tn(gate_low, normed_ffn), tn(up_low, normed_ffn), tn(inner, ffn_grad))
        first = (nt(gate_low, ffn_gate[l]) + nt(up_low, ffn_up[l]), resid, ffn_gain[l:l + 1], middle)
        if not ringed:
            (mix_grad, resid, ffn_gain_grad), _ = exchange("back", 2, first)
        elif l > 0:
            (mix_grad, resid, ffn_gain_grad), pieces = exchange("back", 2, first, Ring(groups, ffn_shapes, True, False), ffn_terms)
        else:
            (mix_grad, resid, ffn_gain_grad), mix_sums[1] = exchange("back", 7, first, Ring(groups, mix_shapes, True, True), mix_terms[1])
        gated_grad = nt(mix_grad, output_proj[l])
        low, up_grad, bias_grad, group_grad = run_backward(z, ups[l], decay_bias[l:l + 1], group_gain[l:l + 1], mixed, scores, gated_grad, seqs)
        mix_terms[l] = (tn(normed, low), tn(gated, mix_grad))
        back = nt(low, cat[l])
        second = (back, resid, attn_gain[l:l + 1], entry)
        if l > 0:
            (ffn_grad, resid, attn_gain_grad), full = exchange("back", 3, second, Ring(groups, ffn_shapes, False, True) if ringed else None, pieces if ringed else ())
        else:
            (input_grad, attn_gain_grad), pieces = exchange("end", 4, second, Ring(groups, ffn_shapes, True, False) if ringed else None, ffn_terms if ringed else ())
        if not ringed:
            mix_sums[l] = lax.psum((mix_terms[l][0][:, :mix_cols], mix_terms[l][1]), "dp")
            ffn_sums[l] = lax.psum(ffn_terms, "dp")
        elif l > 0:
            ffn_sums[l] = full
        down_grad = tn(low[:, mix_cols:mix_cols + rank], normed)
        smalls[l] = ((up_grad[:rank], bias_grad), (down_grad, attn_gain_grad, ffn_gain_grad, jnp.pad(group_grad, ((0, 0), (0, width - HV)))))
    local = jnp.concatenate([part for l in range(depth) for part in smalls[l][0]])
    local = jnp.pad(local, ((0, 16 * groups - local.shape[0]), (0, 0)))
    shared = jnp.concatenate([part for l in range(depth) for part in smalls[l][1]])
    shared = jnp.pad(shared, ((0, 8 * groups - shared.shape[0]), (0, 0)))
    if ringed:
        parts = [Exchange("last", seqs, rows, width), Ring(groups, ffn_shapes, False, True), Ring(groups, mix_shapes + small_shapes, True, True, tensor)]
        layer_output, *sums = run_together("ring_sum", 5, parts, LAST, *final, *pieces, *mix_terms[0], local, shared)
        ffn_sums[0], mix_sums[0], (local, shared) = sums[:3], sums[3:5], sums[5:]
    else:
        (layer_output,), _ = exchange("last", 6, final)
        local = lax.psum(local, "dp")
        shared = lax.psum(shared, ("dp", "tensor"))

    def split(flat, heights):
        found, start = [[] for _ in heights], 0
        for l in range(depth):
            for k, height in enumerate(heights):
                found[k].append(flat[start:start + height])
                start += height
        return [jnp.stack(rows_of) for rows_of in found]

    g_up, g_bias = split(local, (rank, 1))
    g_down, g_attn, g_ffn, g_group = split(shared, (rank, 1, 1, 1))
    cut = lambda a, b: jnp.stack([mix_sums[l][0][:, a:b] for l in range(depth)])
    pick = lambda sums, k: jnp.stack([sums[l][k] for l in range(depth)])
    return (
        layer_output.reshape(seqs, length, width),
        input_grad.reshape(seqs, length, width),
        g_attn[:, 0],
        cut(0, HK),
        cut(HK, 2 * HK),
        cut(2 * HK, 2 * HK + HV),
        cut(2 * HK + HV, mix_cols),
        g_down.transpose(0, 2, 1),
        g_up,
        g_bias[:, 0],
        g_group[:, 0, :HV],
        pick(mix_sums, 1),
        g_ffn[:, 0],
        pick(ffn_sums, 0).transpose(0, 2, 1),
        pick(ffn_sums, 1).transpose(0, 2, 1),
        pick(ffn_sums, 2),
    )


def solution(mesh):
    over, across = P("dp", None, None), P(None, None, "tensor")
    deep = P(None, "tensor", None)
    return jax.shard_map(
        functools.partial(shards, mesh.shape["dp"], mesh.shape["tensor"]),
        mesh=mesh,
        in_specs=(over, P("dp"), P(), across, across, across, across, P(), across, P(None, "tensor"), P(), deep, P(), across, across, deep, over),
        out_specs=(over, over, P(), across, across, across, across, P(), across, P(None, "tensor"), P(), deep, P(), across, across, deep),
        check_vma=False,
    )
```

```python
import functools
import jax, jax.numpy as jnp
from jax import lax
from jax.experimental import pallas as pl
from jax.experimental.pallas import tpu as pltpu
from jax.sharding import PartitionSpec as P
HK, HV, CH = 128, 256, 128
group_epsilon = 1e-05
bf, f32 = jnp.bfloat16, jnp.float32
SCALE = HK ** -0.5

def nn(a, b):
    return lax.dot_general(a, b, (((1,), (0,)), ((), ())), preferred_element_type=f32)
def nt(a, b):
    return lax.dot_general(a, b, (((1,), (1,)), ((), ())), preferred_element_type=f32)
def tn(a, b):
    return lax.dot_general(a, b, (((0,), (0,)), ((), ())), preferred_element_type=f32)

def halves(a):
    top = a.astype(bf)
    return top, (a - top.astype(f32)).astype(bf)

def thirds(a):
    top = a.astype(bf)
    return (top,) + halves(a - top.astype(f32))

def sigmoid(a):
    return 1.0 / (1.0 + jnp.exp(-a))

def log_sigmoid(a):
    return jnp.minimum(a, 0.0) - jnp.log1p(jnp.exp(-jnp.abs(a)))

def steps_below(n):
    out, h = [], 1
    while h < n:
        out.append(h)
        h *= 2
    return out

def decay_sums(ld):
    n = ld.shape[0]
    rows = lax.broadcasted_iota(jnp.int32, ld.shape, 0)
    total, pre, suf = ld, ld, jnp.zeros_like(ld)
    levels = []
    for h in steps_below(n):
        upper = (rows & h) != 0
        levels.append((h, upper, jnp.exp(jnp.where(upper, pre, suf))))
        below, above = pltpu.roll(total, h, 0), pltpu.roll(total, n - h, 0)
        pre = jnp.where(upper, pre + below, pre)
        suf = jnp.where(upper, suf, suf + above)
        total = total + jnp.where(upper, below, above)
    return levels, pre, suf, total

def tile_rows(c):
    return pl.ds(c * CH, CH)

def logits_of(z, up_ref, bias_ref):
    return sum(nn(piece, up_ref[...]) for piece in thirds(z[:, 2 * HK + 2 * HV:])) + bias_ref[...]

def wide_levels(chunks):
    out, h = [], 1
    while h < chunks:
        for base in range(0, chunks, 2 * h):
            out.append((tuple(range(base, base + h)), tuple(range(base + h, base + 2 * h))))
        h *= 2
    return out

def wide_factor(c, group, is_upper, pre, suf, tot):
    arg = pre[tile_rows(c), :] if is_upper else suf[tile_rows(c), :]
    for o in group:
        if (o < c) if is_upper else (o > c):
            arg = arg + tot[pl.ds(o * 8, 1), :]
    return jnp.exp(arg)

def mixer_forward(z_ref, up_ref, bias_ref, gain_ref, gated_ref, mixed_ref, scores_ref, pre, suf, tot):
    chunks = z_ref.shape[0] // CH
    i = lax.broadcasted_iota(jnp.int32, (CH, CH), 0)
    j = lax.broadcasted_iota(jnp.int32, (CH, CH), 1)
    apart = i ^ j
    scores_ref[...] = jnp.zeros_like(scores_ref)
    for c in range(chunks):
        z = z_ref[tile_rows(c), :]
        q, k = z[:, :HK].astype(bf), z[:, HK:2 * HK].astype(bf)
        ld = log_sigmoid(logits_of(z, up_ref, bias_ref)) / 16.0
        levels, p, s, t = decay_sums(ld)
        pre[tile_rows(c), :], suf[tile_rows(c), :], tot[pl.ds(c * 8, 8), :] = p, s, t[:8]
        tile = nt(q, k)
        qf, kf = q.astype(f32), k.astype(f32)
        for h, upper, factor in levels:
            rows = (jnp.where(upper, qf, kf) * factor).astype(bf)
            tile = jnp.where(apart >= h, nt(rows, rows), tile)
        scores_ref[tile_rows(c), tile_rows(c)] = jnp.where(i >= j, tile * SCALE, 0.0).astype(bf)
    for low_group, up_group in wide_levels(chunks):
        q_rows = [(z_ref[tile_rows(c), :HK].astype(bf).astype(f32) * wide_factor(c, up_group, True, pre, suf, tot)).astype(bf) for c in up_group]
        k_rows = [(z_ref[tile_rows(c), HK:2 * HK].astype(bf).astype(f32) * wide_factor(c, low_group, False, pre, suf, tot)).astype(bf) for c in low_group]
        for a, c in enumerate(up_group):
            for b, o in enumerate(low_group):
                scores_ref[tile_rows(c), tile_rows(o)] = (nt(q_rows[a], k_rows[b]) * SCALE).astype(bf)
    for c in range(chunks):
        width = (c + 1) * CH
        mixed = nn(scores_ref[tile_rows(c), :width], z_ref[:width, 2 * HK:2 * HK + HV].astype(bf))
        mixed_ref[tile_rows(c), :] = mixed
        out_gate = z_ref[tile_rows(c), 2 * HK + HV:2 * HK + 2 * HV]
        normed = mixed * lax.rsqrt(jnp.mean(mixed * mixed, axis=-1, keepdims=True) + group_epsilon) * gain_ref[...]
        gated_ref[tile_rows(c), :] = (normed * out_gate * sigmoid(out_gate)).astype(bf)

def mixer_backward(z_ref, up_ref, bias_ref, gain_ref, mixed_ref, scores_ref, grad_ref,
                   out_ref, up_out, bias_out, gain_out, pre, suf, tot, dm_ref, dq_ref, dk_ref, flow):
    chunks = z_ref.shape[0] // CH
    i = lax.broadcasted_iota(jnp.int32, (CH, CH), 0)
    j = lax.broadcasted_iota(jnp.int32, (CH, CH), 1)
    apart = i ^ j
    rows_in = lax.broadcasted_iota(jnp.int32, (CH, HK), 0)

    @pl.when(pl.program_id(0) == 0)
    def _():
        up_out[...] = jnp.zeros_like(up_out)
        bias_out[...] = jnp.zeros_like(bias_out)
        gain_out[...] = jnp.zeros_like(gain_out)

    for c in range(chunks):
        mixed, e = mixed_ref[tile_rows(c), :], grad_ref[tile_rows(c), :]
        g = z_ref[tile_rows(c), 2 * HK + HV:2 * HK + 2 * HV]
        r = lax.rsqrt(jnp.mean(mixed * mixed, axis=-1, keepdims=True) + group_epsilon)
        sig = sigmoid(g)
        unit = mixed * r
        out_ref[tile_rows(c), 2 * HK + HV:2 * HK + 2 * HV] = (e * unit * gain_ref[...] * (sig + g * sig * (1.0 - sig))).astype(bf)
        upstream = e * g * sig
        gain_out[...] += jnp.sum(upstream * unit, axis=0, keepdims=True)
        weighted = upstream * gain_ref[...]
        dm_ref[tile_rows(c), :] = (r * (weighted - unit * jnp.mean(unit * weighted, axis=-1, keepdims=True))).astype(bf)

    def score_grad(c, o):
        return nt(dm_ref[tile_rows(c), :], z_ref[tile_rows(o), 2 * HK:2 * HK + HV].astype(bf)) * SCALE

    for c in range(chunks):
        z = z_ref[tile_rows(c), :]
        q, k = z[:, :HK].astype(bf).astype(f32), z[:, HK:2 * HK].astype(bf).astype(f32)
        ld = log_sigmoid(logits_of(z, up_ref, bias_ref)) / 16.0
        levels, p, s, t = decay_sums(ld)
        pre[tile_rows(c), :], suf[tile_rows(c), :], tot[pl.ds(c * 8, 8), :] = p, s, t[:8]
        ds = score_grad(c, c)
        diagonal = jnp.sum(jnp.where(i == j, ds, 0.0), axis=-1, keepdims=True)
        ds = jnp.where(i > j, ds, 0.0)
        both = ds + ds.T
        dq, dk = diagonal * k, diagonal * q
        fl = jnp.zeros_like(dq)
        for h, upper, factor in levels:
            rows = (jnp.where(upper, q, k) * factor).astype(bf)
            near = jnp.where((apart >= h) & (apart < 2 * h), both, 0.0).astype(bf)
            back = nn(near, rows)
            part = back * factor
            dq, dk = dq + jnp.where(upper, part, 0.0), dk + jnp.where(upper, 0.0, part)
            moved = back * rows.astype(f32)
            fl = fl + jnp.where(upper, moved, -moved)
        dq_ref[tile_rows(c), :], dk_ref[tile_rows(c), :], flow[tile_rows(c), :] = dq, dk, fl
    for low_group, up_group in wide_levels(chunks):
        q_fac = [wide_factor(c, up_group, True, pre, suf, tot) for c in up_group]
        k_fac = [wide_factor(c, low_group, False, pre, suf, tot) for c in low_group]
        q_rows = [(z_ref[tile_rows(c), :HK].astype(bf).astype(f32) * f).astype(bf) for c, f in zip(up_group, q_fac)]
        k_rows = [(z_ref[tile_rows(c), HK:2 * HK].astype(bf).astype(f32) * f).astype(bf) for c, f in zip(low_group, k_fac)]
        grads = [[score_grad(c, o).astype(bf) for o in low_group] for c in up_group]
        for a, c in enumerate(up_group):
            back = sum(nn(grads[a][b], k_rows[b]) for b in range(len(low_group)))
            dq_ref[tile_rows(c), :] += back * q_fac[a]
            flow[tile_rows(c), :] += back * q_rows[a].astype(f32)
        for b, o in enumerate(low_group):
            back = sum(tn(grads[a][b], q_rows[a]) for a in range(len(up_group)))
            dk_ref[tile_rows(o), :] += back * k_fac[b]
            flow[tile_rows(o), :] -= back * k_rows[b].astype(f32)
    later = jnp.zeros((1, HK), f32)
    for c in reversed(range(chunks)):
        out_ref[tile_rows(c), :HK] = dq_ref[tile_rows(c), :].astype(bf)
        out_ref[tile_rows(c), HK:2 * HK] = dk_ref[tile_rows(c), :].astype(bf)
        out_ref[tile_rows(c), 2 * HK:2 * HK + HV] = tn(scores_ref[pl.ds(c * CH, (chunks - c) * CH), tile_rows(c)], dm_ref[pl.ds(c * CH, (chunks - c) * CH), :]).astype(bf)
        fl = flow[tile_rows(c), :]
        for h in steps_below(CH):
            fl = fl + jnp.where(rows_in < CH - h, pltpu.roll(fl, CH - h, 0), 0.0)
        fl = fl + later
        later = fl[:1]
        z = z_ref[tile_rows(c), :]
        logits = logits_of(z, up_ref, bias_ref)
        d_logit = fl * sigmoid(-logits) / 16.0
        bias_out[...] += jnp.sum(d_logit, axis=0, keepdims=True)
        d1, d2 = halves(d_logit)
        l1, l2 = halves(z[:, 2 * HK + 2 * HV:])
        up_out[...] += tn(l1, d1) + tn(l1, d2) + tn(l2, d1)
        out_ref[tile_rows(c), 2 * HK + 2 * HV:] = (nt(d1, up_ref[...]) + nt(d2, up_ref[...])).astype(bf)

def run_backward(z, up, bias, gain, mixed, scores, grad, seqs):
    rows, width = z.shape
    length = rows // seqs
    whole = lambda s: (0, 0)
    mine = lambda s: (s, 0)
    return pl.pallas_call(
        mixer_backward, name="mixer_backward", grid=(seqs,),
        in_specs=[pl.BlockSpec((length, width), mine), pl.BlockSpec(up.shape, whole), pl.BlockSpec(bias.shape, whole), pl.BlockSpec(gain.shape, whole),
                  pl.BlockSpec((length, HV), mine), pl.BlockSpec((length, length), mine), pl.BlockSpec((length, HV), mine)],
        out_specs=[pl.BlockSpec((length, width), mine), pl.BlockSpec(up.shape, whole), pl.BlockSpec(bias.shape, whole), pl.BlockSpec(gain.shape, whole)],
        out_shape=[jax.ShapeDtypeStruct((rows, width), bf), jax.ShapeDtypeStruct(up.shape, f32), jax.ShapeDtypeStruct(bias.shape, f32), jax.ShapeDtypeStruct(gain.shape, f32)],
        scratch_shapes=[pltpu.VMEM((length, HK), f32), pltpu.VMEM((length, HK), f32), pltpu.VMEM((length // CH * 8, HK), f32), pltpu.VMEM((length, HV), bf),
                        pltpu.VMEM((length, HK), f32), pltpu.VMEM((length, HK), f32), pltpu.VMEM((length, HK), f32)],
        compiler_params=pltpu.CompilerParams(vmem_limit_bytes=40 << 20),
        cost_estimate=pl.CostEstimate(flops=rows * length * (HK + HV) * 4, bytes_accessed=rows * width * 6 + rows * HV * 8 + rows * length * 2, transcendentals=rows * HK * 10),
    )(z, up, bias, gain, mixed, scores, grad)


norm_epsilon = 1e-06
MESH = pl.DeviceIdType.MESH
VMEM_SPEC = pl.BlockSpec(memory_space=pltpu.VMEM)
ANY_SPEC = pl.BlockSpec(memory_space=pl.ANY)
DMA = pltpu.SemaphoreType.DMA


def peer_of(index, bit):
    return jnp.where((index // bit) % 2 == 0, index + bit, index - bit)


def rms_unit(h):
    return lax.rsqrt(jnp.mean(h * h, axis=-1, keepdims=True) + norm_epsilon)


def remote(src, dst, send, recv, peer):
    return pltpu.make_async_remote_copy(
        src_ref=src, dst_ref=dst, send_sem=send, recv_sem=recv, device_id=peer, device_id_type=MESH
    )


class Exchange:
    def __init__(self, kind, seqs, rows, width):
        self.kind, self.seqs, self.rows, self.width = kind, seqs, rows, width
        self.own = rows // seqs // 4

    def inputs(self):
        return {"norm": 3, "last": 3, "back": 4, "end": 4}[self.kind]

    def outputs(self):
        shapes = [jax.ShapeDtypeStruct((self.rows, self.width), f32 if self.kind == "end" else bf)]
        if self.kind in ("norm", "back"):
            shapes.append(jax.ShapeDtypeStruct((self.seqs * self.own, self.width), f32))
        if self.kind in ("back", "end"):
            shapes.append(jax.ShapeDtypeStruct((1, self.width), f32))
        return shapes

    def scratch(self):
        seqs, own, width = self.seqs, self.own, self.width
        return [
            pltpu.VMEM((seqs, 2 * own, width), f32), pltpu.VMEM((seqs, own, width), f32), pltpu.VMEM((seqs, own, width), f32),
            pltpu.VMEM((seqs, own, width), f32), pltpu.VMEM((self.rows, width), f32), DMA((5, seqs)), DMA((5, seqs)),
        ]

    def peers(self):
        me = lax.axis_index("tensor")
        return [{"tensor": peer_of(me, 1)}, {"tensor": peer_of(me, 2)}]

    def steps(self, ins, outs, scratch):
        kind, seqs, own = self.kind, self.seqs, self.own
        half, length = 2 * own, 4 * own
        partial, resid, gain = ins[:3]
        full_out = outs[0]
        first, second, passed, kept, gathered, send, recv = scratch
        me = lax.axis_index("tensor")
        core, cross = me % 2, me // 2
        core_peer, cross_peer = self.peers()

        def copy(src, dst, stage, s, peer):
            step = remote(src, dst, send.at[stage, s], recv.at[stage, s], peer)
            step.start()
            return step

        def at(s, c, x, size):
            return pl.ds(pl.multiple_of(s * length + c * half + x * own, own), size)

        def piece(x):
            return pl.ds(pl.multiple_of(x * own, own), own)

        near = [copy(partial.at[at(s, 1 - core, 0, half)], first.at[s], 0, s, core_peer) for s in range(seqs)]
        started = list(near)
        yield
        crossing, over, close, end = [], [], [], []
        for s in range(seqs):
            near[s].wait_recv()
            passed[s] = partial[at(s, core, 1 - cross, own), :] + first[s, piece(1 - cross), :]
            crossing.append(copy(passed.at[s], second.at[s], 1, s, cross_peer))
            kept[s] = partial[at(s, core, cross, own), :] + first[s, piece(cross), :]
        if kind in ("back", "end"):
            outs[-1][...] = jnp.zeros_like(outs[-1])
        for s in range(seqs):
            yield
            crossing[s].wait_recv()
            total = kept[s] + second[s]
            mine = pl.ds(s * own, own)
            if kind == "norm":
                new = resid[mine, :] + total
                outs[1][mine, :] = new
                sent = (new * rms_unit(new) * gain[...]).astype(bf).astype(f32)
            elif kind == "last":
                sent = ((resid[mine, :] + total) * gain[mine, :1]).astype(bf).astype(f32)
            else:
                h = ins[3][mine, :]
                r = rms_unit(h)
                unit = h * r
                outs[-1][...] += jnp.sum(total * unit, axis=0, keepdims=True)
                weighted = total * gain[...]
                new = resid[mine, :] + r * (weighted - unit * jnp.mean(unit * weighted, axis=-1, keepdims=True))
                if kind == "back":
                    outs[1][mine, :] = new
                    sent = new.astype(bf).astype(f32)
                else:
                    sent = new
            gathered[at(s, core, cross, own), :] = sent
            block = gathered.at[at(s, core, cross, own)]
            over.append(copy(block, block, 2, s, cross_peer))
            close.append(copy(block, block, 3, s, core_peer))
        for s in range(seqs):
            yield
            over[s].wait_recv()
            block = gathered.at[at(s, core, 1 - cross, own)]
            end.append(copy(block, block, 4, s, core_peer))
            full_out[at(s, core, 0, half), :] = gathered[at(s, core, 0, half), :].astype(full_out.dtype)
        for s in range(seqs):
            close[s].wait_recv()
            end[s].wait_recv()
            full_out[at(s, 1 - core, 0, half), :] = gathered[at(s, 1 - core, 0, half), :].astype(full_out.dtype)
        for step in started + crossing + over + close + end:
            step.wait_send()


def ring_place(index, n):
    return jnp.where(index % 2 == 0, index // 2, n - 1 - index // 2)


def ring_index(place, n):
    return jnp.where(place < n // 2, 2 * place, 2 * (n - 1 - place) + 1)


def ring_cut(shape, n):
    rows, cols = shape
    if rows % (16 * n) == 0:
        return rows // (2 * n), cols, True
    if rows % (8 * n) == 0 and cols % 256 == 0:
        return rows // n, cols // 2, False
    return None


class Ring:
    def __init__(self, n, shapes, reduce, gather, over_tensor=0):
        self.n, self.shapes, self.reduce, self.gather, self.over_tensor = n, shapes, reduce, gather, over_tensor
        self.cuts = [ring_cut(shape, n) for shape in shapes]
        self.count = len(shapes)

    def inputs(self):
        return self.count

    def in_specs(self):
        return [ANY_SPEC if self.reduce else VMEM_SPEC] * self.count

    def outputs(self):
        if self.gather:
            return [jax.ShapeDtypeStruct(shape, f32) for shape in self.shapes]
        return [jax.ShapeDtypeStruct((2, rows, cols), f32) for rows, cols, _ in self.cuts]

    def out_specs(self):
        return [ANY_SPEC if self.gather else VMEM_SPEC] * self.count

    def scratch(self):
        n, count = self.n, self.count
        found = []
        if self.reduce:
            found += [pltpu.VMEM(shape, f32) for shape in self.shapes]
            found += [pltpu.VMEM((2, n - 1, rows, cols), f32) for rows, cols, _ in self.cuts]
            found += [DMA((count,)), DMA((n - 1, count, 2)), DMA((n - 1, count, 2))]
            if self.over_tensor:
                hops = self.over_tensor - 1
                found += [pltpu.VMEM((hops,) + self.shapes[-1], f32), DMA((hops,)), DMA((hops,))]
        if self.gather:
            found += [DMA((n - 1, count, 2)), DMA((n - 1, count, 2)), DMA((count, 2))]
        return found

    def places(self):
        n = self.n
        place = ring_place(lax.axis_index("dp"), n)
        ahead = ({"dp": ring_index(lax.rem(place + 1, n), n)}, {"dp": ring_index(lax.rem(place + n - 1, n), n)})
        return (place, n - 1 - place), ahead

    def others(self):
        me = lax.axis_index("tensor")
        return [{"tensor": lax.rem(me + hop, self.over_tensor)} for hop in range(1, self.over_tensor)]

    def peers(self):
        return list(self.places()[1])

    def segment(self, a, way, index):
        rows, cols, by_rows = self.cuts[a]
        if by_rows:
            return (pl.ds(pl.multiple_of((index * 2 + way) * rows, rows), rows), pl.ds(0, cols))
        return (pl.ds(pl.multiple_of(index * rows, rows), rows), pl.ds(way * cols, cols))

    def steps(self, ins, outs, scratch):
        n, count = self.n, self.count
        spots, ahead = self.places()
        pairs = [(a, way) for a in range(count) for way in range(2)]
        scratch = list(scratch)
        sends = []
        ends = {}
        if self.reduce:
            own, slots = scratch[:count], scratch[count:2 * count]
            load, rs_send, rs_recv = scratch[2 * count:2 * count + 3]
            scratch = scratch[2 * count + 3:]

            def pass_on(a, way, step, src):
                hop = remote(src, slots[a].at[way, step], rs_send.at[step, a, way], rs_recv.at[step, a, way], ahead[way])
                hop.start()
                sends.append(hop)
                return hop

            late = count - 1 if self.over_tensor else count
            moving = {}
            for a, way in pairs:
                if a < late:
                    moving[a, way] = pass_on(a, way, 0, ins[a].at[self.segment(a, way, spots[way])])
            loads = [pltpu.make_async_copy(ins[a].at[:, pl.ds(0, self.shapes[a][1])], own[a], load.at[a]) for a in range(count)]
            for step in loads:
                step.start()
            if self.over_tensor:
                shared, peer_send, peer_recv = scratch[:3]
                scratch = scratch[3:]
                to_peers = [remote(ins[late], shared.at[hop], peer_send.at[hop], peer_recv.at[hop], other) for hop, other in enumerate(self.others())]
                for step in to_peers:
                    step.start()
            for step in loads:
                step.wait()
            if self.over_tensor:
                for step in to_peers:
                    step.wait()
                own[late][...] += sum(shared[hop] for hop in range(len(to_peers)))
                for way in range(2):
                    moving[late, way] = pass_on(late, way, 0, own[late].at[self.segment(late, way, spots[way])])
            for step in range(n - 1):
                yield
                for a, way in pairs:
                    moving[a, way].wait_recv()
                    self.add(a, way, step, lax.rem(spots[way] + (2 * n - 1) - step, n), slots[a], own[a], None if self.gather or step < n - 2 else outs[a])
                    if step < n - 2:
                        moving[a, way] = pass_on(a, way, step + 1, slots[a].at[way, step])
                    elif self.gather:
                        ends[a, way] = slots[a].at[way, step]
        else:
            for a, way in pairs:
                ends[a, way] = ins[a].at[way]
        if self.gather:
            ag_send, ag_recv, store = scratch[:3]

            def hand_on(a, way, step, src, index):
                hop = remote(src, outs[a].at[self.segment(a, way, index)], ag_send.at[step, a, way], ag_recv.at[step, a, way], ahead[way])
                hop.start()
                sends.append(hop)
                return hop

            stores, moving = [], {}
            for a, way in pairs:
                index = lax.rem(spots[way] + 1, n)
                moving[a, way] = hand_on(a, way, 0, ends[a, way], index)
                kept = pltpu.make_async_copy(ends[a, way], outs[a].at[self.segment(a, way, index)], store.at[a, way])
                kept.start()
                stores.append(kept)
            for step in range(n - 1):
                yield
                for a, way in pairs:
                    index = lax.rem(spots[way] + n - step, n)
                    moving[a, way].wait_recv()
                    if step < n - 2:
                        moving[a, way] = hand_on(a, way, step + 1, outs[a].at[self.segment(a, way, index)], index)
            for kept in stores:
                kept.wait()
        for hop in sends:
            hop.wait_send()

    def add(self, a, way, step, index, slot, own, out):
        rows, cols, _ = self.cuts[a]
        row_ds, col_ds = self.segment(a, way, index)

        @pl.loop(0, rows // 8)
        def _(block):
            here = pl.ds(pl.multiple_of(block * 8, 8), 8)
            there = pl.ds(pl.multiple_of(row_ds.start + block * 8, 8), 8)
            total = slot[way, step, here, :] + own[there, col_ds]
            if out is None:
                slot[way, step, here, :] = total
            else:
                out[way, here, :] = total


def together(parts, order, refs):
    ins, outs, scratch = [], [], []
    at = 0
    for part in parts:
        ins.append(refs[at:at + part.inputs()])
        at += part.inputs()
    for part in parts:
        outs.append(refs[at:at + len(part.outputs())])
        at += len(part.outputs())
    for part in parts:
        scratch.append(refs[at:at + len(part.scratch())])
        at += len(part.scratch())
    barrier = pltpu.get_barrier_semaphore()
    rings = [part for part in parts if isinstance(part, Ring)]
    wide = [part for part in rings if part.over_tensor]
    peers = rings[0].peers() if rings else []
    peers = peers + (wide[0].others() if wide else parts[0].peers())
    for peer in peers:
        pl.semaphore_signal(barrier, inc=1, device_id=peer, device_id_type=MESH)
    pl.semaphore_wait(barrier, len(peers))
    running = [part.steps(i, o, s) for part, i, o, s in zip(parts, ins, outs, scratch)]
    over = object()
    for which in order:
        if which < len(running):
            next(running[which], over)
    for steps in running:
        for _ in steps:
            pass


def run_together(name, collective, parts, order, *arrays):
    in_specs, out_specs, outs, scratch = [], [], [], []
    for part in parts:
        in_specs += part.in_specs() if isinstance(part, Ring) else [VMEM_SPEC] * part.inputs()
        out_specs += part.out_specs() if isinstance(part, Ring) else [VMEM_SPEC] * len(part.outputs())
        outs += part.outputs()
        scratch += part.scratch()

    def kernel(*refs):
        together(parts, order, refs)

    return pl.pallas_call(
        kernel, name=name, in_specs=in_specs, out_specs=out_specs, out_shape=outs, scratch_shapes=scratch,
        compiler_params=pltpu.CompilerParams(collective_id=collective, has_side_effects=True, vmem_limit_bytes=56 << 20),
        cost_estimate=pl.CostEstimate(flops=10**6, bytes_accessed=2 * 10**8, transcendentals=0),
    )(*arrays)


MIXED = (0, 1, 0, 1, 0, 1, 0, 1, 0, 1, 0, 1)


def tiles(total, size):
    return [(start, min(size, total - start)) for start in range(0, total, size)]


class Forward:
    def __init__(self, depth, seqs, length, width, mix_cols, hidden_units):
        self.depth, self.seqs, self.length, self.width = depth, seqs, length, width
        self.z_cols, self.hidden_units = mix_cols + 128, hidden_units
        rows, quarter = seqs * length, seqs * length // 4
        self.saved = []
        for _ in range(depth):
            self.saved += [
                ((rows, width), bf), ((rows, self.z_cols), f32), ((rows, HV), bf), ((rows, HV), f32), ((rows, length), bf),
                ((quarter, width), f32), ((quarter, width), f32), ((rows, width), bf),
            ]

    def call(self, collective, x, gains, ffn_gains, ups, bias, group, cats, heads, ffn_ws):
        depth, seqs, length, width = self.depth, self.seqs, self.length, self.width
        own = length // 4
        weights = list(cats) + list(heads) + list(ffn_ws)
        saved = [jax.ShapeDtypeStruct(shape, kind) for shape, kind in self.saved]
        scratch = [pltpu.VMEM(shape, kind) for shape, kind in self.saved]
        scratch += [pltpu.VMEM(w.shape, w.dtype) for w in weights]
        scratch += [
            pltpu.VMEM((seqs, length, width), f32), pltpu.VMEM((seqs, 2 * own, width), f32), pltpu.VMEM((seqs, own, width), f32),
            pltpu.VMEM((seqs, own, width), f32), pltpu.VMEM((seqs, own, width), f32), pltpu.VMEM((seqs, length, width), f32),
            pltpu.VMEM((length, self.hidden_units), bf),
            pltpu.VMEM((length, HK), f32), pltpu.VMEM((length, HK), f32), pltpu.VMEM((length // CH * 8, HK), f32),
            DMA((len(saved), seqs)), DMA((len(weights),)), DMA((5, seqs)), DMA((5, seqs)),
        ]
        return pl.pallas_call(
            self.kernel, name="forward_blocks",
            in_specs=[VMEM_SPEC] * 6 + [ANY_SPEC] * len(weights), out_specs=[ANY_SPEC] * len(saved), out_shape=saved,
            scratch_shapes=scratch,
            compiler_params=pltpu.CompilerParams(collective_id=collective, has_side_effects=True, vmem_limit_bytes=60 << 20),
            cost_estimate=pl.CostEstimate(flops=10**10, bytes_accessed=2 * 10**8, transcendentals=0),
        )(x, gains, ffn_gains, ups, bias, group, *weights)

    def kernel(self, *refs):
        depth, seqs, length = self.depth, self.seqs, self.length
        half, own = length // 2, length // 4
        kinds = len(self.saved) // depth
        refs = list(refs)

        def take(count):
            found = refs[:count]
            del refs[:count]
            return found

        x, gains, ffn_gains, ups, bias, group = take(6)
        count = 2 * depth + 3 * (depth - 1)
        from_hbm = take(count)
        outs = take(len(self.saved))
        kept_for_later = take(len(self.saved))
        weights = take(count)
        partial, first, second, passed, kept, gathered, inner, pre, suf, tot, store, load, send, recv = take(14)
        me = lax.axis_index("tensor")
        core, cross = me % 2, me // 2
        core_peer, cross_peer = {"tensor": peer_of(me, 1)}, {"tensor": peer_of(me, 2)}
        loads = [pltpu.make_async_copy(src, dst, load.at[k]) for k, (src, dst) in enumerate(zip(from_hbm, weights))]
        order = [k for l in range(depth) for k in [l, depth + l] + [2 * depth + 3 * l + j for j in range(3) if l + 1 < depth]]
        for k in order:
            loads[k].start()
        barrier = pltpu.get_barrier_semaphore()
        for peer in (core_peer, cross_peer):
            pl.semaphore_signal(barrier, inc=1, device_id=peer, device_id_type=MESH)
        pl.semaphore_wait(barrier, 2)
        sent, stores = {}, []

        def copy(src, dst, stage, s, peer):
            if (stage, s) in sent:
                sent[stage, s].wait_send()
            step = remote(src, dst, send.at[stage, s], recv.at[stage, s], peer)
            step.start()
            sent[stage, s] = step
            return step

        def piece(c, x_half, size):
            return pl.ds(pl.multiple_of(c * half + x_half * own, own), size)

        def of_seq(ref, s, height):
            return ref.at[pl.ds(s * height, height)]

        def keep_for_later(k, s):
            height = self.saved[k][0][0] // seqs
            step = pltpu.make_async_copy(of_seq(kept_for_later[k], s, height), of_seq(outs[k], s, height), store.at[k, s])
            step.start()
            stores.append(step)

        def scatter(s):
            copy(partial.at[s, piece(1 - core, 0, half)], first.at[s], 0, s, core_peer)
            sent[0, s].wait_recv()
            for stage in (1, 2, 3, 4):
                if (stage, s) in sent:
                    sent[stage, s].wait_send()
                    del sent[stage, s]
            passed[s] = partial[s, piece(core, 1 - cross, own), :] + first[s, piece(0, 1 - cross, own), :]
            copy(passed.at[s], second.at[s], 1, s, cross_peer)
            kept[s] = partial[s, piece(core, cross, own), :] + first[s, piece(0, cross, own), :]

        def settle(s, resid, new_resid, gain):
            sent[1, s].wait_recv()
            mine = pl.ds(s * own, own)
            new = resid[mine, :] + (kept[s] + second[s])
            new_resid[mine, :] = new
            gathered[s, piece(core, cross, own), :] = (new * rms_unit(new) * gain).astype(bf).astype(f32)
            block = gathered.at[s, piece(core, cross, own)]
            copy(block, block, 2, s, cross_peer)
            copy(block, block, 3, s, core_peer)

        def collect(s, dest):
            sent[2, s].wait_recv()
            block = gathered.at[s, piece(core, 1 - cross, own)]
            copy(block, block, 4, s, core_peer)
            dest[pl.ds(pl.multiple_of(s * length + core * half, half), half), :] = gathered[s, piece(core, 0, half), :].astype(bf)
            sent[3, s].wait_recv()
            sent[4, s].wait_recv()
            dest[pl.ds(pl.multiple_of(s * length + (1 - core) * half, half), half), :] = gathered[s, piece(1 - core, 0, half), :].astype(bf)

        def rows_of(s):
            return pl.ds(s * length, length)

        for l in range(depth):
            normed, z, gated, mixed, scores, entry, middle, normed_ffn = kept_for_later[l * kinds:(l + 1) * kinds]
            for s in range(seqs):
                if l == 0:
                    for part in range(4):
                        block = pl.ds(s * length + part * own, own)
                        h = x[block, :].astype(f32)
                        normed[block, :] = (h * rms_unit(h) * gains[l:l + 1, :]).astype(bf)
                    entry[pl.ds(s * own, own), :] = x[pl.ds(pl.multiple_of(s * length + core * half + cross * own, own), own), :].astype(f32)
                    if s == 0:
                        loads[l].wait()
                else:
                    collect(s, normed)
                    if s == 0:
                        loads[l].wait()
                keep_for_later(l * kinds, s)
                for start, size in tiles(self.z_cols, 256):
                    cols = pl.ds(start, size)
                    z[rows_of(s), cols] = nn(normed[rows_of(s), :], weights[l][:, cols])
                keep_for_later(l * kinds + 1, s)
                mixer_forward(
                    of_seq(z, s, length), ups.at[l], bias.at[pl.ds(l, 1)], group.at[pl.ds(l, 1)], of_seq(gated, s, length),
                    of_seq(mixed, s, length), of_seq(scores, s, length), pre, suf, tot)
                for k in (2, 3, 4):
                    keep_for_later(l * kinds + k, s)
                if s == 0:
                    loads[depth + l].wait()
                if (0, s) in sent:
                    sent[0, s].wait_send()
                    del sent[0, s]
                for start, size in tiles(self.width, 256):
                    cols = pl.ds(start, size)
                    partial[s, :, cols] = nn(gated[rows_of(s), :], weights[depth + l][:, cols])
                scatter(s)
            for s in range(seqs):
                settle(s, entry, middle, ffn_gains[l:l + 1, :])
                keep_for_later(l * kinds + 5, s)
                keep_for_later(l * kinds + 6, s)
            if l + 1 == depth:
                break
            gate_w, up_w, down_w = weights[2 * depth + 3 * l:2 * depth + 3 * l + 3]
            for s in range(seqs):
                collect(s, normed_ffn)
                keep_for_later(l * kinds + 7, s)
                if s == 0:
                    for j in range(3):
                        loads[2 * depth + 3 * l + j].wait()
                for start, size in tiles(self.hidden_units, 256):
                    cols = pl.ds(start, size)
                    gate_act = nt(normed_ffn[rows_of(s), :], gate_w[cols, :])
                    up_act = nt(normed_ffn[rows_of(s), :], up_w[cols, :])
                    inner[:, cols] = (gate_act * sigmoid(gate_act) * up_act).astype(bf)
                sent[0, s].wait_send()
                del sent[0, s]
                for start, size in tiles(self.width, 256):
                    cols = pl.ds(start, size)
                    partial[s, :, cols] = nn(inner[...], down_w[:, cols])
                scatter(s)
            for s in range(seqs):
                settle(s, middle, kept_for_later[(l + 1) * kinds + 5], gains[l + 1:l + 2, :])
        for s in range(seqs):
            collect(s, kept_for_later[(depth - 1) * kinds + 7])
            keep_for_later((depth - 1) * kinds + 7, s)
        for step in sent.values():
            step.wait_send()
        for step in stores:
            step.wait()


def shards(
    groups, tensor, layer_input, seq_lengths, attn_gain, query_proj, key_proj, value_proj, gate_proj,
    decay_down, decay_up, decay_bias, group_gain, output_proj, ffn_gain, ffn_gate, ffn_up, ffn_down, cotangent,
):
    seqs, length, width = layer_input.shape
    depth = attn_gain.shape[0]
    rank = decay_down.shape[2]
    rows = seqs * length
    own = length // 4
    me = lax.axis_index("tensor")
    core, cross = me % 2, me // 2
    mix_cols = 2 * HK + 2 * HV
    hidden_units = ffn_gate.shape[2]
    ffn_shapes = [(hidden_units, width)] * 3
    mix_shapes = [(width, mix_cols), (output_proj.shape[1], width)]
    small_shapes = [(16 * groups, HK), (8 * groups, width)]
    ringed = all(ring_cut(shape, groups) for shape in ffn_shapes + mix_shapes + small_shapes)

    def mine(full):
        parts = full.reshape(seqs, 4, own, full.shape[-1])
        return lax.dynamic_slice_in_dim(parts, core * 2 + cross, 1, axis=1).reshape(seqs * own, full.shape[-1])

    def exchange(kind, number, arrays, ring=None, ring_arrays=()):
        parts = [Exchange(kind, seqs, rows, width)] + ([ring] if ring is not None else [])
        outs = run_together("exchange_" + kind, number, parts, MIXED, *arrays, *ring_arrays)
        cut = len(parts[0].outputs())
        return outs[:cut], outs[cut:]

    keep = (jnp.arange(length, dtype=jnp.int32)[None, :] < seq_lengths[:, None]).astype(f32).reshape(rows, 1)
    keep_mine = jnp.broadcast_to(mine(keep), (seqs * own, 128))
    cat = [
        jnp.concatenate([query_proj[l], key_proj[l], value_proj[l], gate_proj[l], jnp.pad(decay_down[l], ((0, 0), (0, 128 - rank)))], axis=1)
        for l in range(depth)
    ]
    ups = jnp.pad(decay_up, ((0, 0), (0, 128 - rank), (0, 0)))
    gate_t, up_t = ffn_gate.transpose(0, 2, 1), ffn_up.transpose(0, 2, 1)
    found = Forward(depth, seqs, length, width, mix_cols, hidden_units).call(
        8, layer_input.reshape(rows, width), attn_gain, ffn_gain, ups, decay_bias, group_gain, cat, list(output_proj),
        [w[l] for l in range(depth - 1) for w in (gate_t, up_t, ffn_down)])
    kinds = len(found) // depth
    saved = []
    for l in range(depth):
        normed, z, gated, mixed, scores, entry, middle, normed_ffn = found[l * kinds:(l + 1) * kinds]
        gate_act, up_act = nt(normed_ffn, gate_t[l]), nt(normed_ffn, up_t[l])
        inner = (gate_act * sigmoid(gate_act) * up_act).astype(bf)
        saved.append((entry, normed, z, gated, mixed, scores, middle, normed_ffn, gate_act, up_act, inner))
    out = nn(inner, ffn_down[depth - 1])
    final = (out, middle, keep_mine)
    ffn_grad = cotangent.reshape(rows, width) * keep.astype(bf)
    resid = mine(cotangent.reshape(rows, width)).astype(f32) * keep_mine[:, :1]
    smalls, mix_terms, ffn_sums, mix_sums = [None] * depth, [None] * depth, [None] * depth, [None] * depth
    for l in reversed(range(depth)):
        entry, normed, z, gated, mixed, scores, middle, normed_ffn, gate_act, up_act, inner = saved[l]
        inner_grad = nt(ffn_grad, ffn_down[l])
        sig = sigmoid(gate_act)
        gate_low = (inner_grad * up_act * sig * (1.0 + gate_act * (1.0 - sig))).astype(bf)
        up_low = (inner_grad * gate_act * sig).astype(bf)
        ffn_terms = (tn(gate_low, normed_ffn), tn(up_low, normed_ffn), tn(inner, ffn_grad))
        first = (nn(gate_low, gate_t[l]) + nn(up_low, up_t[l]), resid, ffn_gain[l:l + 1], middle)
        if not ringed:
            (mix_grad, resid, ffn_gain_grad), _ = exchange("back", 2, first)
        else:
            (mix_grad, resid, ffn_gain_grad), pieces = exchange("back", 2, first, Ring(groups, ffn_shapes, True, False), ffn_terms)
        gated_grad = nt(mix_grad, output_proj[l])
        low, up_grad, bias_grad, group_grad = run_backward(z, ups[l], decay_bias[l:l + 1], group_gain[l:l + 1], mixed, scores, gated_grad, seqs)
        mix_terms[l] = (tn(normed, low), tn(gated, mix_grad))
        back = nt(low, cat[l])
        second = (back, resid, attn_gain[l:l + 1], entry)
        if l > 0:
            (ffn_grad, resid, attn_gain_grad), full = exchange("back", 3, second, Ring(groups, ffn_shapes, False, True) if ringed else None, pieces if ringed else ())
        else:
            (input_grad, attn_gain_grad), full = exchange("end", 4, second, Ring(groups, ffn_shapes, False, True) if ringed else None, pieces if ringed else ())
        if not ringed:
            mix_sums[l] = lax.psum((mix_terms[l][0][:, :mix_cols], mix_terms[l][1]), "dp")
            ffn_sums[l] = lax.psum(ffn_terms, "dp")
        else:
            ffn_sums[l] = full
        down_grad = tn(low[:, mix_cols:mix_cols + rank], normed)
        smalls[l] = ((up_grad[:rank], bias_grad), (down_grad, attn_gain_grad, ffn_gain_grad, jnp.pad(group_grad, ((0, 0), (0, width - HV)))))
    local = jnp.concatenate([part for l in range(depth) for part in smalls[l][0]])
    local = jnp.pad(local, ((0, 16 * groups - local.shape[0]), (0, 0)))
    shared = jnp.concatenate([part for l in range(depth) for part in smalls[l][1]])
    shared = jnp.pad(shared, ((0, 8 * groups - shared.shape[0]), (0, 0)))
    if ringed:
        parts = [Exchange("last", seqs, rows, width), Ring(groups, mix_shapes * depth + small_shapes, True, True, tensor)]
        terms = [term for l in reversed(range(depth)) for term in mix_terms[l]]
        layer_output, *sums, local, shared = run_together("ring_sum", 5, parts, MIXED, *final, *terms, local, shared)
        for l in range(depth):
            mix_sums[depth - 1 - l] = sums[2 * l:2 * l + 2]
    else:
        (layer_output,), _ = exchange("last", 6, final)
        local = lax.psum(local, "dp")
        shared = lax.psum(shared, ("dp", "tensor"))

    def split(flat, heights):
        found, start = [[] for _ in heights], 0
        for l in range(depth):
            for k, height in enumerate(heights):
                found[k].append(flat[start:start + height])
                start += height
        return [jnp.stack(rows_of) for rows_of in found]

    g_up, g_bias = split(local, (rank, 1))
    g_down, g_attn, g_ffn, g_group = split(shared, (rank, 1, 1, 1))
    cut = lambda a, b: jnp.stack([mix_sums[l][0][:, a:b] for l in range(depth)])
    pick = lambda sums, k: jnp.stack([sums[l][k] for l in range(depth)])
    return (
        layer_output.reshape(seqs, length, width),
        input_grad.reshape(seqs, length, width),
        g_attn[:, 0],
        cut(0, HK),
        cut(HK, 2 * HK),
        cut(2 * HK, 2 * HK + HV),
        cut(2 * HK + HV, mix_cols),
        g_down.transpose(0, 2, 1),
        g_up,
        g_bias[:, 0],
        g_group[:, 0, :HV],
        pick(mix_sums, 1),
        g_ffn[:, 0],
        pick(ffn_sums, 0).transpose(0, 2, 1),
        pick(ffn_sums, 1).transpose(0, 2, 1),
        pick(ffn_sums, 2),
    )


def solution(mesh):
    over, across = P("dp", None, None), P(None, None, "tensor")
    deep = P(None, "tensor", None)
    return jax.shard_map(
        functools.partial(shards, mesh.shape["dp"], mesh.shape["tensor"]),
        mesh=mesh,
        in_specs=(over, P("dp"), P(), across, across, across, across, P(), across, P(None, "tensor"), P(), deep, P(), across, across, deep, over),
        out_specs=(over, over, P(), across, across, across, across, P(), across, P(None, "tensor"), P(), deep, P(), across, across, deep),
        check_vma=False,
    )
```

```python
import functools
import jax, jax.numpy as jnp
from jax import lax
from jax.experimental import pallas as pl
from jax.experimental.pallas import tpu as pltpu
from jax.sharding import PartitionSpec as P
HK, HV, CH = 128, 256, 128
group_epsilon = 1e-05
bf, f32 = jnp.bfloat16, jnp.float32
SCALE = HK ** -0.5

def nn(a, b):
    return lax.dot_general(a, b, (((1,), (0,)), ((), ())), preferred_element_type=f32)
def nt(a, b):
    return lax.dot_general(a, b, (((1,), (1,)), ((), ())), preferred_element_type=f32)
def tn(a, b):
    return lax.dot_general(a, b, (((0,), (0,)), ((), ())), preferred_element_type=f32)

def halves(a):
    top = a.astype(bf)
    return top, (a - top.astype(f32)).astype(bf)

def thirds(a):
    top = a.astype(bf)
    return (top,) + halves(a - top.astype(f32))

def sigmoid(a):
    return 1.0 / (1.0 + jnp.exp(-a))

def log_sigmoid(a):
    return jnp.minimum(a, 0.0) - jnp.log1p(jnp.exp(-jnp.abs(a)))

def steps_below(n):
    out, h = [], 1
    while h < n:
        out.append(h)
        h *= 2
    return out

def decay_sums(ld):
    n = ld.shape[0]
    rows = lax.broadcasted_iota(jnp.int32, ld.shape, 0)
    total, pre, suf = ld, ld, jnp.zeros_like(ld)
    levels = []
    for h in steps_below(n):
        upper = (rows & h) != 0
        levels.append((h, upper, jnp.exp(jnp.where(upper, pre, suf))))
        below, above = pltpu.roll(total, h, 0), pltpu.roll(total, n - h, 0)
        pre = jnp.where(upper, pre + below, pre)
        suf = jnp.where(upper, suf, suf + above)
        total = total + jnp.where(upper, below, above)
    return levels, pre, suf, total

def tile_rows(c):
    return pl.ds(c * CH, CH)

def logits_of(z, up_ref, bias_ref):
    return sum(nn(piece, up_ref[...]) for piece in thirds(z[:, 2 * HK + 2 * HV:])) + bias_ref[...]

def wide_levels(chunks):
    out, h = [], 1
    while h < chunks:
        for base in range(0, chunks, 2 * h):
            out.append((tuple(range(base, base + h)), tuple(range(base + h, base + 2 * h))))
        h *= 2
    return out

def wide_factor(c, group, is_upper, pre, suf, tot):
    arg = pre[tile_rows(c), :] if is_upper else suf[tile_rows(c), :]
    for o in group:
        if (o < c) if is_upper else (o > c):
            arg = arg + tot[pl.ds(o * 8, 1), :]
    return jnp.exp(arg)

def mixer_forward(z_ref, up_ref, bias_ref, gain_ref, gated_ref, mixed_ref, scores_ref, pre, suf, tot):
    chunks = z_ref.shape[0] // CH
    i = lax.broadcasted_iota(jnp.int32, (CH, CH), 0)
    j = lax.broadcasted_iota(jnp.int32, (CH, CH), 1)
    apart = i ^ j
    scores_ref[...] = jnp.zeros_like(scores_ref)
    for c in range(chunks):
        z = z_ref[tile_rows(c), :]
        q, k = z[:, :HK].astype(bf), z[:, HK:2 * HK].astype(bf)
        ld = log_sigmoid(logits_of(z, up_ref, bias_ref)) / 16.0
        levels, p, s, t = decay_sums(ld)
        pre[tile_rows(c), :], suf[tile_rows(c), :], tot[pl.ds(c * 8, 8), :] = p, s, t[:8]
        tile = nt(q, k)
        qf, kf = q.astype(f32), k.astype(f32)
        for h, upper, factor in levels:
            rows = (jnp.where(upper, qf, kf) * factor).astype(bf)
            tile = jnp.where(apart >= h, nt(rows, rows), tile)
        scores_ref[tile_rows(c), tile_rows(c)] = jnp.where(i >= j, tile * SCALE, 0.0).astype(bf)
    for low_group, up_group in wide_levels(chunks):
        q_rows = [(z_ref[tile_rows(c), :HK].astype(bf).astype(f32) * wide_factor(c, up_group, True, pre, suf, tot)).astype(bf) for c in up_group]
        k_rows = [(z_ref[tile_rows(c), HK:2 * HK].astype(bf).astype(f32) * wide_factor(c, low_group, False, pre, suf, tot)).astype(bf) for c in low_group]
        for a, c in enumerate(up_group):
            for b, o in enumerate(low_group):
                scores_ref[tile_rows(c), tile_rows(o)] = (nt(q_rows[a], k_rows[b]) * SCALE).astype(bf)
    for c in range(chunks):
        width = (c + 1) * CH
        mixed = nn(scores_ref[tile_rows(c), :width], z_ref[:width, 2 * HK:2 * HK + HV].astype(bf))
        mixed_ref[tile_rows(c), :] = mixed
        out_gate = z_ref[tile_rows(c), 2 * HK + HV:2 * HK + 2 * HV]
        normed = mixed * lax.rsqrt(jnp.mean(mixed * mixed, axis=-1, keepdims=True) + group_epsilon) * gain_ref[...]
        gated_ref[tile_rows(c), :] = (normed * out_gate * sigmoid(out_gate)).astype(bf)

def mixer_backward(fresh, z_ref, up_ref, bias_ref, gain_ref, mixed_ref, scores_ref, grad_ref,
                   out_ref, up_out, bias_out, gain_out, pre, suf, tot, dm_ref, dq_ref, dk_ref, flow):
    chunks = z_ref.shape[0] // CH
    i = lax.broadcasted_iota(jnp.int32, (CH, CH), 0)
    j = lax.broadcasted_iota(jnp.int32, (CH, CH), 1)
    apart = i ^ j
    rows_in = lax.broadcasted_iota(jnp.int32, (CH, HK), 0)

    if fresh:
        up_out[...] = jnp.zeros_like(up_out)
        bias_out[...] = jnp.zeros_like(bias_out)
        gain_out[...] = jnp.zeros_like(gain_out)
    for c in range(chunks):
        mixed, e = mixed_ref[tile_rows(c), :], grad_ref[tile_rows(c), :]
        g = z_ref[tile_rows(c), 2 * HK + HV:2 * HK + 2 * HV]
        r = lax.rsqrt(jnp.mean(mixed * mixed, axis=-1, keepdims=True) + group_epsilon)
        sig = sigmoid(g)
        unit = mixed * r
        out_ref[tile_rows(c), 2 * HK + HV:2 * HK + 2 * HV] = (e * unit * gain_ref[...] * (sig + g * sig * (1.0 - sig))).astype(bf)
        upstream = e * g * sig
        gain_out[...] += jnp.sum(upstream * unit, axis=0, keepdims=True)
        weighted = upstream * gain_ref[...]
        dm_ref[tile_rows(c), :] = (r * (weighted - unit * jnp.mean(unit * weighted, axis=-1, keepdims=True))).astype(bf)

    def score_grad(c, o):
        return nt(dm_ref[tile_rows(c), :], z_ref[tile_rows(o), 2 * HK:2 * HK + HV].astype(bf)) * SCALE

    for c in range(chunks):
        z = z_ref[tile_rows(c), :]
        q, k = z[:, :HK].astype(bf).astype(f32), z[:, HK:2 * HK].astype(bf).astype(f32)
        ld = log_sigmoid(logits_of(z, up_ref, bias_ref)) / 16.0
        levels, p, s, t = decay_sums(ld)
        pre[tile_rows(c), :], suf[tile_rows(c), :], tot[pl.ds(c * 8, 8), :] = p, s, t[:8]
        ds = score_grad(c, c)
        diagonal = jnp.sum(jnp.where(i == j, ds, 0.0), axis=-1, keepdims=True)
        ds = jnp.where(i > j, ds, 0.0)
        both = ds + ds.T
        dq, dk = diagonal * k, diagonal * q
        fl = jnp.zeros_like(dq)
        for h, upper, factor in levels:
            rows = (jnp.where(upper, q, k) * factor).astype(bf)
            near = jnp.where((apart >= h) & (apart < 2 * h), both, 0.0).astype(bf)
            back = nn(near, rows)
            part = back * factor
            dq, dk = dq + jnp.where(upper, part, 0.0), dk + jnp.where(upper, 0.0, part)
            moved = back * rows.astype(f32)
            fl = fl + jnp.where(upper, moved, -moved)
        dq_ref[tile_rows(c), :], dk_ref[tile_rows(c), :], flow[tile_rows(c), :] = dq, dk, fl
    for low_group, up_group in wide_levels(chunks):
        q_fac = [wide_factor(c, up_group, True, pre, suf, tot) for c in up_group]
        k_fac = [wide_factor(c, low_group, False, pre, suf, tot) for c in low_group]
        q_rows = [(z_ref[tile_rows(c), :HK].astype(bf).astype(f32) * f).astype(bf) for c, f in zip(up_group, q_fac)]
        k_rows = [(z_ref[tile_rows(c), HK:2 * HK].astype(bf).astype(f32) * f).astype(bf) for c, f in zip(low_group, k_fac)]
        grads = [[score_grad(c, o).astype(bf) for o in low_group] for c in up_group]
        for a, c in enumerate(up_group):
            back = sum(nn(grads[a][b], k_rows[b]) for b in range(len(low_group)))
            dq_ref[tile_rows(c), :] += back * q_fac[a]
            flow[tile_rows(c), :] += back * q_rows[a].astype(f32)
        for b, o in enumerate(low_group):
            back = sum(tn(grads[a][b], q_rows[a]) for a in range(len(up_group)))
            dk_ref[tile_rows(o), :] += back * k_fac[b]
            flow[tile_rows(o), :] -= back * k_rows[b].astype(f32)
    later = jnp.zeros((1, HK), f32)
    for c in reversed(range(chunks)):
        out_ref[tile_rows(c), :HK] = dq_ref[tile_rows(c), :].astype(bf)
        out_ref[tile_rows(c), HK:2 * HK] = dk_ref[tile_rows(c), :].astype(bf)
        out_ref[tile_rows(c), 2 * HK:2 * HK + HV] = tn(scores_ref[pl.ds(c * CH, (chunks - c) * CH), tile_rows(c)], dm_ref[pl.ds(c * CH, (chunks - c) * CH), :]).astype(bf)
        fl = flow[tile_rows(c), :]
        for h in steps_below(CH):
            fl = fl + jnp.where(rows_in < CH - h, pltpu.roll(fl, CH - h, 0), 0.0)
        fl = fl + later
        later = fl[:1]
        z = z_ref[tile_rows(c), :]
        logits = logits_of(z, up_ref, bias_ref)
        d_logit = fl * sigmoid(-logits) / 16.0
        bias_out[...] += jnp.sum(d_logit, axis=0, keepdims=True)
        d1, d2 = halves(d_logit)
        l1, l2 = halves(z[:, 2 * HK + 2 * HV:])
        up_out[...] += tn(l1, d1) + tn(l1, d2) + tn(l2, d1)
        out_ref[tile_rows(c), 2 * HK + 2 * HV:] = (nt(d1, up_ref[...]) + nt(d2, up_ref[...])).astype(bf)


norm_epsilon = 1e-06
MESH = pl.DeviceIdType.MESH
VMEM_SPEC = pl.BlockSpec(memory_space=pltpu.VMEM)
ANY_SPEC = pl.BlockSpec(memory_space=pl.ANY)
DMA = pltpu.SemaphoreType.DMA
RING = 8


def peer_of(index, bit):
    return jnp.where((index // bit) % 2 == 0, index + bit, index - bit)


def rms_unit(h):
    return lax.rsqrt(jnp.mean(h * h, axis=-1, keepdims=True) + norm_epsilon)


def remote(src, dst, send, recv, peer):
    return pltpu.make_async_remote_copy(
        src_ref=src, dst_ref=dst, send_sem=send, recv_sem=recv, device_id=peer, device_id_type=MESH
    )


def ring_place(n):
    index = lax.rem(lax.axis_index("dp"), n)
    return jnp.where(index % 2 == 0, index // 2, n - 1 - index // 2)


def ring_peer(ahead, n):
    place = lax.rem(ring_place(n) + ahead, n)
    index = lax.axis_index("dp")
    return {"dp": index - lax.rem(index, n) + jnp.where(place < n // 2, 2 * place, 2 * (n - 1 - place) + 1)}


def ring_cut(shape, n):
    rows, cols = shape
    if rows % (16 * n) == 0:
        return rows // (2 * n), cols, True
    if rows % (8 * n) == 0 and cols % 256 == 0:
        return rows // n, cols // 2, False
    return None


def tiles(total, size):
    return [(start, min(size, total - start)) for start in range(0, total, size)]


class Forward:
    def __init__(self, depth, seqs, length, width, mix_cols, hidden_units):
        self.depth, self.seqs, self.length, self.width = depth, seqs, length, width
        self.z_cols, self.hidden_units = mix_cols + 128, hidden_units
        rows, quarter = seqs * length, seqs * length // 4
        self.saved = []
        for _ in range(depth):
            self.saved += [
                ((rows, width), bf), ((rows, self.z_cols), f32), ((rows, HV), bf), ((rows, HV), f32), ((rows, length), bf),
                ((quarter, width), f32), ((quarter, width), f32), ((rows, width), bf),
            ]

    def call(self, collective, x, gains, ffn_gains, ups, bias, group, cats, stacked):
        depth, seqs, length, width = self.depth, self.seqs, self.length, self.width
        own = length // 4
        weights = [(w.shape, w.dtype) for w in cats] + [(stacked[0].shape[1:], bf)] * depth
        weights += [(w.shape[1:], bf) for _ in range(depth - 1) for w in stacked[1:]]
        saved = [jax.ShapeDtypeStruct(shape, kind) for shape, kind in self.saved]
        scratch = [pltpu.VMEM(shape, kind) for shape, kind in self.saved]
        scratch += [pltpu.VMEM(shape, kind) for shape, kind in weights]
        scratch += [
            pltpu.VMEM((seqs, length, width), f32), pltpu.VMEM((seqs, 2 * own, width), f32), pltpu.VMEM((seqs, own, width), f32),
            pltpu.VMEM((seqs, own, width), f32), pltpu.VMEM((seqs, own, width), f32), pltpu.VMEM((seqs, length, width), f32),
            pltpu.VMEM((length, self.hidden_units), bf),
            pltpu.VMEM((length, HK), f32), pltpu.VMEM((length, HK), f32), pltpu.VMEM((length // CH * 8, HK), f32),
            DMA((len(saved), seqs)), DMA((len(weights),)), DMA((5, seqs)), DMA((5, seqs)),
        ]
        return pl.pallas_call(
            self.kernel, name="forward_blocks",
            in_specs=[VMEM_SPEC] * 6 + [ANY_SPEC] * (depth + len(stacked)), out_specs=[ANY_SPEC] * len(saved), out_shape=saved,
            scratch_shapes=scratch,
            compiler_params=pltpu.CompilerParams(collective_id=collective, has_side_effects=True, vmem_limit_bytes=60 << 20),
            cost_estimate=pl.CostEstimate(flops=10**10, bytes_accessed=2 * 10**8, transcendentals=0),
        )(x, gains, ffn_gains, ups, bias, group, *cats, *stacked)

    def kernel(self, *refs):
        depth, seqs, length = self.depth, self.seqs, self.length
        half, own = length // 2, length // 4
        kinds = len(self.saved) // depth
        refs = list(refs)

        def take(count):
            found = refs[:count]
            del refs[:count]
            return found

        x, gains, ffn_gains, ups, bias, group = take(6)
        count = 2 * depth + 3 * (depth - 1)
        cats, stacked = take(depth), take(4)
        from_hbm = cats + [stacked[0].at[l] for l in range(depth)] + [w.at[l] for l in range(depth - 1) for w in stacked[1:]]
        outs = take(len(self.saved))
        kept_for_later = take(len(self.saved))
        weights = take(count)
        partial, first, second, passed, kept, gathered, inner, pre, suf, tot, store, load, send, recv = take(14)
        me = lax.axis_index("tensor")
        core, cross = me % 2, me // 2
        core_peer, cross_peer = {"tensor": peer_of(me, 1)}, {"tensor": peer_of(me, 2)}
        loads = [pltpu.make_async_copy(src, dst, load.at[k]) for k, (src, dst) in enumerate(zip(from_hbm, weights))]
        order = [k for l in range(depth) for k in [l, depth + l] + [2 * depth + 3 * l + j for j in range(3) if l + 1 < depth]]
        for k in order:
            loads[k].start()
        barrier = pltpu.get_barrier_semaphore()
        for peer in (core_peer, cross_peer):
            pl.semaphore_signal(barrier, inc=1, device_id=peer, device_id_type=MESH)
        pl.semaphore_wait(barrier, 2)
        sent, stores = {}, []

        def copy(src, dst, stage, s, peer):
            if (stage, s) in sent:
                sent[stage, s].wait_send()
            step = remote(src, dst, send.at[stage, s], recv.at[stage, s], peer)
            step.start()
            sent[stage, s] = step
            return step

        def piece(c, x_half, size):
            return pl.ds(pl.multiple_of(c * half + x_half * own, own), size)

        def of_seq(ref, s, height):
            return ref.at[pl.ds(s * height, height)]

        def keep_for_later(k, s):
            height = self.saved[k][0][0] // seqs
            step = pltpu.make_async_copy(of_seq(kept_for_later[k], s, height), of_seq(outs[k], s, height), store.at[k, s])
            step.start()
            stores.append(step)

        def scatter(s):
            copy(partial.at[s, piece(1 - core, 0, half)], first.at[s], 0, s, core_peer)
            sent[0, s].wait_recv()
            for stage in (1, 2, 3, 4):
                if (stage, s) in sent:
                    sent[stage, s].wait_send()
                    del sent[stage, s]
            passed[s] = partial[s, piece(core, 1 - cross, own), :] + first[s, piece(0, 1 - cross, own), :]
            copy(passed.at[s], second.at[s], 1, s, cross_peer)
            kept[s] = partial[s, piece(core, cross, own), :] + first[s, piece(0, cross, own), :]

        def settle(s, resid, new_resid, gain):
            sent[1, s].wait_recv()
            mine = pl.ds(s * own, own)
            new = resid[mine, :] + (kept[s] + second[s])
            new_resid[mine, :] = new
            gathered[s, piece(core, cross, own), :] = (new * rms_unit(new) * gain).astype(bf).astype(f32)
            block = gathered.at[s, piece(core, cross, own)]
            copy(block, block, 2, s, cross_peer)
            copy(block, block, 3, s, core_peer)

        def collect(s, dest):
            sent[2, s].wait_recv()
            block = gathered.at[s, piece(core, 1 - cross, own)]
            copy(block, block, 4, s, core_peer)
            dest[pl.ds(pl.multiple_of(s * length + core * half, half), half), :] = gathered[s, piece(core, 0, half), :].astype(bf)
            sent[3, s].wait_recv()
            sent[4, s].wait_recv()
            dest[pl.ds(pl.multiple_of(s * length + (1 - core) * half, half), half), :] = gathered[s, piece(1 - core, 0, half), :].astype(bf)

        def rows_of(s):
            return pl.ds(s * length, length)

        for l in range(depth):
            normed, z, gated, mixed, scores, entry, middle, normed_ffn = kept_for_later[l * kinds:(l + 1) * kinds]
            for s in range(seqs):
                if l == 0:
                    for part in range(4):
                        block = pl.ds(s * length + part * own, own)
                        h = x[block, :].astype(f32)
                        normed[block, :] = (h * rms_unit(h) * gains[l:l + 1, :]).astype(bf)
                    entry[pl.ds(s * own, own), :] = x[pl.ds(pl.multiple_of(s * length + core * half + cross * own, own), own), :].astype(f32)
                    if s == 0:
                        loads[l].wait()
                else:
                    collect(s, normed)
                    if s == 0:
                        loads[l].wait()
                keep_for_later(l * kinds, s)
                for start, size in tiles(self.z_cols, 256):
                    cols = pl.ds(start, size)
                    z[rows_of(s), cols] = nn(normed[rows_of(s), :], weights[l][:, cols])
                keep_for_later(l * kinds + 1, s)
                mixer_forward(
                    of_seq(z, s, length), ups.at[l], bias.at[pl.ds(l, 1)], group.at[pl.ds(l, 1)], of_seq(gated, s, length),
                    of_seq(mixed, s, length), of_seq(scores, s, length), pre, suf, tot)
                for k in (2, 3, 4):
                    keep_for_later(l * kinds + k, s)
                if s == 0:
                    loads[depth + l].wait()
                if (0, s) in sent:
                    sent[0, s].wait_send()
                    del sent[0, s]
                for start, size in tiles(self.width, 256):
                    cols = pl.ds(start, size)
                    partial[s, :, cols] = nn(gated[rows_of(s), :], weights[depth + l][:, cols])
                scatter(s)
            for s in range(seqs):
                settle(s, entry, middle, ffn_gains[l:l + 1, :])
                keep_for_later(l * kinds + 5, s)
                keep_for_later(l * kinds + 6, s)
            if l + 1 == depth:
                break
            gate_w, up_w, down_w = weights[2 * depth + 3 * l:2 * depth + 3 * l + 3]
            for s in range(seqs):
                collect(s, normed_ffn)
                keep_for_later(l * kinds + 7, s)
                if s == 0:
                    for j in range(3):
                        loads[2 * depth + 3 * l + j].wait()
                for start, size in tiles(self.hidden_units, 256):
                    cols = pl.ds(start, size)
                    gate_act = nt(normed_ffn[rows_of(s), :], gate_w[cols, :])
                    up_act = nt(normed_ffn[rows_of(s), :], up_w[cols, :])
                    inner[:, cols] = (gate_act * sigmoid(gate_act) * up_act).astype(bf)
                sent[0, s].wait_send()
                del sent[0, s]
                for start, size in tiles(self.width, 256):
                    cols = pl.ds(start, size)
                    partial[s, :, cols] = nn(inner[...], down_w[:, cols])
                scatter(s)
            for s in range(seqs):
                settle(s, middle, kept_for_later[(l + 1) * kinds + 5], gains[l + 1:l + 2, :])
        for s in range(seqs):
            collect(s, kept_for_later[(depth - 1) * kinds + 7])
            keep_for_later((depth - 1) * kinds + 7, s)
        for step in sent.values():
            step.wait_send()
        for step in stores:
            step.wait()


class RingJob:
    def __init__(self, n, shapes, reduce, gather):
        self.n, self.shapes, self.reduce, self.gather = n, shapes, reduce, gather
        self.cuts = [ring_cut(shape, n) for shape in shapes]
        self.pairs = [(a, way) for a in range(len(shapes)) for way in range(2)]

    def slots(self):
        return [pltpu.VMEM((2, self.n - 1, rows, cols), f32) for rows, cols, _ in self.cuts] if self.reduce else []

    def sems(self):
        each = DMA((self.n - 1, len(self.shapes), 2))
        return [each, each] * (self.reduce + self.gather) + ([DMA((len(self.shapes), 2))] if self.gather else [])

    def pieces(self):
        return [jax.ShapeDtypeStruct((2, rows, cols), f32) for rows, cols, _ in self.cuts]

    def full(self):
        return [jax.ShapeDtypeStruct(shape, f32) for shape in self.shapes]

    def segment(self, a, way, back):
        n = self.n
        place = ring_place(n)
        index = lax.rem((place if way == 0 else n - 1 - place) + (2 * n - back), n)
        rows, cols, by_rows = self.cuts[a]
        if by_rows:
            return (pl.ds(pl.multiple_of((index * 2 + way) * rows, rows), rows), pl.ds(0, cols))
        return (pl.ds(pl.multiple_of(index * rows, rows), rows), pl.ds(way * cols, cols))

    def hop(self, src, dst, sems, step, a, way):
        peer = ring_peer(1 if way == 0 else self.n - 1, self.n)
        return remote(src, dst, sems[0].at[step, a, way], sems[1].at[step, a, way], peer)

    def steps(self, own, slots, sems, pieces, outs):
        n = self.n
        if self.reduce:
            rs, sems = sems[:2], sems[2:]
            for a, way in self.pairs:
                self.hop(own[a].at[self.segment(a, way, 0)], slots[a].at[way, 0], rs, 0, a, way).start()
            for step in range(n - 1):
                yield
                for a, way in self.pairs:
                    slot = slots[a].at[way, step]
                    self.hop(slot, slot, rs, step, a, way).wait_recv()
                    self.add(a, way, slot, own[a], slot if self.gather or step < n - 2 else pieces[a].at[way], step + 1)
                    if step < n - 2:
                        self.hop(slot, slots[a].at[way, step + 1], rs, step + 1, a, way).start()
                    elif self.gather:
                        self.begin(a, way, slot, sems, outs)
        else:
            for a, way in self.pairs:
                self.begin(a, way, pieces[a].at[way], sems, outs)
        if self.gather:
            for step in range(n - 1):
                yield
                for a, way in self.pairs:
                    piece = outs[a].at[self.segment(a, way, step)]
                    self.hop(piece, piece, sems, step, a, way).wait_recv()
                    if step < n - 2:
                        self.hop(piece, piece, sems, step + 1, a, way).start()
            for a, way in self.pairs:
                end = slots[a].at[way, n - 2] if self.reduce else pieces[a].at[way]
                pltpu.make_async_copy(end, outs[a].at[self.segment(a, way, n - 1)], sems[2].at[a, way]).wait()
        for step in range(n - 1):
            for a, way in self.pairs:
                if self.reduce:
                    self.hop(slots[a].at[way, 0], slots[a].at[way, 0], rs, step, a, way).wait_send()
                if self.gather:
                    piece = outs[a].at[self.segment(a, way, 0)]
                    self.hop(piece, piece, sems, step, a, way).wait_send()

    def begin(self, a, way, piece, sems, outs):
        place = outs[a].at[self.segment(a, way, self.n - 1)]
        self.hop(piece, place, sems, 0, a, way).start()
        pltpu.make_async_copy(piece, place, sems[2].at[a, way]).start()

    def add(self, a, way, slot, own, out, back):
        row_ds, col_ds = self.segment(a, way, back)

        @pl.loop(0, self.cuts[a][0] // 8)
        def _(block):
            here = pl.ds(pl.multiple_of(block * 8, 8), 8)
            there = pl.ds(pl.multiple_of(row_ds.start + block * 8, 8), 8)
            out[here, :] = slot[here, :] + own[there, col_ds]


def fill(dst, total, size, make):
    for start, extent in tiles(total, size):
        cols = pl.ds(start, extent)
        dst[:, cols] = make(cols)


class Backward:
    def __init__(self, top, l, n, tensor, seqs, length, width, mix_cols, hidden_units, rank):
        self.top, self.l, self.n, self.tensor, self.rank = top, l, n, tensor, rank
        self.seqs, self.length, self.width, self.mix_cols, self.hidden_units = seqs, length, width, mix_cols, hidden_units
        self.ffn = RingJob(n, [(hidden_units, width)] * 3, True, True)
        mix_shapes = [(width, mix_cols), (HV, width)]
        self.mix = RingJob(n, mix_shapes, True, not top)
        self.above = RingJob(n, mix_shapes, False, True)
        self.small = RingJob(n, [(16 * n, HK), (8 * n, width)], True, True)

    def small_outs(self):
        width = self.width
        return [jax.ShapeDtypeStruct(shape, f32) for shape in ((128, HK), (1, HK), (128, width), (1, width), (1, width), (1, HV))]

    def call(self, collective, params, arrays, extra):
        seqs, length, width = self.seqs, self.length, self.width
        rows, own = seqs * length, length // 4
        wide = jax.ShapeDtypeStruct((rows, width), bf)
        wide32, quarter = jax.ShapeDtypeStruct((rows, width), f32), jax.ShapeDtypeStruct((seqs * own, width), f32)
        smalls = self.small_outs()
        if self.top:
            outs = [wide32, wide, quarter] + self.ffn.full()
            vmem_outs = self.mix.pieces() + smalls
            vmem_ins = 0
        else:
            outs = [wide32, wide] + self.ffn.full() + self.mix.full() + self.above.full() + self.small.full()
            vmem_outs = []
            vmem_ins = len(extra) - 2
        scratch = [pltpu.VMEM(shape.shape, f32) for shape in self.ffn.full() + self.mix.full()]
        scratch += self.ffn.slots() + self.mix.slots() + self.ffn.sems() + self.mix.sems()
        if not self.top:
            scratch += self.above.sems() + [pltpu.VMEM(shape.shape, f32) for shape in self.small.full()] + self.small.slots() + self.small.sems()
            scratch += [pltpu.VMEM((self.tensor - 1, 8 * self.n, width), f32), DMA((self.tensor - 1,)), DMA((self.tensor - 1,))]
            scratch += [pltpu.VMEM(shape.shape, f32) for shape in smalls]
        scratch += [
            pltpu.VMEM((seqs, length, width), f32), pltpu.VMEM((seqs, 2 * own, width), f32), pltpu.VMEM((seqs, own, width), f32),
            pltpu.VMEM((seqs, length, width), f32), pltpu.VMEM((rows, width), bf), pltpu.VMEM((rows, width), bf),
            pltpu.VMEM(quarter.shape, f32), pltpu.VMEM(quarter.shape, f32), pltpu.VMEM(quarter.shape, f32),
            DMA((24,)), DMA((5, seqs)), DMA((5, seqs)),
        ]
        return pl.pallas_call(
            self.kernel, name="backward_top" if self.top else "backward_low",
            in_specs=[VMEM_SPEC] * len(params) + [ANY_SPEC] * len(arrays) + [VMEM_SPEC] * vmem_ins + [ANY_SPEC] * (len(extra) - vmem_ins),
            out_specs=[ANY_SPEC] * len(outs) + [VMEM_SPEC] * len(vmem_outs), out_shape=outs + vmem_outs, scratch_shapes=scratch,
            compiler_params=pltpu.CompilerParams(collective_id=collective, has_side_effects=True, vmem_limit_bytes=61 << 20),
            cost_estimate=pl.CostEstimate(flops=10**10, bytes_accessed=3 * 10**8, transcendentals=0),
        )(*params, *arrays, *extra)

    def kernel(self, *refs):
        top, l, seqs, length, width, rank = self.top, self.l, self.seqs, self.length, self.width, self.rank
        mix_cols, hidden_units = self.mix_cols, self.hidden_units
        half, own, rows = length // 2, length // 4, seqs * length
        refs = list(refs)

        def take(count):
            found = refs[:count]
            del refs[:count]
            return found

        gains, ffn_gains, ups, bias, group = take(5)
        normed_ffn, ffn_grad, resid_in, middle_in, entry_in, z_in, mixed_in, scores_in, gated_in, normed_in = take(10)
        gate_in, up_in, down_in, cat_in, heads_in = take(5)
        if top:
            out_partial, out_grad, out_resid = take(3)
            ffn_outs, mix_outs = take(3), None
            mix_pieces, smalls = take(2), take(6)
        else:
            above_pieces, smalls_above, keep = take(2), take(6), take(1)[0]
            last_partial, last_middle = take(2)
            out_input, out_layer = take(2)
            ffn_outs, mix_outs, above_outs, small_outs = take(3), take(2), take(2), take(2)
            mix_pieces = None
        ffn_own, mix_own, ffn_slots, mix_slots = take(3), take(2), take(3), take(2)
        ffn_sems, mix_sems = take(len(self.ffn.sems())), take(len(self.mix.sems()))
        if not top:
            above_sems, small_own, small_slots, small_sems = take(len(self.above.sems())), take(2), take(2), take(len(self.small.sems()))
            shared, peer_send, peer_recv = take(3)
            smalls = take(6)
        up_sum, bias_sum, down_sum, attn_sum, ffn_sum, group_sum = smalls
        partial, first, second, gathered, rows_in, grad, resid, middle, entry, load, send, recv = take(12)
        pending = set()

        def ids():
            me = lax.axis_index("tensor")
            return me % 2, me // 2, {"tensor": peer_of(me, 1)}, {"tensor": peer_of(me, 2)}

        def piece(c, x_half, size):
            return pl.ds(pl.multiple_of(c * half + x_half * own, own), size)

        def of_seq(ref, s, height):
            return ref.at[pl.ds(s * height, height)]

        def plain(stage, s):
            src = (partial.at[s, pl.ds(0, half)], partial.at[s, pl.ds(0, own)])[stage] if stage < 2 else gathered.at[s, pl.ds(0, own)]
            dst = (first.at[s], second.at[s])[stage] if stage < 2 else src
            return remote(src, dst, send.at[stage, s], recv.at[stage, s], ids()[2 if stage in (0, 3, 4) else 3])

        def launch(src, dst, stage, s, peer):
            remote(src, dst, send.at[stage, s], recv.at[stage, s], peer).start()
            pending.add((stage, s))

        def freed(s, stages):
            for stage in stages:
                if (stage, s) in pending:
                    plain(stage, s).wait_send()
                    pending.discard((stage, s))

        def scatter(s):
            core, cross, core_peer, cross_peer = ids()
            launch(partial.at[s, piece(1 - core, 0, half)], first.at[s], 0, s, core_peer)
            plain(0, s).wait_recv()
            freed(s, (2, 3, 4))
            partial[s, piece(core, 1 - cross, own), :] += first[s, piece(0, 1 - cross, own), :]
            launch(partial.at[s, piece(core, 1 - cross, own)], second.at[s], 1, s, cross_peer)
            partial[s, piece(core, cross, own), :] += first[s, piece(0, cross, own), :]

        def arrived(s):
            core, cross, _, _ = ids()
            plain(1, s).wait_recv()
            return partial[s, piece(core, cross, own), :] + second[s]

        def publish(s, sent):
            core, cross, core_peer, cross_peer = ids()
            gathered[s, piece(core, cross, own), :] = sent
            block = gathered.at[s, piece(core, cross, own)]
            launch(block, block, 2, s, cross_peer)
            launch(block, block, 3, s, core_peer)

        def settle(s, h_ref, gain, gain_sum, rounded):
            total = arrived(s)
            mine = pl.ds(s * own, own)
            h = h_ref[mine, :]
            r = rms_unit(h)
            unit = h * r
            here = jnp.sum(total * unit, axis=0, keepdims=True)
            gain_sum[...] = here if s == 0 else gain_sum[...] + here
            weighted = total * gain
            new = resid[mine, :] + r * (weighted - unit * jnp.mean(unit * weighted, axis=-1, keepdims=True))
            resid[mine, :] = new
            publish(s, new.astype(bf).astype(f32) if rounded else new)

        def collect(s, dest):
            core, cross, core_peer, _ = ids()
            plain(2, s).wait_recv()
            block = gathered.at[s, piece(core, 1 - cross, own)]
            launch(block, block, 4, s, core_peer)
            if dest is not None:
                dest[pl.ds(pl.multiple_of(s * length + core * half, half), half), :] = gathered[s, piece(core, 0, half), :].astype(bf)
            plain(3, s).wait_recv()
            plain(4, s).wait_recv()
            if dest is not None:
                dest[pl.ds(pl.multiple_of(s * length + (1 - core) * half, half), half), :] = gathered[s, piece(1 - core, 0, half), :].astype(bf)

        jobs = []
        over = object()

        def pump(count=1):
            for _ in range(count):
                for job in list(jobs):
                    if next(job, over) is over:
                        jobs.remove(job)

        def begin(job):
            next(job)
            jobs.append(job)

        def local(src, dst, k):
            return pltpu.make_async_copy(src, dst, load.at[k])

        def rows_of(s):
            return pl.ds(s * length, length)

        basics = [(normed_ffn, rows_in, 0), (ffn_grad, grad, 1), (resid_in, resid, 2), (middle_in, middle, 3), (entry_in, entry, 4)]
        for src, dst, k in basics:
            local(src, dst, k).start()
        barrier = pltpu.get_barrier_semaphore()
        peers = [ring_peer(hop, self.n) for hop in (1, self.n - 1)]
        peers += list(ids()[2:]) if top else [{"tensor": lax.rem(lax.axis_index("tensor") + hop, self.tensor)} for hop in range(1, self.tensor)]
        for peer in peers:
            pl.semaphore_signal(barrier, inc=1, device_id=peer, device_id_type=MESH)
        pl.semaphore_wait(barrier, len(peers))
        if not top:
            begin(self.above.steps(None, None, above_sems, above_pieces, above_outs))

        def ffn_phase(gate_w, up_w, down_w, inner, gate_low, up_low):
            weights = [(gate_in.at[l], gate_w, 5), (up_in.at[l], up_w, 6), (down_in.at[l], down_w, 7)]
            for src, dst, k in weights:
                local(src, dst, k).start()
            for src, dst, k in basics + weights:
                local(src, dst, k).wait()
            for s in range(seqs):
                here = rows_of(s)
                for start, size in tiles(hidden_units, 256):
                    cols = pl.ds(start, size)
                    gate_act, up_act = nt(rows_in[here, :], gate_w[cols, :]), nt(rows_in[here, :], up_w[cols, :])
                    inner_grad = nt(grad[here, :], down_w[cols, :])
                    sig = sigmoid(gate_act)
                    swish = gate_act * sig
                    inner[here, cols] = (swish * up_act).astype(bf)
                    gate_low[here, cols] = (inner_grad * up_act * sig * (1.0 + gate_act * (1.0 - sig))).astype(bf)
                    up_low[here, cols] = (inner_grad * swish).astype(bf)
                pump()
            fill(ffn_own[0], width, 512, lambda cols: tn(gate_low[...], rows_in[:, cols]))
            fill(ffn_own[1], width, 512, lambda cols: tn(up_low[...], rows_in[:, cols]))
            pump()
            fill(ffn_own[2], width, 512, lambda cols: tn(inner[...], grad[:, cols]))
            begin(self.ffn.steps(ffn_own, ffn_slots, ffn_sems, None, ffn_outs))
            if top:
                for s in range(seqs):
                    fill(partial.at[s], width, 256, lambda cols: nn(inner[rows_of(s), :], down_w[:, cols]))
                    local(partial.at[s], of_seq(out_partial, s, length), 8 + s).start()
            for s in range(seqs):
                if top:
                    local(partial.at[s], of_seq(out_partial, s, length), 8 + s).wait()
                fill(partial.at[s], width, 256, lambda cols: nn(gate_low[rows_of(s), :], gate_w[:, cols]) + nn(up_low[rows_of(s), :], up_w[:, cols]))
                scatter(s)
                pump()

        hidden = (hidden_units, width)
        pl.run_scoped(ffn_phase, *[pltpu.VMEM(hidden, bf)] * 3, *[pltpu.VMEM((rows, hidden_units), bf)] * 3)

        def mixer_phase(cat, heads, z, mixed, scores, gated, low, ggrad, pre, suf, tot, dm, dq, dk, flow):
            once = [(cat_in, cat, 10), (heads_in.at[l], heads, 11), (gated_in, gated, 12), (normed_in, rows_in, 13)]
            each = [[(of_seq(src, s, length), dst, 14 + k) for k, (src, dst) in enumerate(((z_in, z), (mixed_in, mixed), (scores_in, scores)))] for s in range(seqs)]
            for src, dst, k in once + each[0]:
                local(src, dst, k).start()
            for s in range(seqs):
                settle(s, middle, ffn_gains[l:l + 1, :], ffn_sum, True)
                pump()
            for src, dst, k in once:
                local(src, dst, k).wait()
            for s in range(seqs):
                collect(s, grad)
                for src, dst, k in each[s]:
                    local(src, dst, k).wait()
                ggrad[...] = nt(grad[rows_of(s), :], heads[...])
                mixer_backward(
                    s == 0, z, ups.at[l], bias.at[pl.ds(l, 1)], group.at[pl.ds(l, 1)], mixed, scores, ggrad, of_seq(low, s, length),
                    up_sum, bias_sum, group_sum, pre, suf, tot, dm, dq, dk, flow)
                if s + 1 < seqs:
                    for src, dst, k in each[s + 1]:
                        local(src, dst, k).start()
                freed(s, (0, 1))
                fill(partial.at[s], width, 256, lambda cols: nt(low[rows_of(s), :], cat[cols, :]))
                scatter(s)
                pump()
            fill(mix_own[0], mix_cols, 256, lambda cols: tn(rows_in[...], low[:, cols]))
            fill(mix_own[1], width, 512, lambda cols: tn(gated[...], grad[:, cols]))
            begin(self.mix.steps(mix_own, mix_slots, mix_sems, mix_pieces, mix_outs))
            down_sum[...] = tn(low[:, mix_cols:], rows_in[...])

        f32s = lambda count: [pltpu.VMEM((length, HK), f32)] * count
        pl.run_scoped(
            mixer_phase, pltpu.VMEM((width, mix_cols + 128), bf), pltpu.VMEM((HV, width), bf), pltpu.VMEM((length, mix_cols + 128), f32),
            pltpu.VMEM((length, HV), f32), pltpu.VMEM((length, length), bf), pltpu.VMEM((rows, HV), bf), pltpu.VMEM((rows, mix_cols + 128), bf),
            pltpu.VMEM((length, HV), f32), *f32s(2), pltpu.VMEM((length // CH * 8, HK), f32), pltpu.VMEM((length, HV), bf), *f32s(3))
        for s in range(seqs):
            pump()
            settle(s, entry, gains[l:l + 1, :], attn_sum, top)
        if top:
            local(resid, out_resid, 20).start()
            for s in range(seqs):
                pump()
                collect(s, grad)
                local(of_seq(grad, s, length), of_seq(out_grad, s, length), 21 + s).start()
            local(resid, out_resid, 20).wait()
            for s in range(seqs):
                local(of_seq(grad, s, length), of_seq(out_grad, s, length), 21 + s).wait()
        else:
            small_own[0][...] = jnp.zeros_like(small_own[0])
            small_own[1][...] = jnp.zeros_like(small_own[1])
            at0 = at1 = 0
            for terms in (smalls, smalls_above):
                small_own[0][at0:at0 + rank, :] = terms[0][:rank, :]
                small_own[0][at0 + rank:at0 + rank + 1, :] = terms[1][...]
                small_own[1][at1:at1 + rank, :] = terms[2][:rank, :]
                for k in (3, 4):
                    small_own[1][at1 + rank + k - 3:at1 + rank + k - 2, :] = terms[k][...]
                small_own[1][at1 + rank + 2:at1 + rank + 3, :HV] = terms[5][...]
                at0, at1 = at0 + rank + 8, at1 + rank + 8
            hops = range(self.tensor - 1)

            def to_peer(hop):
                peer = {"tensor": lax.rem(lax.axis_index("tensor") + hop + 1, self.tensor)}
                return remote(small_own[1], shared.at[hop], peer_send.at[hop], peer_recv.at[hop], peer)

            for hop in hops:
                to_peer(hop).start()
            local(last_middle, middle, 20).start()
            for s in range(seqs):
                freed(s, (0, 1))
                local(of_seq(last_partial, s, length), partial.at[s], 8 + s).start()
            pump()
            for hop in hops:
                to_peer(hop).wait()
            small_own[1][...] += sum(shared[hop] for hop in hops)
            begin(self.small.steps(small_own, small_slots, small_sems, None, small_outs))
            for s in range(seqs):
                collect(s, None)
                local(gathered.at[s], of_seq(out_input, s, length), 21 + s).start()
                pump()
            local(last_middle, middle, 20).wait()
            for s in range(seqs):
                local(gathered.at[s], of_seq(out_input, s, length), 21 + s).wait()
                local(of_seq(last_partial, s, length), partial.at[s], 8 + s).wait()
                scatter(s)
                pump()
            for s in range(seqs):
                total = arrived(s)
                mine = pl.ds(s * own, own)
                publish(s, ((middle[mine, :] + total) * keep[mine, :1]).astype(bf).astype(f32))
                pump()
            for s in range(seqs):
                collect(s, grad)
                local(of_seq(grad, s, length), of_seq(out_layer, s, length), 21 + s).start()
                pump()
            for s in range(seqs):
                local(of_seq(grad, s, length), of_seq(out_layer, s, length), 21 + s).wait()
        while jobs:
            pump()
        for s in range(seqs):
            freed(s, range(5))


def shards(
    groups, tensor, layer_input, seq_lengths, attn_gain, query_proj, key_proj, value_proj, gate_proj,
    decay_down, decay_up, decay_bias, group_gain, output_proj, ffn_gain, ffn_gate, ffn_up, ffn_down, cotangent,
):
    seqs, length, width = layer_input.shape
    depth = attn_gain.shape[0]
    rank = decay_down.shape[2]
    rows = seqs * length
    own = length // 4
    me = lax.axis_index("tensor")
    core, cross = me % 2, me // 2
    mix_cols = 2 * HK + 2 * HV
    hidden_units = ffn_gate.shape[2]
    ring = RING if groups % RING == 0 else groups
    def mine(full):
        parts = full.reshape(seqs, 4, own, full.shape[-1])
        return lax.dynamic_slice_in_dim(parts, core * 2 + cross, 1, axis=1).reshape(seqs * own, full.shape[-1])

    keep = (jnp.arange(length, dtype=jnp.int32)[None, :] < seq_lengths[:, None]).astype(f32).reshape(rows, 1)
    keep_mine = jnp.broadcast_to(mine(keep), (seqs * own, 128))
    cat = [
        jnp.concatenate([query_proj[l], key_proj[l], value_proj[l], gate_proj[l], jnp.pad(decay_down[l], ((0, 0), (0, 128 - rank)))], axis=1)
        for l in range(depth)
    ]
    ups = jnp.pad(decay_up, ((0, 0), (0, 128 - rank), (0, 0)))
    gate_t, up_t = ffn_gate.transpose(0, 2, 1), ffn_up.transpose(0, 2, 1)
    found = Forward(depth, seqs, length, width, mix_cols, hidden_units).call(
        0, layer_input.reshape(rows, width), attn_gain, ffn_gain, ups, decay_bias, group_gain, cat, (output_proj, gate_t, up_t, ffn_down))
    kinds = len(found) // depth
    ffn_grad = cotangent.reshape(rows, width) * keep.astype(bf)
    resid = mine(cotangent.reshape(rows, width)).astype(f32) * keep_mine[:, :1]
    params = (attn_gain, ffn_gain, ups, decay_bias, group_gain)

    def backward(top, l, ffn_grad, resid, extra):
        normed, z, gated, mixed, scores, entry, middle, normed_ffn = found[l * kinds:(l + 1) * kinds]
        arrays = (normed_ffn, ffn_grad, resid, middle, entry, z, mixed, scores, gated, normed, gate_t, up_t, ffn_down, cat[l], output_proj)
        return Backward(top, l, ring, tensor, seqs, length, width, mix_cols, hidden_units, rank).call(1 + l, params, arrays, extra)

    ffn_sums, mix_sums = [None] * depth, [None] * depth
    last_partial, ffn_grad, resid, *found_top = backward(True, 1, ffn_grad, resid, ())
    ffn_sums[1] = found_top[:3]
    extra = (*found_top[3:], keep_mine, last_partial, found[kinds + 6])
    input_grad, layer_output, *sums = backward(False, 0, ffn_grad, resid, extra)
    if groups > ring:
        found_sums = lax.psum(tuple(part * (1.0 / ring) for part in (*sums, *ffn_sums[1])), "dp")
        sums, ffn_sums[1] = found_sums[:-3], found_sums[-3:]
    ffn_sums[0], mix_sums[0], mix_sums[1], (local, shared) = sums[:3], sums[3:5], sums[5:7], sums[7:]

    step = rank + 8
    pack = lambda flat, at, height: jnp.stack([flat[l * step + at:l * step + at + height] for l in range(depth)])
    g_up, g_bias = pack(local, 0, rank), pack(local, rank, 1)
    g_down, g_attn, g_ffn, g_group = pack(shared, 0, rank), pack(shared, rank, 1), pack(shared, rank + 1, 1), pack(shared, rank + 2, 1)
    cut = lambda a, b: jnp.stack([mix_sums[l][0][:, a:b] for l in range(depth)])
    pick = lambda sums, k: jnp.stack([sums[l][k] for l in range(depth)])
    return (
        layer_output.reshape(seqs, length, width),
        input_grad.reshape(seqs, length, width),
        g_attn[:, 0],
        cut(0, HK),
        cut(HK, 2 * HK),
        cut(2 * HK, 2 * HK + HV),
        cut(2 * HK + HV, mix_cols),
        g_down.transpose(0, 2, 1),
        g_up,
        g_bias[:, 0],
        g_group[:, 0, :HV],
        pick(mix_sums, 1),
        g_ffn[:, 0],
        pick(ffn_sums, 0).transpose(0, 2, 1),
        pick(ffn_sums, 1).transpose(0, 2, 1),
        pick(ffn_sums, 2),
    )


def solution(mesh):
    over, across = P("dp", None, None), P(None, None, "tensor")
    deep = P(None, "tensor", None)
    return jax.shard_map(
        functools.partial(shards, mesh.shape["dp"], mesh.shape["tensor"]),
        mesh=mesh,
        in_specs=(over, P("dp"), P(), across, across, across, across, P(), across, P(None, "tensor"), P(), deep, P(), across, across, deep, over),
        out_specs=(over, over, P(), across, across, across, across, P(), across, P(None, "tensor"), P(), deep, P(), across, across, deep),
        check_vma=False,
    )
```

```python
import functools
import jax, jax.numpy as jnp
from jax import lax
from jax.experimental import pallas as pl
from jax.experimental.pallas import tpu as pltpu
from jax.sharding import PartitionSpec as P
HK, HV, CH = 128, 256, 128
group_epsilon = 1e-05
bf, f32 = jnp.bfloat16, jnp.float32
SCALE = HK ** -0.5

def nn(a, b):
    return lax.dot_general(a, b, (((1,), (0,)), ((), ())), preferred_element_type=f32)
def nt(a, b):
    return lax.dot_general(a, b, (((1,), (1,)), ((), ())), preferred_element_type=f32)
def tn(a, b):
    return lax.dot_general(a, b, (((0,), (0,)), ((), ())), preferred_element_type=f32)

def halves(a):
    top = a.astype(bf)
    return top, (a - top.astype(f32)).astype(bf)

def thirds(a):
    top = a.astype(bf)
    return (top,) + halves(a - top.astype(f32))

def sigmoid(a):
    return 1.0 / (1.0 + jnp.exp(-a))

def log_sigmoid(a):
    return jnp.minimum(a, 0.0) - jnp.log1p(jnp.exp(-jnp.abs(a)))

def steps_below(n):
    out, h = [], 1
    while h < n:
        out.append(h)
        h *= 2
    return out

def decay_sums(ld):
    n = ld.shape[0]
    rows = lax.broadcasted_iota(jnp.int32, ld.shape, 0)
    total, pre, suf = ld, ld, jnp.zeros_like(ld)
    levels = []
    for h in steps_below(n):
        upper = (rows & h) != 0
        levels.append((h, upper, jnp.exp(jnp.where(upper, pre, suf))))
        below, above = pltpu.roll(total, h, 0), pltpu.roll(total, n - h, 0)
        pre = jnp.where(upper, pre + below, pre)
        suf = jnp.where(upper, suf, suf + above)
        total = total + jnp.where(upper, below, above)
    return levels, pre, suf, total

def tile_rows(c):
    return pl.ds(c * CH, CH)

def logits_of(z, up_ref, bias_ref):
    return sum(nn(piece, up_ref[...]) for piece in thirds(z[:, 2 * HK + 2 * HV:])) + bias_ref[...]

def wide_levels(chunks):
    out, h = [], 1
    while h < chunks:
        for base in range(0, chunks, 2 * h):
            out.append((tuple(range(base, base + h)), tuple(range(base + h, base + 2 * h))))
        h *= 2
    return out

def wide_factor(c, group, is_upper, pre, suf, tot):
    arg = pre[tile_rows(c), :] if is_upper else suf[tile_rows(c), :]
    for o in group:
        if (o < c) if is_upper else (o > c):
            arg = arg + tot[pl.ds(o * 8, 1), :]
    return jnp.exp(arg)

def mixer_forward(z_ref, up_ref, bias_ref, gain_ref, gated_ref, mixed_ref, scores_ref, pre, suf, tot):
    chunks = z_ref.shape[0] // CH
    i = lax.broadcasted_iota(jnp.int32, (CH, CH), 0)
    j = lax.broadcasted_iota(jnp.int32, (CH, CH), 1)
    apart = i ^ j
    scores_ref[...] = jnp.zeros_like(scores_ref)
    for c in range(chunks):
        z = z_ref[tile_rows(c), :]
        q, k = z[:, :HK].astype(bf), z[:, HK:2 * HK].astype(bf)
        ld = log_sigmoid(logits_of(z, up_ref, bias_ref)) / 16.0
        levels, p, s, t = decay_sums(ld)
        pre[tile_rows(c), :], suf[tile_rows(c), :], tot[pl.ds(c * 8, 8), :] = p, s, t[:8]
        tile = nt(q, k)
        qf, kf = q.astype(f32), k.astype(f32)
        for h, upper, factor in levels:
            rows = (jnp.where(upper, qf, kf) * factor).astype(bf)
            tile = jnp.where(apart >= h, nt(rows, rows), tile)
        scores_ref[tile_rows(c), tile_rows(c)] = jnp.where(i >= j, tile * SCALE, 0.0).astype(bf)
    for low_group, up_group in wide_levels(chunks):
        q_rows = [(z_ref[tile_rows(c), :HK].astype(bf).astype(f32) * wide_factor(c, up_group, True, pre, suf, tot)).astype(bf) for c in up_group]
        k_rows = [(z_ref[tile_rows(c), HK:2 * HK].astype(bf).astype(f32) * wide_factor(c, low_group, False, pre, suf, tot)).astype(bf) for c in low_group]
        for a, c in enumerate(up_group):
            for b, o in enumerate(low_group):
                scores_ref[tile_rows(c), tile_rows(o)] = (nt(q_rows[a], k_rows[b]) * SCALE).astype(bf)
    for c in range(chunks):
        width = (c + 1) * CH
        mixed = nn(scores_ref[tile_rows(c), :width], z_ref[:width, 2 * HK:2 * HK + HV].astype(bf))
        mixed_ref[tile_rows(c), :] = mixed
        out_gate = z_ref[tile_rows(c), 2 * HK + HV:2 * HK + 2 * HV]
        normed = mixed * lax.rsqrt(jnp.mean(mixed * mixed, axis=-1, keepdims=True) + group_epsilon) * gain_ref[...]
        gated_ref[tile_rows(c), :] = (normed * out_gate * sigmoid(out_gate)).astype(bf)

def mixer_backward(fresh, z_ref, up_ref, bias_ref, gain_ref, mixed_ref, scores_ref, grad_ref,
                   out_ref, up_out, bias_out, gain_out, pre, suf, tot, dm_ref, dq_ref, dk_ref, flow):
    chunks = z_ref.shape[0] // CH
    i = lax.broadcasted_iota(jnp.int32, (CH, CH), 0)
    j = lax.broadcasted_iota(jnp.int32, (CH, CH), 1)
    apart = i ^ j
    rows_in = lax.broadcasted_iota(jnp.int32, (CH, HK), 0)

    if fresh:
        up_out[...] = jnp.zeros_like(up_out)
        bias_out[...] = jnp.zeros_like(bias_out)
        gain_out[...] = jnp.zeros_like(gain_out)
    for c in range(chunks):
        mixed, e = mixed_ref[tile_rows(c), :], grad_ref[tile_rows(c), :]
        g = z_ref[tile_rows(c), 2 * HK + HV:2 * HK + 2 * HV]
        r = lax.rsqrt(jnp.mean(mixed * mixed, axis=-1, keepdims=True) + group_epsilon)
        sig = sigmoid(g)
        unit = mixed * r
        out_ref[tile_rows(c), 2 * HK + HV:2 * HK + 2 * HV] = (e * unit * gain_ref[...] * (sig + g * sig * (1.0 - sig))).astype(bf)
        upstream = e * g * sig
        gain_out[...] += jnp.sum(upstream * unit, axis=0, keepdims=True)
        weighted = upstream * gain_ref[...]
        dm_ref[tile_rows(c), :] = (r * (weighted - unit * jnp.mean(unit * weighted, axis=-1, keepdims=True))).astype(bf)

    def score_grad(c, o):
        return nt(dm_ref[tile_rows(c), :], z_ref[tile_rows(o), 2 * HK:2 * HK + HV].astype(bf)) * SCALE

    for c in range(chunks):
        z = z_ref[tile_rows(c), :]
        q, k = z[:, :HK].astype(bf).astype(f32), z[:, HK:2 * HK].astype(bf).astype(f32)
        ld = log_sigmoid(logits_of(z, up_ref, bias_ref)) / 16.0
        levels, p, s, t = decay_sums(ld)
        pre[tile_rows(c), :], suf[tile_rows(c), :], tot[pl.ds(c * 8, 8), :] = p, s, t[:8]
        ds = score_grad(c, c)
        diagonal = jnp.sum(jnp.where(i == j, ds, 0.0), axis=-1, keepdims=True)
        ds = jnp.where(i > j, ds, 0.0)
        both = ds + ds.T
        dq, dk = diagonal * k, diagonal * q
        fl = jnp.zeros_like(dq)
        for h, upper, factor in levels:
            rows = (jnp.where(upper, q, k) * factor).astype(bf)
            near = jnp.where((apart >= h) & (apart < 2 * h), both, 0.0).astype(bf)
            back = nn(near, rows)
            part = back * factor
            dq, dk = dq + jnp.where(upper, part, 0.0), dk + jnp.where(upper, 0.0, part)
            moved = back * rows.astype(f32)
            fl = fl + jnp.where(upper, moved, -moved)
        dq_ref[tile_rows(c), :], dk_ref[tile_rows(c), :], flow[tile_rows(c), :] = dq, dk, fl
    for low_group, up_group in wide_levels(chunks):
        q_fac = [wide_factor(c, up_group, True, pre, suf, tot) for c in up_group]
        k_fac = [wide_factor(c, low_group, False, pre, suf, tot) for c in low_group]
        q_rows = [(z_ref[tile_rows(c), :HK].astype(bf).astype(f32) * f).astype(bf) for c, f in zip(up_group, q_fac)]
        k_rows = [(z_ref[tile_rows(c), HK:2 * HK].astype(bf).astype(f32) * f).astype(bf) for c, f in zip(low_group, k_fac)]
        grads = [[score_grad(c, o).astype(bf) for o in low_group] for c in up_group]
        for a, c in enumerate(up_group):
            back = sum(nn(grads[a][b], k_rows[b]) for b in range(len(low_group)))
            dq_ref[tile_rows(c), :] += back * q_fac[a]
            flow[tile_rows(c), :] += back * q_rows[a].astype(f32)
        for b, o in enumerate(low_group):
            back = sum(tn(grads[a][b], q_rows[a]) for a in range(len(up_group)))
            dk_ref[tile_rows(o), :] += back * k_fac[b]
            flow[tile_rows(o), :] -= back * k_rows[b].astype(f32)
    later = jnp.zeros((1, HK), f32)
    for c in reversed(range(chunks)):
        out_ref[tile_rows(c), :HK] = dq_ref[tile_rows(c), :].astype(bf)
        out_ref[tile_rows(c), HK:2 * HK] = dk_ref[tile_rows(c), :].astype(bf)
        out_ref[tile_rows(c), 2 * HK:2 * HK + HV] = tn(scores_ref[pl.ds(c * CH, (chunks - c) * CH), tile_rows(c)], dm_ref[pl.ds(c * CH, (chunks - c) * CH), :]).astype(bf)
        fl = flow[tile_rows(c), :]
        for h in steps_below(CH):
            fl = fl + jnp.where(rows_in < CH - h, pltpu.roll(fl, CH - h, 0), 0.0)
        fl = fl + later
        later = fl[:1]
        z = z_ref[tile_rows(c), :]
        logits = logits_of(z, up_ref, bias_ref)
        d_logit = fl * sigmoid(-logits) / 16.0
        bias_out[...] += jnp.sum(d_logit, axis=0, keepdims=True)
        d1, d2 = halves(d_logit)
        l1, l2 = halves(z[:, 2 * HK + 2 * HV:])
        up_out[...] += tn(l1, d1) + tn(l1, d2) + tn(l2, d1)
        out_ref[tile_rows(c), 2 * HK + 2 * HV:] = (nt(d1, up_ref[...]) + nt(d2, up_ref[...])).astype(bf)


norm_epsilon = 1e-06
MESH = pl.DeviceIdType.MESH
VMEM_SPEC = pl.BlockSpec(memory_space=pltpu.VMEM)
ANY_SPEC = pl.BlockSpec(memory_space=pl.ANY)
DMA = pltpu.SemaphoreType.DMA
RING = 8


def peer_of(index, bit):
    return jnp.where((index // bit) % 2 == 0, index + bit, index - bit)


def rms_unit(h):
    return lax.rsqrt(jnp.mean(h * h, axis=-1, keepdims=True) + norm_epsilon)


def remote(src, dst, send, recv, peer):
    return pltpu.make_async_remote_copy(
        src_ref=src, dst_ref=dst, send_sem=send, recv_sem=recv, device_id=peer, device_id_type=MESH
    )


def ring_place(n):
    index = lax.rem(lax.axis_index("dp"), n)
    return jnp.where(index % 2 == 0, index // 2, n - 1 - index // 2)


def ring_peer(ahead, n):
    place = lax.rem(ring_place(n) + ahead, n)
    index = lax.axis_index("dp")
    return {"dp": index - lax.rem(index, n) + jnp.where(place < n // 2, 2 * place, 2 * (n - 1 - place) + 1)}


def ring_cut(shape, n):
    rows, cols = shape
    if rows % (16 * n) == 0:
        return rows // (2 * n), cols, True
    if rows % (8 * n) == 0 and cols % 256 == 0:
        return rows // n, cols // 2, False
    return None


def tiles(total, size):
    return [(start, min(size, total - start)) for start in range(0, total, size)]


class Forward:
    def __init__(self, depth, seqs, length, width, mix_cols, hidden_units):
        self.depth, self.seqs, self.length, self.width = depth, seqs, length, width
        self.z_cols, self.hidden_units = mix_cols + 128, hidden_units
        rows, quarter = seqs * length, seqs * length // 4
        self.saved = []
        for _ in range(depth):
            self.saved += [
                ((rows, width), bf), ((rows, self.z_cols), f32), ((rows, HV), bf), ((rows, HV), f32), ((rows, length), bf),
                ((quarter, width), f32), ((quarter, width), f32), ((rows, width), bf),
            ]

    def call(self, collective, x, gains, ffn_gains, ups, bias, group, cats, stacked):
        depth, seqs, length, width = self.depth, self.seqs, self.length, self.width
        own = length // 4
        weights = [(w.shape, w.dtype) for w in cats] + [(stacked[0].shape[1:], bf)] * depth
        weights += [(w.shape[1:], bf) for _ in range(depth - 1) for w in stacked[1:]]
        saved = [jax.ShapeDtypeStruct(shape, kind) for shape, kind in self.saved]
        scratch = [pltpu.VMEM(shape, kind) for shape, kind in self.saved]
        scratch += [pltpu.VMEM(shape, kind) for shape, kind in weights]
        scratch += [
            pltpu.VMEM((seqs, length, width), f32), pltpu.VMEM((seqs, 2 * own, width), f32), pltpu.VMEM((seqs, own, width), f32),
            pltpu.VMEM((seqs, own, width), f32), pltpu.VMEM((seqs, own, width), f32), pltpu.VMEM((seqs, length, width), f32),
            pltpu.VMEM((length, self.hidden_units), bf),
            pltpu.VMEM((length, HK), f32), pltpu.VMEM((length, HK), f32), pltpu.VMEM((length // CH * 8, HK), f32),
            DMA((len(saved), seqs)), DMA((len(weights),)), DMA((5, seqs)), DMA((5, seqs)),
        ]
        return pl.pallas_call(
            self.kernel, name="forward_blocks",
            in_specs=[VMEM_SPEC] * 6 + [ANY_SPEC] * (depth + len(stacked)), out_specs=[ANY_SPEC] * len(saved), out_shape=saved,
            scratch_shapes=scratch,
            compiler_params=pltpu.CompilerParams(collective_id=collective, has_side_effects=True, vmem_limit_bytes=60 << 20),
            cost_estimate=pl.CostEstimate(flops=10**10, bytes_accessed=2 * 10**8, transcendentals=0),
        )(x, gains, ffn_gains, ups, bias, group, *cats, *stacked)

    def kernel(self, *refs):
        depth, seqs, length = self.depth, self.seqs, self.length
        half, own = length // 2, length // 4
        kinds = len(self.saved) // depth
        refs = list(refs)

        def take(count):
            found = refs[:count]
            del refs[:count]
            return found

        x, gains, ffn_gains, ups, bias, group = take(6)
        count = 2 * depth + 3 * (depth - 1)
        cats, stacked = take(depth), take(4)
        from_hbm = cats + [stacked[0].at[l] for l in range(depth)] + [w.at[l] for l in range(depth - 1) for w in stacked[1:]]
        outs = take(len(self.saved))
        kept_for_later = take(len(self.saved))
        weights = take(count)
        partial, first, second, passed, kept, gathered, inner, pre, suf, tot, store, load, send, recv = take(14)
        me = lax.axis_index("tensor")
        core, cross = me % 2, me // 2
        core_peer, cross_peer = {"tensor": peer_of(me, 1)}, {"tensor": peer_of(me, 2)}
        loads = [pltpu.make_async_copy(src, dst, load.at[k]) for k, (src, dst) in enumerate(zip(from_hbm, weights))]
        order = [k for l in range(depth) for k in [l, depth + l] + [2 * depth + 3 * l + j for j in range(3) if l + 1 < depth]]
        for k in order:
            loads[k].start()
        barrier = pltpu.get_barrier_semaphore()
        for peer in (core_peer, cross_peer):
            pl.semaphore_signal(barrier, inc=1, device_id=peer, device_id_type=MESH)
        pl.semaphore_wait(barrier, 2)
        sent, stores = {}, []

        def copy(src, dst, stage, s, peer):
            if (stage, s) in sent:
                sent[stage, s].wait_send()
            step = remote(src, dst, send.at[stage, s], recv.at[stage, s], peer)
            step.start()
            sent[stage, s] = step
            return step

        def piece(c, x_half, size):
            return pl.ds(pl.multiple_of(c * half + x_half * own, own), size)

        def of_seq(ref, s, height):
            return ref.at[pl.ds(s * height, height)]

        def keep_for_later(k, s):
            height = self.saved[k][0][0] // seqs
            step = pltpu.make_async_copy(of_seq(kept_for_later[k], s, height), of_seq(outs[k], s, height), store.at[k, s])
            step.start()
            stores.append(step)

        def scatter(s):
            copy(partial.at[s, piece(1 - core, 0, half)], first.at[s], 0, s, core_peer)
            sent[0, s].wait_recv()
            for stage in (1, 2, 3, 4):
                if (stage, s) in sent:
                    sent[stage, s].wait_send()
                    del sent[stage, s]
            passed[s] = partial[s, piece(core, 1 - cross, own), :] + first[s, piece(0, 1 - cross, own), :]
            copy(passed.at[s], second.at[s], 1, s, cross_peer)
            kept[s] = partial[s, piece(core, cross, own), :] + first[s, piece(0, cross, own), :]

        def settle(s, resid, new_resid, gain):
            sent[1, s].wait_recv()
            mine = pl.ds(s * own, own)
            new = resid[mine, :] + (kept[s] + second[s])
            new_resid[mine, :] = new
            gathered[s, piece(core, cross, own), :] = (new * rms_unit(new) * gain).astype(bf).astype(f32)
            block = gathered.at[s, piece(core, cross, own)]
            copy(block, block, 2, s, cross_peer)
            copy(block, block, 3, s, core_peer)

        def collect(s, dest):
            sent[2, s].wait_recv()
            block = gathered.at[s, piece(core, 1 - cross, own)]
            copy(block, block, 4, s, core_peer)
            dest[pl.ds(pl.multiple_of(s * length + core * half, half), half), :] = gathered[s, piece(core, 0, half), :].astype(bf)
            sent[3, s].wait_recv()
            sent[4, s].wait_recv()
            dest[pl.ds(pl.multiple_of(s * length + (1 - core) * half, half), half), :] = gathered[s, piece(1 - core, 0, half), :].astype(bf)

        def rows_of(s):
            return pl.ds(s * length, length)

        for l in range(depth):
            normed, z, gated, mixed, scores, entry, middle, normed_ffn = kept_for_later[l * kinds:(l + 1) * kinds]
            for s in range(seqs):
                if l == 0:
                    for part in range(4):
                        block = pl.ds(s * length + part * own, own)
                        h = x[block, :].astype(f32)
                        normed[block, :] = (h * rms_unit(h) * gains[l:l + 1, :]).astype(bf)
                    entry[pl.ds(s * own, own), :] = x[pl.ds(pl.multiple_of(s * length + core * half + cross * own, own), own), :].astype(f32)
                    if s == 0:
                        loads[l].wait()
                else:
                    collect(s, normed)
                    if s == 0:
                        loads[l].wait()
                keep_for_later(l * kinds, s)
                for start, size in tiles(self.z_cols, 256):
                    cols = pl.ds(start, size)
                    z[rows_of(s), cols] = nn(normed[rows_of(s), :], weights[l][:, cols])
                keep_for_later(l * kinds + 1, s)
                mixer_forward(
                    of_seq(z, s, length), ups.at[l], bias.at[pl.ds(l, 1)], group.at[pl.ds(l, 1)], of_seq(gated, s, length),
                    of_seq(mixed, s, length), of_seq(scores, s, length), pre, suf, tot)
                for k in (2, 3, 4):
                    keep_for_later(l * kinds + k, s)
                if s == 0:
                    loads[depth + l].wait()
                if (0, s) in sent:
                    sent[0, s].wait_send()
                    del sent[0, s]
                for start, size in tiles(self.width, 256):
                    cols = pl.ds(start, size)
                    partial[s, :, cols] = nn(gated[rows_of(s), :], weights[depth + l][:, cols])
                scatter(s)
            for s in range(seqs):
                settle(s, entry, middle, ffn_gains[l:l + 1, :])
                keep_for_later(l * kinds + 5, s)
                keep_for_later(l * kinds + 6, s)
            if l + 1 == depth:
                break
            gate_w, up_w, down_w = weights[2 * depth + 3 * l:2 * depth + 3 * l + 3]
            for s in range(seqs):
                collect(s, normed_ffn)
                keep_for_later(l * kinds + 7, s)
                if s == 0:
                    for j in range(3):
                        loads[2 * depth + 3 * l + j].wait()
                for start, size in tiles(self.hidden_units, 256):
                    cols = pl.ds(start, size)
                    gate_act = nt(normed_ffn[rows_of(s), :], gate_w[cols, :])
                    up_act = nt(normed_ffn[rows_of(s), :], up_w[cols, :])
                    inner[:, cols] = (gate_act * sigmoid(gate_act) * up_act).astype(bf)
                sent[0, s].wait_send()
                del sent[0, s]
                for start, size in tiles(self.width, 256):
                    cols = pl.ds(start, size)
                    partial[s, :, cols] = nn(inner[...], down_w[:, cols])
                scatter(s)
            for s in range(seqs):
                settle(s, middle, kept_for_later[(l + 1) * kinds + 5], gains[l + 1:l + 2, :])
        for s in range(seqs):
            collect(s, kept_for_later[(depth - 1) * kinds + 7])
            keep_for_later((depth - 1) * kinds + 7, s)
        for step in sent.values():
            step.wait_send()
        for step in stores:
            step.wait()


class RingJob:
    def __init__(self, n, shapes, reduce, gather):
        self.n, self.shapes, self.reduce, self.gather = n, shapes, reduce, gather
        self.cuts = [ring_cut(shape, n) for shape in shapes]
        self.pairs = [(a, way) for a in range(len(shapes)) for way in range(2)]

    def slots(self):
        return [pltpu.VMEM((2, self.n - 1, rows, cols), f32) for rows, cols, _ in self.cuts] if self.reduce else []

    def sems(self):
        each = DMA((self.n - 1, len(self.shapes), 2))
        return [each, each] * (self.reduce + self.gather) + ([DMA((len(self.shapes), 2))] if self.gather else [])

    def pieces(self):
        return [jax.ShapeDtypeStruct((2, rows, cols), f32) for rows, cols, _ in self.cuts]

    def full(self):
        return [jax.ShapeDtypeStruct(shape, f32) for shape in self.shapes]

    def segment(self, a, way, back):
        n = self.n
        place = ring_place(n)
        index = lax.rem((place if way == 0 else n - 1 - place) + (2 * n - back), n)
        rows, cols, by_rows = self.cuts[a]
        if by_rows:
            return (pl.ds(pl.multiple_of((index * 2 + way) * rows, rows), rows), pl.ds(0, cols))
        return (pl.ds(pl.multiple_of(index * rows, rows), rows), pl.ds(way * cols, cols))

    def hop(self, src, dst, sems, step, a, way):
        peer = ring_peer(1 if way == 0 else self.n - 1, self.n)
        return remote(src, dst, sems[0].at[step, a, way], sems[1].at[step, a, way], peer)

    def steps(self, own, slots, sems, pieces, outs):
        n = self.n
        if self.reduce:
            rs, sems = sems[:2], sems[2:]
            for a, way in self.pairs:
                self.hop(own[a].at[self.segment(a, way, 0)], slots[a].at[way, 0], rs, 0, a, way).start()
            for step in range(n - 1):
                yield
                for a, way in self.pairs:
                    slot = slots[a].at[way, step]
                    self.hop(slot, slot, rs, step, a, way).wait_recv()
                    self.add(a, way, slot, own[a], slot if self.gather or step < n - 2 else pieces[a].at[way], step + 1)
                    if step < n - 2:
                        self.hop(slot, slots[a].at[way, step + 1], rs, step + 1, a, way).start()
                    elif self.gather:
                        self.begin(a, way, slot, sems, outs)
        else:
            for a, way in self.pairs:
                self.begin(a, way, pieces[a].at[way], sems, outs)
        if self.gather:
            for step in range(n - 1):
                yield
                for a, way in self.pairs:
                    piece = outs[a].at[self.segment(a, way, step)]
                    self.hop(piece, piece, sems, step, a, way).wait_recv()
                    if step < n - 2:
                        self.hop(piece, piece, sems, step + 1, a, way).start()
            for a, way in self.pairs:
                end = slots[a].at[way, n - 2] if self.reduce else pieces[a].at[way]
                pltpu.make_async_copy(end, outs[a].at[self.segment(a, way, n - 1)], sems[2].at[a, way]).wait()
        for step in range(n - 1):
            for a, way in self.pairs:
                if self.reduce:
                    self.hop(slots[a].at[way, 0], slots[a].at[way, 0], rs, step, a, way).wait_send()
                if self.gather:
                    piece = outs[a].at[self.segment(a, way, 0)]
                    self.hop(piece, piece, sems, step, a, way).wait_send()

    def begin(self, a, way, piece, sems, outs):
        place = outs[a].at[self.segment(a, way, self.n - 1)]
        self.hop(piece, place, sems, 0, a, way).start()
        pltpu.make_async_copy(piece, place, sems[2].at[a, way]).start()

    def add(self, a, way, slot, own, out, back):
        row_ds, col_ds = self.segment(a, way, back)

        @pl.loop(0, self.cuts[a][0] // 8)
        def _(block):
            here = pl.ds(pl.multiple_of(block * 8, 8), 8)
            there = pl.ds(pl.multiple_of(row_ds.start + block * 8, 8), 8)
            out[here, :] = slot[here, :] + own[there, col_ds]


def fill(dst, total, size, make):
    for start, extent in tiles(total, size):
        cols = pl.ds(start, extent)
        dst[:, cols] = make(cols)


class Backward:
    def __init__(self, top, l, n, tensor, seqs, length, width, mix_cols, hidden_units, rank):
        self.top, self.l, self.n, self.tensor, self.rank = top, l, n, tensor, rank
        self.seqs, self.length, self.width, self.mix_cols, self.hidden_units = seqs, length, width, mix_cols, hidden_units
        self.ffn = RingJob(n, [(hidden_units, width)] * 3, True, True)
        mix_shapes = [(width, mix_cols), (HV, width)]
        self.mix = RingJob(n, mix_shapes, True, not top)
        self.above = RingJob(n, mix_shapes, False, True)
        self.small = RingJob(n, [(16 * n, HK), (8 * n, width)], True, True)

    def small_outs(self):
        width = self.width
        return [jax.ShapeDtypeStruct(shape, f32) for shape in ((128, HK), (1, HK), (128, width), (1, width), (1, width), (1, HV))]

    def call(self, collective, params, arrays, extra):
        seqs, length, width = self.seqs, self.length, self.width
        rows, own = seqs * length, length // 4
        wide = jax.ShapeDtypeStruct((rows, width), bf)
        wide32, quarter = jax.ShapeDtypeStruct((rows, width), f32), jax.ShapeDtypeStruct((seqs * own, width), f32)
        smalls = self.small_outs()
        if self.top:
            outs = [wide32, wide, quarter] + self.ffn.full()
            vmem_outs = self.mix.pieces() + smalls
            vmem_ins = 0
        else:
            outs = [wide32, wide] + self.ffn.full() + self.mix.full() + self.above.full() + self.small.full()
            vmem_outs = []
            vmem_ins = len(extra) - 2
        scratch = [pltpu.VMEM(shape.shape, f32) for shape in self.ffn.full() + self.mix.full()]
        scratch += self.ffn.slots() + self.mix.slots() + self.ffn.sems() + self.mix.sems()
        if not self.top:
            scratch += self.above.sems() + [pltpu.VMEM(shape.shape, f32) for shape in self.small.full()] + self.small.slots() + self.small.sems()
            scratch += [pltpu.VMEM((self.tensor - 1, 8 * self.n, width), f32), DMA((self.tensor - 1,)), DMA((self.tensor - 1,))]
            scratch += [pltpu.VMEM(shape.shape, f32) for shape in smalls]
        scratch += [
            pltpu.VMEM((seqs, length, width), f32), pltpu.VMEM((seqs, 2 * own, width), f32), pltpu.VMEM((seqs, own, width), f32),
            pltpu.VMEM((seqs, length, width), f32), pltpu.VMEM((rows, width), bf), pltpu.VMEM((rows, width), bf),
            pltpu.VMEM(quarter.shape, f32), pltpu.VMEM(quarter.shape, f32), pltpu.VMEM(quarter.shape, f32),
            DMA((24,)), DMA((5, seqs)), DMA((5, seqs)),
        ]
        return pl.pallas_call(
            self.kernel, name="backward_top" if self.top else "backward_low",
            in_specs=[VMEM_SPEC] * len(params) + [ANY_SPEC] * len(arrays) + [VMEM_SPEC] * vmem_ins + [ANY_SPEC] * (len(extra) - vmem_ins),
            out_specs=[ANY_SPEC] * len(outs) + [VMEM_SPEC] * len(vmem_outs), out_shape=outs + vmem_outs, scratch_shapes=scratch,
            compiler_params=pltpu.CompilerParams(collective_id=collective, has_side_effects=True, vmem_limit_bytes=61 << 20),
            cost_estimate=pl.CostEstimate(flops=10**10, bytes_accessed=3 * 10**8, transcendentals=0),
        )(*params, *arrays, *extra)

    def kernel(self, *refs):
        top, l, seqs, length, width, rank = self.top, self.l, self.seqs, self.length, self.width, self.rank
        mix_cols, hidden_units = self.mix_cols, self.hidden_units
        half, own, rows = length // 2, length // 4, seqs * length
        refs = list(refs)

        def take(count):
            found = refs[:count]
            del refs[:count]
            return found

        gains, ffn_gains, ups, bias, group = take(5)
        normed_ffn, ffn_grad, resid_in, middle_in, entry_in, z_in, mixed_in, scores_in, gated_in, normed_in = take(10)
        gate_in, up_in, down_in, cat_in, heads_in = take(5)
        if top:
            out_partial, out_grad, out_resid = take(3)
            ffn_outs, mix_outs = take(3), None
            mix_pieces, smalls = take(2), take(6)
        else:
            above_pieces, smalls_above, keep = take(2), take(6), take(1)[0]
            last_partial, last_middle = take(2)
            out_input, out_layer = take(2)
            ffn_outs, mix_outs, above_outs, small_outs = take(3), take(2), take(2), take(2)
            mix_pieces = None
        ffn_own, mix_own, ffn_slots, mix_slots = take(3), take(2), take(3), take(2)
        ffn_sems, mix_sems = take(len(self.ffn.sems())), take(len(self.mix.sems()))
        if not top:
            above_sems, small_own, small_slots, small_sems = take(len(self.above.sems())), take(2), take(2), take(len(self.small.sems()))
            shared, peer_send, peer_recv = take(3)
            smalls = take(6)
        up_sum, bias_sum, down_sum, attn_sum, ffn_sum, group_sum = smalls
        partial, first, second, gathered, rows_in, grad, resid, middle, entry, load, send, recv = take(12)
        pending = set()

        def ids():
            me = lax.axis_index("tensor")
            return me % 2, me // 2, {"tensor": peer_of(me, 1)}, {"tensor": peer_of(me, 2)}

        def piece(c, x_half, size):
            return pl.ds(pl.multiple_of(c * half + x_half * own, own), size)

        def of_seq(ref, s, height):
            return ref.at[pl.ds(s * height, height)]

        def plain(stage, s):
            src = (partial.at[s, pl.ds(0, half)], partial.at[s, pl.ds(0, own)])[stage] if stage < 2 else gathered.at[s, pl.ds(0, own)]
            dst = (first.at[s], second.at[s])[stage] if stage < 2 else src
            return remote(src, dst, send.at[stage, s], recv.at[stage, s], ids()[2 if stage in (0, 3, 4) else 3])

        def launch(src, dst, stage, s, peer):
            remote(src, dst, send.at[stage, s], recv.at[stage, s], peer).start()
            pending.add((stage, s))

        def freed(s, stages):
            for stage in stages:
                if (stage, s) in pending:
                    plain(stage, s).wait_send()
                    pending.discard((stage, s))

        def scatter(s):
            core, cross, core_peer, cross_peer = ids()
            launch(partial.at[s, piece(1 - core, 0, half)], first.at[s], 0, s, core_peer)
            plain(0, s).wait_recv()
            freed(s, (2, 3, 4))
            partial[s, piece(core, 1 - cross, own), :] += first[s, piece(0, 1 - cross, own), :]
            launch(partial.at[s, piece(core, 1 - cross, own)], second.at[s], 1, s, cross_peer)
            partial[s, piece(core, cross, own), :] += first[s, piece(0, cross, own), :]

        def arrived(s):
            core, cross, _, _ = ids()
            plain(1, s).wait_recv()
            return partial[s, piece(core, cross, own), :] + second[s]

        def publish(s, sent):
            core, cross, core_peer, cross_peer = ids()
            gathered[s, piece(core, cross, own), :] = sent
            block = gathered.at[s, piece(core, cross, own)]
            launch(block, block, 2, s, cross_peer)
            launch(block, block, 3, s, core_peer)

        def settle(s, h_ref, gain, gain_sum, rounded):
            total = arrived(s)
            mine = pl.ds(s * own, own)
            h = h_ref[mine, :]
            r = rms_unit(h)
            unit = h * r
            here = jnp.sum(total * unit, axis=0, keepdims=True)
            gain_sum[...] = here if s == 0 else gain_sum[...] + here
            weighted = total * gain
            new = resid[mine, :] + r * (weighted - unit * jnp.mean(unit * weighted, axis=-1, keepdims=True))
            resid[mine, :] = new
            publish(s, new.astype(bf).astype(f32) if rounded else new)

        def collect(s, dest):
            core, cross, core_peer, _ = ids()
            plain(2, s).wait_recv()
            block = gathered.at[s, piece(core, 1 - cross, own)]
            launch(block, block, 4, s, core_peer)
            if dest is not None:
                dest[pl.ds(pl.multiple_of(s * length + core * half, half), half), :] = gathered[s, piece(core, 0, half), :].astype(bf)
            plain(3, s).wait_recv()
            plain(4, s).wait_recv()
            if dest is not None:
                dest[pl.ds(pl.multiple_of(s * length + (1 - core) * half, half), half), :] = gathered[s, piece(1 - core, 0, half), :].astype(bf)

        jobs = []
        over = object()

        def pump(count=1):
            for _ in range(count):
                turns = max([times for _, times in jobs], default=0)
                for turn in range(turns):
                    for job in list(jobs):
                        if turn < job[1] and next(job[0], over) is over:
                            jobs.remove(job)

        def begin(job, times=1):
            next(job)
            jobs.append((job, times))

        def local(src, dst, k):
            return pltpu.make_async_copy(src, dst, load.at[k])

        def rows_of(s):
            return pl.ds(s * length, length)

        basics = [(normed_ffn, rows_in, 0), (ffn_grad, grad, 1), (resid_in, resid, 2), (middle_in, middle, 3), (entry_in, entry, 4)]
        for src, dst, k in basics:
            local(src, dst, k).start()
        barrier = pltpu.get_barrier_semaphore()
        peers = [ring_peer(hop, self.n) for hop in (1, self.n - 1)]
        peers += list(ids()[2:]) if top else [{"tensor": lax.rem(lax.axis_index("tensor") + hop, self.tensor)} for hop in range(1, self.tensor)]
        for peer in peers:
            pl.semaphore_signal(barrier, inc=1, device_id=peer, device_id_type=MESH)
        pl.semaphore_wait(barrier, len(peers))
        if not top:
            begin(self.above.steps(None, None, above_sems, above_pieces, above_outs))

        def ffn_phase(gate_w, up_w, down_w, inner, gate_low, up_low):
            weights = [(gate_in.at[l], gate_w, 5), (up_in.at[l], up_w, 6), (down_in.at[l], down_w, 7)]
            for src, dst, k in weights:
                local(src, dst, k).start()
            for src, dst, k in basics + weights:
                local(src, dst, k).wait()
            for s in range(seqs):
                here = rows_of(s)
                for start, size in tiles(hidden_units, 256):
                    cols = pl.ds(start, size)
                    gate_act, up_act = nt(rows_in[here, :], gate_w[cols, :]), nt(rows_in[here, :], up_w[cols, :])
                    inner_grad = nt(grad[here, :], down_w[cols, :])
                    sig = sigmoid(gate_act)
                    swish = gate_act * sig
                    inner[here, cols] = (swish * up_act).astype(bf)
                    gate_low[here, cols] = (inner_grad * up_act * sig * (1.0 + gate_act * (1.0 - sig))).astype(bf)
                    up_low[here, cols] = (inner_grad * swish).astype(bf)
                pump()
            fill(ffn_own[0], width, 512, lambda cols: tn(gate_low[...], rows_in[:, cols]))
            fill(ffn_own[1], width, 512, lambda cols: tn(up_low[...], rows_in[:, cols]))
            pump()
            fill(ffn_own[2], width, 512, lambda cols: tn(inner[...], grad[:, cols]))
            begin(self.ffn.steps(ffn_own, ffn_slots, ffn_sems, None, ffn_outs))
            if top:
                for s in range(seqs):
                    fill(partial.at[s], width, 256, lambda cols: nn(inner[rows_of(s), :], down_w[:, cols]))
                    local(partial.at[s], of_seq(out_partial, s, length), 8 + s).start()
            for s in range(seqs):
                if top:
                    local(partial.at[s], of_seq(out_partial, s, length), 8 + s).wait()
                fill(partial.at[s], width, 256, lambda cols: nn(gate_low[rows_of(s), :], gate_w[:, cols]) + nn(up_low[rows_of(s), :], up_w[:, cols]))
                scatter(s)
                pump()

        hidden = (hidden_units, width)
        pl.run_scoped(ffn_phase, *[pltpu.VMEM(hidden, bf)] * 3, *[pltpu.VMEM((rows, hidden_units), bf)] * 3)

        def mixer_phase(cat, heads, z, mixed, scores, gated, low, ggrad, pre, suf, tot, dm, dq, dk, flow):
            once = [(cat_in, cat, 10), (heads_in.at[l], heads, 11), (gated_in, gated, 12), (normed_in, rows_in, 13)]
            each = [[(of_seq(src, s, length), dst, 14 + k) for k, (src, dst) in enumerate(((z_in, z), (mixed_in, mixed), (scores_in, scores)))] for s in range(seqs)]
            for src, dst, k in once + each[0]:
                local(src, dst, k).start()
            for s in range(seqs):
                settle(s, middle, ffn_gains[l:l + 1, :], ffn_sum, True)
                pump()
            for src, dst, k in once:
                local(src, dst, k).wait()
            for s in range(seqs):
                collect(s, grad)
                for src, dst, k in each[s]:
                    local(src, dst, k).wait()
                ggrad[...] = nt(grad[rows_of(s), :], heads[...])
                mixer_backward(
                    s == 0, z, ups.at[l], bias.at[pl.ds(l, 1)], group.at[pl.ds(l, 1)], mixed, scores, ggrad, of_seq(low, s, length),
                    up_sum, bias_sum, group_sum, pre, suf, tot, dm, dq, dk, flow)
                if s + 1 < seqs:
                    for src, dst, k in each[s + 1]:
                        local(src, dst, k).start()
                freed(s, (0, 1))
                fill(partial.at[s], width, 256, lambda cols: nt(low[rows_of(s), :], cat[cols, :]))
                scatter(s)
                pump()
            fill(mix_own[0], mix_cols, 256, lambda cols: tn(rows_in[...], low[:, cols]))
            fill(mix_own[1], width, 512, lambda cols: tn(gated[...], grad[:, cols]))
            begin(self.mix.steps(mix_own, mix_slots, mix_sems, mix_pieces, mix_outs), 1 if top else 2)
            down_sum[...] = tn(low[:, mix_cols:], rows_in[...])

        f32s = lambda count: [pltpu.VMEM((length, HK), f32)] * count
        pl.run_scoped(
            mixer_phase, pltpu.VMEM((width, mix_cols + 128), bf), pltpu.VMEM((HV, width), bf), pltpu.VMEM((length, mix_cols + 128), f32),
            pltpu.VMEM((length, HV), f32), pltpu.VMEM((length, length), bf), pltpu.VMEM((rows, HV), bf), pltpu.VMEM((rows, mix_cols + 128), bf),
            pltpu.VMEM((length, HV), f32), *f32s(2), pltpu.VMEM((length // CH * 8, HK), f32), pltpu.VMEM((length, HV), bf), *f32s(3))
        for s in range(seqs):
            pump()
            settle(s, entry, gains[l:l + 1, :], attn_sum, top)
        if top:
            local(resid, out_resid, 20).start()
            for s in range(seqs):
                pump()
                collect(s, grad)
                local(of_seq(grad, s, length), of_seq(out_grad, s, length), 21 + s).start()
            local(resid, out_resid, 20).wait()
            for s in range(seqs):
                local(of_seq(grad, s, length), of_seq(out_grad, s, length), 21 + s).wait()
        else:
            small_own[0][...] = jnp.zeros_like(small_own[0])
            small_own[1][...] = jnp.zeros_like(small_own[1])
            at0 = at1 = 0
            for terms in (smalls, smalls_above):
                small_own[0][at0:at0 + rank, :] = terms[0][:rank, :]
                small_own[0][at0 + rank:at0 + rank + 1, :] = terms[1][...]
                small_own[1][at1:at1 + rank, :] = terms[2][:rank, :]
                for k in (3, 4):
                    small_own[1][at1 + rank + k - 3:at1 + rank + k - 2, :] = terms[k][...]
                small_own[1][at1 + rank + 2:at1 + rank + 3, :HV] = terms[5][...]
                at0, at1 = at0 + rank + 8, at1 + rank + 8
            hops = range(self.tensor - 1)

            def to_peer(hop):
                peer = {"tensor": lax.rem(lax.axis_index("tensor") + hop + 1, self.tensor)}
                return remote(small_own[1], shared.at[hop], peer_send.at[hop], peer_recv.at[hop], peer)

            for hop in hops:
                to_peer(hop).start()
            local(last_middle, middle, 20).start()
            for s in range(seqs):
                freed(s, (0, 1))
                local(of_seq(last_partial, s, length), partial.at[s], 8 + s).start()
            pump()
            for hop in hops:
                to_peer(hop).wait()
            small_own[1][...] += sum(shared[hop] for hop in hops)
            begin(self.small.steps(small_own, small_slots, small_sems, None, small_outs), 2)
            for s in range(seqs):
                collect(s, None)
                local(gathered.at[s], of_seq(out_input, s, length), 21 + s).start()
                pump()
            local(last_middle, middle, 20).wait()
            for s in range(seqs):
                local(gathered.at[s], of_seq(out_input, s, length), 21 + s).wait()
                local(of_seq(last_partial, s, length), partial.at[s], 8 + s).wait()
                scatter(s)
                pump()
            for s in range(seqs):
                total = arrived(s)
                mine = pl.ds(s * own, own)
                publish(s, ((middle[mine, :] + total) * keep[mine, :1]).astype(bf).astype(f32))
                pump()
            for s in range(seqs):
                collect(s, grad)
                local(of_seq(grad, s, length), of_seq(out_layer, s, length), 21 + s).start()
                pump()
            for s in range(seqs):
                local(of_seq(grad, s, length), of_seq(out_layer, s, length), 21 + s).wait()
        while jobs:
            pump()
        for s in range(seqs):
            freed(s, range(5))


class Finish:
    def __init__(self, rows, width, mix_cols, hidden_units, rank):
        self.rank, self.width = rank, width
        self.cols = ((0, HK), (HK, HK), (2 * HK, HV), (2 * HK + HV, HV))
        f = lambda *shape: jax.ShapeDtypeStruct(shape, f32)
        self.big = [f(2, hidden_units, width)] * 3 + [f(2, width, size) for _, size in self.cols] + [f(2, HV, width), f(rows, width)]
        self.big += [jax.ShapeDtypeStruct((rows, width), bf)]
        self.small = [f(2, rank, HK), f(2, HK), f(2, rank, width), f(2, width), f(2, width), f(2, HV)]

    def call(self, ffn, mix, rows_out, local, shared):
        arrays = list(ffn) + list(mix) + list(rows_out)
        return pl.pallas_call(
            self.kernel, name="finish", in_specs=[ANY_SPEC] * len(arrays) + [VMEM_SPEC] * 2,
            out_specs=[ANY_SPEC] * len(self.big) + [VMEM_SPEC] * len(self.small), out_shape=self.big + self.small,
            scratch_shapes=[pltpu.VMEM(a.shape, a.dtype) for a in arrays] + [DMA((len(arrays),)), DMA((24,))],
            compiler_params=pltpu.CompilerParams(vmem_limit_bytes=60 << 20),
            cost_estimate=pl.CostEstimate(flops=10**6, bytes_accessed=64 * 10**6, transcendentals=0),
        )(*arrays, local, shared)

    def kernel(self, *refs):
        rank, width = self.rank, self.width
        ins, (local, shared), outs, small = refs[:12], refs[12:14], refs[14:24], refs[24:30]
        load, store = refs[-2:]
        held = refs[30:42]
        loads = [pltpu.make_async_copy(src, dst, load.at[k]) for k, (src, dst) in enumerate(zip(ins, held))]
        for step in loads:
            step.start()
        stores = []

        def put(src, dst):
            step = pltpu.make_async_copy(src, dst, store.at[len(stores)])
            step.start()
            stores.append(step)

        for l in range(2):
            for k in range(3):
                loads[3 * l + k].wait()
                put(held[3 * l + k], outs[k].at[l])
        for l in range(2):
            loads[6 + 2 * l].wait()
            for k, (start, size) in enumerate(self.cols):
                put(held[6 + 2 * l].at[:, pl.ds(start, size)], outs[3 + k].at[l])
            loads[7 + 2 * l].wait()
            put(held[7 + 2 * l], outs[7].at[l])
        for k in range(2):
            loads[10 + k].wait()
            put(held[10 + k], outs[8 + k])
        up, bias, down, attn, ffn_gain, group = small
        for l in range(2):
            at = l * (rank + 8)
            up[l] = local[at:at + rank, :]
            bias[l:l + 1, :] = local[at + rank:at + rank + 1, :]
            down[l] = shared[at:at + rank, :]
            attn[l:l + 1, :] = shared[at + rank:at + rank + 1, :]
            ffn_gain[l:l + 1, :] = shared[at + rank + 1:at + rank + 2, :]
            group[l:l + 1, :] = shared[at + rank + 2:at + rank + 3, :HV]
        for step in stores:
            step.wait()


def shards(
    groups, tensor, layer_input, seq_lengths, attn_gain, query_proj, key_proj, value_proj, gate_proj,
    decay_down, decay_up, decay_bias, group_gain, output_proj, ffn_gain, ffn_gate, ffn_up, ffn_down, cotangent,
):
    seqs, length, width = layer_input.shape
    depth = attn_gain.shape[0]
    rank = decay_down.shape[2]
    rows = seqs * length
    own = length // 4
    me = lax.axis_index("tensor")
    core, cross = me % 2, me // 2
    mix_cols = 2 * HK + 2 * HV
    hidden_units = ffn_gate.shape[2]
    ring = RING if groups % RING == 0 else groups
    def mine(full):
        parts = full.reshape(seqs, 4, own, full.shape[-1])
        return lax.dynamic_slice_in_dim(parts, core * 2 + cross, 1, axis=1).reshape(seqs * own, full.shape[-1])

    keep = (jnp.arange(length, dtype=jnp.int32)[None, :] < seq_lengths[:, None]).astype(f32).reshape(rows, 1)
    keep_mine = jnp.broadcast_to(mine(keep), (seqs * own, 128))
    cat = [
        jnp.concatenate([query_proj[l], key_proj[l], value_proj[l], gate_proj[l], jnp.pad(decay_down[l], ((0, 0), (0, 128 - rank)))], axis=1)
        for l in range(depth)
    ]
    ups = jnp.pad(decay_up, ((0, 0), (0, 128 - rank), (0, 0)))
    gate_t, up_t = ffn_gate.transpose(0, 2, 1), ffn_up.transpose(0, 2, 1)
    found = Forward(depth, seqs, length, width, mix_cols, hidden_units).call(
        0, layer_input.reshape(rows, width), attn_gain, ffn_gain, ups, decay_bias, group_gain, cat, (output_proj, gate_t, up_t, ffn_down))
    kinds = len(found) // depth
    ffn_grad = cotangent.reshape(rows, width) * keep.astype(bf)
    resid = mine(cotangent.reshape(rows, width)).astype(f32) * keep_mine[:, :1]
    params = (attn_gain, ffn_gain, ups, decay_bias, group_gain)

    def backward(top, l, ffn_grad, resid, extra):
        normed, z, gated, mixed, scores, entry, middle, normed_ffn = found[l * kinds:(l + 1) * kinds]
        arrays = (normed_ffn, ffn_grad, resid, middle, entry, z, mixed, scores, gated, normed, gate_t, up_t, ffn_down, cat[l], output_proj)
        return Backward(top, l, ring, tensor, seqs, length, width, mix_cols, hidden_units, rank).call(1 + l, params, arrays, extra)

    ffn_sums, mix_sums = [None] * depth, [None] * depth
    last_partial, ffn_grad, resid, *found_top = backward(True, 1, ffn_grad, resid, ())
    ffn_sums[1] = found_top[:3]
    extra = (*found_top[3:], keep_mine, last_partial, found[kinds + 6])
    input_grad, layer_output, *sums = backward(False, 0, ffn_grad, resid, extra)
    if groups > ring:
        found_sums = lax.psum(tuple(part * (1.0 / ring) for part in (*sums, *ffn_sums[1])), "dp")
        sums, ffn_sums[1] = found_sums[:-3], found_sums[-3:]
    ffn_sums[0], mix_sums[0], mix_sums[1], (local, shared) = sums[:3], sums[3:5], sums[5:7], sums[7:]

    done = Finish(rows, width, mix_cols, hidden_units, rank).call(
        (*ffn_sums[0], *ffn_sums[1]), (*mix_sums[0], *mix_sums[1]), (input_grad, layer_output), local, shared)
    gate, up, down, query, key, value, out_gate, head, input_grad, layer_output, d_up, d_bias, d_down, attn, ffn, group = done
    return (
        layer_output.reshape(seqs, length, width),
        input_grad.reshape(seqs, length, width),
        attn,
        query,
        key,
        value,
        out_gate,
        d_down.transpose(0, 2, 1),
        d_up,
        d_bias,
        group,
        head,
        ffn,
        gate.transpose(0, 2, 1),
        up.transpose(0, 2, 1),
        down,
    )


def solution(mesh):
    over, across = P("dp", None, None), P(None, None, "tensor")
    deep = P(None, "tensor", None)
    return jax.shard_map(
        functools.partial(shards, mesh.shape["dp"], mesh.shape["tensor"]),
        mesh=mesh,
        in_specs=(over, P("dp"), P(), across, across, across, across, P(), across, P(None, "tensor"), P(), deep, P(), across, across, deep, over),
        out_specs=(over, over, P(), across, across, across, across, P(), across, P(None, "tensor"), P(), deep, P(), across, across, deep),
        check_vma=False,
    )
```

```python
import functools
import jax, jax.numpy as jnp
from jax import lax
from jax.experimental import pallas as pl
from jax.experimental.pallas import tpu as pltpu
from jax.sharding import PartitionSpec as P
HK, HV, CH = 128, 256, 128
group_epsilon = 1e-05
bf, f32 = jnp.bfloat16, jnp.float32
SCALE = HK ** -0.5

def nn(a, b):
    return lax.dot_general(a, b, (((1,), (0,)), ((), ())), preferred_element_type=f32)
def nt(a, b):
    return lax.dot_general(a, b, (((1,), (1,)), ((), ())), preferred_element_type=f32)
def tn(a, b):
    return lax.dot_general(a, b, (((0,), (0,)), ((), ())), preferred_element_type=f32)

def halves(a):
    top = a.astype(bf)
    return top, (a - top.astype(f32)).astype(bf)

def thirds(a):
    top = a.astype(bf)
    return (top,) + halves(a - top.astype(f32))

def sigmoid(a):
    return 1.0 / (1.0 + jnp.exp(-a))

def log_sigmoid(a):
    return jnp.minimum(a, 0.0) - jnp.log1p(jnp.exp(-jnp.abs(a)))

def steps_below(n):
    out, h = [], 1
    while h < n:
        out.append(h)
        h *= 2
    return out

def decay_sums(ld):
    n = ld.shape[0]
    rows = lax.broadcasted_iota(jnp.int32, ld.shape, 0)
    total, pre, suf = ld, ld, jnp.zeros_like(ld)
    levels = []
    for h in steps_below(n):
        upper = (rows & h) != 0
        levels.append((h, upper, jnp.exp(jnp.where(upper, pre, suf))))
        below, above = pltpu.roll(total, h, 0), pltpu.roll(total, n - h, 0)
        pre = jnp.where(upper, pre + below, pre)
        suf = jnp.where(upper, suf, suf + above)
        total = total + jnp.where(upper, below, above)
    return levels, pre, suf, total

def tile_rows(c):
    return pl.ds(c * CH, CH)

def logits_of(z, up_ref, bias_ref):
    return sum(nn(piece, up_ref[...]) for piece in thirds(z[:, 2 * HK + 2 * HV:])) + bias_ref[...]

def wide_levels(chunks):
    out, h = [], 1
    while h < chunks:
        for base in range(0, chunks, 2 * h):
            out.append((tuple(range(base, base + h)), tuple(range(base + h, base + 2 * h))))
        h *= 2
    return out

def wide_factor(c, group, is_upper, pre, suf, tot):
    arg = pre[tile_rows(c), :] if is_upper else suf[tile_rows(c), :]
    for o in group:
        if (o < c) if is_upper else (o > c):
            arg = arg + tot[pl.ds(o * 8, 1), :]
    return jnp.exp(arg)

def mixer_forward(z_ref, up_ref, bias_ref, gain_ref, gated_ref, mixed_ref, scores_ref, pre, suf, tot):
    chunks = z_ref.shape[0] // CH
    i = lax.broadcasted_iota(jnp.int32, (CH, CH), 0)
    j = lax.broadcasted_iota(jnp.int32, (CH, CH), 1)
    apart = i ^ j
    scores_ref[...] = jnp.zeros_like(scores_ref)
    for c in range(chunks):
        z = z_ref[tile_rows(c), :]
        q, k = z[:, :HK].astype(bf), z[:, HK:2 * HK].astype(bf)
        ld = log_sigmoid(logits_of(z, up_ref, bias_ref)) / 16.0
        levels, p, s, t = decay_sums(ld)
        pre[tile_rows(c), :], suf[tile_rows(c), :], tot[pl.ds(c * 8, 8), :] = p, s, t[:8]
        tile = nt(q, k)
        qf, kf = q.astype(f32), k.astype(f32)
        for h, upper, factor in levels:
            rows = (jnp.where(upper, qf, kf) * factor).astype(bf)
            tile = jnp.where(apart >= h, nt(rows, rows), tile)
        scores_ref[tile_rows(c), tile_rows(c)] = jnp.where(i >= j, tile * SCALE, 0.0).astype(bf)
    for low_group, up_group in wide_levels(chunks):
        q_rows = [(z_ref[tile_rows(c), :HK].astype(bf).astype(f32) * wide_factor(c, up_group, True, pre, suf, tot)).astype(bf) for c in up_group]
        k_rows = [(z_ref[tile_rows(c), HK:2 * HK].astype(bf).astype(f32) * wide_factor(c, low_group, False, pre, suf, tot)).astype(bf) for c in low_group]
        for a, c in enumerate(up_group):
            for b, o in enumerate(low_group):
                scores_ref[tile_rows(c), tile_rows(o)] = (nt(q_rows[a], k_rows[b]) * SCALE).astype(bf)
    for c in range(chunks):
        width = (c + 1) * CH
        mixed = nn(scores_ref[tile_rows(c), :width], z_ref[:width, 2 * HK:2 * HK + HV].astype(bf))
        mixed_ref[tile_rows(c), :] = mixed
        out_gate = z_ref[tile_rows(c), 2 * HK + HV:2 * HK + 2 * HV]
        normed = mixed * lax.rsqrt(jnp.mean(mixed * mixed, axis=-1, keepdims=True) + group_epsilon) * gain_ref[...]
        gated_ref[tile_rows(c), :] = (normed * out_gate * sigmoid(out_gate)).astype(bf)

def mixer_backward(fresh, z_ref, up_ref, bias_ref, gain_ref, mixed_ref, scores_ref, grad_ref,
                   out_ref, up_out, bias_out, gain_out, pre, suf, tot, dm_ref, dq_ref, dk_ref, flow):
    chunks = z_ref.shape[0] // CH
    i = lax.broadcasted_iota(jnp.int32, (CH, CH), 0)
    j = lax.broadcasted_iota(jnp.int32, (CH, CH), 1)
    apart = i ^ j
    rows_in = lax.broadcasted_iota(jnp.int32, (CH, HK), 0)

    if fresh:
        up_out[...] = jnp.zeros_like(up_out)
        bias_out[...] = jnp.zeros_like(bias_out)
        gain_out[...] = jnp.zeros_like(gain_out)
    for c in range(chunks):
        mixed, e = mixed_ref[tile_rows(c), :], grad_ref[tile_rows(c), :]
        g = z_ref[tile_rows(c), 2 * HK + HV:2 * HK + 2 * HV]
        r = lax.rsqrt(jnp.mean(mixed * mixed, axis=-1, keepdims=True) + group_epsilon)
        sig = sigmoid(g)
        unit = mixed * r
        out_ref[tile_rows(c), 2 * HK + HV:2 * HK + 2 * HV] = (e * unit * gain_ref[...] * (sig + g * sig * (1.0 - sig))).astype(bf)
        upstream = e * g * sig
        gain_out[...] += jnp.sum(upstream * unit, axis=0, keepdims=True)
        weighted = upstream * gain_ref[...]
        dm_ref[tile_rows(c), :] = (r * (weighted - unit * jnp.mean(unit * weighted, axis=-1, keepdims=True))).astype(bf)

    def score_grad(c, o):
        return nt(dm_ref[tile_rows(c), :], z_ref[tile_rows(o), 2 * HK:2 * HK + HV].astype(bf)) * SCALE

    for c in range(chunks):
        z = z_ref[tile_rows(c), :]
        q, k = z[:, :HK].astype(bf).astype(f32), z[:, HK:2 * HK].astype(bf).astype(f32)
        ld = log_sigmoid(logits_of(z, up_ref, bias_ref)) / 16.0
        levels, p, s, t = decay_sums(ld)
        pre[tile_rows(c), :], suf[tile_rows(c), :], tot[pl.ds(c * 8, 8), :] = p, s, t[:8]
        ds = score_grad(c, c)
        diagonal = jnp.sum(jnp.where(i == j, ds, 0.0), axis=-1, keepdims=True)
        ds = jnp.where(i > j, ds, 0.0)
        both = ds + ds.T
        dq, dk = diagonal * k, diagonal * q
        fl = jnp.zeros_like(dq)
        for h, upper, factor in levels:
            rows = (jnp.where(upper, q, k) * factor).astype(bf)
            near = jnp.where((apart >= h) & (apart < 2 * h), both, 0.0).astype(bf)
            back = nn(near, rows)
            part = back * factor
            dq, dk = dq + jnp.where(upper, part, 0.0), dk + jnp.where(upper, 0.0, part)
            moved = back * rows.astype(f32)
            fl = fl + jnp.where(upper, moved, -moved)
        dq_ref[tile_rows(c), :], dk_ref[tile_rows(c), :], flow[tile_rows(c), :] = dq, dk, fl
    for low_group, up_group in wide_levels(chunks):
        q_fac = [wide_factor(c, up_group, True, pre, suf, tot) for c in up_group]
        k_fac = [wide_factor(c, low_group, False, pre, suf, tot) for c in low_group]
        q_rows = [(z_ref[tile_rows(c), :HK].astype(bf).astype(f32) * f).astype(bf) for c, f in zip(up_group, q_fac)]
        k_rows = [(z_ref[tile_rows(c), HK:2 * HK].astype(bf).astype(f32) * f).astype(bf) for c, f in zip(low_group, k_fac)]
        grads = [[score_grad(c, o).astype(bf) for o in low_group] for c in up_group]
        for a, c in enumerate(up_group):
            back = sum(nn(grads[a][b], k_rows[b]) for b in range(len(low_group)))
            dq_ref[tile_rows(c), :] += back * q_fac[a]
            flow[tile_rows(c), :] += back * q_rows[a].astype(f32)
        for b, o in enumerate(low_group):
            back = sum(tn(grads[a][b], q_rows[a]) for a in range(len(up_group)))
            dk_ref[tile_rows(o), :] += back * k_fac[b]
            flow[tile_rows(o), :] -= back * k_rows[b].astype(f32)
    later = jnp.zeros((1, HK), f32)
    for c in reversed(range(chunks)):
        out_ref[tile_rows(c), :HK] = dq_ref[tile_rows(c), :].astype(bf)
        out_ref[tile_rows(c), HK:2 * HK] = dk_ref[tile_rows(c), :].astype(bf)
        out_ref[tile_rows(c), 2 * HK:2 * HK + HV] = tn(scores_ref[pl.ds(c * CH, (chunks - c) * CH), tile_rows(c)], dm_ref[pl.ds(c * CH, (chunks - c) * CH), :]).astype(bf)
        fl = flow[tile_rows(c), :]
        for h in steps_below(CH):
            fl = fl + jnp.where(rows_in < CH - h, pltpu.roll(fl, CH - h, 0), 0.0)
        fl = fl + later
        later = fl[:1]
        z = z_ref[tile_rows(c), :]
        logits = logits_of(z, up_ref, bias_ref)
        d_logit = fl * sigmoid(-logits) / 16.0
        bias_out[...] += jnp.sum(d_logit, axis=0, keepdims=True)
        d1, d2 = halves(d_logit)
        l1, l2 = halves(z[:, 2 * HK + 2 * HV:])
        up_out[...] += tn(l1, d1) + tn(l1, d2) + tn(l2, d1)
        out_ref[tile_rows(c), 2 * HK + 2 * HV:] = (nt(d1, up_ref[...]) + nt(d2, up_ref[...])).astype(bf)


norm_epsilon = 1e-06
MESH = pl.DeviceIdType.MESH
VMEM_SPEC = pl.BlockSpec(memory_space=pltpu.VMEM)
ANY_SPEC = pl.BlockSpec(memory_space=pl.ANY)
DMA = pltpu.SemaphoreType.DMA
RING = 8


def peer_of(index, bit):
    return jnp.where((index // bit) % 2 == 0, index + bit, index - bit)


def rms_unit(h):
    return lax.rsqrt(jnp.mean(h * h, axis=-1, keepdims=True) + norm_epsilon)


def remote(src, dst, send, recv, peer):
    return pltpu.make_async_remote_copy(
        src_ref=src, dst_ref=dst, send_sem=send, recv_sem=recv, device_id=peer, device_id_type=MESH
    )


def ring_place(n):
    index = lax.rem(lax.axis_index("dp"), n)
    return jnp.where(index % 2 == 0, index // 2, n - 1 - index // 2)


def ring_peer(ahead, n):
    place = lax.rem(ring_place(n) + ahead, n)
    index = lax.axis_index("dp")
    return {"dp": index - lax.rem(index, n) + jnp.where(place < n // 2, 2 * place, 2 * (n - 1 - place) + 1)}


def ring_cut(shape, n):
    rows, cols = shape
    if rows % (16 * n) == 0:
        return rows // (2 * n), cols, True
    if rows % (8 * n) == 0 and cols % 256 == 0:
        return rows // n, cols // 2, False
    return None


def tiles(total, size):
    return [(start, min(size, total - start)) for start in range(0, total, size)]


def raw_weights(l, proj, cat, decay_down, down_w, decay_up, up_w, heads, head_w):
    moves, at = [], 0
    for w in proj:
        size = w.shape[2]
        moves.append((w.at[l], cat.at[:, pl.ds(at, size)]))
        at += size
    rank = decay_down.shape[1]
    return moves + [(decay_down.at[l], down_w.at[pl.ds(0, rank)]), (decay_up.at[l], up_w.at[pl.ds(0, rank)]), (heads.at[l], head_w)]


def ffn_tile(here, cols, rows_in, grad, gate_w, up_w, down_w, inner, gate_low, up_low):
    gate_act, up_act = nt(rows_in[here, :], gate_w[cols, :]), nt(rows_in[here, :], up_w[cols, :])
    inner_grad = nt(grad[here, :], down_w[cols, :])
    sig = sigmoid(gate_act)
    swish = gate_act * sig
    inner[here, cols] = (swish * up_act).astype(bf)
    gate_low[here, cols] = (inner_grad * up_act * sig * (1.0 + gate_act * (1.0 - sig))).astype(bf)
    up_low[here, cols] = (inner_grad * swish).astype(bf)


class Forward:
    def __init__(self, depth, seqs, length, width, mix_cols, hidden_units):
        self.depth, self.seqs, self.length, self.width = depth, seqs, length, width
        self.mix_cols, self.z_cols, self.hidden_units = mix_cols, mix_cols + 128, hidden_units
        rows, quarter = seqs * length, seqs * length // 4
        self.saved = []
        for _ in range(depth):
            self.saved += [
                ((rows, width), bf), ((rows, self.z_cols), f32), ((rows, HV), bf), ((rows, HV), f32), ((rows, length), bf),
                ((quarter, width), f32), ((quarter, width), f32), ((rows, width), bf),
            ]
        self.saved += [((rows, width), bf)] + [((rows, hidden_units), bf)] * 3

    def call(self, collective, lengths, params, x, cotangent, proj, decay, heads, ffn_ws):
        depth, seqs, length, width = self.depth, self.seqs, self.length, self.width
        own = length // 4
        saved = [jax.ShapeDtypeStruct(shape, kind) for shape, kind in self.saved]
        scratch = [pltpu.VMEM(shape, kind) for shape, kind in self.saved]
        scratch += [pltpu.VMEM(x.shape, bf)]
        scratch += [pltpu.VMEM((width, self.mix_cols), bf), pltpu.VMEM((128, width), bf), pltpu.VMEM((128, HK), bf), pltpu.VMEM((HV, width), bf)] * depth
        scratch += [pltpu.VMEM((self.hidden_units, width), bf)] * 3
        scratch += [
            pltpu.VMEM((seqs, length, width), f32), pltpu.VMEM((seqs, 2 * own, width), f32), pltpu.VMEM((seqs, own, width), f32),
            pltpu.VMEM((seqs, length, width), f32),
            pltpu.VMEM((length, HK), f32), pltpu.VMEM((length, HK), f32), pltpu.VMEM((length // CH * 8, HK), f32),
            DMA((len(saved), seqs)), DMA((7 * depth + 8,)), DMA((5, seqs)), DMA((5, seqs)),
        ]
        smem = pl.BlockSpec(memory_space=pltpu.SMEM)
        arrays = (x, cotangent, *proj, *decay, heads, *ffn_ws)
        return pl.pallas_call(
            self.kernel, name="forward_blocks",
            in_specs=[smem] + [VMEM_SPEC] * len(params) + [ANY_SPEC] * len(arrays), out_specs=[ANY_SPEC] * len(saved), out_shape=saved,
            scratch_shapes=scratch,
            compiler_params=pltpu.CompilerParams(collective_id=collective, has_side_effects=True, vmem_limit_bytes=61 << 20),
            cost_estimate=pl.CostEstimate(flops=10**10, bytes_accessed=2 * 10**8, transcendentals=0),
        )(lengths, *params, *arrays)

    def kernel(self, *refs):
        depth, seqs, length = self.depth, self.seqs, self.length
        half, own = length // 2, length // 4
        kinds = 8
        refs = list(refs)

        def take(count):
            found = refs[:count]
            del refs[:count]
            return found

        lengths, gains, ffn_gains, bias, group = take(5)
        x_in, cotangent = take(2)
        proj, (decay_down, decay_up), heads, ffn_ws = take(4), take(2), take(1)[0], take(3)
        outs = take(len(self.saved))
        kept_for_later = take(len(self.saved))
        x = take(1)[0]
        mixer_w = [take(4) for _ in range(depth)]
        gate_w, up_w, down_w = take(3)
        partial, first, second, gathered, pre, suf, tot, store, load, send, recv = take(11)
        grad, inner, gate_low, up_low = kept_for_later[depth * kinds:]
        me = lax.axis_index("tensor")
        core, cross = me % 2, me // 2
        core_peer, cross_peer = {"tensor": peer_of(me, 1)}, {"tensor": peer_of(me, 2)}

        def local(src, dst, k):
            return pltpu.make_async_copy(src, dst, load.at[k])

        def of_seq(ref, s, height):
            return ref.at[pl.ds(s * height, height)]

        x_loads = [local(of_seq(x_in, s, length), of_seq(x, s, length), s) for s in range(seqs)]
        mixer_loads = []
        for l in range(depth):
            cat, low_w, up_map, head_w = mixer_w[l]
            moves = raw_weights(l, proj, cat, decay_down, low_w, decay_up, up_map, heads, head_w)
            mixer_loads.append([local(src, dst, 8 + 7 * l + k) for k, (src, dst) in enumerate(moves)])

        def ffn_loads(l):
            return [local(src.at[l], dst, 2 + k) for k, (src, dst) in enumerate(zip(ffn_ws, (gate_w, up_w, down_w)))]

        grad_load = local(cotangent, grad, 5)
        for l in range(depth):
            mixer_w[l][1][...] = jnp.zeros_like(mixer_w[l][1])
            mixer_w[l][2][...] = jnp.zeros_like(mixer_w[l][2])
        for step in x_loads[:1] + mixer_loads[0] + x_loads[1:] + ffn_loads(0) + [step for loads in mixer_loads[1:] for step in loads] + [grad_load]:
            step.start()
        barrier = pltpu.get_barrier_semaphore()
        for peer in (core_peer, cross_peer):
            pl.semaphore_signal(barrier, inc=1, device_id=peer, device_id_type=MESH)
        pl.semaphore_wait(barrier, 2)
        sent, stores = {}, []

        def copy(src, dst, stage, s, peer):
            step = remote(src, dst, send.at[stage, s], recv.at[stage, s], peer)
            step.start()
            sent[stage, s] = step

        def freed(s, stages):
            for stage in stages:
                if (stage, s) in sent:
                    sent.pop((stage, s)).wait_send()

        def piece(c, x_half, size):
            return pl.ds(pl.multiple_of(c * half + x_half * own, own), size)

        def keep_for_later(k, s):
            height = self.saved[k][0][0] // seqs
            step = pltpu.make_async_copy(of_seq(kept_for_later[k], s, height), of_seq(outs[k], s, height), store.at[k, s])
            step.start()
            stores.append(step)

        def scatter(s):
            copy(partial.at[s, piece(1 - core, 0, half)], first.at[s], 0, s, core_peer)
            sent[0, s].wait_recv()
            freed(s, (2, 3, 4))
            partial[s, piece(core, 1 - cross, own), :] += first[s, piece(0, 1 - cross, own), :]
            copy(partial.at[s, piece(core, 1 - cross, own)], second.at[s], 1, s, cross_peer)
            partial[s, piece(core, cross, own), :] += first[s, piece(0, cross, own), :]

        def settle(s, resid, new_resid, gain):
            sent[1, s].wait_recv()
            mine = pl.ds(s * own, own)
            new = resid[mine, :] + (partial[s, piece(core, cross, own), :] + second[s])
            new_resid[mine, :] = new
            gathered[s, piece(core, cross, own), :] = (new * rms_unit(new) * gain).astype(bf).astype(f32)
            block = gathered.at[s, piece(core, cross, own)]
            copy(block, block, 2, s, cross_peer)
            copy(block, block, 3, s, core_peer)

        def collect(s, dest):
            sent[2, s].wait_recv()
            block = gathered.at[s, piece(core, 1 - cross, own)]
            copy(block, block, 4, s, core_peer)
            dest[pl.ds(pl.multiple_of(s * length + core * half, half), half), :] = gathered[s, piece(core, 0, half), :].astype(bf)
            sent[3, s].wait_recv()
            sent[4, s].wait_recv()
            dest[pl.ds(pl.multiple_of(s * length + (1 - core) * half, half), half), :] = gathered[s, piece(1 - core, 0, half), :].astype(bf)

        def rows_of(s):
            return pl.ds(s * length, length)

        for l in range(depth):
            normed, z, gated, mixed, scores, entry, middle, normed_ffn = kept_for_later[l * kinds:(l + 1) * kinds]
            cat, low_w, up_map, head_w = mixer_w[l]
            for s in range(seqs):
                if l == 0:
                    x_loads[s].wait()
                    for part in range(4):
                        block = pl.ds(s * length + part * own, own)
                        h = x[block, :].astype(f32)
                        normed[block, :] = (h * rms_unit(h) * gains[l:l + 1, :]).astype(bf)
                    entry[pl.ds(s * own, own), :] = x[pl.ds(pl.multiple_of(s * length + core * half + cross * own, own), own), :].astype(f32)
                else:
                    collect(s, normed)
                if s == 0:
                    for step in mixer_loads[l]:
                        step.wait()
                keep_for_later(l * kinds, s)
                for start, size in tiles(self.mix_cols, 256):
                    cols = pl.ds(start, size)
                    z[rows_of(s), cols] = nn(normed[rows_of(s), :], cat[:, cols])
                z[rows_of(s), pl.ds(self.mix_cols, 128)] = nt(normed[rows_of(s), :], low_w[...])
                keep_for_later(l * kinds + 1, s)
                mixer_forward(
                    of_seq(z, s, length), up_map, bias.at[pl.ds(l, 1)], group.at[pl.ds(l, 1)], of_seq(gated, s, length),
                    of_seq(mixed, s, length), of_seq(scores, s, length), pre, suf, tot)
                for k in (2, 3, 4):
                    keep_for_later(l * kinds + k, s)
                freed(s, (0, 1))
                for start, size in tiles(self.width, 256):
                    cols = pl.ds(start, size)
                    partial[s, :, cols] = nn(gated[rows_of(s), :], head_w[:, cols])
                scatter(s)
            for s in range(seqs):
                settle(s, entry, middle, ffn_gains[l:l + 1, :])
                keep_for_later(l * kinds + 5, s)
                keep_for_later(l * kinds + 6, s)
            if l + 1 == depth:
                break
            for s in range(seqs):
                collect(s, normed_ffn)
                keep_for_later(l * kinds + 7, s)
                if s == 0:
                    for step in ffn_loads(l):
                        step.wait()
                for start, size in tiles(self.hidden_units, 256):
                    cols = pl.ds(start, size)
                    gate_act = nt(normed_ffn[rows_of(s), :], gate_w[cols, :])
                    up_act = nt(normed_ffn[rows_of(s), :], up_w[cols, :])
                    inner[rows_of(s), cols] = (gate_act * sigmoid(gate_act) * up_act).astype(bf)
                freed(s, (0, 1))
                for start, size in tiles(self.width, 256):
                    cols = pl.ds(start, size)
                    partial[s, :, cols] = nn(inner[rows_of(s), :], down_w[:, cols])
                if s + 1 == seqs:
                    for step in ffn_loads(l + 1):
                        step.start()
                scatter(s)
            for s in range(seqs):
                settle(s, middle, kept_for_later[(l + 1) * kinds + 5], gains[l + 1:l + 2, :])
        grad_load.wait()
        for s in range(seqs):
            kept = lax.broadcasted_iota(jnp.int32, (length, 1), 0) < lengths[s]
            grad[rows_of(s), :] = jnp.where(kept, grad[rows_of(s), :].astype(f32), 0.0).astype(bf)
            keep_for_later(depth * kinds, s)
        normed_ffn = kept_for_later[(depth - 1) * kinds + 7]
        for step in ffn_loads(depth - 1):
            step.wait()
        for s in range(seqs):
            collect(s, normed_ffn)
            keep_for_later((depth - 1) * kinds + 7, s)
            for start, size in tiles(self.hidden_units, 256):
                ffn_tile(rows_of(s), pl.ds(start, size), normed_ffn, grad, gate_w, up_w, down_w, inner, gate_low, up_low)
            for k in range(3):
                keep_for_later(depth * kinds + 1 + k, s)
        for s in range(seqs):
            freed(s, range(5))
        for step in stores:
            step.wait()


class RingJob:
    def __init__(self, n, shapes, reduce, gather):
        self.n, self.shapes, self.reduce, self.gather = n, shapes, reduce, gather
        self.cuts = [ring_cut(shape, n) for shape in shapes]
        self.pairs = [(a, way) for a in range(len(shapes)) for way in range(2)]

    def slots(self):
        return [pltpu.VMEM((2, self.n - 1, rows, cols), f32) for rows, cols, _ in self.cuts] if self.reduce else []

    def sems(self):
        each = DMA((self.n - 1, len(self.shapes), 2))
        return [each, each] * (self.reduce + self.gather) + ([DMA((len(self.shapes), 2))] if self.gather else [])

    def pieces(self):
        return [jax.ShapeDtypeStruct((2, rows, cols), f32) for rows, cols, _ in self.cuts]

    def full(self):
        return [jax.ShapeDtypeStruct(shape, f32) for shape in self.shapes]

    def segment(self, a, way, back):
        n = self.n
        place = ring_place(n)
        index = lax.rem((place if way == 0 else n - 1 - place) + (2 * n - back), n)
        rows, cols, by_rows = self.cuts[a]
        if by_rows:
            return (pl.ds(pl.multiple_of((index * 2 + way) * rows, rows), rows), pl.ds(0, cols))
        return (pl.ds(pl.multiple_of(index * rows, rows), rows), pl.ds(way * cols, cols))

    def hop(self, src, dst, sems, step, a, way):
        peer = ring_peer(1 if way == 0 else self.n - 1, self.n)
        return remote(src, dst, sems[0].at[step, a, way], sems[1].at[step, a, way], peer)

    def steps(self, own, slots, sems, pieces, outs):
        n = self.n
        if self.reduce:
            rs, sems = sems[:2], sems[2:]
            for a, way in self.pairs:
                self.hop(own[a].at[self.segment(a, way, 0)], slots[a].at[way, 0], rs, 0, a, way).start()
            for step in range(n - 1):
                yield
                for a, way in self.pairs:
                    slot = slots[a].at[way, step]
                    self.hop(slot, slot, rs, step, a, way).wait_recv()
                    self.add(a, way, slot, own[a], slot if self.gather or step < n - 2 else pieces[a].at[way], step + 1)
                    if step < n - 2:
                        self.hop(slot, slots[a].at[way, step + 1], rs, step + 1, a, way).start()
                    elif self.gather:
                        self.begin(a, way, slot, sems, outs)
        else:
            for a, way in self.pairs:
                self.begin(a, way, pieces[a].at[way], sems, outs)
        if self.gather:
            for step in range(n - 1):
                yield
                for a, way in self.pairs:
                    piece = outs[a].at[self.segment(a, way, step)]
                    self.hop(piece, piece, sems, step, a, way).wait_recv()
                    if step < n - 2:
                        self.hop(piece, piece, sems, step + 1, a, way).start()
            for a, way in self.pairs:
                end = slots[a].at[way, n - 2] if self.reduce else pieces[a].at[way]
                pltpu.make_async_copy(end, outs[a].at[self.segment(a, way, n - 1)], sems[2].at[a, way]).wait()
        for step in range(n - 1):
            for a, way in self.pairs:
                if self.reduce:
                    self.hop(slots[a].at[way, 0], slots[a].at[way, 0], rs, step, a, way).wait_send()
                if self.gather:
                    piece = outs[a].at[self.segment(a, way, 0)]
                    self.hop(piece, piece, sems, step, a, way).wait_send()

    def begin(self, a, way, piece, sems, outs):
        place = outs[a].at[self.segment(a, way, self.n - 1)]
        self.hop(piece, place, sems, 0, a, way).start()
        pltpu.make_async_copy(piece, place, sems[2].at[a, way]).start()

    def add(self, a, way, slot, own, out, back):
        row_ds, col_ds = self.segment(a, way, back)

        @pl.loop(0, self.cuts[a][0] // 8)
        def _(block):
            here = pl.ds(pl.multiple_of(block * 8, 8), 8)
            there = pl.ds(pl.multiple_of(row_ds.start + block * 8, 8), 8)
            out[here, :] = slot[here, :] + own[there, col_ds]


def fill(dst, total, size, make):
    for start, extent in tiles(total, size):
        cols = pl.ds(start, extent)
        dst[:, cols] = make(cols)


class Backward:
    def __init__(self, top, l, n, tensor, seqs, length, width, mix_cols, hidden_units, rank):
        self.top, self.l, self.n, self.tensor, self.rank = top, l, n, tensor, rank
        self.seqs, self.length, self.width, self.mix_cols, self.hidden_units = seqs, length, width, mix_cols, hidden_units
        self.ffn = [RingJob(n, [(hidden_units, width)], True, True) for _ in range(3)]
        mix_shapes = [(width, mix_cols), (HV, width)]
        self.mix = RingJob(n, mix_shapes, True, not top)
        self.above = RingJob(n, mix_shapes, False, True)
        self.small = RingJob(n, [(16 * n, HK), (8 * n, width)], True, True)

    def small_outs(self):
        width = self.width
        return [jax.ShapeDtypeStruct(shape, f32) for shape in ((128, HK), (1, HK), (128, width), (1, width), (1, width), (1, HV))]

    def call(self, collective, lengths, params, arrays, extra):
        seqs, length, width = self.seqs, self.length, self.width
        rows, own = seqs * length, length // 4
        wide = jax.ShapeDtypeStruct((rows, width), bf)
        wide32, quarter = jax.ShapeDtypeStruct((rows, width), f32), jax.ShapeDtypeStruct((seqs * own, width), f32)
        smalls = self.small_outs()
        if self.top:
            outs = [wide32, wide, quarter] + [job.full()[0] for job in self.ffn]
            vmem_outs = self.mix.pieces() + smalls
            vmem_ins = 0
        else:
            outs = [wide32, wide] + [job.full()[0] for job in self.ffn] + self.mix.full() + self.above.full() + self.small.full()
            vmem_outs = []
            vmem_ins = len(extra) - 2
        scratch = [pltpu.VMEM(shape.shape, f32) for shape in [job.full()[0] for job in self.ffn] + self.mix.full()]
        scratch += [job.slots()[0] for job in self.ffn] + self.mix.slots() + [sem for job in self.ffn for sem in job.sems()] + self.mix.sems()
        if not self.top:
            scratch += self.above.sems() + [pltpu.VMEM(shape.shape, f32) for shape in self.small.full()] + self.small.slots() + self.small.sems()
            scratch += [pltpu.VMEM((self.tensor - 1, 8 * self.n, width), f32), DMA((self.tensor - 1,)), DMA((self.tensor - 1,))]
            scratch += [pltpu.VMEM(shape.shape, f32) for shape in smalls]
        scratch += [
            pltpu.VMEM((seqs, length, width), f32), pltpu.VMEM((seqs, 2 * own, width), f32), pltpu.VMEM((seqs, own, width), f32),
            pltpu.VMEM((seqs, length, width), f32), pltpu.VMEM((rows, width), bf), pltpu.VMEM((rows, width), bf),
            pltpu.VMEM(quarter.shape, f32), pltpu.VMEM(quarter.shape, f32), pltpu.VMEM(quarter.shape, f32),
            DMA((40,)), DMA((5, seqs)), DMA((5, seqs)),
        ]
        return pl.pallas_call(
            self.kernel, name="backward_top" if self.top else "backward_low",
            in_specs=[pl.BlockSpec(memory_space=pltpu.SMEM)] + [VMEM_SPEC] * len(params) + [ANY_SPEC] * len(arrays) + [VMEM_SPEC] * vmem_ins + [ANY_SPEC] * (len(extra) - vmem_ins),
            out_specs=[ANY_SPEC] * len(outs) + [VMEM_SPEC] * len(vmem_outs), out_shape=outs + vmem_outs, scratch_shapes=scratch,
            compiler_params=pltpu.CompilerParams(collective_id=collective, has_side_effects=True, vmem_limit_bytes=61 << 20),
            cost_estimate=pl.CostEstimate(flops=10**10, bytes_accessed=3 * 10**8, transcendentals=0),
        )(lengths, *params, *arrays, *extra)

    def kernel(self, *refs):
        top, l, seqs, length, width, rank = self.top, self.l, self.seqs, self.length, self.width, self.rank
        mix_cols, hidden_units = self.mix_cols, self.hidden_units
        half, own, rows = length // 2, length // 4, seqs * length
        refs = list(refs)

        def take(count):
            found = refs[:count]
            del refs[:count]
            return found

        lengths, gains, ffn_gains, bias, group = take(5)
        normed_ffn, ffn_grad, from_above, middle_in, entry_in, z_in, mixed_in, scores_in, gated_in, normed_in = take(10)
        proj, (decay_down, decay_up), heads_in, ffn_ws = take(4), take(2), take(1)[0], take(3)
        if top:
            acts = take(3)
            out_partial, out_grad, out_resid = take(3)
            ffn_outs, mix_outs = take(3), None
            mix_pieces, smalls = take(2), take(6)
        else:
            above_pieces, smalls_above = take(2), take(6)
            last_partial, last_middle = take(2)
            out_input, out_layer = take(2)
            ffn_outs, mix_outs, above_outs, small_outs = take(3), take(2), take(2), take(2)
            mix_pieces = None
        ffn_own, mix_own, ffn_slots, mix_slots = take(3), take(2), take(3), take(2)
        ffn_sems, mix_sems = [take(len(job.sems())) for job in self.ffn], take(len(self.mix.sems()))
        if not top:
            above_sems, small_own, small_slots, small_sems = take(len(self.above.sems())), take(2), take(2), take(len(self.small.sems()))
            shared, peer_send, peer_recv = take(3)
            smalls = take(6)
        up_sum, bias_sum, down_sum, attn_sum, ffn_sum, group_sum = smalls
        partial, first, second, gathered, rows_in, grad, resid, middle, entry, load, send, recv = take(12)
        pending = set()

        def ids():
            me = lax.axis_index("tensor")
            return me % 2, me // 2, {"tensor": peer_of(me, 1)}, {"tensor": peer_of(me, 2)}

        def piece(c, x_half, size):
            return pl.ds(pl.multiple_of(c * half + x_half * own, own), size)

        def of_seq(ref, s, height):
            return ref.at[pl.ds(s * height, height)]

        def plain(stage, s):
            src = (partial.at[s, pl.ds(0, half)], partial.at[s, pl.ds(0, own)])[stage] if stage < 2 else gathered.at[s, pl.ds(0, own)]
            dst = (first.at[s], second.at[s])[stage] if stage < 2 else src
            return remote(src, dst, send.at[stage, s], recv.at[stage, s], ids()[2 if stage in (0, 3, 4) else 3])

        def launch(src, dst, stage, s, peer):
            remote(src, dst, send.at[stage, s], recv.at[stage, s], peer).start()
            pending.add((stage, s))

        def freed(s, stages):
            for stage in stages:
                if (stage, s) in pending:
                    plain(stage, s).wait_send()
                    pending.discard((stage, s))

        def scatter(s):
            core, cross, core_peer, cross_peer = ids()
            launch(partial.at[s, piece(1 - core, 0, half)], first.at[s], 0, s, core_peer)
            plain(0, s).wait_recv()
            freed(s, (2, 3, 4))
            partial[s, piece(core, 1 - cross, own), :] += first[s, piece(0, 1 - cross, own), :]
            launch(partial.at[s, piece(core, 1 - cross, own)], second.at[s], 1, s, cross_peer)
            partial[s, piece(core, cross, own), :] += first[s, piece(0, cross, own), :]

        def arrived(s):
            core, cross, _, _ = ids()
            plain(1, s).wait_recv()
            return partial[s, piece(core, cross, own), :] + second[s]

        def publish(s, sent):
            core, cross, core_peer, cross_peer = ids()
            gathered[s, piece(core, cross, own), :] = sent
            block = gathered.at[s, piece(core, cross, own)]
            launch(block, block, 2, s, cross_peer)
            launch(block, block, 3, s, core_peer)

        def settle(s, h_ref, gain, gain_sum, rounded):
            total = arrived(s)
            mine = pl.ds(s * own, own)
            h = h_ref[mine, :]
            r = rms_unit(h)
            unit = h * r
            here = jnp.sum(total * unit, axis=0, keepdims=True)
            gain_sum[...] = here if s == 0 else gain_sum[...] + here
            weighted = total * gain
            new = resid[mine, :] + r * (weighted - unit * jnp.mean(unit * weighted, axis=-1, keepdims=True))
            resid[mine, :] = new
            publish(s, new.astype(bf).astype(f32) if rounded else new)

        def collect(s, dest):
            core, cross, core_peer, _ = ids()
            plain(2, s).wait_recv()
            block = gathered.at[s, piece(core, 1 - cross, own)]
            launch(block, block, 4, s, core_peer)
            if dest is not None:
                dest[pl.ds(pl.multiple_of(s * length + core * half, half), half), :] = gathered[s, piece(core, 0, half), :].astype(bf)
            plain(3, s).wait_recv()
            plain(4, s).wait_recv()
            if dest is not None:
                dest[pl.ds(pl.multiple_of(s * length + (1 - core) * half, half), half), :] = gathered[s, piece(1 - core, 0, half), :].astype(bf)

        jobs = []
        over = object()

        def pump(count=1):
            for _ in range(count):
                turns = max([times for _, times in jobs], default=0)
                for turn in range(turns):
                    for job in list(jobs):
                        if turn < job[1] and next(job[0], over) is over:
                            jobs.remove(job)

        def begin(job, times=1):
            next(job)
            jobs.append((job, times))

        def local(src, dst, k):
            return pltpu.make_async_copy(src, dst, load.at[k])

        def rows_of(s):
            return pl.ds(s * length, length)

        basics = [(normed_ffn, rows_in, 0), (ffn_grad, grad, 1), (middle_in, middle, 3), (entry_in, entry, 4)] + ([] if top else [(from_above, resid, 2)])
        for src, dst, k in basics:
            local(src, dst, k).start()
        barrier = pltpu.get_barrier_semaphore()
        peers = [ring_peer(hop, self.n) for hop in (1, self.n - 1)]
        peers += list(ids()[2:]) if top else [{"tensor": lax.rem(lax.axis_index("tensor") + hop, self.tensor)} for hop in range(1, self.tensor)]
        for peer in peers:
            pl.semaphore_signal(barrier, inc=1, device_id=peer, device_id_type=MESH)
        pl.semaphore_wait(barrier, len(peers))
        if not top:
            begin(self.above.steps(None, None, above_sems, above_pieces, above_outs))

        def ffn_phase(gate_w, up_w, down_w, inner, gate_low, up_low):
            weights = [(src.at[l], dst, 5 + k) for k, (src, dst) in enumerate(zip(ffn_ws, (gate_w, up_w, down_w)))]
            if top:
                for k, (src, dst) in enumerate(zip(acts, (inner, gate_low, up_low))):
                    local(src, dst, 17 + k).start()
            for src, dst, k in weights:
                local(src, dst, k).start()
            for src, dst, k in basics[:2]:
                local(src, dst, k).wait()
            if top:
                local(acts[0], inner, 17).wait()
            else:
                for src, dst, k in weights:
                    local(src, dst, k).wait()
                for s in range(seqs):
                    for start, size in tiles(hidden_units, 256):
                        ffn_tile(rows_of(s), pl.ds(start, size), rows_in, grad, gate_w, up_w, down_w, inner, gate_low, up_low)
                    pump()
            fill(ffn_own[2], width, 512, lambda cols: tn(inner[...], grad[:, cols]))
            begin(self.ffn[2].steps(ffn_own[2:], ffn_slots[2:], ffn_sems[2], None, ffn_outs[2:]))
            if top:
                for k, (src, dst) in enumerate(zip(acts, (inner, gate_low, up_low))):
                    if k > 0:
                        local(src, dst, 17 + k).wait()
            for k, low_rows in ((0, gate_low), (1, up_low)):
                fill(ffn_own[k], width, 512, lambda cols: tn(low_rows[...], rows_in[:, cols]))
                begin(self.ffn[k].steps(ffn_own[k:k + 1], ffn_slots[k:k + 1], ffn_sems[k], None, ffn_outs[k:k + 1]))
            if top:
                for src, dst, k in weights:
                    local(src, dst, k).wait()
            for src, dst, k in basics[2:]:
                local(src, dst, k).wait()
            if top:
                core, cross, _, _ = ids()
                for s in range(seqs):
                    mine = pl.ds(pl.multiple_of(s * length + core * half + cross * own, own), own)
                    resid[pl.ds(s * own, own), :] = grad[mine, :].astype(f32)
            if top:
                for s in range(seqs):
                    fill(partial.at[s], width, 256, lambda cols: nn(inner[rows_of(s), :], down_w[:, cols]))
                    local(partial.at[s], of_seq(out_partial, s, length), 8 + s).start()
            for s in range(seqs):
                if top:
                    local(partial.at[s], of_seq(out_partial, s, length), 8 + s).wait()
                fill(partial.at[s], width, 256, lambda cols: nn(gate_low[rows_of(s), :], gate_w[:, cols]) + nn(up_low[rows_of(s), :], up_w[:, cols]))
                scatter(s)
                pump()

        hidden = (hidden_units, width)
        pl.run_scoped(ffn_phase, *[pltpu.VMEM(hidden, bf)] * 3, *[pltpu.VMEM((rows, hidden_units), bf)] * 3)

        def mixer_phase(cat, low_w, up_map, heads, z, mixed, scores, gated, low, ggrad, pre, suf, tot, dm, dq, dk, flow):
            low_w[...] = jnp.zeros_like(low_w)
            up_map[...] = jnp.zeros_like(up_map)
            moves = raw_weights(l, proj, cat, decay_down, low_w, decay_up, up_map, heads_in, heads) + [(gated_in, gated), (normed_in, rows_in)]
            once = [(src, dst, 24 + k) for k, (src, dst) in enumerate(moves)]
            each = [[(of_seq(src, s, length), dst, 14 + k) for k, (src, dst) in enumerate(((z_in, z), (mixed_in, mixed), (scores_in, scores)))] for s in range(seqs)]
            for src, dst, k in once + each[0]:
                local(src, dst, k).start()
            for s in range(seqs):
                settle(s, middle, ffn_gains[l:l + 1, :], ffn_sum, True)
                pump()
            for src, dst, k in once:
                local(src, dst, k).wait()
            for s in range(seqs):
                collect(s, grad)
                for src, dst, k in each[s]:
                    local(src, dst, k).wait()
                ggrad[...] = nt(grad[rows_of(s), :], heads[...])
                mixer_backward(
                    s == 0, z, up_map, bias.at[pl.ds(l, 1)], group.at[pl.ds(l, 1)], mixed, scores, ggrad, of_seq(low, s, length),
                    up_sum, bias_sum, group_sum, pre, suf, tot, dm, dq, dk, flow)
                if s + 1 < seqs:
                    for src, dst, k in each[s + 1]:
                        local(src, dst, k).start()
                freed(s, (0, 1))
                fill(partial.at[s], width, 256, lambda cols: nt(low[rows_of(s), :mix_cols], cat[cols, :]) + nn(low[rows_of(s), mix_cols:], low_w[:, cols]))
                scatter(s)
                pump()
            fill(mix_own[0], mix_cols, 256, lambda cols: tn(rows_in[...], low[:, cols]))
            fill(mix_own[1], width, 512, lambda cols: tn(gated[...], grad[:, cols]))
            begin(self.mix.steps(mix_own, mix_slots, mix_sems, mix_pieces, mix_outs))
            down_sum[...] = tn(low[:, mix_cols:], rows_in[...])

        f32s = lambda count: [pltpu.VMEM((length, HK), f32)] * count
        pl.run_scoped(
            mixer_phase, pltpu.VMEM((width, mix_cols), bf), pltpu.VMEM((128, width), bf), pltpu.VMEM((128, HK), bf), pltpu.VMEM((HV, width), bf), pltpu.VMEM((length, mix_cols + 128), f32),
            pltpu.VMEM((length, HV), f32), pltpu.VMEM((length, length), bf), pltpu.VMEM((rows, HV), bf), pltpu.VMEM((rows, mix_cols + 128), bf),
            pltpu.VMEM((length, HV), f32), *f32s(2), pltpu.VMEM((length // CH * 8, HK), f32), pltpu.VMEM((length, HV), bf), *f32s(3))
        for s in range(seqs):
            pump()
            settle(s, entry, gains[l:l + 1, :], attn_sum, top)
        if top:
            local(resid, out_resid, 20).start()
            for s in range(seqs):
                pump()
                collect(s, grad)
                local(of_seq(grad, s, length), of_seq(out_grad, s, length), 21 + s).start()
            local(resid, out_resid, 20).wait()
            for s in range(seqs):
                local(of_seq(grad, s, length), of_seq(out_grad, s, length), 21 + s).wait()
        else:
            small_own[0][...] = jnp.zeros_like(small_own[0])
            small_own[1][...] = jnp.zeros_like(small_own[1])
            at0 = at1 = 0
            for terms in (smalls, smalls_above):
                small_own[0][at0:at0 + rank, :] = terms[0][:rank, :]
                small_own[0][at0 + rank:at0 + rank + 1, :] = terms[1][...]
                small_own[1][at1:at1 + rank, :] = terms[2][:rank, :]
                for k in (3, 4):
                    small_own[1][at1 + rank + k - 3:at1 + rank + k - 2, :] = terms[k][...]
                small_own[1][at1 + rank + 2:at1 + rank + 3, :HV] = terms[5][...]
                at0, at1 = at0 + rank + 8, at1 + rank + 8
            hops = range(self.tensor - 1)

            def to_peer(hop):
                peer = {"tensor": lax.rem(lax.axis_index("tensor") + hop + 1, self.tensor)}
                return remote(small_own[1], shared.at[hop], peer_send.at[hop], peer_recv.at[hop], peer)

            for hop in hops:
                to_peer(hop).start()
            local(last_middle, middle, 20).start()
            for s in range(seqs):
                freed(s, (0, 1))
                local(of_seq(last_partial, s, length), partial.at[s], 8 + s).start()
            pump()
            for hop in hops:
                to_peer(hop).wait()
            small_own[1][...] += sum(shared[hop] for hop in hops)
            begin(self.small.steps(small_own, small_slots, small_sems, None, small_outs))
            for s in range(seqs):
                collect(s, None)
                local(gathered.at[s], of_seq(out_input, s, length), 21 + s).start()
                pump()
            local(last_middle, middle, 20).wait()
            for s in range(seqs):
                local(gathered.at[s], of_seq(out_input, s, length), 21 + s).wait()
                local(of_seq(last_partial, s, length), partial.at[s], 8 + s).wait()
                scatter(s)
                pump()
            for s in range(seqs):
                total = arrived(s)
                mine = pl.ds(s * own, own)
                core, cross, _, _ = ids()
                row = lax.broadcasted_iota(jnp.int32, (own, 1), 0) + (core * half + cross * own)
                publish(s, jnp.where(row < lengths[s], middle[mine, :] + total, 0.0).astype(bf).astype(f32))
                pump()
            for s in range(seqs):
                collect(s, grad)
                local(of_seq(grad, s, length), of_seq(out_layer, s, length), 21 + s).start()
                pump()
            for s in range(seqs):
                local(of_seq(grad, s, length), of_seq(out_layer, s, length), 21 + s).wait()
        while jobs:
            pump()
        for s in range(seqs):
            freed(s, range(5))


class Finish:
    def __init__(self, rows, width, mix_cols, hidden_units, rank):
        self.rank, self.width = rank, width
        self.cols = ((0, HK), (HK, HK), (2 * HK, HV), (2 * HK + HV, HV))
        f = lambda *shape: jax.ShapeDtypeStruct(shape, f32)
        self.big = [f(2, hidden_units, width)] * 3 + [f(2, width, size) for _, size in self.cols] + [f(2, HV, width), f(rows, width)]
        self.big += [jax.ShapeDtypeStruct((rows, width), bf)]
        self.small = [f(2, rank, HK), f(2, HK), f(2, rank, width), f(2, width), f(2, width), f(2, HV)]

    def call(self, ffn, mix, rows_out, local, shared):
        arrays = list(ffn) + list(mix) + list(rows_out)
        return pl.pallas_call(
            self.kernel, name="finish", in_specs=[ANY_SPEC] * len(arrays) + [VMEM_SPEC] * 2,
            out_specs=[ANY_SPEC] * len(self.big) + [VMEM_SPEC] * len(self.small), out_shape=self.big + self.small,
            scratch_shapes=[pltpu.VMEM(a.shape, a.dtype) for a in arrays] + [DMA((len(arrays),)), DMA((24,))],
            compiler_params=pltpu.CompilerParams(vmem_limit_bytes=60 << 20),
            cost_estimate=pl.CostEstimate(flops=10**6, bytes_accessed=64 * 10**6, transcendentals=0),
        )(*arrays, local, shared)

    def kernel(self, *refs):
        rank, width = self.rank, self.width
        ins, (local, shared), outs, small = refs[:12], refs[12:14], refs[14:24], refs[24:30]
        load, store = refs[-2:]
        held = refs[30:42]
        loads = [pltpu.make_async_copy(src, dst, load.at[k]) for k, (src, dst) in enumerate(zip(ins, held))]
        for step in loads:
            step.start()
        stores = []

        def put(src, dst):
            step = pltpu.make_async_copy(src, dst, store.at[len(stores)])
            step.start()
            stores.append(step)

        for l in range(2):
            for k in range(3):
                loads[3 * l + k].wait()
                put(held[3 * l + k], outs[k].at[l])
        for l in range(2):
            loads[6 + 2 * l].wait()
            for k, (start, size) in enumerate(self.cols):
                put(held[6 + 2 * l].at[:, pl.ds(start, size)], outs[3 + k].at[l])
            loads[7 + 2 * l].wait()
            put(held[7 + 2 * l], outs[7].at[l])
        for k in range(2):
            loads[10 + k].wait()
            put(held[10 + k], outs[8 + k])
        up, bias, down, attn, ffn_gain, group = small
        for l in range(2):
            at = l * (rank + 8)
            up[l] = local[at:at + rank, :]
            bias[l:l + 1, :] = local[at + rank:at + rank + 1, :]
            down[l] = shared[at:at + rank, :]
            attn[l:l + 1, :] = shared[at + rank:at + rank + 1, :]
            ffn_gain[l:l + 1, :] = shared[at + rank + 1:at + rank + 2, :]
            group[l:l + 1, :] = shared[at + rank + 2:at + rank + 3, :HV]
        for step in stores:
            step.wait()


def shards(
    groups, tensor, layer_input, seq_lengths, attn_gain, query_proj, key_proj, value_proj, gate_proj,
    decay_down, decay_up, decay_bias, group_gain, output_proj, ffn_gain, ffn_gate, ffn_up, ffn_down, cotangent,
):
    seqs, length, width = layer_input.shape
    depth = attn_gain.shape[0]
    rank = decay_down.shape[2]
    rows = seqs * length
    mix_cols = 2 * HK + 2 * HV
    hidden_units = ffn_gate.shape[2]
    ring = RING if groups % RING == 0 else groups
    proj = (query_proj, key_proj, value_proj, gate_proj)
    decay = (decay_down.transpose(0, 2, 1), decay_up)
    ffn_ws = (ffn_gate.transpose(0, 2, 1), ffn_up.transpose(0, 2, 1), ffn_down)
    params = (attn_gain, ffn_gain, decay_bias, group_gain)
    found = Forward(depth, seqs, length, width, mix_cols, hidden_units).call(
        0, seq_lengths, params, layer_input.reshape(rows, width), cotangent.reshape(rows, width), proj, decay, output_proj, ffn_ws)
    kinds = 8
    acts = found[depth * kinds:]

    def backward(top, l, ffn_grad, resid, extra):
        normed, z, gated, mixed, scores, entry, middle, normed_ffn = found[l * kinds:(l + 1) * kinds]
        arrays = (normed_ffn, ffn_grad, resid, middle, entry, z, mixed, scores, gated, normed, *proj, *decay, output_proj, *ffn_ws)
        return Backward(top, l, ring, tensor, seqs, length, width, mix_cols, hidden_units, rank).call(1 + l, seq_lengths, params, arrays, extra)

    ffn_sums, mix_sums = [None] * depth, [None] * depth
    last_partial, ffn_grad, resid, *found_top = backward(True, 1, acts[0], found[kinds + 6], acts[1:])
    ffn_sums[1] = found_top[:3]
    extra = (*found_top[3:], last_partial, found[kinds + 6])
    input_grad, layer_output, *sums = backward(False, 0, ffn_grad, resid, extra)
    if groups > ring:
        found_sums = lax.psum(tuple(part * (1.0 / ring) for part in (*sums, *ffn_sums[1])), "dp")
        sums, ffn_sums[1] = found_sums[:-3], found_sums[-3:]
    ffn_sums[0], mix_sums[0], mix_sums[1], (local, shared) = sums[:3], sums[3:5], sums[5:7], sums[7:]

    done = Finish(rows, width, mix_cols, hidden_units, rank).call(
        (*ffn_sums[0], *ffn_sums[1]), (*mix_sums[0], *mix_sums[1]), (input_grad, layer_output), local, shared)
    gate, up, down, query, key, value, out_gate, head, input_grad, layer_output, d_up, d_bias, d_down, attn, ffn, group = done
    return (
        layer_output.reshape(seqs, length, width),
        input_grad.reshape(seqs, length, width),
        attn,
        query,
        key,
        value,
        out_gate,
        d_down.transpose(0, 2, 1),
        d_up,
        d_bias,
        group,
        head,
        ffn,
        gate.transpose(0, 2, 1),
        up.transpose(0, 2, 1),
        down,
    )


def solution(mesh):
    over, across = P("dp", None, None), P(None, None, "tensor")
    deep = P(None, "tensor", None)
    return jax.shard_map(
        functools.partial(shards, mesh.shape["dp"], mesh.shape["tensor"]),
        mesh=mesh,
        in_specs=(over, P("dp"), P(), across, across, across, across, P(), across, P(None, "tensor"), P(), deep, P(), across, across, deep, over),
        out_specs=(over, over, P(), across, across, across, across, P(), across, P(None, "tensor"), P(), deep, P(), across, across, deep),
        check_vma=False,
    )
```

```python
import functools
import jax, jax.numpy as jnp
from jax import lax
from jax.experimental import pallas as pl
from jax.experimental.pallas import tpu as pltpu
from jax.sharding import PartitionSpec as P
HK, HV, CH = 128, 256, 128
group_epsilon = 1e-05
bf, f32 = jnp.bfloat16, jnp.float32
SCALE = HK ** -0.5

def nn(a, b):
    return lax.dot_general(a, b, (((1,), (0,)), ((), ())), preferred_element_type=f32)
def nt(a, b):
    return lax.dot_general(a, b, (((1,), (1,)), ((), ())), preferred_element_type=f32)
def tn(a, b):
    return lax.dot_general(a, b, (((0,), (0,)), ((), ())), preferred_element_type=f32)

def halves(a):
    top = a.astype(bf)
    return top, (a - top.astype(f32)).astype(bf)

def thirds(a):
    top = a.astype(bf)
    return (top,) + halves(a - top.astype(f32))

def sigmoid(a):
    return 1.0 / (1.0 + jnp.exp(-a))

def log_sigmoid(a):
    return jnp.minimum(a, 0.0) - jnp.log1p(jnp.exp(-jnp.abs(a)))

def steps_below(n):
    out, h = [], 1
    while h < n:
        out.append(h)
        h *= 2
    return out

def decay_sums(ld):
    n = ld.shape[0]
    rows = lax.broadcasted_iota(jnp.int32, ld.shape, 0)
    total, pre, suf = ld, ld, jnp.zeros_like(ld)
    levels = []
    for h in steps_below(n):
        upper = (rows & h) != 0
        levels.append((h, upper, jnp.exp(jnp.where(upper, pre, suf))))
        below, above = pltpu.roll(total, h, 0), pltpu.roll(total, n - h, 0)
        pre = jnp.where(upper, pre + below, pre)
        suf = jnp.where(upper, suf, suf + above)
        total = total + jnp.where(upper, below, above)
    return levels, pre, suf, total

def tile_rows(c):
    return pl.ds(c * CH, CH)

def logits_of(z, up_ref, bias_ref):
    return sum(nn(piece, up_ref[...]) for piece in thirds(z[:, 2 * HK + 2 * HV:])) + bias_ref[...]

def wide_levels(chunks):
    out, h = [], 1
    while h < chunks:
        for base in range(0, chunks, 2 * h):
            out.append((tuple(range(base, base + h)), tuple(range(base + h, base + 2 * h))))
        h *= 2
    return out

def wide_factor(c, group, is_upper, pre, suf, tot):
    arg = pre[tile_rows(c), :] if is_upper else suf[tile_rows(c), :]
    for o in group:
        if (o < c) if is_upper else (o > c):
            arg = arg + tot[pl.ds(o * 8, 1), :]
    return jnp.exp(arg)

def mixer_forward(z_ref, up_ref, bias_ref, gain_ref, gated_ref, mixed_ref, scores_ref, pre, suf, tot):
    chunks = z_ref.shape[0] // CH
    i = lax.broadcasted_iota(jnp.int32, (CH, CH), 0)
    j = lax.broadcasted_iota(jnp.int32, (CH, CH), 1)
    apart = i ^ j
    scores_ref[...] = jnp.zeros_like(scores_ref)
    for c in range(chunks):
        z = z_ref[tile_rows(c), :]
        q, k = z[:, :HK].astype(bf), z[:, HK:2 * HK].astype(bf)
        ld = log_sigmoid(logits_of(z, up_ref, bias_ref)) / 16.0
        levels, p, s, t = decay_sums(ld)
        pre[tile_rows(c), :], suf[tile_rows(c), :], tot[pl.ds(c * 8, 8), :] = p, s, t[:8]
        tile = nt(q, k)
        qf, kf = q.astype(f32), k.astype(f32)
        for h, upper, factor in levels:
            rows = (jnp.where(upper, qf, kf) * factor).astype(bf)
            tile = jnp.where(apart >= h, nt(rows, rows), tile)
        scores_ref[tile_rows(c), tile_rows(c)] = jnp.where(i >= j, tile * SCALE, 0.0).astype(bf)
    for low_group, up_group in wide_levels(chunks):
        q_rows = [(z_ref[tile_rows(c), :HK].astype(bf).astype(f32) * wide_factor(c, up_group, True, pre, suf, tot)).astype(bf) for c in up_group]
        k_rows = [(z_ref[tile_rows(c), HK:2 * HK].astype(bf).astype(f32) * wide_factor(c, low_group, False, pre, suf, tot)).astype(bf) for c in low_group]
        for a, c in enumerate(up_group):
            for b, o in enumerate(low_group):
                scores_ref[tile_rows(c), tile_rows(o)] = (nt(q_rows[a], k_rows[b]) * SCALE).astype(bf)
    for c in range(chunks):
        width = (c + 1) * CH
        mixed = nn(scores_ref[tile_rows(c), :width], z_ref[:width, 2 * HK:2 * HK + HV].astype(bf))
        mixed_ref[tile_rows(c), :] = mixed
        out_gate = z_ref[tile_rows(c), 2 * HK + HV:2 * HK + 2 * HV]
        normed = mixed * lax.rsqrt(jnp.mean(mixed * mixed, axis=-1, keepdims=True) + group_epsilon) * gain_ref[...]
        gated_ref[tile_rows(c), :] = (normed * out_gate * sigmoid(out_gate)).astype(bf)

def mixer_backward(fresh, z_ref, up_ref, bias_ref, gain_ref, mixed_ref, scores_ref, grad_ref,
                   out_ref, up_out, bias_out, gain_out, pre, suf, tot, dm_ref, dq_ref, dk_ref, flow):
    chunks = z_ref.shape[0] // CH
    i = lax.broadcasted_iota(jnp.int32, (CH, CH), 0)
    j = lax.broadcasted_iota(jnp.int32, (CH, CH), 1)
    apart = i ^ j
    rows_in = lax.broadcasted_iota(jnp.int32, (CH, HK), 0)

    if fresh:
        up_out[...] = jnp.zeros_like(up_out)
        bias_out[...] = jnp.zeros_like(bias_out)
        gain_out[...] = jnp.zeros_like(gain_out)
    for c in range(chunks):
        mixed, e = mixed_ref[tile_rows(c), :], grad_ref[tile_rows(c), :]
        g = z_ref[tile_rows(c), 2 * HK + HV:2 * HK + 2 * HV]
        r = lax.rsqrt(jnp.mean(mixed * mixed, axis=-1, keepdims=True) + group_epsilon)
        sig = sigmoid(g)
        unit = mixed * r
        out_ref[tile_rows(c), 2 * HK + HV:2 * HK + 2 * HV] = (e * unit * gain_ref[...] * (sig + g * sig * (1.0 - sig))).astype(bf)
        upstream = e * g * sig
        gain_out[...] += jnp.sum(upstream * unit, axis=0, keepdims=True)
        weighted = upstream * gain_ref[...]
        dm_ref[tile_rows(c), :] = (r * (weighted - unit * jnp.mean(unit * weighted, axis=-1, keepdims=True))).astype(bf)

    def score_grad(c, o):
        return nt(dm_ref[tile_rows(c), :], z_ref[tile_rows(o), 2 * HK:2 * HK + HV].astype(bf)) * SCALE

    for c in range(chunks):
        z = z_ref[tile_rows(c), :]
        q, k = z[:, :HK].astype(bf).astype(f32), z[:, HK:2 * HK].astype(bf).astype(f32)
        ld = log_sigmoid(logits_of(z, up_ref, bias_ref)) / 16.0
        levels, p, s, t = decay_sums(ld)
        pre[tile_rows(c), :], suf[tile_rows(c), :], tot[pl.ds(c * 8, 8), :] = p, s, t[:8]
        ds = score_grad(c, c)
        diagonal = jnp.sum(jnp.where(i == j, ds, 0.0), axis=-1, keepdims=True)
        ds = jnp.where(i > j, ds, 0.0)
        both = ds + ds.T
        dq, dk = diagonal * k, diagonal * q
        fl = jnp.zeros_like(dq)
        for h, upper, factor in levels:
            rows = (jnp.where(upper, q, k) * factor).astype(bf)
            near = jnp.where((apart >= h) & (apart < 2 * h), both, 0.0).astype(bf)
            back = nn(near, rows)
            part = back * factor
            dq, dk = dq + jnp.where(upper, part, 0.0), dk + jnp.where(upper, 0.0, part)
            moved = back * rows.astype(f32)
            fl = fl + jnp.where(upper, moved, -moved)
        dq_ref[tile_rows(c), :], dk_ref[tile_rows(c), :], flow[tile_rows(c), :] = dq, dk, fl
    for low_group, up_group in wide_levels(chunks):
        q_fac = [wide_factor(c, up_group, True, pre, suf, tot) for c in up_group]
        k_fac = [wide_factor(c, low_group, False, pre, suf, tot) for c in low_group]
        q_rows = [(z_ref[tile_rows(c), :HK].astype(bf).astype(f32) * f).astype(bf) for c, f in zip(up_group, q_fac)]
        k_rows = [(z_ref[tile_rows(c), HK:2 * HK].astype(bf).astype(f32) * f).astype(bf) for c, f in zip(low_group, k_fac)]
        grads = [[score_grad(c, o).astype(bf) for o in low_group] for c in up_group]
        for a, c in enumerate(up_group):
            back = sum(nn(grads[a][b], k_rows[b]) for b in range(len(low_group)))
            dq_ref[tile_rows(c), :] += back * q_fac[a]
            flow[tile_rows(c), :] += back * q_rows[a].astype(f32)
        for b, o in enumerate(low_group):
            back = sum(tn(grads[a][b], q_rows[a]) for a in range(len(up_group)))
            dk_ref[tile_rows(o), :] += back * k_fac[b]
            flow[tile_rows(o), :] -= back * k_rows[b].astype(f32)
    later = jnp.zeros((1, HK), f32)
    for c in reversed(range(chunks)):
        out_ref[tile_rows(c), :HK] = dq_ref[tile_rows(c), :].astype(bf)
        out_ref[tile_rows(c), HK:2 * HK] = dk_ref[tile_rows(c), :].astype(bf)
        out_ref[tile_rows(c), 2 * HK:2 * HK + HV] = tn(scores_ref[pl.ds(c * CH, (chunks - c) * CH), tile_rows(c)], dm_ref[pl.ds(c * CH, (chunks - c) * CH), :]).astype(bf)
        fl = flow[tile_rows(c), :]
        for h in steps_below(CH):
            fl = fl + jnp.where(rows_in < CH - h, pltpu.roll(fl, CH - h, 0), 0.0)
        fl = fl + later
        later = fl[:1]
        z = z_ref[tile_rows(c), :]
        logits = logits_of(z, up_ref, bias_ref)
        d_logit = fl * sigmoid(-logits) / 16.0
        bias_out[...] += jnp.sum(d_logit, axis=0, keepdims=True)
        d1, d2 = halves(d_logit)
        l1, l2 = halves(z[:, 2 * HK + 2 * HV:])
        up_out[...] += tn(l1, d1) + tn(l1, d2) + tn(l2, d1)
        out_ref[tile_rows(c), 2 * HK + 2 * HV:] = (nt(d1, up_ref[...]) + nt(d2, up_ref[...])).astype(bf)


norm_epsilon = 1e-06
MESH = pl.DeviceIdType.MESH
VMEM_SPEC = pl.BlockSpec(memory_space=pltpu.VMEM)
ANY_SPEC = pl.BlockSpec(memory_space=pl.ANY)
DMA = pltpu.SemaphoreType.DMA
RING = 8


def peer_of(index, bit):
    return jnp.where((index // bit) % 2 == 0, index + bit, index - bit)


def rms_unit(h):
    return lax.rsqrt(jnp.mean(h * h, axis=-1, keepdims=True) + norm_epsilon)


def remote(src, dst, send, recv, peer):
    return pltpu.make_async_remote_copy(
        src_ref=src, dst_ref=dst, send_sem=send, recv_sem=recv, device_id=peer, device_id_type=MESH
    )


def ring_place(n):
    index = lax.rem(lax.axis_index("dp"), n)
    return jnp.where(index % 2 == 0, index // 2, n - 1 - index // 2)


def ring_peer(ahead, n):
    place = lax.rem(ring_place(n) + ahead, n)
    index = lax.axis_index("dp")
    return {"dp": index - lax.rem(index, n) + jnp.where(place < n // 2, 2 * place, 2 * (n - 1 - place) + 1)}


def ring_cut(shape, n):
    rows, cols = shape
    if rows % (16 * n) == 0:
        return rows // (2 * n), cols, True
    if rows % (8 * n) == 0 and cols % 256 == 0:
        return rows // n, cols // 2, False
    return None


def tiles(total, size):
    return [(start, min(size, total - start)) for start in range(0, total, size)]


def raw_weights(l, proj, cat, decay_down, down_w, decay_up, up_w, heads, head_w):
    moves, at = [], 0
    for w in proj:
        size = w.shape[2]
        moves.append((w.at[l], cat.at[:, pl.ds(at, size)]))
        at += size
    rank = decay_down.shape[1]
    return moves + [(decay_down.at[l], down_w.at[pl.ds(0, rank)]), (decay_up.at[l], up_w.at[pl.ds(0, rank)]), (heads.at[l], head_w)]


def ffn_tile(here, cols, rows_in, grad, gate_w, up_w, down_w, inner, gate_low, up_low):
    gate_act, up_act = nt(rows_in[here, :], gate_w[cols, :]), nt(rows_in[here, :], up_w[cols, :])
    inner_grad = nt(grad[here, :], down_w[cols, :])
    sig = sigmoid(gate_act)
    swish = gate_act * sig
    inner[here, cols] = (swish * up_act).astype(bf)
    gate_low[here, cols] = (inner_grad * up_act * sig * (1.0 + gate_act * (1.0 - sig))).astype(bf)
    up_low[here, cols] = (inner_grad * swish).astype(bf)


class Forward:
    def __init__(self, depth, seqs, length, width, mix_cols, hidden_units):
        self.depth, self.seqs, self.length, self.width = depth, seqs, length, width
        self.mix_cols, self.z_cols, self.hidden_units = mix_cols, mix_cols + 128, hidden_units
        rows, quarter = seqs * length, seqs * length // 4
        self.saved = []
        for _ in range(depth):
            self.saved += [
                ((rows, width), bf), ((rows, self.z_cols), f32), ((rows, HV), bf), ((rows, HV), f32), ((rows, length), bf),
                ((quarter, width), f32), ((quarter, width), f32), ((rows, width), bf),
            ]
        self.saved += [((rows, width), bf)] + [((rows, hidden_units), bf)] * 3

    def call(self, collective, lengths, params, x, cotangent, proj, decay, heads, ffn_ws):
        depth, seqs, length, width = self.depth, self.seqs, self.length, self.width
        own = length // 4
        saved = [jax.ShapeDtypeStruct(shape, kind) for shape, kind in self.saved]
        scratch = [pltpu.VMEM(shape, kind) for shape, kind in self.saved]
        scratch += [pltpu.VMEM(x.shape, bf)]
        scratch += [pltpu.VMEM((width, self.mix_cols), bf), pltpu.VMEM((128, width), bf), pltpu.VMEM((128, HK), bf), pltpu.VMEM((HV, width), bf)] * depth
        scratch += [pltpu.VMEM((self.hidden_units, width), bf)] * 3
        scratch += [
            pltpu.VMEM((seqs, length, width), f32), pltpu.VMEM((seqs, 2 * own, width), f32), pltpu.VMEM((seqs, own, width), f32),
            pltpu.VMEM((seqs, length, width), f32),
            pltpu.VMEM((length, HK), f32), pltpu.VMEM((length, HK), f32), pltpu.VMEM((length // CH * 8, HK), f32),
            DMA((len(saved), seqs)), DMA((7 * depth + 8,)), DMA((5, seqs)), DMA((5, seqs)),
        ]
        smem = pl.BlockSpec(memory_space=pltpu.SMEM)
        arrays = (x, cotangent, *proj, *decay, heads, *ffn_ws)
        return pl.pallas_call(
            self.kernel, name="forward_blocks",
            in_specs=[smem] + [VMEM_SPEC] * len(params) + [ANY_SPEC] * len(arrays), out_specs=[ANY_SPEC] * len(saved), out_shape=saved,
            scratch_shapes=scratch,
            compiler_params=pltpu.CompilerParams(collective_id=collective, has_side_effects=True, vmem_limit_bytes=61 << 20),
            cost_estimate=pl.CostEstimate(flops=10**10, bytes_accessed=2 * 10**8, transcendentals=0),
        )(lengths, *params, *arrays)

    def kernel(self, *refs):
        depth, seqs, length = self.depth, self.seqs, self.length
        half, own = length // 2, length // 4
        kinds = 8
        refs = list(refs)

        def take(count):
            found = refs[:count]
            del refs[:count]
            return found

        lengths, gains, ffn_gains, bias, group = take(5)
        x_in, cotangent = take(2)
        proj, (decay_down, decay_up), heads, ffn_ws = take(4), take(2), take(1)[0], take(3)
        outs = take(len(self.saved))
        kept_for_later = take(len(self.saved))
        x = take(1)[0]
        mixer_w = [take(4) for _ in range(depth)]
        gate_w, up_w, down_w = take(3)
        partial, first, second, gathered, pre, suf, tot, store, load, send, recv = take(11)
        grad, inner, gate_low, up_low = kept_for_later[depth * kinds:]
        me = lax.axis_index("tensor")
        core, cross = me % 2, me // 2
        core_peer, cross_peer = {"tensor": peer_of(me, 1)}, {"tensor": peer_of(me, 2)}

        def local(src, dst, k):
            return pltpu.make_async_copy(src, dst, load.at[k])

        def of_seq(ref, s, height):
            return ref.at[pl.ds(s * height, height)]

        x_loads = [local(of_seq(x_in, s, length), of_seq(x, s, length), s) for s in range(seqs)]
        mixer_loads = []
        for l in range(depth):
            cat, low_w, up_map, head_w = mixer_w[l]
            moves = raw_weights(l, proj, cat, decay_down, low_w, decay_up, up_map, heads, head_w)
            mixer_loads.append([local(src, dst, 8 + 7 * l + k) for k, (src, dst) in enumerate(moves)])

        def ffn_loads(l):
            return [local(src.at[l], dst, 2 + k) for k, (src, dst) in enumerate(zip(ffn_ws, (gate_w, up_w, down_w)))]

        grad_load = local(cotangent, grad, 5)
        for l in range(depth):
            mixer_w[l][1][...] = jnp.zeros_like(mixer_w[l][1])
            mixer_w[l][2][...] = jnp.zeros_like(mixer_w[l][2])
        for step in x_loads[:1] + mixer_loads[0] + x_loads[1:] + ffn_loads(0) + [step for loads in mixer_loads[1:] for step in loads] + [grad_load]:
            step.start()
        barrier = pltpu.get_barrier_semaphore()
        for peer in (core_peer, cross_peer):
            pl.semaphore_signal(barrier, inc=1, device_id=peer, device_id_type=MESH)
        pl.semaphore_wait(barrier, 2)
        sent, stores = {}, []

        def copy(src, dst, stage, s, peer):
            step = remote(src, dst, send.at[stage, s], recv.at[stage, s], peer)
            step.start()
            sent[stage, s] = step

        def freed(s, stages):
            for stage in stages:
                if (stage, s) in sent:
                    sent.pop((stage, s)).wait_send()

        def piece(c, x_half, size):
            return pl.ds(pl.multiple_of(c * half + x_half * own, own), size)

        def keep_for_later(k, s):
            height = self.saved[k][0][0] // seqs
            step = pltpu.make_async_copy(of_seq(kept_for_later[k], s, height), of_seq(outs[k], s, height), store.at[k, s])
            step.start()
            stores.append(step)

        def scatter(s):
            copy(partial.at[s, piece(1 - core, 0, half)], first.at[s], 0, s, core_peer)
            sent[0, s].wait_recv()
            freed(s, (2, 3, 4))
            partial[s, piece(core, 1 - cross, own), :] += first[s, piece(0, 1 - cross, own), :]
            copy(partial.at[s, piece(core, 1 - cross, own)], second.at[s], 1, s, cross_peer)
            partial[s, piece(core, cross, own), :] += first[s, piece(0, cross, own), :]

        def settle(s, resid, new_resid, gain):
            sent[1, s].wait_recv()
            mine = pl.ds(s * own, own)
            new = resid[mine, :] + (partial[s, piece(core, cross, own), :] + second[s])
            new_resid[mine, :] = new
            gathered[s, piece(core, cross, own), :] = (new * rms_unit(new) * gain).astype(bf).astype(f32)
            block = gathered.at[s, piece(core, cross, own)]
            copy(block, block, 2, s, cross_peer)
            copy(block, block, 3, s, core_peer)

        def collect(s, dest):
            sent[2, s].wait_recv()
            block = gathered.at[s, piece(core, 1 - cross, own)]
            copy(block, block, 4, s, core_peer)
            dest[pl.ds(pl.multiple_of(s * length + core * half, half), half), :] = gathered[s, piece(core, 0, half), :].astype(bf)
            sent[3, s].wait_recv()
            sent[4, s].wait_recv()
            dest[pl.ds(pl.multiple_of(s * length + (1 - core) * half, half), half), :] = gathered[s, piece(1 - core, 0, half), :].astype(bf)

        def rows_of(s):
            return pl.ds(s * length, length)

        for l in range(depth):
            normed, z, gated, mixed, scores, entry, middle, normed_ffn = kept_for_later[l * kinds:(l + 1) * kinds]
            cat, low_w, up_map, head_w = mixer_w[l]
            for s in range(seqs):
                if l == 0:
                    x_loads[s].wait()
                    for part in range(4):
                        block = pl.ds(s * length + part * own, own)
                        h = x[block, :].astype(f32)
                        normed[block, :] = (h * rms_unit(h) * gains[l:l + 1, :]).astype(bf)
                    entry[pl.ds(s * own, own), :] = x[pl.ds(pl.multiple_of(s * length + core * half + cross * own, own), own), :].astype(f32)
                else:
                    collect(s, normed)
                if s == 0:
                    for step in mixer_loads[l]:
                        step.wait()
                keep_for_later(l * kinds, s)
                for start, size in tiles(self.mix_cols, 256):
                    cols = pl.ds(start, size)
                    z[rows_of(s), cols] = nn(normed[rows_of(s), :], cat[:, cols])
                z[rows_of(s), pl.ds(self.mix_cols, 128)] = nt(normed[rows_of(s), :], low_w[...])
                keep_for_later(l * kinds + 1, s)
                mixer_forward(
                    of_seq(z, s, length), up_map, bias.at[pl.ds(l, 1)], group.at[pl.ds(l, 1)], of_seq(gated, s, length),
                    of_seq(mixed, s, length), of_seq(scores, s, length), pre, suf, tot)
                for k in (2, 3, 4):
                    keep_for_later(l * kinds + k, s)
                freed(s, (0, 1))
                for start, size in tiles(self.width, 256):
                    cols = pl.ds(start, size)
                    partial[s, :, cols] = nn(gated[rows_of(s), :], head_w[:, cols])
                scatter(s)
            for s in range(seqs):
                settle(s, entry, middle, ffn_gains[l:l + 1, :])
                keep_for_later(l * kinds + 5, s)
                keep_for_later(l * kinds + 6, s)
            if l + 1 == depth:
                break
            for s in range(seqs):
                collect(s, normed_ffn)
                keep_for_later(l * kinds + 7, s)
                if s == 0:
                    for step in ffn_loads(l):
                        step.wait()
                for start, size in tiles(self.hidden_units, 256):
                    cols = pl.ds(start, size)
                    gate_act = nt(normed_ffn[rows_of(s), :], gate_w[cols, :])
                    up_act = nt(normed_ffn[rows_of(s), :], up_w[cols, :])
                    inner[rows_of(s), cols] = (gate_act * sigmoid(gate_act) * up_act).astype(bf)
                freed(s, (0, 1))
                for start, size in tiles(self.width, 256):
                    cols = pl.ds(start, size)
                    partial[s, :, cols] = nn(inner[rows_of(s), :], down_w[:, cols])
                if s + 1 == seqs:
                    for step in ffn_loads(l + 1):
                        step.start()
                scatter(s)
            for s in range(seqs):
                settle(s, middle, kept_for_later[(l + 1) * kinds + 5], gains[l + 1:l + 2, :])
        grad_load.wait()
        for s in range(seqs):
            kept = lax.broadcasted_iota(jnp.int32, (length, 1), 0) < lengths[s]
            grad[rows_of(s), :] = jnp.where(kept, grad[rows_of(s), :].astype(f32), 0.0).astype(bf)
            keep_for_later(depth * kinds, s)
        normed_ffn = kept_for_later[(depth - 1) * kinds + 7]
        for step in ffn_loads(depth - 1):
            step.wait()
        for s in range(seqs):
            collect(s, normed_ffn)
            keep_for_later((depth - 1) * kinds + 7, s)
            for start, size in tiles(self.hidden_units, 256):
                ffn_tile(rows_of(s), pl.ds(start, size), normed_ffn, grad, gate_w, up_w, down_w, inner, gate_low, up_low)
            for k in range(3):
                keep_for_later(depth * kinds + 1 + k, s)
        for s in range(seqs):
            freed(s, range(5))
        for step in stores:
            step.wait()


class RingJob:
    def __init__(self, n, shapes, reduce, gather):
        self.n, self.shapes, self.reduce, self.gather = n, shapes, reduce, gather
        self.cuts = [ring_cut(shape, n) for shape in shapes]
        self.pairs = [(a, way) for a in range(len(shapes)) for way in range(2)]

    def slots(self):
        return [pltpu.VMEM((2, self.n - 1, rows, cols), f32) for rows, cols, _ in self.cuts] if self.reduce else []

    def sems(self):
        each = DMA((self.n - 1, len(self.shapes), 2))
        return [each, each] * (self.reduce + self.gather) + ([DMA((len(self.shapes), 2))] if self.gather else [])

    def pieces(self):
        return [jax.ShapeDtypeStruct((2, rows, cols), f32) for rows, cols, _ in self.cuts]

    def full(self):
        return [jax.ShapeDtypeStruct(shape, f32) for shape in self.shapes]

    def segment(self, a, way, back):
        n = self.n
        place = ring_place(n)
        index = lax.rem((place if way == 0 else n - 1 - place) + (2 * n - back), n)
        rows, cols, by_rows = self.cuts[a]
        if by_rows:
            return (pl.ds(pl.multiple_of((index * 2 + way) * rows, rows), rows), pl.ds(0, cols))
        return (pl.ds(pl.multiple_of(index * rows, rows), rows), pl.ds(way * cols, cols))

    def hop(self, src, dst, sems, step, a, way):
        peer = ring_peer(1 if way == 0 else self.n - 1, self.n)
        return remote(src, dst, sems[0].at[step, a, way], sems[1].at[step, a, way], peer)

    def steps(self, own, slots, sems, pieces, outs):
        n = self.n
        if self.reduce:
            rs, sems = sems[:2], sems[2:]
            for a, way in self.pairs:
                self.hop(own[a].at[self.segment(a, way, 0)], slots[a].at[way, 0], rs, 0, a, way).start()
            for step in range(n - 1):
                yield
                for a, way in self.pairs:
                    slot = slots[a].at[way, step]
                    self.hop(slot, slot, rs, step, a, way).wait_recv()
                    self.add(a, way, slot, own[a], slot if self.gather or step < n - 2 else pieces[a].at[way], step + 1)
                    if step < n - 2:
                        self.hop(slot, slots[a].at[way, step + 1], rs, step + 1, a, way).start()
                    elif self.gather:
                        self.begin(a, way, slot, sems, outs)
        else:
            for a, way in self.pairs:
                self.begin(a, way, pieces[a].at[way], sems, outs)
        if self.gather:
            for step in range(n - 1):
                yield
                for a, way in self.pairs:
                    piece = outs[a].at[self.segment(a, way, step)]
                    self.hop(piece, piece, sems, step, a, way).wait_recv()
                    if step < n - 2:
                        self.hop(piece, piece, sems, step + 1, a, way).start()
            for a, way in self.pairs:
                end = slots[a].at[way, n - 2] if self.reduce else pieces[a].at[way]
                pltpu.make_async_copy(end, outs[a].at[self.segment(a, way, n - 1)], sems[2].at[a, way]).wait()
        for step in range(n - 1):
            for a, way in self.pairs:
                if self.reduce:
                    self.hop(slots[a].at[way, 0], slots[a].at[way, 0], rs, step, a, way).wait_send()
                if self.gather:
                    piece = outs[a].at[self.segment(a, way, 0)]
                    self.hop(piece, piece, sems, step, a, way).wait_send()

    def begin(self, a, way, piece, sems, outs):
        place = outs[a].at[self.segment(a, way, self.n - 1)]
        self.hop(piece, place, sems, 0, a, way).start()
        pltpu.make_async_copy(piece, place, sems[2].at[a, way]).start()

    def add(self, a, way, slot, own, out, back):
        row_ds, col_ds = self.segment(a, way, back)

        @pl.loop(0, self.cuts[a][0] // 8)
        def _(block):
            here = pl.ds(pl.multiple_of(block * 8, 8), 8)
            there = pl.ds(pl.multiple_of(row_ds.start + block * 8, 8), 8)
            out[here, :] = slot[here, :] + own[there, col_ds]


ROUNDS = 13
TREES = (
    (0, ((0, 5, 7), (1, 7, 6), (2, 3, 1), (3, 6, 4), (4, 4, 2), (5, 2, 0), (8, 1, 0))),
    (0, ((0, 7, 6), (1, 5, 3), (1, 6, 4), (2, 3, 2), (2, 4, 2), (3, 2, 0), (7, 1, 0))),
    (0, ((1, 5, 7), (2, 7, 6), (4, 6, 4), (5, 4, 2), (6, 2, 0), (7, 3, 1), (9, 1, 0))),
    (0, ((4, 4, 6), (6, 6, 7), (8, 7, 5), (9, 5, 3), (10, 3, 2), (11, 2, 0), (12, 1, 0))),
    (0, ((4, 7, 6), (5, 6, 4), (7, 4, 5), (8, 5, 3), (10, 3, 1), (11, 1, 0), (12, 2, 0))),
    (0, ((5, 6, 7), (6, 4, 2), (6, 7, 5), (7, 5, 3), (8, 3, 1), (9, 2, 0), (10, 1, 0))),
    (2, ((0, 7, 5), (2, 6, 4), (3, 1, 0), (3, 3, 5), (7, 0, 2), (8, 5, 4), (11, 4, 2))),
    (2, ((9, 7, 5), (10, 6, 4), (11, 1, 3), (11, 5, 4), (12, 0, 2), (12, 3, 2), (12, 4, 2))),
)

SHARDS = 4 * len(TREES)
WAYS = ("across", "up", "down")


def mirrored(place, image):
    return (place ^ 1 if image & 1 else place) ^ (6 if image & 2 else 0)


def way_of(src, dst):
    return 0 if dst == src ^ 1 else (1 if dst == src + 2 else 2)


def hop_tables():
    blank = lambda: [[[-1] * 8 for _ in WAYS] for _ in range(ROUNDS)]
    sends, arrives, slot_there, slot_here, back_sends, back_owned, back_arrives = (blank() for _ in range(7))
    owned, hops = [[] for _ in range(8)], []
    for t, (root, tree) in enumerate(TREES):
        for image in range(4):
            shard = 4 * t + image
            owner = mirrored(root, image)
            owned[owner].append(shard)
            for when, src, dst in tree:
                hops.append((when, mirrored(src, image), mirrored(dst, image), shard, owner))
    used = [0] * 8
    for when, src, dst, shard, owner in sorted(hops):
        way = way_of(src, dst)
        assert sends[when][way][src] < 0
        sends[when][way][src] = arrives[when][way][dst] = shard
        slot_there[when][way][src] = slot_here[when][way][dst] = used[dst]
        used[dst] += 1
        later, back = ROUNDS - 1 - when, way_of(dst, src)
        back_sends[later][back][dst] = back_arrives[later][back][src] = shard
        back_owned[later][back][dst] = int(dst == owner)
    return sends, arrives, slot_there, slot_here, back_sends, back_owned, back_arrives, owned, max(used)


SENDS, ARRIVES, SLOT_THERE, SLOT_HERE, BACK_SENDS, BACK_OWNED, BACK_ARRIVES, OWNED, SLOTS = hop_tables()
MOST_OWNED = max(len(shards_of) for shards_of in OWNED)


def block_place():
    return lax.rem(lax.axis_index("dp"), RING)


def look_up(row):
    place = block_place()
    found = jnp.int32(-1)
    for p, value in enumerate(row):
        if value != -1:
            found = jnp.where(place == p, jnp.int32(value), found)
    return found


def block_peer(way):
    place = block_place()
    step = (jnp.where(place % 2 == 0, 1, -1), 2, -2)[way]
    return {"dp": lax.axis_index("dp") + step}


def shard_cut(shape):
    rows, cols = shape
    if rows % (8 * SHARDS) == 0:
        return rows // SHARDS, cols, 1
    assert rows * 4 % (8 * SHARDS) == 0 and cols % 512 == 0
    return rows * 4 // SHARDS, cols // 4, 4


class BlockSum:
    def __init__(self, shapes, reduce, gather):
        self.shapes, self.reduce, self.gather = shapes, reduce, gather
        self.cuts = [shard_cut(shape) for shape in shapes]

    def slots(self):
        return [pltpu.VMEM((SLOTS, rows, cols), f32) for rows, cols, _ in self.cuts] if self.reduce else []

    def sems(self):
        each = DMA((ROUNDS, len(WAYS), len(self.shapes)))
        return [each, each] * (self.reduce + self.gather) + ([DMA((MOST_OWNED, len(self.shapes)))] if self.gather else [])

    def full(self):
        return [jax.ShapeDtypeStruct(shape, f32) for shape in self.shapes]

    def segment(self, a, shard):
        rows, cols, beside = self.cuts[a]
        if beside == 1:
            return (pl.ds(pl.multiple_of(shard * rows, rows), rows), pl.ds(0, cols))
        return (pl.ds(pl.multiple_of(shard // beside * rows, rows), rows), pl.ds(pl.multiple_of(shard % beside * cols, cols), cols))

    def hop(self, src, dst, sems, step, way, a):
        return remote(src, dst, sems[0].at[step, way, a], sems[1].at[step, way, a], block_peer(way))

    def arrays(self):
        return range(len(self.shapes))

    def steps(self, own, slots, sems, pieces, outs):
        rs = sems[:2] if self.reduce else None
        ag = sems[2 * self.reduce:] if self.gather else None
        if self.reduce:
            for a in self.arrays():
                self.send(own, slots, rs, 0, a)
            for step in range(ROUNDS):
                yield
                for a in self.arrays():
                    self.receive(own, slots, rs, step, a)
                    if step + 1 < ROUNDS:
                        self.send(own, slots, rs, step + 1, a)
        if self.gather:
            for k in range(MOST_OWNED):
                shard = look_up([shards_of[k] if k < len(shards_of) else -1 for shards_of in OWNED])

                @pl.when(shard >= 0)
                def _():
                    for a in self.arrays():
                        here = self.segment(a, shard)
                        pltpu.make_async_copy(own[a].at[here], outs[a].at[here], ag[2].at[k, a]).start()
            for a in self.arrays():
                self.send_back(own, outs, ag, 0, a)
            for step in range(ROUNDS):
                yield
                for a in self.arrays():
                    self.receive_back(outs, ag, step, a)
                    if step + 1 < ROUNDS:
                        self.send_back(own, outs, ag, step + 1, a)
            for k in range(MOST_OWNED):
                shard = look_up([shards_of[k] if k < len(shards_of) else -1 for shards_of in OWNED])

                @pl.when(shard >= 0)
                def _():
                    for a in self.arrays():
                        here = self.segment(a, shard)
                        pltpu.make_async_copy(own[a].at[here], outs[a].at[here], ag[2].at[k, a]).wait()
        for table, pair in ((SENDS, rs), (BACK_SENDS, ag)):
            for step in range(ROUNDS if pair else 0):
                for way in range(len(WAYS)):
                    shard = look_up(table[step][way])

                    @pl.when(shard >= 0)
                    def _():
                        for a in self.arrays():
                            piece = own[a].at[self.segment(a, shard)]
                            self.hop(piece, piece, pair, step, way, a).wait_send()

    def send(self, own, slots, sems, step, a):
        for way in range(len(WAYS)):
            shard, there = look_up(SENDS[step][way]), look_up(SLOT_THERE[step][way])

            @pl.when(shard >= 0)
            def _():
                self.hop(own[a].at[self.segment(a, shard)], slots[a].at[there], sems, step, way, a).start()

    def receive(self, own, slots, sems, step, a):
        for way in range(len(WAYS)):
            shard, here = look_up(ARRIVES[step][way]), look_up(SLOT_HERE[step][way])

            @pl.when(shard >= 0)
            def _():
                slot = slots[a].at[here]
                self.hop(slot, slot, sems, step, way, a).wait_recv()
                row_ds, col_ds = self.segment(a, shard)

                @pl.loop(0, self.cuts[a][0] // 8)
                def _(block):
                    rows = pl.ds(pl.multiple_of(row_ds.start + block * 8, 8), 8)
                    own[a][rows, col_ds] += slots[a][here, pl.ds(pl.multiple_of(block * 8, 8), 8), :]

    def send_back(self, own, outs, sems, step, a):
        for way in range(len(WAYS)):
            shard, mine = look_up(BACK_SENDS[step][way]), look_up(BACK_OWNED[step][way])
            for source, holds in ((own, 1), (outs, 0)):
                if any(entry == holds for entry in BACK_OWNED[step][way]):
                    @pl.when(jnp.logical_and(shard >= 0, mine == holds))
                    def _():
                        here = self.segment(a, shard)
                        self.hop(source[a].at[here], outs[a].at[here], sems, step, way, a).start()

    def receive_back(self, outs, sems, step, a):
        for way in range(len(WAYS)):
            shard = look_up(BACK_ARRIVES[step][way])

            @pl.when(shard >= 0)
            def _():
                piece = outs[a].at[self.segment(a, shard)]
                self.hop(piece, piece, sems, step, way, a).wait_recv()


def fill(dst, total, size, make):
    for start, extent in tiles(total, size):
        cols = pl.ds(start, extent)
        dst[:, cols] = make(cols)


class Backward:
    def __init__(self, top, l, n, tensor, seqs, length, width, mix_cols, hidden_units, rank):
        self.top, self.l, self.n, self.tensor, self.rank = top, l, n, tensor, rank
        self.seqs, self.length, self.width, self.mix_cols, self.hidden_units = seqs, length, width, mix_cols, hidden_units
        hidden = [(hidden_units, width)]
        self.ffn = [RingJob(n, hidden, True, True) if top else BlockSum(hidden, True, True) for _ in range(3)]
        mix_shapes = [(width, mix_cols), (HV, width)]
        self.mix = RingJob(n, mix_shapes, True, not top)
        self.above = RingJob(n, mix_shapes, False, True)
        self.small = RingJob(n, [(16 * n, HK), (8 * n, width)], True, True)

    def small_outs(self):
        width = self.width
        return [jax.ShapeDtypeStruct(shape, f32) for shape in ((128, HK), (1, HK), (128, width), (1, width), (1, width), (1, HV))]

    def call(self, collective, lengths, params, arrays, extra):
        seqs, length, width = self.seqs, self.length, self.width
        rows, own = seqs * length, length // 4
        wide = jax.ShapeDtypeStruct((rows, width), bf)
        wide32, quarter = jax.ShapeDtypeStruct((rows, width), f32), jax.ShapeDtypeStruct((seqs * own, width), f32)
        smalls = self.small_outs()
        if self.top:
            outs = [wide32, wide, quarter] + [job.full()[0] for job in self.ffn]
            vmem_outs = self.mix.pieces() + smalls
            vmem_ins = 0
        else:
            outs = [wide32, wide] + [job.full()[0] for job in self.ffn] + self.mix.full() + self.above.full() + self.small.full()
            vmem_outs = []
            vmem_ins = len(extra) - 2
        scratch = [pltpu.VMEM(shape.shape, f32) for shape in [job.full()[0] for job in self.ffn] + self.mix.full()]
        scratch += [job.slots()[0] for job in self.ffn] + self.mix.slots() + [sem for job in self.ffn for sem in job.sems()] + self.mix.sems()
        if not self.top:
            scratch += self.above.sems() + [pltpu.VMEM(shape.shape, f32) for shape in self.small.full()] + self.small.slots() + self.small.sems()
            scratch += [pltpu.VMEM((self.tensor - 1, 8 * self.n, width), f32), DMA((self.tensor - 1,)), DMA((self.tensor - 1,))]
            scratch += [pltpu.VMEM(shape.shape, f32) for shape in smalls]
        scratch += [
            pltpu.VMEM((seqs, length, width), f32), pltpu.VMEM((seqs, 2 * own, width), f32), pltpu.VMEM((seqs, own, width), f32),
            pltpu.VMEM((seqs, length, width), f32), pltpu.VMEM((rows, width), bf), pltpu.VMEM((rows, width), bf),
            pltpu.VMEM(quarter.shape, f32), pltpu.VMEM(quarter.shape, f32), pltpu.VMEM(quarter.shape, f32),
            DMA((40,)), DMA((5, seqs)), DMA((5, seqs)),
        ]
        return pl.pallas_call(
            self.kernel, name="backward_top" if self.top else "backward_low",
            in_specs=[pl.BlockSpec(memory_space=pltpu.SMEM)] + [VMEM_SPEC] * len(params) + [ANY_SPEC] * len(arrays) + [VMEM_SPEC] * vmem_ins + [ANY_SPEC] * (len(extra) - vmem_ins),
            out_specs=[ANY_SPEC] * len(outs) + [VMEM_SPEC] * len(vmem_outs), out_shape=outs + vmem_outs, scratch_shapes=scratch,
            compiler_params=pltpu.CompilerParams(collective_id=collective, has_side_effects=True, vmem_limit_bytes=61 << 20),
            cost_estimate=pl.CostEstimate(flops=10**10, bytes_accessed=3 * 10**8, transcendentals=0),
        )(lengths, *params, *arrays, *extra)

    def kernel(self, *refs):
        top, l, seqs, length, width, rank = self.top, self.l, self.seqs, self.length, self.width, self.rank
        mix_cols, hidden_units = self.mix_cols, self.hidden_units
        half, own, rows = length // 2, length // 4, seqs * length
        refs = list(refs)

        def take(count):
            found = refs[:count]
            del refs[:count]
            return found

        lengths, gains, ffn_gains, bias, group = take(5)
        normed_ffn, ffn_grad, from_above, middle_in, entry_in, z_in, mixed_in, scores_in, gated_in, normed_in = take(10)
        proj, (decay_down, decay_up), heads_in, ffn_ws = take(4), take(2), take(1)[0], take(3)
        if top:
            acts = take(3)
            out_partial, out_grad, out_resid = take(3)
            ffn_outs, mix_outs = take(3), None
            mix_pieces, smalls = take(2), take(6)
        else:
            above_pieces, smalls_above = take(2), take(6)
            last_partial, last_middle = take(2)
            out_input, out_layer = take(2)
            ffn_outs, mix_outs, above_outs, small_outs = take(3), take(2), take(2), take(2)
            mix_pieces = None
        ffn_own, mix_own, ffn_slots, mix_slots = take(3), take(2), take(3), take(2)
        ffn_sems, mix_sems = [take(len(job.sems())) for job in self.ffn], take(len(self.mix.sems()))
        if not top:
            above_sems, small_own, small_slots, small_sems = take(len(self.above.sems())), take(2), take(2), take(len(self.small.sems()))
            shared, peer_send, peer_recv = take(3)
            smalls = take(6)
        up_sum, bias_sum, down_sum, attn_sum, ffn_sum, group_sum = smalls
        partial, first, second, gathered, rows_in, grad, resid, middle, entry, load, send, recv = take(12)
        pending = set()

        def ids():
            me = lax.axis_index("tensor")
            return me % 2, me // 2, {"tensor": peer_of(me, 1)}, {"tensor": peer_of(me, 2)}

        def piece(c, x_half, size):
            return pl.ds(pl.multiple_of(c * half + x_half * own, own), size)

        def of_seq(ref, s, height):
            return ref.at[pl.ds(s * height, height)]

        def plain(stage, s):
            src = (partial.at[s, pl.ds(0, half)], partial.at[s, pl.ds(0, own)])[stage] if stage < 2 else gathered.at[s, pl.ds(0, own)]
            dst = (first.at[s], second.at[s])[stage] if stage < 2 else src
            return remote(src, dst, send.at[stage, s], recv.at[stage, s], ids()[2 if stage in (0, 3, 4) else 3])

        def launch(src, dst, stage, s, peer):
            remote(src, dst, send.at[stage, s], recv.at[stage, s], peer).start()
            pending.add((stage, s))

        def freed(s, stages):
            for stage in stages:
                if (stage, s) in pending:
                    plain(stage, s).wait_send()
                    pending.discard((stage, s))

        def scatter(s):
            core, cross, core_peer, cross_peer = ids()
            launch(partial.at[s, piece(1 - core, 0, half)], first.at[s], 0, s, core_peer)
            plain(0, s).wait_recv()
            freed(s, (2, 3, 4))
            partial[s, piece(core, 1 - cross, own), :] += first[s, piece(0, 1 - cross, own), :]
            launch(partial.at[s, piece(core, 1 - cross, own)], second.at[s], 1, s, cross_peer)
            partial[s, piece(core, cross, own), :] += first[s, piece(0, cross, own), :]

        def arrived(s):
            core, cross, _, _ = ids()
            plain(1, s).wait_recv()
            return partial[s, piece(core, cross, own), :] + second[s]

        def publish(s, sent):
            core, cross, core_peer, cross_peer = ids()
            gathered[s, piece(core, cross, own), :] = sent
            block = gathered.at[s, piece(core, cross, own)]
            launch(block, block, 2, s, cross_peer)
            launch(block, block, 3, s, core_peer)

        def settle(s, h_ref, gain, gain_sum, rounded):
            total = arrived(s)
            mine = pl.ds(s * own, own)
            h = h_ref[mine, :]
            r = rms_unit(h)
            unit = h * r
            here = jnp.sum(total * unit, axis=0, keepdims=True)
            gain_sum[...] = here if s == 0 else gain_sum[...] + here
            weighted = total * gain
            new = resid[mine, :] + r * (weighted - unit * jnp.mean(unit * weighted, axis=-1, keepdims=True))
            resid[mine, :] = new
            publish(s, new.astype(bf).astype(f32) if rounded else new)

        def collect(s, dest):
            core, cross, core_peer, _ = ids()
            plain(2, s).wait_recv()
            block = gathered.at[s, piece(core, 1 - cross, own)]
            launch(block, block, 4, s, core_peer)
            if dest is not None:
                dest[pl.ds(pl.multiple_of(s * length + core * half, half), half), :] = gathered[s, piece(core, 0, half), :].astype(bf)
            plain(3, s).wait_recv()
            plain(4, s).wait_recv()
            if dest is not None:
                dest[pl.ds(pl.multiple_of(s * length + (1 - core) * half, half), half), :] = gathered[s, piece(1 - core, 0, half), :].astype(bf)

        jobs = []
        over = object()

        def pump(count=1):
            for _ in range(count):
                turns = max([times for _, times in jobs], default=0)
                for turn in range(turns):
                    for job in list(jobs):
                        if turn < job[1] and next(job[0], over) is over:
                            jobs.remove(job)

        def begin(job, times=1):
            next(job)
            jobs.append((job, times))

        def local(src, dst, k):
            return pltpu.make_async_copy(src, dst, load.at[k])

        def rows_of(s):
            return pl.ds(s * length, length)

        basics = [(normed_ffn, rows_in, 0), (ffn_grad, grad, 1), (middle_in, middle, 3), (entry_in, entry, 4)] + ([] if top else [(from_above, resid, 2)])
        for src, dst, k in basics:
            local(src, dst, k).start()
        barrier = pltpu.get_barrier_semaphore()
        level = block_place() // 2
        core_peer, cross_peer = ids()[2:]
        peers = [core_peer, cross_peer] if top else [{"tensor": lax.rem(lax.axis_index("tensor") + hop, self.tensor)} for hop in range(1, self.tensor)]
        for peer in peers + [block_peer(0)]:
            pl.semaphore_signal(barrier, inc=1, device_id=peer, device_id_type=MESH)
        for way, there in ((1, level < RING // 2 - 1), (2, level > 0)):
            @pl.when(there)
            def _():
                pl.semaphore_signal(barrier, inc=1, device_id=block_peer(way), device_id_type=MESH)
        pl.semaphore_wait(barrier, len(peers) + jnp.where(jnp.logical_and(level > 0, level < RING // 2 - 1), 3, 2))
        if not top:
            begin(self.above.steps(None, None, above_sems, above_pieces, above_outs))

        def ffn_phase(gate_w, up_w, down_w, inner, gate_low, up_low):
            weights = [(src.at[l], dst, 5 + k) for k, (src, dst) in enumerate(zip(ffn_ws, (gate_w, up_w, down_w)))]
            if top:
                for k, (src, dst) in enumerate(zip(acts, (inner, gate_low, up_low))):
                    local(src, dst, 17 + k).start()
            for src, dst, k in weights:
                local(src, dst, k).start()
            for src, dst, k in basics[:2]:
                local(src, dst, k).wait()
            if top:
                local(acts[0], inner, 17).wait()
            else:
                for src, dst, k in weights:
                    local(src, dst, k).wait()
                for s in range(seqs):
                    for start, size in tiles(hidden_units, 256):
                        ffn_tile(rows_of(s), pl.ds(start, size), rows_in, grad, gate_w, up_w, down_w, inner, gate_low, up_low)
                    pump()
            fill(ffn_own[2], width, 512, lambda cols: tn(inner[...], grad[:, cols]))
            begin(self.ffn[2].steps(ffn_own[2:], ffn_slots[2:], ffn_sems[2], None, ffn_outs[2:]))
            if top:
                for k, (src, dst) in enumerate(zip(acts, (inner, gate_low, up_low))):
                    if k > 0:
                        local(src, dst, 17 + k).wait()
            for k, low_rows in ((0, gate_low), (1, up_low)):
                fill(ffn_own[k], width, 512, lambda cols: tn(low_rows[...], rows_in[:, cols]))
                begin(self.ffn[k].steps(ffn_own[k:k + 1], ffn_slots[k:k + 1], ffn_sems[k], None, ffn_outs[k:k + 1]))
            if top:
                for src, dst, k in weights:
                    local(src, dst, k).wait()
            for src, dst, k in basics[2:]:
                local(src, dst, k).wait()
            if top:
                core, cross, _, _ = ids()
                for s in range(seqs):
                    mine = pl.ds(pl.multiple_of(s * length + core * half + cross * own, own), own)
                    resid[pl.ds(s * own, own), :] = grad[mine, :].astype(f32)
            if top:
                for s in range(seqs):
                    fill(partial.at[s], width, 256, lambda cols: nn(inner[rows_of(s), :], down_w[:, cols]))
                    local(partial.at[s], of_seq(out_partial, s, length), 8 + s).start()
            for s in range(seqs):
                if top:
                    local(partial.at[s], of_seq(out_partial, s, length), 8 + s).wait()
                fill(partial.at[s], width, 256, lambda cols: nn(gate_low[rows_of(s), :], gate_w[:, cols]) + nn(up_low[rows_of(s), :], up_w[:, cols]))
                scatter(s)
                pump()

        hidden = (hidden_units, width)
        pl.run_scoped(ffn_phase, *[pltpu.VMEM(hidden, bf)] * 3, *[pltpu.VMEM((rows, hidden_units), bf)] * 3)

        def mixer_phase(cat, low_w, up_map, heads, z, mixed, scores, gated, low, ggrad, pre, suf, tot, dm, dq, dk, flow):
            low_w[...] = jnp.zeros_like(low_w)
            up_map[...] = jnp.zeros_like(up_map)
            moves = raw_weights(l, proj, cat, decay_down, low_w, decay_up, up_map, heads_in, heads) + [(gated_in, gated), (normed_in, rows_in)]
            once = [(src, dst, 24 + k) for k, (src, dst) in enumerate(moves)]
            each = [[(of_seq(src, s, length), dst, 14 + k) for k, (src, dst) in enumerate(((z_in, z), (mixed_in, mixed), (scores_in, scores)))] for s in range(seqs)]
            for src, dst, k in once + each[0]:
                local(src, dst, k).start()
            for s in range(seqs):
                settle(s, middle, ffn_gains[l:l + 1, :], ffn_sum, True)
                pump()
            for src, dst, k in once:
                local(src, dst, k).wait()
            for s in range(seqs):
                collect(s, grad)
                for src, dst, k in each[s]:
                    local(src, dst, k).wait()
                ggrad[...] = nt(grad[rows_of(s), :], heads[...])
                mixer_backward(
                    s == 0, z, up_map, bias.at[pl.ds(l, 1)], group.at[pl.ds(l, 1)], mixed, scores, ggrad, of_seq(low, s, length),
                    up_sum, bias_sum, group_sum, pre, suf, tot, dm, dq, dk, flow)
                if s + 1 < seqs:
                    for src, dst, k in each[s + 1]:
                        local(src, dst, k).start()
                freed(s, (0, 1))
                fill(partial.at[s], width, 256, lambda cols: nt(low[rows_of(s), :mix_cols], cat[cols, :]) + nn(low[rows_of(s), mix_cols:], low_w[:, cols]))
                scatter(s)
                pump()
            fill(mix_own[0], mix_cols, 256, lambda cols: tn(rows_in[...], low[:, cols]))
            fill(mix_own[1], width, 512, lambda cols: tn(gated[...], grad[:, cols]))
            begin(self.mix.steps(mix_own, mix_slots, mix_sems, mix_pieces, mix_outs))
            down_sum[...] = tn(low[:, mix_cols:], rows_in[...])

        f32s = lambda count: [pltpu.VMEM((length, HK), f32)] * count
        pl.run_scoped(
            mixer_phase, pltpu.VMEM((width, mix_cols), bf), pltpu.VMEM((128, width), bf), pltpu.VMEM((128, HK), bf), pltpu.VMEM((HV, width), bf), pltpu.VMEM((length, mix_cols + 128), f32),
            pltpu.VMEM((length, HV), f32), pltpu.VMEM((length, length), bf), pltpu.VMEM((rows, HV), bf), pltpu.VMEM((rows, mix_cols + 128), bf),
            pltpu.VMEM((length, HV), f32), *f32s(2), pltpu.VMEM((length // CH * 8, HK), f32), pltpu.VMEM((length, HV), bf), *f32s(3))
        for s in range(seqs):
            pump()
            settle(s, entry, gains[l:l + 1, :], attn_sum, top)
        if top:
            local(resid, out_resid, 20).start()
            for s in range(seqs):
                pump()
                collect(s, grad)
                local(of_seq(grad, s, length), of_seq(out_grad, s, length), 21 + s).start()
            local(resid, out_resid, 20).wait()
            for s in range(seqs):
                local(of_seq(grad, s, length), of_seq(out_grad, s, length), 21 + s).wait()
        else:
            small_own[0][...] = jnp.zeros_like(small_own[0])
            small_own[1][...] = jnp.zeros_like(small_own[1])
            at0 = at1 = 0
            for terms in (smalls, smalls_above):
                small_own[0][at0:at0 + rank, :] = terms[0][:rank, :]
                small_own[0][at0 + rank:at0 + rank + 1, :] = terms[1][...]
                small_own[1][at1:at1 + rank, :] = terms[2][:rank, :]
                for k in (3, 4):
                    small_own[1][at1 + rank + k - 3:at1 + rank + k - 2, :] = terms[k][...]
                small_own[1][at1 + rank + 2:at1 + rank + 3, :HV] = terms[5][...]
                at0, at1 = at0 + rank + 8, at1 + rank + 8
            hops = range(self.tensor - 1)

            def to_peer(hop):
                peer = {"tensor": lax.rem(lax.axis_index("tensor") + hop + 1, self.tensor)}
                return remote(small_own[1], shared.at[hop], peer_send.at[hop], peer_recv.at[hop], peer)

            for hop in hops:
                to_peer(hop).start()
            local(last_middle, middle, 20).start()
            for s in range(seqs):
                freed(s, (0, 1))
                local(of_seq(last_partial, s, length), partial.at[s], 8 + s).start()
            pump()
            for hop in hops:
                to_peer(hop).wait()
            small_own[1][...] += sum(shared[hop] for hop in hops)
            begin(self.small.steps(small_own, small_slots, small_sems, None, small_outs))
            for s in range(seqs):
                collect(s, None)
                local(gathered.at[s], of_seq(out_input, s, length), 21 + s).start()
                pump()
            local(last_middle, middle, 20).wait()
            for s in range(seqs):
                local(gathered.at[s], of_seq(out_input, s, length), 21 + s).wait()
                local(of_seq(last_partial, s, length), partial.at[s], 8 + s).wait()
                scatter(s)
                pump()
            for s in range(seqs):
                total = arrived(s)
                mine = pl.ds(s * own, own)
                core, cross, _, _ = ids()
                row = lax.broadcasted_iota(jnp.int32, (own, 1), 0) + (core * half + cross * own)
                publish(s, jnp.where(row < lengths[s], middle[mine, :] + total, 0.0).astype(bf).astype(f32))
                pump()
            for s in range(seqs):
                collect(s, grad)
                local(of_seq(grad, s, length), of_seq(out_layer, s, length), 21 + s).start()
                pump()
            for s in range(seqs):
                local(of_seq(grad, s, length), of_seq(out_layer, s, length), 21 + s).wait()
        while jobs:
            pump()
        for s in range(seqs):
            freed(s, range(5))


class Finish:
    def __init__(self, rows, width, mix_cols, hidden_units, rank):
        self.rank, self.width = rank, width
        self.cols = ((0, HK), (HK, HK), (2 * HK, HV), (2 * HK + HV, HV))
        f = lambda *shape: jax.ShapeDtypeStruct(shape, f32)
        self.big = [f(2, hidden_units, width)] * 3 + [f(2, width, size) for _, size in self.cols] + [f(2, HV, width), f(rows, width)]
        self.big += [jax.ShapeDtypeStruct((rows, width), bf)]
        self.small = [f(2, rank, HK), f(2, HK), f(2, rank, width), f(2, width), f(2, width), f(2, HV)]

    def call(self, ffn, mix, rows_out, local, shared):
        arrays = list(ffn) + list(mix) + list(rows_out)
        return pl.pallas_call(
            self.kernel, name="finish", in_specs=[ANY_SPEC] * len(arrays) + [VMEM_SPEC] * 2,
            out_specs=[ANY_SPEC] * len(self.big) + [VMEM_SPEC] * len(self.small), out_shape=self.big + self.small,
            scratch_shapes=[pltpu.VMEM(a.shape, a.dtype) for a in arrays] + [DMA((len(arrays),)), DMA((24,))],
            compiler_params=pltpu.CompilerParams(vmem_limit_bytes=60 << 20),
            cost_estimate=pl.CostEstimate(flops=10**6, bytes_accessed=64 * 10**6, transcendentals=0),
        )(*arrays, local, shared)

    def kernel(self, *refs):
        rank, width = self.rank, self.width
        ins, (local, shared), outs, small = refs[:12], refs[12:14], refs[14:24], refs[24:30]
        load, store = refs[-2:]
        held = refs[30:42]
        loads = [pltpu.make_async_copy(src, dst, load.at[k]) for k, (src, dst) in enumerate(zip(ins, held))]
        for step in loads:
            step.start()
        stores = []

        def put(src, dst):
            step = pltpu.make_async_copy(src, dst, store.at[len(stores)])
            step.start()
            stores.append(step)

        for l in range(2):
            for k in range(3):
                loads[3 * l + k].wait()
                put(held[3 * l + k], outs[k].at[l])
        for l in range(2):
            loads[6 + 2 * l].wait()
            for k, (start, size) in enumerate(self.cols):
                put(held[6 + 2 * l].at[:, pl.ds(start, size)], outs[3 + k].at[l])
            loads[7 + 2 * l].wait()
            put(held[7 + 2 * l], outs[7].at[l])
        for k in range(2):
            loads[10 + k].wait()
            put(held[10 + k], outs[8 + k])
        up, bias, down, attn, ffn_gain, group = small
        for l in range(2):
            at = l * (rank + 8)
            up[l] = local[at:at + rank, :]
            bias[l:l + 1, :] = local[at + rank:at + rank + 1, :]
            down[l] = shared[at:at + rank, :]
            attn[l:l + 1, :] = shared[at + rank:at + rank + 1, :]
            ffn_gain[l:l + 1, :] = shared[at + rank + 1:at + rank + 2, :]
            group[l:l + 1, :] = shared[at + rank + 2:at + rank + 3, :HV]
        for step in stores:
            step.wait()


def shards(
    groups, tensor, layer_input, seq_lengths, attn_gain, query_proj, key_proj, value_proj, gate_proj,
    decay_down, decay_up, decay_bias, group_gain, output_proj, ffn_gain, ffn_gate, ffn_up, ffn_down, cotangent,
):
    seqs, length, width = layer_input.shape
    depth = attn_gain.shape[0]
    rank = decay_down.shape[2]
    rows = seqs * length
    mix_cols = 2 * HK + 2 * HV
    hidden_units = ffn_gate.shape[2]
    assert groups % RING == 0
    ring = RING
    proj = (query_proj, key_proj, value_proj, gate_proj)
    decay = (decay_down.transpose(0, 2, 1), decay_up)
    ffn_ws = (ffn_gate.transpose(0, 2, 1), ffn_up.transpose(0, 2, 1), ffn_down)
    params = (attn_gain, ffn_gain, decay_bias, group_gain)
    found = Forward(depth, seqs, length, width, mix_cols, hidden_units).call(
        0, seq_lengths, params, layer_input.reshape(rows, width), cotangent.reshape(rows, width), proj, decay, output_proj, ffn_ws)
    kinds = 8
    acts = found[depth * kinds:]

    def backward(top, l, ffn_grad, resid, extra):
        normed, z, gated, mixed, scores, entry, middle, normed_ffn = found[l * kinds:(l + 1) * kinds]
        arrays = (normed_ffn, ffn_grad, resid, middle, entry, z, mixed, scores, gated, normed, *proj, *decay, output_proj, *ffn_ws)
        return Backward(top, l, ring, tensor, seqs, length, width, mix_cols, hidden_units, rank).call(1 + l, seq_lengths, params, arrays, extra)

    ffn_sums, mix_sums = [None] * depth, [None] * depth
    last_partial, ffn_grad, resid, *found_top = backward(True, 1, acts[0], found[kinds + 6], acts[1:])
    ffn_sums[1] = found_top[:3]
    extra = (*found_top[3:], last_partial, found[kinds + 6])
    input_grad, layer_output, *sums = backward(False, 0, ffn_grad, resid, extra)
    if groups > ring:
        found_sums = lax.psum(tuple(part * (1.0 / ring) for part in (*sums, *ffn_sums[1])), "dp")
        sums, ffn_sums[1] = found_sums[:-3], found_sums[-3:]
    ffn_sums[0], mix_sums[0], mix_sums[1], (local, shared) = sums[:3], sums[3:5], sums[5:7], sums[7:]

    done = Finish(rows, width, mix_cols, hidden_units, rank).call(
        (*ffn_sums[0], *ffn_sums[1]), (*mix_sums[0], *mix_sums[1]), (input_grad, layer_output), local, shared)
    gate, up, down, query, key, value, out_gate, head, input_grad, layer_output, d_up, d_bias, d_down, attn, ffn, group = done
    return (
        layer_output.reshape(seqs, length, width),
        input_grad.reshape(seqs, length, width),
        attn,
        query,
        key,
        value,
        out_gate,
        d_down.transpose(0, 2, 1),
        d_up,
        d_bias,
        group,
        head,
        ffn,
        gate.transpose(0, 2, 1),
        up.transpose(0, 2, 1),
        down,
    )


def solution(mesh):
    over, across = P("dp", None, None), P(None, None, "tensor")
    deep = P(None, "tensor", None)
    return jax.shard_map(
        functools.partial(shards, mesh.shape["dp"], mesh.shape["tensor"]),
        mesh=mesh,
        in_specs=(over, P("dp"), P(), across, across, across, across, P(), across, P(None, "tensor"), P(), deep, P(), across, across, deep, over),
        out_specs=(over, over, P(), across, across, across, across, P(), across, P(None, "tensor"), P(), deep, P(), across, across, deep),
        check_vma=False,
    )
```

```python
import functools
import jax, jax.numpy as jnp
from jax import lax
from jax.experimental import pallas as pl
from jax.experimental.pallas import tpu as pltpu
from jax.sharding import PartitionSpec as P
HK, HV, CH = 128, 256, 128
group_epsilon = 1e-05
bf, f32 = jnp.bfloat16, jnp.float32
SCALE = HK ** -0.5

def nn(a, b):
    return lax.dot_general(a, b, (((1,), (0,)), ((), ())), preferred_element_type=f32)
def nt(a, b):
    return lax.dot_general(a, b, (((1,), (1,)), ((), ())), preferred_element_type=f32)
def tn(a, b):
    return lax.dot_general(a, b, (((0,), (0,)), ((), ())), preferred_element_type=f32)

def halves(a):
    top = a.astype(bf)
    return top, (a - top.astype(f32)).astype(bf)

def thirds(a):
    top = a.astype(bf)
    return (top,) + halves(a - top.astype(f32))

def sigmoid(a):
    return 1.0 / (1.0 + jnp.exp(-a))

def log_sigmoid(a):
    return jnp.minimum(a, 0.0) - jnp.log1p(jnp.exp(-jnp.abs(a)))

def steps_below(n):
    out, h = [], 1
    while h < n:
        out.append(h)
        h *= 2
    return out

def decay_sums(ld):
    n = ld.shape[0]
    rows = lax.broadcasted_iota(jnp.int32, ld.shape, 0)
    total, pre, suf = ld, ld, jnp.zeros_like(ld)
    levels = []
    for h in steps_below(n):
        upper = (rows & h) != 0
        levels.append((h, upper, jnp.exp(jnp.where(upper, pre, suf))))
        below, above = pltpu.roll(total, h, 0), pltpu.roll(total, n - h, 0)
        pre = jnp.where(upper, pre + below, pre)
        suf = jnp.where(upper, suf, suf + above)
        total = total + jnp.where(upper, below, above)
    return levels, pre, suf, total

def tile_rows(c):
    return pl.ds(c * CH, CH)

def logits_of(z, up_ref, bias_ref):
    return sum(nn(piece, up_ref[...]) for piece in thirds(z[:, 2 * HK + 2 * HV:])) + bias_ref[...]

def wide_levels(chunks):
    out, h = [], 1
    while h < chunks:
        for base in range(0, chunks, 2 * h):
            out.append((tuple(range(base, base + h)), tuple(range(base + h, base + 2 * h))))
        h *= 2
    return out

def wide_factor(c, group, is_upper, pre, suf, tot):
    arg = pre[tile_rows(c), :] if is_upper else suf[tile_rows(c), :]
    for o in group:
        if (o < c) if is_upper else (o > c):
            arg = arg + tot[pl.ds(o * 8, 1), :]
    return jnp.exp(arg)

def mixer_forward(z_ref, up_ref, bias_ref, gain_ref, gated_ref, mixed_ref, scores_ref, pre, suf, tot):
    chunks = z_ref.shape[0] // CH
    i = lax.broadcasted_iota(jnp.int32, (CH, CH), 0)
    j = lax.broadcasted_iota(jnp.int32, (CH, CH), 1)
    apart = i ^ j
    scores_ref[...] = jnp.zeros_like(scores_ref)
    for c in range(chunks):
        z = z_ref[tile_rows(c), :]
        q, k = z[:, :HK].astype(bf), z[:, HK:2 * HK].astype(bf)
        ld = log_sigmoid(logits_of(z, up_ref, bias_ref)) / 16.0
        levels, p, s, t = decay_sums(ld)
        pre[tile_rows(c), :], suf[tile_rows(c), :], tot[pl.ds(c * 8, 8), :] = p, s, t[:8]
        tile = nt(q, k)
        qf, kf = q.astype(f32), k.astype(f32)
        for h, upper, factor in levels:
            rows = (jnp.where(upper, qf, kf) * factor).astype(bf)
            tile = jnp.where(apart >= h, nt(rows, rows), tile)
        scores_ref[tile_rows(c), tile_rows(c)] = jnp.where(i >= j, tile * SCALE, 0.0).astype(bf)
    for low_group, up_group in wide_levels(chunks):
        q_rows = [(z_ref[tile_rows(c), :HK].astype(bf).astype(f32) * wide_factor(c, up_group, True, pre, suf, tot)).astype(bf) for c in up_group]
        k_rows = [(z_ref[tile_rows(c), HK:2 * HK].astype(bf).astype(f32) * wide_factor(c, low_group, False, pre, suf, tot)).astype(bf) for c in low_group]
        for a, c in enumerate(up_group):
            for b, o in enumerate(low_group):
                scores_ref[tile_rows(c), tile_rows(o)] = (nt(q_rows[a], k_rows[b]) * SCALE).astype(bf)
    for c in range(chunks):
        width = (c + 1) * CH
        mixed = nn(scores_ref[tile_rows(c), :width], z_ref[:width, 2 * HK:2 * HK + HV].astype(bf))
        mixed_ref[tile_rows(c), :] = mixed
        out_gate = z_ref[tile_rows(c), 2 * HK + HV:2 * HK + 2 * HV]
        normed = mixed * lax.rsqrt(jnp.mean(mixed * mixed, axis=-1, keepdims=True) + group_epsilon) * gain_ref[...]
        gated_ref[tile_rows(c), :] = (normed * out_gate * sigmoid(out_gate)).astype(bf)

def mixer_backward(fresh, z_ref, up_ref, bias_ref, gain_ref, mixed_ref, scores_ref, grad_ref,
                   out_ref, up_out, bias_out, gain_out, pre, suf, tot, dm_ref, dq_ref, dk_ref, flow):
    chunks = z_ref.shape[0] // CH
    i = lax.broadcasted_iota(jnp.int32, (CH, CH), 0)
    j = lax.broadcasted_iota(jnp.int32, (CH, CH), 1)
    apart = i ^ j
    rows_in = lax.broadcasted_iota(jnp.int32, (CH, HK), 0)

    if fresh:
        up_out[...] = jnp.zeros_like(up_out)
        bias_out[...] = jnp.zeros_like(bias_out)
        gain_out[...] = jnp.zeros_like(gain_out)
    for c in range(chunks):
        mixed, e = mixed_ref[tile_rows(c), :], grad_ref[tile_rows(c), :]
        g = z_ref[tile_rows(c), 2 * HK + HV:2 * HK + 2 * HV]
        r = lax.rsqrt(jnp.mean(mixed * mixed, axis=-1, keepdims=True) + group_epsilon)
        sig = sigmoid(g)
        unit = mixed * r
        out_ref[tile_rows(c), 2 * HK + HV:2 * HK + 2 * HV] = (e * unit * gain_ref[...] * (sig + g * sig * (1.0 - sig))).astype(bf)
        upstream = e * g * sig
        gain_out[...] += jnp.sum(upstream * unit, axis=0, keepdims=True)
        weighted = upstream * gain_ref[...]
        dm_ref[tile_rows(c), :] = (r * (weighted - unit * jnp.mean(unit * weighted, axis=-1, keepdims=True))).astype(bf)

    def score_grad(c, o):
        return nt(dm_ref[tile_rows(c), :], z_ref[tile_rows(o), 2 * HK:2 * HK + HV].astype(bf)) * SCALE

    for c in range(chunks):
        z = z_ref[tile_rows(c), :]
        q, k = z[:, :HK].astype(bf).astype(f32), z[:, HK:2 * HK].astype(bf).astype(f32)
        ld = log_sigmoid(logits_of(z, up_ref, bias_ref)) / 16.0
        levels, p, s, t = decay_sums(ld)
        pre[tile_rows(c), :], suf[tile_rows(c), :], tot[pl.ds(c * 8, 8), :] = p, s, t[:8]
        ds = score_grad(c, c)
        diagonal = jnp.sum(jnp.where(i == j, ds, 0.0), axis=-1, keepdims=True)
        ds = jnp.where(i > j, ds, 0.0)
        both = ds + ds.T
        dq, dk = diagonal * k, diagonal * q
        fl = jnp.zeros_like(dq)
        for h, upper, factor in levels:
            rows = (jnp.where(upper, q, k) * factor).astype(bf)
            near = jnp.where((apart >= h) & (apart < 2 * h), both, 0.0).astype(bf)
            back = nn(near, rows)
            part = back * factor
            dq, dk = dq + jnp.where(upper, part, 0.0), dk + jnp.where(upper, 0.0, part)
            moved = back * rows.astype(f32)
            fl = fl + jnp.where(upper, moved, -moved)
        dq_ref[tile_rows(c), :], dk_ref[tile_rows(c), :], flow[tile_rows(c), :] = dq, dk, fl
    for low_group, up_group in wide_levels(chunks):
        q_fac = [wide_factor(c, up_group, True, pre, suf, tot) for c in up_group]
        k_fac = [wide_factor(c, low_group, False, pre, suf, tot) for c in low_group]
        q_rows = [(z_ref[tile_rows(c), :HK].astype(bf).astype(f32) * f).astype(bf) for c, f in zip(up_group, q_fac)]
        k_rows = [(z_ref[tile_rows(c), HK:2 * HK].astype(bf).astype(f32) * f).astype(bf) for c, f in zip(low_group, k_fac)]
        grads = [[score_grad(c, o).astype(bf) for o in low_group] for c in up_group]
        for a, c in enumerate(up_group):
            back = sum(nn(grads[a][b], k_rows[b]) for b in range(len(low_group)))
            dq_ref[tile_rows(c), :] += back * q_fac[a]
            flow[tile_rows(c), :] += back * q_rows[a].astype(f32)
        for b, o in enumerate(low_group):
            back = sum(tn(grads[a][b], q_rows[a]) for a in range(len(up_group)))
            dk_ref[tile_rows(o), :] += back * k_fac[b]
            flow[tile_rows(o), :] -= back * k_rows[b].astype(f32)
    later = jnp.zeros((1, HK), f32)
    for c in reversed(range(chunks)):
        out_ref[tile_rows(c), :HK] = dq_ref[tile_rows(c), :].astype(bf)
        out_ref[tile_rows(c), HK:2 * HK] = dk_ref[tile_rows(c), :].astype(bf)
        out_ref[tile_rows(c), 2 * HK:2 * HK + HV] = tn(scores_ref[pl.ds(c * CH, (chunks - c) * CH), tile_rows(c)], dm_ref[pl.ds(c * CH, (chunks - c) * CH), :]).astype(bf)
        fl = flow[tile_rows(c), :]
        for h in steps_below(CH):
            fl = fl + jnp.where(rows_in < CH - h, pltpu.roll(fl, CH - h, 0), 0.0)
        fl = fl + later
        later = fl[:1]
        z = z_ref[tile_rows(c), :]
        logits = logits_of(z, up_ref, bias_ref)
        d_logit = fl * sigmoid(-logits) / 16.0
        bias_out[...] += jnp.sum(d_logit, axis=0, keepdims=True)
        d1, d2 = halves(d_logit)
        l1, l2 = halves(z[:, 2 * HK + 2 * HV:])
        up_out[...] += tn(l1, d1) + tn(l1, d2) + tn(l2, d1)
        out_ref[tile_rows(c), 2 * HK + 2 * HV:] = (nt(d1, up_ref[...]) + nt(d2, up_ref[...])).astype(bf)


norm_epsilon = 1e-06
MESH = pl.DeviceIdType.MESH
VMEM_SPEC = pl.BlockSpec(memory_space=pltpu.VMEM)
ANY_SPEC = pl.BlockSpec(memory_space=pl.ANY)
DMA = pltpu.SemaphoreType.DMA
RING = 8


def peer_of(index, bit):
    return jnp.where((index // bit) % 2 == 0, index + bit, index - bit)


def rms_unit(h):
    return lax.rsqrt(jnp.mean(h * h, axis=-1, keepdims=True) + norm_epsilon)


def remote(src, dst, send, recv, peer):
    return pltpu.make_async_remote_copy(
        src_ref=src, dst_ref=dst, send_sem=send, recv_sem=recv, device_id=peer, device_id_type=MESH
    )


def ring_place(n):
    index = lax.rem(lax.axis_index("dp"), n)
    return jnp.where(index % 2 == 0, index // 2, n - 1 - index // 2)


def ring_peer(ahead, n):
    place = lax.rem(ring_place(n) + ahead, n)
    index = lax.axis_index("dp")
    return {"dp": index - lax.rem(index, n) + jnp.where(place < n // 2, 2 * place, 2 * (n - 1 - place) + 1)}


def ring_cut(shape, n):
    rows, cols = shape
    if rows % (16 * n) == 0:
        return rows // (2 * n), cols, True
    if rows % (8 * n) == 0 and cols % 256 == 0:
        return rows // n, cols // 2, False
    return None


def tiles(total, size):
    return [(start, min(size, total - start)) for start in range(0, total, size)]


def raw_weights(l, proj, cat, decay_down, down_w, decay_up, up_w, heads, head_w):
    moves, at = [], 0
    for w in proj:
        size = w.shape[2]
        moves.append((w.at[l], cat.at[:, pl.ds(at, size)]))
        at += size
    rank = decay_down.shape[1]
    return moves + [(decay_down.at[l], down_w.at[pl.ds(0, rank)]), (decay_up.at[l], up_w.at[pl.ds(0, rank)]), (heads.at[l], head_w)]


def ffn_tile(here, cols, rows_in, grad, gate_w, up_w, down_w, inner, gate_low, up_low):
    gate_act, up_act = nt(rows_in[here, :], gate_w[cols, :]), nt(rows_in[here, :], up_w[cols, :])
    inner_grad = nt(grad[here, :], down_w[cols, :])
    sig = sigmoid(gate_act)
    swish = gate_act * sig
    inner[here, cols] = (swish * up_act).astype(bf)
    gate_low[here, cols] = (inner_grad * up_act * sig * (1.0 + gate_act * (1.0 - sig))).astype(bf)
    up_low[here, cols] = (inner_grad * swish).astype(bf)


class Forward:
    def __init__(self, depth, seqs, length, width, mix_cols, hidden_units):
        self.depth, self.seqs, self.length, self.width = depth, seqs, length, width
        self.mix_cols, self.z_cols, self.hidden_units = mix_cols, mix_cols + 128, hidden_units
        rows, quarter = seqs * length, seqs * length // 4
        self.saved = []
        for _ in range(depth):
            self.saved += [
                ((rows, width), bf), ((rows, self.z_cols), f32), ((rows, HV), bf), ((rows, HV), f32), ((rows, length), bf),
                ((quarter, width), f32), ((quarter, width), f32), ((rows, width), bf),
            ]
        self.saved += [((rows, width), bf)] + [((rows, hidden_units), bf)] * 3

    def call(self, collective, lengths, params, x, cotangent, proj, decay, heads, ffn_ws):
        depth, seqs, length, width = self.depth, self.seqs, self.length, self.width
        own = length // 4
        saved = [jax.ShapeDtypeStruct(shape, kind) for shape, kind in self.saved]
        scratch = [pltpu.VMEM(shape, kind) for shape, kind in self.saved]
        scratch += [pltpu.VMEM(x.shape, bf)]
        scratch += [pltpu.VMEM((width, self.mix_cols), bf), pltpu.VMEM((128, width), bf), pltpu.VMEM((128, HK), bf), pltpu.VMEM((HV, width), bf)] * depth
        scratch += [pltpu.VMEM((self.hidden_units, width), bf)] * 3
        scratch += [
            pltpu.VMEM((seqs, length, width), f32), pltpu.VMEM((seqs, 2 * own, width), f32), pltpu.VMEM((seqs, own, width), f32),
            pltpu.VMEM((seqs, length, width), f32),
            pltpu.VMEM((length, HK), f32), pltpu.VMEM((length, HK), f32), pltpu.VMEM((length // CH * 8, HK), f32),
            DMA((len(saved), seqs)), DMA((7 * depth + 8,)), DMA((5, seqs)), DMA((5, seqs)),
        ]
        smem = pl.BlockSpec(memory_space=pltpu.SMEM)
        arrays = (x, cotangent, *proj, *decay, heads, *ffn_ws)
        return pl.pallas_call(
            self.kernel, name="forward_blocks",
            in_specs=[smem] + [VMEM_SPEC] * len(params) + [ANY_SPEC] * len(arrays), out_specs=[ANY_SPEC] * len(saved), out_shape=saved,
            scratch_shapes=scratch,
            compiler_params=pltpu.CompilerParams(collective_id=collective, has_side_effects=True, vmem_limit_bytes=61 << 20),
            cost_estimate=pl.CostEstimate(flops=10**10, bytes_accessed=2 * 10**8, transcendentals=0),
        )(lengths, *params, *arrays)

    def kernel(self, *refs):
        depth, seqs, length = self.depth, self.seqs, self.length
        half, own = length // 2, length // 4
        kinds = 8
        refs = list(refs)

        def take(count):
            found = refs[:count]
            del refs[:count]
            return found

        lengths, gains, ffn_gains, bias, group = take(5)
        x_in, cotangent = take(2)
        proj, (decay_down, decay_up), heads, ffn_ws = take(4), take(2), take(1)[0], take(3)
        outs = take(len(self.saved))
        kept_for_later = take(len(self.saved))
        x = take(1)[0]
        mixer_w = [take(4) for _ in range(depth)]
        gate_w, up_w, down_w = take(3)
        partial, first, second, gathered, pre, suf, tot, store, load, send, recv = take(11)
        grad, inner, gate_low, up_low = kept_for_later[depth * kinds:]
        me = lax.axis_index("tensor")
        core, cross = me % 2, me // 2
        core_peer, cross_peer = {"tensor": peer_of(me, 1)}, {"tensor": peer_of(me, 2)}

        def local(src, dst, k):
            return pltpu.make_async_copy(src, dst, load.at[k])

        def of_seq(ref, s, height):
            return ref.at[pl.ds(s * height, height)]

        x_loads = [local(of_seq(x_in, s, length), of_seq(x, s, length), s) for s in range(seqs)]
        mixer_loads = []
        for l in range(depth):
            cat, low_w, up_map, head_w = mixer_w[l]
            moves = raw_weights(l, proj, cat, decay_down, low_w, decay_up, up_map, heads, head_w)
            mixer_loads.append([local(src, dst, 8 + 7 * l + k) for k, (src, dst) in enumerate(moves)])

        def ffn_loads(l):
            return [local(src.at[l], dst, 2 + k) for k, (src, dst) in enumerate(zip(ffn_ws, (gate_w, up_w, down_w)))]

        grad_load = local(cotangent, grad, 5)
        for l in range(depth):
            mixer_w[l][1][...] = jnp.zeros_like(mixer_w[l][1])
            mixer_w[l][2][...] = jnp.zeros_like(mixer_w[l][2])
        for step in x_loads[:1] + mixer_loads[0] + x_loads[1:] + ffn_loads(0) + [step for loads in mixer_loads[1:] for step in loads] + [grad_load]:
            step.start()
        barrier = pltpu.get_barrier_semaphore()
        for peer in (core_peer, cross_peer):
            pl.semaphore_signal(barrier, inc=1, device_id=peer, device_id_type=MESH)
        pl.semaphore_wait(barrier, 2)
        sent, stores = {}, []

        def copy(src, dst, stage, s, peer):
            step = remote(src, dst, send.at[stage, s], recv.at[stage, s], peer)
            step.start()
            sent[stage, s] = step

        def freed(s, stages):
            for stage in stages:
                if (stage, s) in sent:
                    sent.pop((stage, s)).wait_send()

        def piece(c, x_half, size):
            return pl.ds(pl.multiple_of(c * half + x_half * own, own), size)

        def keep_for_later(k, s):
            height = self.saved[k][0][0] // seqs
            step = pltpu.make_async_copy(of_seq(kept_for_later[k], s, height), of_seq(outs[k], s, height), store.at[k, s])
            step.start()
            stores.append(step)

        def scatter(s):
            copy(partial.at[s, piece(1 - core, 0, half)], first.at[s], 0, s, core_peer)
            sent[0, s].wait_recv()
            freed(s, (2, 3, 4))
            partial[s, piece(core, 1 - cross, own), :] += first[s, piece(0, 1 - cross, own), :]
            copy(partial.at[s, piece(core, 1 - cross, own)], second.at[s], 1, s, cross_peer)
            partial[s, piece(core, cross, own), :] += first[s, piece(0, cross, own), :]

        def settle(s, resid, new_resid, gain):
            sent[1, s].wait_recv()
            mine = pl.ds(s * own, own)
            new = resid[mine, :] + (partial[s, piece(core, cross, own), :] + second[s])
            new_resid[mine, :] = new
            gathered[s, piece(core, cross, own), :] = (new * rms_unit(new) * gain).astype(bf).astype(f32)
            block = gathered.at[s, piece(core, cross, own)]
            copy(block, block, 2, s, cross_peer)
            copy(block, block, 3, s, core_peer)

        def collect(s, dest):
            sent[2, s].wait_recv()
            block = gathered.at[s, piece(core, 1 - cross, own)]
            copy(block, block, 4, s, core_peer)
            dest[pl.ds(pl.multiple_of(s * length + core * half, half), half), :] = gathered[s, piece(core, 0, half), :].astype(bf)
            sent[3, s].wait_recv()
            sent[4, s].wait_recv()
            dest[pl.ds(pl.multiple_of(s * length + (1 - core) * half, half), half), :] = gathered[s, piece(1 - core, 0, half), :].astype(bf)

        def rows_of(s):
            return pl.ds(s * length, length)

        for l in range(depth):
            normed, z, gated, mixed, scores, entry, middle, normed_ffn = kept_for_later[l * kinds:(l + 1) * kinds]
            cat, low_w, up_map, head_w = mixer_w[l]
            for s in range(seqs):
                if l == 0:
                    x_loads[s].wait()
                    for part in range(4):
                        block = pl.ds(s * length + part * own, own)
                        h = x[block, :].astype(f32)
                        normed[block, :] = (h * rms_unit(h) * gains[l:l + 1, :]).astype(bf)
                    entry[pl.ds(s * own, own), :] = x[pl.ds(pl.multiple_of(s * length + core * half + cross * own, own), own), :].astype(f32)
                else:
                    collect(s, normed)
                if s == 0:
                    for step in mixer_loads[l]:
                        step.wait()
                keep_for_later(l * kinds, s)
                for start, size in tiles(self.mix_cols, 256):
                    cols = pl.ds(start, size)
                    z[rows_of(s), cols] = nn(normed[rows_of(s), :], cat[:, cols])
                z[rows_of(s), pl.ds(self.mix_cols, 128)] = nt(normed[rows_of(s), :], low_w[...])
                keep_for_later(l * kinds + 1, s)
                mixer_forward(
                    of_seq(z, s, length), up_map, bias.at[pl.ds(l, 1)], group.at[pl.ds(l, 1)], of_seq(gated, s, length),
                    of_seq(mixed, s, length), of_seq(scores, s, length), pre, suf, tot)
                for k in (2, 3, 4):
                    keep_for_later(l * kinds + k, s)
                freed(s, (0, 1))
                for start, size in tiles(self.width, 256):
                    cols = pl.ds(start, size)
                    partial[s, :, cols] = nn(gated[rows_of(s), :], head_w[:, cols])
                scatter(s)
            for s in range(seqs):
                settle(s, entry, middle, ffn_gains[l:l + 1, :])
                keep_for_later(l * kinds + 5, s)
                keep_for_later(l * kinds + 6, s)
            if l + 1 == depth:
                break
            for s in range(seqs):
                collect(s, normed_ffn)
                keep_for_later(l * kinds + 7, s)
                if s == 0:
                    for step in ffn_loads(l):
                        step.wait()
                for start, size in tiles(self.hidden_units, 256):
                    cols = pl.ds(start, size)
                    gate_act = nt(normed_ffn[rows_of(s), :], gate_w[cols, :])
                    up_act = nt(normed_ffn[rows_of(s), :], up_w[cols, :])
                    inner[rows_of(s), cols] = (gate_act * sigmoid(gate_act) * up_act).astype(bf)
                freed(s, (0, 1))
                for start, size in tiles(self.width, 256):
                    cols = pl.ds(start, size)
                    partial[s, :, cols] = nn(inner[rows_of(s), :], down_w[:, cols])
                if s + 1 == seqs:
                    for step in ffn_loads(l + 1):
                        step.start()
                scatter(s)
            for s in range(seqs):
                settle(s, middle, kept_for_later[(l + 1) * kinds + 5], gains[l + 1:l + 2, :])
        grad_load.wait()
        for s in range(seqs):
            kept = lax.broadcasted_iota(jnp.int32, (length, 1), 0) < lengths[s]
            grad[rows_of(s), :] = jnp.where(kept, grad[rows_of(s), :].astype(f32), 0.0).astype(bf)
            keep_for_later(depth * kinds, s)
        normed_ffn = kept_for_later[(depth - 1) * kinds + 7]
        for step in ffn_loads(depth - 1):
            step.wait()
        for s in range(seqs):
            collect(s, normed_ffn)
            keep_for_later((depth - 1) * kinds + 7, s)
            for start, size in tiles(self.hidden_units, 256):
                ffn_tile(rows_of(s), pl.ds(start, size), normed_ffn, grad, gate_w, up_w, down_w, inner, gate_low, up_low)
            for k in range(3):
                keep_for_later(depth * kinds + 1 + k, s)
        for s in range(seqs):
            freed(s, range(5))
        for step in stores:
            step.wait()


class RingJob:
    def __init__(self, n, shapes, reduce, gather):
        self.n, self.shapes, self.reduce, self.gather = n, shapes, reduce, gather
        self.cuts = [ring_cut(shape, n) for shape in shapes]
        self.pairs = [(a, way) for a in range(len(shapes)) for way in range(2)]

    def slots(self):
        return [pltpu.VMEM((2, self.n - 1, rows, cols), f32) for rows, cols, _ in self.cuts] if self.reduce else []

    def sems(self):
        each = DMA((self.n - 1, len(self.shapes), 2))
        return [each, each] * (self.reduce + self.gather) + ([DMA((len(self.shapes), 2))] if self.gather else [])

    def pieces(self):
        return [jax.ShapeDtypeStruct((2, rows, cols), f32) for rows, cols, _ in self.cuts]

    def full(self):
        return [jax.ShapeDtypeStruct(shape, f32) for shape in self.shapes]

    def segment(self, a, way, back):
        n = self.n
        place = ring_place(n)
        index = lax.rem((place if way == 0 else n - 1 - place) + (2 * n - back), n)
        rows, cols, by_rows = self.cuts[a]
        if by_rows:
            return (pl.ds(pl.multiple_of((index * 2 + way) * rows, rows), rows), pl.ds(0, cols))
        return (pl.ds(pl.multiple_of(index * rows, rows), rows), pl.ds(way * cols, cols))

    def hop(self, src, dst, sems, step, a, way):
        peer = ring_peer(1 if way == 0 else self.n - 1, self.n)
        return remote(src, dst, sems[0].at[step, a, way], sems[1].at[step, a, way], peer)

    def steps(self, own, slots, sems, pieces, outs):
        n = self.n
        if self.reduce:
            rs, sems = sems[:2], sems[2:]
            for a, way in self.pairs:
                self.hop(own[a].at[self.segment(a, way, 0)], slots[a].at[way, 0], rs, 0, a, way).start()
            for step in range(n - 1):
                yield
                for a, way in self.pairs:
                    slot = slots[a].at[way, step]
                    self.hop(slot, slot, rs, step, a, way).wait_recv()
                    self.add(a, way, slot, own[a], slot if self.gather or step < n - 2 else pieces[a].at[way], step + 1)
                    if step < n - 2:
                        self.hop(slot, slots[a].at[way, step + 1], rs, step + 1, a, way).start()
                    elif self.gather:
                        self.begin(a, way, slot, sems, outs)
        else:
            for a, way in self.pairs:
                self.begin(a, way, pieces[a].at[way], sems, outs)
        if self.gather:
            for step in range(n - 1):
                yield
                for a, way in self.pairs:
                    piece = outs[a].at[self.segment(a, way, step)]
                    self.hop(piece, piece, sems, step, a, way).wait_recv()
                    if step < n - 2:
                        self.hop(piece, piece, sems, step + 1, a, way).start()
            for a, way in self.pairs:
                end = slots[a].at[way, n - 2] if self.reduce else pieces[a].at[way]
                pltpu.make_async_copy(end, outs[a].at[self.segment(a, way, n - 1)], sems[2].at[a, way]).wait()
        for step in range(n - 1):
            for a, way in self.pairs:
                if self.reduce:
                    self.hop(slots[a].at[way, 0], slots[a].at[way, 0], rs, step, a, way).wait_send()
                if self.gather:
                    piece = outs[a].at[self.segment(a, way, 0)]
                    self.hop(piece, piece, sems, step, a, way).wait_send()

    def begin(self, a, way, piece, sems, outs):
        place = outs[a].at[self.segment(a, way, self.n - 1)]
        self.hop(piece, place, sems, 0, a, way).start()
        pltpu.make_async_copy(piece, place, sems[2].at[a, way]).start()

    def add(self, a, way, slot, own, out, back):
        row_ds, col_ds = self.segment(a, way, back)

        @pl.loop(0, self.cuts[a][0] // 8)
        def _(block):
            here = pl.ds(pl.multiple_of(block * 8, 8), 8)
            there = pl.ds(pl.multiple_of(row_ds.start + block * 8, 8), 8)
            out[here, :] = slot[here, :] + own[there, col_ds]


ROUNDS = 13
TREES = (
    (0, ((0, 5, 7), (1, 7, 6), (2, 3, 1), (3, 6, 4), (4, 4, 2), (5, 2, 0), (8, 1, 0))),
    (0, ((0, 7, 6), (1, 5, 3), (1, 6, 4), (2, 3, 2), (2, 4, 2), (3, 2, 0), (7, 1, 0))),
    (0, ((1, 5, 7), (2, 7, 6), (4, 6, 4), (5, 4, 2), (6, 2, 0), (7, 3, 1), (9, 1, 0))),
    (0, ((4, 4, 6), (6, 6, 7), (8, 7, 5), (9, 5, 3), (10, 3, 2), (11, 2, 0), (12, 1, 0))),
    (0, ((4, 7, 6), (5, 6, 4), (7, 4, 5), (8, 5, 3), (10, 3, 1), (11, 1, 0), (12, 2, 0))),
    (0, ((5, 6, 7), (6, 4, 2), (6, 7, 5), (7, 5, 3), (8, 3, 1), (9, 2, 0), (10, 1, 0))),
    (2, ((0, 7, 5), (2, 6, 4), (3, 1, 0), (3, 3, 5), (7, 0, 2), (8, 5, 4), (11, 4, 2))),
    (2, ((9, 7, 5), (10, 6, 4), (11, 1, 3), (11, 5, 4), (12, 0, 2), (12, 3, 2), (12, 4, 2))),
)

SHARDS = 4 * len(TREES)
WAYS = ("across", "up", "down")


def mirrored(place, image):
    return (place ^ 1 if image & 1 else place) ^ (6 if image & 2 else 0)


def way_of(src, dst):
    return 0 if dst == src ^ 1 else (1 if dst == src + 2 else 2)


def hop_tables():
    blank = lambda: [[[-1] * 8 for _ in WAYS] for _ in range(ROUNDS)]
    sends, arrives, slot_there, slot_here, back_sends, back_owned, back_arrives = (blank() for _ in range(7))
    owned, hops = [[] for _ in range(8)], []
    for t, (root, tree) in enumerate(TREES):
        for image in range(4):
            shard = 4 * t + image
            owner = mirrored(root, image)
            owned[owner].append(shard)
            for when, src, dst in tree:
                hops.append((when, mirrored(src, image), mirrored(dst, image), shard, owner))
    used = [0] * 8
    for when, src, dst, shard, owner in sorted(hops):
        way = way_of(src, dst)
        assert sends[when][way][src] < 0
        sends[when][way][src] = arrives[when][way][dst] = shard
        slot_there[when][way][src] = slot_here[when][way][dst] = used[dst]
        used[dst] += 1
        later, back = ROUNDS - 1 - when, way_of(dst, src)
        back_sends[later][back][dst] = back_arrives[later][back][src] = shard
        back_owned[later][back][dst] = int(dst == owner)
    return sends, arrives, slot_there, slot_here, back_sends, back_owned, back_arrives, owned, max(used)


SENDS, ARRIVES, SLOT_THERE, SLOT_HERE, BACK_SENDS, BACK_OWNED, BACK_ARRIVES, OWNED, SLOTS = hop_tables()
MOST_OWNED = max(len(shards_of) for shards_of in OWNED)


def block_place():
    return lax.rem(lax.axis_index("dp"), RING)


def look_up(row):
    place = block_place()
    found = jnp.int32(-1)
    for p, value in enumerate(row):
        if value != -1:
            found = jnp.where(place == p, jnp.int32(value), found)
    return found


def block_peer(way):
    place = block_place()
    step = (jnp.where(place % 2 == 0, 1, -1), 2, -2)[way]
    return {"dp": lax.axis_index("dp") + step}


def shard_cut(shape):
    rows, cols = shape
    if rows % (8 * SHARDS) == 0:
        return rows // SHARDS, cols, 1
    assert rows * 4 % (8 * SHARDS) == 0 and cols % 512 == 0
    return rows * 4 // SHARDS, cols // 4, 4


class BlockSum:
    def __init__(self, shapes, reduce, gather):
        self.shapes, self.reduce, self.gather = shapes, reduce, gather
        self.cuts = [shard_cut(shape) for shape in shapes]

    def slots(self):
        return [pltpu.VMEM((SLOTS, rows, cols), f32) for rows, cols, _ in self.cuts] if self.reduce else []

    def sems(self):
        each = DMA((ROUNDS, len(WAYS), len(self.shapes)))
        return [each, each] * (self.reduce + self.gather) + ([DMA((MOST_OWNED, len(self.shapes)))] if self.gather else [])

    def full(self):
        return [jax.ShapeDtypeStruct(shape, f32) for shape in self.shapes]

    def segment(self, a, shard):
        rows, cols, beside = self.cuts[a]
        if beside == 1:
            return (pl.ds(pl.multiple_of(shard * rows, rows), rows), pl.ds(0, cols))
        return (pl.ds(pl.multiple_of(shard // beside * rows, rows), rows), pl.ds(pl.multiple_of(shard % beside * cols, cols), cols))

    def hop(self, src, dst, sems, step, way, a):
        return remote(src, dst, sems[0].at[step, way, a], sems[1].at[step, way, a], block_peer(way))

    def arrays(self):
        return range(len(self.shapes))

    def steps(self, own, slots, sems, pieces, outs):
        rs = sems[:2] if self.reduce else None
        ag = sems[2 * self.reduce:] if self.gather else None
        if self.reduce:
            for a in self.arrays():
                self.send(own, slots, rs, 0, a)
            for step in range(ROUNDS):
                yield
                for a in self.arrays():
                    self.receive(own, slots, rs, step, a)
                    if step + 1 < ROUNDS:
                        self.send(own, slots, rs, step + 1, a)
        if self.gather:
            for k in range(MOST_OWNED):
                shard = look_up([shards_of[k] if k < len(shards_of) else -1 for shards_of in OWNED])

                @pl.when(shard >= 0)
                def _():
                    for a in self.arrays():
                        here = self.segment(a, shard)
                        pltpu.make_async_copy(own[a].at[here], outs[a].at[here], ag[2].at[k, a]).start()
            for a in self.arrays():
                self.send_back(own, outs, ag, 0, a)
            for step in range(ROUNDS):
                yield
                for a in self.arrays():
                    self.receive_back(outs, ag, step, a)
                    if step + 1 < ROUNDS:
                        self.send_back(own, outs, ag, step + 1, a)
            for k in range(MOST_OWNED):
                shard = look_up([shards_of[k] if k < len(shards_of) else -1 for shards_of in OWNED])

                @pl.when(shard >= 0)
                def _():
                    for a in self.arrays():
                        here = self.segment(a, shard)
                        pltpu.make_async_copy(own[a].at[here], outs[a].at[here], ag[2].at[k, a]).wait()
        for table, pair in ((SENDS, rs), (BACK_SENDS, ag)):
            for step in range(ROUNDS if pair else 0):
                for way in range(len(WAYS)):
                    shard = look_up(table[step][way])

                    @pl.when(shard >= 0)
                    def _():
                        for a in self.arrays():
                            piece = own[a].at[self.segment(a, shard)]
                            self.hop(piece, piece, pair, step, way, a).wait_send()

    def send(self, own, slots, sems, step, a):
        for way in range(len(WAYS)):
            shard, there = look_up(SENDS[step][way]), look_up(SLOT_THERE[step][way])

            @pl.when(shard >= 0)
            def _():
                self.hop(own[a].at[self.segment(a, shard)], slots[a].at[there], sems, step, way, a).start()

    def receive(self, own, slots, sems, step, a):
        for way in range(len(WAYS)):
            shard, here = look_up(ARRIVES[step][way]), look_up(SLOT_HERE[step][way])

            @pl.when(shard >= 0)
            def _():
                slot = slots[a].at[here]
                self.hop(slot, slot, sems, step, way, a).wait_recv()
                row_ds, col_ds = self.segment(a, shard)

                @pl.loop(0, self.cuts[a][0] // 8)
                def _(block):
                    rows = pl.ds(pl.multiple_of(row_ds.start + block * 8, 8), 8)
                    own[a][rows, col_ds] += slots[a][here, pl.ds(pl.multiple_of(block * 8, 8), 8), :]

    def send_back(self, own, outs, sems, step, a):
        for way in range(len(WAYS)):
            shard, mine = look_up(BACK_SENDS[step][way]), look_up(BACK_OWNED[step][way])
            for source, holds in ((own, 1), (outs, 0)):
                if any(entry == holds for entry in BACK_OWNED[step][way]):
                    @pl.when(jnp.logical_and(shard >= 0, mine == holds))
                    def _():
                        here = self.segment(a, shard)
                        self.hop(source[a].at[here], outs[a].at[here], sems, step, way, a).start()

    def receive_back(self, outs, sems, step, a):
        for way in range(len(WAYS)):
            shard = look_up(BACK_ARRIVES[step][way])

            @pl.when(shard >= 0)
            def _():
                piece = outs[a].at[self.segment(a, shard)]
                self.hop(piece, piece, sems, step, way, a).wait_recv()


class HalvingSum:
    def __init__(self, shapes):
        self.shapes = shapes

    def slots(self):
        return [pltpu.VMEM((shape[0] - shape[0] // 8, shape[1]), f32) for shape in self.shapes]

    def sems(self):
        each = DMA((6, len(self.shapes)))
        return [each, each, DMA((len(self.shapes),))]

    def full(self):
        return [jax.ShapeDtypeStruct(shape, f32) for shape in self.shapes]

    def block(self, a, level, other):
        place, start, size = block_place(), 0, self.shapes[a][0]
        for k in range(level):
            size //= 2
            bit = place // (1, 2, 4)[k] % 2
            start = start + (1 - bit if other and k == level - 1 else bit) * size
        return pl.ds(pl.multiple_of(start, size), size)

    def hop(self, src, dst, sems, step, a):
        bit = (1, 2, 4, 4, 2, 1)[step]
        place = block_place()
        peer = {"dp": lax.axis_index("dp") + jnp.where(place // bit % 2 == 0, bit, -bit)}
        return remote(src, dst, sems[0].at[step, a], sems[1].at[step, a], peer)

    def slot(self, a, slots, step):
        rows = self.shapes[a][0]
        start = sum(rows >> (k + 1) for k in range(step))
        return slots[a].at[pl.ds(start, rows >> (step + 1))]

    def steps(self, own, slots, sems, pieces, outs):
        arrays = range(len(self.shapes))
        for step in range(3):
            for a in arrays:
                self.hop(own[a].at[self.block(a, step + 1, True)], self.slot(a, slots, step), sems, step, a).start()
            yield
            for a in arrays:
                slot = self.slot(a, slots, step)
                self.hop(slot, slot, sems, step, a).wait_recv()
                own[a][self.block(a, step + 1, False), :] += slot[...]
        for a in arrays:
            mine = self.block(a, 3, False)
            pltpu.make_async_copy(own[a].at[mine], outs[a].at[mine], sems[2].at[a]).start()
        for step in range(3, 6):
            for a in arrays:
                mine = self.block(a, 6 - step, False)
                if step == 3:
                    pltpu.make_async_copy(own[a].at[mine], outs[a].at[mine], sems[2].at[a]).wait()
                self.hop(outs[a].at[mine], outs[a].at[mine], sems, step, a).start()
            yield
            for a in arrays:
                theirs = outs[a].at[self.block(a, 6 - step, True)]
                self.hop(theirs, theirs, sems, step, a).wait_recv()
        for step in range(6):
            for a in arrays:
                slot = self.slot(a, slots, step if step < 3 else 5 - step)
                self.hop(slot, slot, sems, step, a).wait_send()


def fill(dst, total, size, make):
    for start, extent in tiles(total, size):
        cols = pl.ds(start, extent)
        dst[:, cols] = make(cols)


class Backward:
    def __init__(self, top, l, n, tensor, seqs, length, width, mix_cols, hidden_units, rank):
        self.top, self.l, self.n, self.tensor, self.rank = top, l, n, tensor, rank
        self.seqs, self.length, self.width, self.mix_cols, self.hidden_units = seqs, length, width, mix_cols, hidden_units
        hidden = [(hidden_units, width)]
        self.ffn = [RingJob(n, hidden, True, True) if top else BlockSum(hidden, True, True) for _ in range(3)]
        mix_shapes = [(width, mix_cols), (HV, width)]
        self.mix = RingJob(n, mix_shapes, True, not top)
        self.above = RingJob(n, mix_shapes, False, True)
        self.small = HalvingSum([(8 * n, HK), (8 * n, width)])

    def small_outs(self):
        width = self.width
        return [jax.ShapeDtypeStruct(shape, f32) for shape in ((128, HK), (1, HK), (128, width), (1, width), (1, width), (1, HV))]

    def call(self, collective, lengths, params, arrays, extra):
        seqs, length, width = self.seqs, self.length, self.width
        rows, own = seqs * length, length // 4
        wide = jax.ShapeDtypeStruct((rows, width), bf)
        wide32, quarter = jax.ShapeDtypeStruct((rows, width), f32), jax.ShapeDtypeStruct((seqs * own, width), f32)
        smalls = self.small_outs()
        if self.top:
            outs = [wide32, wide, quarter] + [job.full()[0] for job in self.ffn]
            vmem_outs = self.mix.pieces() + smalls
            vmem_ins = 0
        else:
            outs = [wide32, wide] + [job.full()[0] for job in self.ffn] + self.mix.full() + self.above.full() + self.small.full()
            vmem_outs = []
            vmem_ins = len(extra) - 2
        scratch = [pltpu.VMEM(shape.shape, f32) for shape in [job.full()[0] for job in self.ffn] + self.mix.full()]
        scratch += [job.slots()[0] for job in self.ffn] + self.mix.slots() + [sem for job in self.ffn for sem in job.sems()] + self.mix.sems()
        if not self.top:
            scratch += self.above.sems() + [pltpu.VMEM(shape.shape, f32) for shape in self.small.full()] + self.small.slots() + self.small.sems()
            scratch += [pltpu.VMEM((self.tensor - 1, 8 * self.n, width), f32), DMA((self.tensor - 1,)), DMA((self.tensor - 1,))]
            scratch += [pltpu.VMEM(shape.shape, f32) for shape in smalls]
        scratch += [
            pltpu.VMEM((seqs, length, width), f32), pltpu.VMEM((seqs, 2 * own, width), f32), pltpu.VMEM((seqs, own, width), f32),
            pltpu.VMEM((seqs, length, width), f32), pltpu.VMEM((rows, width), bf), pltpu.VMEM((rows, width), bf),
            pltpu.VMEM(quarter.shape, f32), pltpu.VMEM(quarter.shape, f32), pltpu.VMEM(quarter.shape, f32),
            DMA((40,)), DMA((5, seqs)), DMA((5, seqs)),
        ]
        return pl.pallas_call(
            self.kernel, name="backward_top" if self.top else "backward_low",
            in_specs=[pl.BlockSpec(memory_space=pltpu.SMEM)] + [VMEM_SPEC] * len(params) + [ANY_SPEC] * len(arrays) + [VMEM_SPEC] * vmem_ins + [ANY_SPEC] * (len(extra) - vmem_ins),
            out_specs=[ANY_SPEC] * len(outs) + [VMEM_SPEC] * len(vmem_outs), out_shape=outs + vmem_outs, scratch_shapes=scratch,
            compiler_params=pltpu.CompilerParams(collective_id=collective, has_side_effects=True, vmem_limit_bytes=61 << 20),
            cost_estimate=pl.CostEstimate(flops=10**10, bytes_accessed=3 * 10**8, transcendentals=0),
        )(lengths, *params, *arrays, *extra)

    def kernel(self, *refs):
        top, l, seqs, length, width, rank = self.top, self.l, self.seqs, self.length, self.width, self.rank
        mix_cols, hidden_units = self.mix_cols, self.hidden_units
        half, own, rows = length // 2, length // 4, seqs * length
        refs = list(refs)

        def take(count):
            found = refs[:count]
            del refs[:count]
            return found

        lengths, gains, ffn_gains, bias, group = take(5)
        normed_ffn, ffn_grad, from_above, middle_in, entry_in, z_in, mixed_in, scores_in, gated_in, normed_in = take(10)
        proj, (decay_down, decay_up), heads_in, ffn_ws = take(4), take(2), take(1)[0], take(3)
        if top:
            acts = take(3)
            out_partial, out_grad, out_resid = take(3)
            ffn_outs, mix_outs = take(3), None
            mix_pieces, smalls = take(2), take(6)
        else:
            above_pieces, smalls_above = take(2), take(6)
            last_partial, last_middle = take(2)
            out_input, out_layer = take(2)
            ffn_outs, mix_outs, above_outs, small_outs = take(3), take(2), take(2), take(2)
            mix_pieces = None
        ffn_own, mix_own, ffn_slots, mix_slots = take(3), take(2), take(3), take(2)
        ffn_sems, mix_sems = [take(len(job.sems())) for job in self.ffn], take(len(self.mix.sems()))
        if not top:
            above_sems, small_own, small_slots, small_sems = take(len(self.above.sems())), take(2), take(2), take(len(self.small.sems()))
            shared, peer_send, peer_recv = take(3)
            smalls = take(6)
        up_sum, bias_sum, down_sum, attn_sum, ffn_sum, group_sum = smalls
        partial, first, second, gathered, rows_in, grad, resid, middle, entry, load, send, recv = take(12)
        pending = set()

        def ids():
            me = lax.axis_index("tensor")
            return me % 2, me // 2, {"tensor": peer_of(me, 1)}, {"tensor": peer_of(me, 2)}

        def piece(c, x_half, size):
            return pl.ds(pl.multiple_of(c * half + x_half * own, own), size)

        def of_seq(ref, s, height):
            return ref.at[pl.ds(s * height, height)]

        def plain(stage, s):
            src = (partial.at[s, pl.ds(0, half)], partial.at[s, pl.ds(0, own)])[stage] if stage < 2 else gathered.at[s, pl.ds(0, own)]
            dst = (first.at[s], second.at[s])[stage] if stage < 2 else src
            return remote(src, dst, send.at[stage, s], recv.at[stage, s], ids()[2 if stage in (0, 3, 4) else 3])

        def launch(src, dst, stage, s, peer):
            remote(src, dst, send.at[stage, s], recv.at[stage, s], peer).start()
            pending.add((stage, s))

        def freed(s, stages):
            for stage in stages:
                if (stage, s) in pending:
                    plain(stage, s).wait_send()
                    pending.discard((stage, s))

        def scatter(s):
            core, cross, core_peer, cross_peer = ids()
            launch(partial.at[s, piece(1 - core, 0, half)], first.at[s], 0, s, core_peer)
            plain(0, s).wait_recv()
            freed(s, (2, 3, 4))
            partial[s, piece(core, 1 - cross, own), :] += first[s, piece(0, 1 - cross, own), :]
            launch(partial.at[s, piece(core, 1 - cross, own)], second.at[s], 1, s, cross_peer)
            partial[s, piece(core, cross, own), :] += first[s, piece(0, cross, own), :]

        def arrived(s):
            core, cross, _, _ = ids()
            plain(1, s).wait_recv()
            return partial[s, piece(core, cross, own), :] + second[s]

        def publish(s, sent):
            core, cross, core_peer, cross_peer = ids()
            gathered[s, piece(core, cross, own), :] = sent
            block = gathered.at[s, piece(core, cross, own)]
            launch(block, block, 2, s, cross_peer)
            launch(block, block, 3, s, core_peer)

        def settle(s, h_ref, gain, gain_sum, rounded):
            total = arrived(s)
            mine = pl.ds(s * own, own)
            h = h_ref[mine, :]
            r = rms_unit(h)
            unit = h * r
            here = jnp.sum(total * unit, axis=0, keepdims=True)
            gain_sum[...] = here if s == 0 else gain_sum[...] + here
            weighted = total * gain
            new = resid[mine, :] + r * (weighted - unit * jnp.mean(unit * weighted, axis=-1, keepdims=True))
            resid[mine, :] = new
            publish(s, new.astype(bf).astype(f32) if rounded else new)

        def collect(s, dest):
            core, cross, core_peer, _ = ids()
            plain(2, s).wait_recv()
            block = gathered.at[s, piece(core, 1 - cross, own)]
            launch(block, block, 4, s, core_peer)
            if dest is not None:
                dest[pl.ds(pl.multiple_of(s * length + core * half, half), half), :] = gathered[s, piece(core, 0, half), :].astype(bf)
            plain(3, s).wait_recv()
            plain(4, s).wait_recv()
            if dest is not None:
                dest[pl.ds(pl.multiple_of(s * length + (1 - core) * half, half), half), :] = gathered[s, piece(1 - core, 0, half), :].astype(bf)

        jobs = []
        over = object()

        def pump(count=1):
            for _ in range(count):
                turns = max([times for _, times in jobs], default=0)
                for turn in range(turns):
                    for job in list(jobs):
                        if turn < job[1] and next(job[0], over) is over:
                            jobs.remove(job)

        def begin(job, times=1):
            next(job)
            jobs.append((job, times))

        def local(src, dst, k):
            return pltpu.make_async_copy(src, dst, load.at[k])

        def rows_of(s):
            return pl.ds(s * length, length)

        basics = [(normed_ffn, rows_in, 0), (ffn_grad, grad, 1), (middle_in, middle, 3), (entry_in, entry, 4)] + ([] if top else [(from_above, resid, 2)])
        for src, dst, k in basics:
            local(src, dst, k).start()
        barrier = pltpu.get_barrier_semaphore()
        level = block_place() // 2
        core_peer, cross_peer = ids()[2:]
        peers = [core_peer, cross_peer] if top else [{"tensor": lax.rem(lax.axis_index("tensor") + hop, self.tensor)} for hop in range(1, self.tensor)]
        if not top:
            peers.append({"dp": lax.axis_index("dp") + jnp.where(level // 2 == 0, 4, -4)})
        for peer in peers + [block_peer(0)]:
            pl.semaphore_signal(barrier, inc=1, device_id=peer, device_id_type=MESH)
        for way, there in ((1, level < RING // 2 - 1), (2, level > 0)):
            @pl.when(there)
            def _():
                pl.semaphore_signal(barrier, inc=1, device_id=block_peer(way), device_id_type=MESH)
        pl.semaphore_wait(barrier, len(peers) + jnp.where(jnp.logical_and(level > 0, level < RING // 2 - 1), 3, 2))
        if not top:
            begin(self.above.steps(None, None, above_sems, above_pieces, above_outs))

        def ffn_phase(gate_w, up_w, down_w, inner, gate_low, up_low):
            weights = [(src.at[l], dst, 5 + k) for k, (src, dst) in enumerate(zip(ffn_ws, (gate_w, up_w, down_w)))]
            if top:
                for k, (src, dst) in enumerate(zip(acts, (inner, gate_low, up_low))):
                    local(src, dst, 17 + k).start()
            for src, dst, k in weights:
                local(src, dst, k).start()
            for src, dst, k in basics[:2]:
                local(src, dst, k).wait()
            if top:
                local(acts[0], inner, 17).wait()
            else:
                for src, dst, k in weights:
                    local(src, dst, k).wait()
                for s in range(seqs):
                    for start, size in tiles(hidden_units, 256):
                        ffn_tile(rows_of(s), pl.ds(start, size), rows_in, grad, gate_w, up_w, down_w, inner, gate_low, up_low)
                    pump()
            fill(ffn_own[2], width, 512, lambda cols: tn(inner[...], grad[:, cols]))
            begin(self.ffn[2].steps(ffn_own[2:], ffn_slots[2:], ffn_sems[2], None, ffn_outs[2:]))
            if top:
                for k, (src, dst) in enumerate(zip(acts, (inner, gate_low, up_low))):
                    if k > 0:
                        local(src, dst, 17 + k).wait()
            for k, low_rows in ((0, gate_low), (1, up_low)):
                fill(ffn_own[k], width, 512, lambda cols: tn(low_rows[...], rows_in[:, cols]))
                begin(self.ffn[k].steps(ffn_own[k:k + 1], ffn_slots[k:k + 1], ffn_sems[k], None, ffn_outs[k:k + 1]))
            if top:
                for src, dst, k in weights:
                    local(src, dst, k).wait()
            for src, dst, k in basics[2:]:
                local(src, dst, k).wait()
            if top:
                core, cross, _, _ = ids()
                for s in range(seqs):
                    mine = pl.ds(pl.multiple_of(s * length + core * half + cross * own, own), own)
                    resid[pl.ds(s * own, own), :] = grad[mine, :].astype(f32)
            if top:
                for s in range(seqs):
                    fill(partial.at[s], width, 256, lambda cols: nn(inner[rows_of(s), :], down_w[:, cols]))
                    local(partial.at[s], of_seq(out_partial, s, length), 8 + s).start()
            for s in range(seqs):
                if top:
                    local(partial.at[s], of_seq(out_partial, s, length), 8 + s).wait()
                fill(partial.at[s], width, 256, lambda cols: nn(gate_low[rows_of(s), :], gate_w[:, cols]) + nn(up_low[rows_of(s), :], up_w[:, cols]))
                scatter(s)
                pump()

        hidden = (hidden_units, width)
        pl.run_scoped(ffn_phase, *[pltpu.VMEM(hidden, bf)] * 3, *[pltpu.VMEM((rows, hidden_units), bf)] * 3)

        def mixer_phase(cat, low_w, up_map, heads, z, mixed, scores, gated, low, ggrad, pre, suf, tot, dm, dq, dk, flow):
            low_w[...] = jnp.zeros_like(low_w)
            up_map[...] = jnp.zeros_like(up_map)
            moves = raw_weights(l, proj, cat, decay_down, low_w, decay_up, up_map, heads_in, heads) + [(gated_in, gated), (normed_in, rows_in)]
            once = [(src, dst, 24 + k) for k, (src, dst) in enumerate(moves)]
            each = [[(of_seq(src, s, length), dst, 14 + k) for k, (src, dst) in enumerate(((z_in, z), (mixed_in, mixed), (scores_in, scores)))] for s in range(seqs)]
            for src, dst, k in once + each[0]:
                local(src, dst, k).start()
            for s in range(seqs):
                settle(s, middle, ffn_gains[l:l + 1, :], ffn_sum, True)
                pump()
            for src, dst, k in once:
                local(src, dst, k).wait()
            for s in range(seqs):
                collect(s, grad)
                for src, dst, k in each[s]:
                    local(src, dst, k).wait()
                ggrad[...] = nt(grad[rows_of(s), :], heads[...])
                mixer_backward(
                    s == 0, z, up_map, bias.at[pl.ds(l, 1)], group.at[pl.ds(l, 1)], mixed, scores, ggrad, of_seq(low, s, length),
                    up_sum, bias_sum, group_sum, pre, suf, tot, dm, dq, dk, flow)
                if not top:
                    pump()
                if s + 1 < seqs:
                    for src, dst, k in each[s + 1]:
                        local(src, dst, k).start()
                freed(s, (0, 1))
                fill(partial.at[s], width, 256, lambda cols: nt(low[rows_of(s), :mix_cols], cat[cols, :]) + nn(low[rows_of(s), mix_cols:], low_w[:, cols]))
                scatter(s)
                pump()
            fill(mix_own[0], mix_cols, 256, lambda cols: tn(rows_in[...], low[:, cols]))
            fill(mix_own[1], width, 512, lambda cols: tn(gated[...], grad[:, cols]))
            begin(self.mix.steps(mix_own, mix_slots, mix_sems, mix_pieces, mix_outs))
            down_sum[...] = tn(low[:, mix_cols:], rows_in[...])

        f32s = lambda count: [pltpu.VMEM((length, HK), f32)] * count
        pl.run_scoped(
            mixer_phase, pltpu.VMEM((width, mix_cols), bf), pltpu.VMEM((128, width), bf), pltpu.VMEM((128, HK), bf), pltpu.VMEM((HV, width), bf), pltpu.VMEM((length, mix_cols + 128), f32),
            pltpu.VMEM((length, HV), f32), pltpu.VMEM((length, length), bf), pltpu.VMEM((rows, HV), bf), pltpu.VMEM((rows, mix_cols + 128), bf),
            pltpu.VMEM((length, HV), f32), *f32s(2), pltpu.VMEM((length // CH * 8, HK), f32), pltpu.VMEM((length, HV), bf), *f32s(3))
        for s in range(seqs):
            pump()
            settle(s, entry, gains[l:l + 1, :], attn_sum, top)
        if top:
            local(resid, out_resid, 20).start()
            for s in range(seqs):
                pump()
                collect(s, grad)
                local(of_seq(grad, s, length), of_seq(out_grad, s, length), 21 + s).start()
            local(resid, out_resid, 20).wait()
            for s in range(seqs):
                local(of_seq(grad, s, length), of_seq(out_grad, s, length), 21 + s).wait()
        else:
            small_own[0][...] = jnp.zeros_like(small_own[0])
            small_own[1][...] = jnp.zeros_like(small_own[1])
            at0 = at1 = 0
            for terms in (smalls, smalls_above):
                small_own[0][at0:at0 + rank, :] = terms[0][:rank, :]
                small_own[0][at0 + rank:at0 + rank + 1, :] = terms[1][...]
                small_own[1][at1:at1 + rank, :] = terms[2][:rank, :]
                for k in (3, 4):
                    small_own[1][at1 + rank + k - 3:at1 + rank + k - 2, :] = terms[k][...]
                small_own[1][at1 + rank + 2:at1 + rank + 3, :HV] = terms[5][...]
                at0, at1 = at0 + rank + 8, at1 + rank + 8
            hops = range(self.tensor - 1)

            def to_peer(hop):
                peer = {"tensor": lax.rem(lax.axis_index("tensor") + hop + 1, self.tensor)}
                return remote(small_own[1], shared.at[hop], peer_send.at[hop], peer_recv.at[hop], peer)

            for hop in hops:
                to_peer(hop).start()
            local(last_middle, middle, 20).start()
            for s in range(seqs):
                freed(s, (0, 1))
                local(of_seq(last_partial, s, length), partial.at[s], 8 + s).start()
            pump()
            for hop in hops:
                to_peer(hop).wait()
            small_own[1][...] += sum(shared[hop] for hop in hops)
            begin(self.small.steps(small_own, small_slots, small_sems, None, small_outs))
            for s in range(seqs):
                collect(s, None)
                local(gathered.at[s], of_seq(out_input, s, length), 21 + s).start()
                pump()
            local(last_middle, middle, 20).wait()
            for s in range(seqs):
                local(gathered.at[s], of_seq(out_input, s, length), 21 + s).wait()
                local(of_seq(last_partial, s, length), partial.at[s], 8 + s).wait()
                scatter(s)
                pump()
            for s in range(seqs):
                total = arrived(s)
                mine = pl.ds(s * own, own)
                core, cross, _, _ = ids()
                row = lax.broadcasted_iota(jnp.int32, (own, 1), 0) + (core * half + cross * own)
                publish(s, jnp.where(row < lengths[s], middle[mine, :] + total, 0.0).astype(bf).astype(f32))
                pump()
            for s in range(seqs):
                collect(s, grad)
                local(of_seq(grad, s, length), of_seq(out_layer, s, length), 21 + s).start()
                pump()
            for s in range(seqs):
                local(of_seq(grad, s, length), of_seq(out_layer, s, length), 21 + s).wait()
        while jobs:
            pump()
        for s in range(seqs):
            freed(s, range(5))


class Finish:
    def __init__(self, rows, width, mix_cols, hidden_units, rank):
        self.rank, self.width = rank, width
        self.cols = ((0, HK), (HK, HK), (2 * HK, HV), (2 * HK + HV, HV))
        f = lambda *shape: jax.ShapeDtypeStruct(shape, f32)
        self.big = [f(2, hidden_units, width)] * 3 + [f(2, width, size) for _, size in self.cols] + [f(2, HV, width), f(rows, width)]
        self.big += [jax.ShapeDtypeStruct((rows, width), bf)]
        self.small = [f(2, rank, HK), f(2, HK), f(2, rank, width), f(2, width), f(2, width), f(2, HV)]

    def call(self, ffn, mix, rows_out, local, shared):
        arrays = list(ffn) + list(mix) + list(rows_out)
        return pl.pallas_call(
            self.kernel, name="finish", in_specs=[ANY_SPEC] * len(arrays) + [VMEM_SPEC] * 2,
            out_specs=[ANY_SPEC] * len(self.big) + [VMEM_SPEC] * len(self.small), out_shape=self.big + self.small,
            scratch_shapes=[pltpu.VMEM(a.shape, a.dtype) for a in arrays] + [DMA((len(arrays),)), DMA((24,))],
            compiler_params=pltpu.CompilerParams(vmem_limit_bytes=60 << 20),
            cost_estimate=pl.CostEstimate(flops=10**6, bytes_accessed=64 * 10**6, transcendentals=0),
        )(*arrays, local, shared)

    def kernel(self, *refs):
        rank, width = self.rank, self.width
        ins, (local, shared), outs, small = refs[:12], refs[12:14], refs[14:24], refs[24:30]
        load, store = refs[-2:]
        held = refs[30:42]
        loads = [pltpu.make_async_copy(src, dst, load.at[k]) for k, (src, dst) in enumerate(zip(ins, held))]
        for step in loads:
            step.start()
        stores = []

        def put(src, dst):
            step = pltpu.make_async_copy(src, dst, store.at[len(stores)])
            step.start()
            stores.append(step)

        for l in range(2):
            for k in range(3):
                loads[3 * l + k].wait()
                put(held[3 * l + k], outs[k].at[l])
        for l in range(2):
            loads[6 + 2 * l].wait()
            for k, (start, size) in enumerate(self.cols):
                put(held[6 + 2 * l].at[:, pl.ds(start, size)], outs[3 + k].at[l])
            loads[7 + 2 * l].wait()
            put(held[7 + 2 * l], outs[7].at[l])
        for k in range(2):
            loads[10 + k].wait()
            put(held[10 + k], outs[8 + k])
        up, bias, down, attn, ffn_gain, group = small
        for l in range(2):
            at = l * (rank + 8)
            up[l] = local[at:at + rank, :]
            bias[l:l + 1, :] = local[at + rank:at + rank + 1, :]
            down[l] = shared[at:at + rank, :]
            attn[l:l + 1, :] = shared[at + rank:at + rank + 1, :]
            ffn_gain[l:l + 1, :] = shared[at + rank + 1:at + rank + 2, :]
            group[l:l + 1, :] = shared[at + rank + 2:at + rank + 3, :HV]
        for step in stores:
            step.wait()


def shards(
    groups, tensor, layer_input, seq_lengths, attn_gain, query_proj, key_proj, value_proj, gate_proj,
    decay_down, decay_up, decay_bias, group_gain, output_proj, ffn_gain, ffn_gate, ffn_up, ffn_down, cotangent,
):
    seqs, length, width = layer_input.shape
    depth = attn_gain.shape[0]
    rank = decay_down.shape[2]
    rows = seqs * length
    mix_cols = 2 * HK + 2 * HV
    hidden_units = ffn_gate.shape[2]
    assert groups % RING == 0
    ring = RING
    proj = (query_proj, key_proj, value_proj, gate_proj)
    decay = (decay_down.transpose(0, 2, 1), decay_up)
    ffn_ws = (ffn_gate.transpose(0, 2, 1), ffn_up.transpose(0, 2, 1), ffn_down)
    params = (attn_gain, ffn_gain, decay_bias, group_gain)
    found = Forward(depth, seqs, length, width, mix_cols, hidden_units).call(
        0, seq_lengths, params, layer_input.reshape(rows, width), cotangent.reshape(rows, width), proj, decay, output_proj, ffn_ws)
    kinds = 8
    acts = found[depth * kinds:]

    def backward(top, l, ffn_grad, resid, extra):
        normed, z, gated, mixed, scores, entry, middle, normed_ffn = found[l * kinds:(l + 1) * kinds]
        arrays = (normed_ffn, ffn_grad, resid, middle, entry, z, mixed, scores, gated, normed, *proj, *decay, output_proj, *ffn_ws)
        return Backward(top, l, ring, tensor, seqs, length, width, mix_cols, hidden_units, rank).call(1 + l, seq_lengths, params, arrays, extra)

    ffn_sums, mix_sums = [None] * depth, [None] * depth
    last_partial, ffn_grad, resid, *found_top = backward(True, 1, acts[0], found[kinds + 6], acts[1:])
    ffn_sums[1] = found_top[:3]
    extra = (*found_top[3:], last_partial, found[kinds + 6])
    input_grad, layer_output, *sums = backward(False, 0, ffn_grad, resid, extra)
    if groups > ring:
        found_sums = lax.psum(tuple(part * (1.0 / ring) for part in (*sums, *ffn_sums[1])), "dp")
        sums, ffn_sums[1] = found_sums[:-3], found_sums[-3:]
    ffn_sums[0], mix_sums[0], mix_sums[1], (local, shared) = sums[:3], sums[3:5], sums[5:7], sums[7:]

    done = Finish(rows, width, mix_cols, hidden_units, rank).call(
        (*ffn_sums[0], *ffn_sums[1]), (*mix_sums[0], *mix_sums[1]), (input_grad, layer_output), local, shared)
    gate, up, down, query, key, value, out_gate, head, input_grad, layer_output, d_up, d_bias, d_down, attn, ffn, group = done
    return (
        layer_output.reshape(seqs, length, width),
        input_grad.reshape(seqs, length, width),
        attn,
        query,
        key,
        value,
        out_gate,
        d_down.transpose(0, 2, 1),
        d_up,
        d_bias,
        group,
        head,
        ffn,
        gate.transpose(0, 2, 1),
        up.transpose(0, 2, 1),
        down,
    )


def solution(mesh):
    over, across = P("dp", None, None), P(None, None, "tensor")
    deep = P(None, "tensor", None)
    return jax.shard_map(
        functools.partial(shards, mesh.shape["dp"], mesh.shape["tensor"]),
        mesh=mesh,
        in_specs=(over, P("dp"), P(), across, across, across, across, P(), across, P(None, "tensor"), P(), deep, P(), across, across, deep, over),
        out_specs=(over, over, P(), across, across, across, across, P(), across, P(None, "tensor"), P(), deep, P(), across, across, deep),
        check_vma=False,
    )
```

```python
import functools
import jax, jax.numpy as jnp
from jax import lax
from jax.experimental import pallas as pl
from jax.experimental.pallas import tpu as pltpu
from jax.sharding import PartitionSpec as P
HK, HV, CH = 128, 256, 128
group_epsilon = 1e-05
bf, f32 = jnp.bfloat16, jnp.float32
SCALE = HK ** -0.5

def nn(a, b):
    return lax.dot_general(a, b, (((1,), (0,)), ((), ())), preferred_element_type=f32)
def nt(a, b):
    return lax.dot_general(a, b, (((1,), (1,)), ((), ())), preferred_element_type=f32)
def tn(a, b):
    return lax.dot_general(a, b, (((0,), (0,)), ((), ())), preferred_element_type=f32)

def halves(a):
    top = a.astype(bf)
    return top, (a - top.astype(f32)).astype(bf)

def thirds(a):
    top = a.astype(bf)
    return (top,) + halves(a - top.astype(f32))

def sigmoid(a):
    return 1.0 / (1.0 + jnp.exp(-a))

def log_sigmoid(a):
    return jnp.minimum(a, 0.0) - jnp.log1p(jnp.exp(-jnp.abs(a)))

def steps_below(n):
    out, h = [], 1
    while h < n:
        out.append(h)
        h *= 2
    return out

def decay_sums(ld):
    n = ld.shape[0]
    rows = lax.broadcasted_iota(jnp.int32, ld.shape, 0)
    total, pre, suf = ld, ld, jnp.zeros_like(ld)
    levels = []
    for h in steps_below(n):
        upper = (rows & h) != 0
        levels.append((h, upper, jnp.exp(jnp.where(upper, pre, suf))))
        below, above = pltpu.roll(total, h, 0), pltpu.roll(total, n - h, 0)
        pre = jnp.where(upper, pre + below, pre)
        suf = jnp.where(upper, suf, suf + above)
        total = total + jnp.where(upper, below, above)
    return levels, pre, suf, total

def tile_rows(c):
    return pl.ds(c * CH, CH)

def logits_of(z, up_ref, bias_ref):
    return sum(nn(piece, up_ref[...]) for piece in thirds(z[:, 2 * HK + 2 * HV:])) + bias_ref[...]

def wide_levels(chunks):
    out, h = [], 1
    while h < chunks:
        for base in range(0, chunks, 2 * h):
            out.append((tuple(range(base, base + h)), tuple(range(base + h, base + 2 * h))))
        h *= 2
    return out

def wide_factor(c, group, is_upper, pre, suf, tot):
    arg = pre[tile_rows(c), :] if is_upper else suf[tile_rows(c), :]
    for o in group:
        if (o < c) if is_upper else (o > c):
            arg = arg + tot[pl.ds(o * 8, 1), :]
    return jnp.exp(arg)

def mixer_forward(z_ref, up_ref, bias_ref, gain_ref, gated_ref, mixed_ref, scores_ref, pre, suf, tot):
    chunks = z_ref.shape[0] // CH
    i = lax.broadcasted_iota(jnp.int32, (CH, CH), 0)
    j = lax.broadcasted_iota(jnp.int32, (CH, CH), 1)
    apart = i ^ j
    scores_ref[...] = jnp.zeros_like(scores_ref)
    for c in range(chunks):
        z = z_ref[tile_rows(c), :]
        q, k = z[:, :HK].astype(bf), z[:, HK:2 * HK].astype(bf)
        ld = log_sigmoid(logits_of(z, up_ref, bias_ref)) / 16.0
        levels, p, s, t = decay_sums(ld)
        pre[tile_rows(c), :], suf[tile_rows(c), :], tot[pl.ds(c * 8, 8), :] = p, s, t[:8]
        tile = nt(q, k)
        qf, kf = q.astype(f32), k.astype(f32)
        for h, upper, factor in levels:
            rows = (jnp.where(upper, qf, kf) * factor).astype(bf)
            tile = jnp.where(apart >= h, nt(rows, rows), tile)
        scores_ref[tile_rows(c), tile_rows(c)] = jnp.where(i >= j, tile * SCALE, 0.0).astype(bf)
    for low_group, up_group in wide_levels(chunks):
        q_rows = [(z_ref[tile_rows(c), :HK].astype(bf).astype(f32) * wide_factor(c, up_group, True, pre, suf, tot)).astype(bf) for c in up_group]
        k_rows = [(z_ref[tile_rows(c), HK:2 * HK].astype(bf).astype(f32) * wide_factor(c, low_group, False, pre, suf, tot)).astype(bf) for c in low_group]
        for a, c in enumerate(up_group):
            for b, o in enumerate(low_group):
                scores_ref[tile_rows(c), tile_rows(o)] = (nt(q_rows[a], k_rows[b]) * SCALE).astype(bf)
    for c in range(chunks):
        width = (c + 1) * CH
        mixed = nn(scores_ref[tile_rows(c), :width], z_ref[:width, 2 * HK:2 * HK + HV].astype(bf))
        mixed_ref[tile_rows(c), :] = mixed
        out_gate = z_ref[tile_rows(c), 2 * HK + HV:2 * HK + 2 * HV]
        normed = mixed * lax.rsqrt(jnp.mean(mixed * mixed, axis=-1, keepdims=True) + group_epsilon) * gain_ref[...]
        gated_ref[tile_rows(c), :] = (normed * out_gate * sigmoid(out_gate)).astype(bf)

def mixer_backward(fresh, z_ref, up_ref, bias_ref, gain_ref, mixed_ref, scores_ref, grad_ref,
                   out_ref, up_out, bias_out, gain_out, pre, suf, tot, dm_ref, dq_ref, dk_ref, flow):
    chunks = z_ref.shape[0] // CH
    i = lax.broadcasted_iota(jnp.int32, (CH, CH), 0)
    j = lax.broadcasted_iota(jnp.int32, (CH, CH), 1)
    apart = i ^ j
    rows_in = lax.broadcasted_iota(jnp.int32, (CH, HK), 0)

    if fresh:
        up_out[...] = jnp.zeros_like(up_out)
        bias_out[...] = jnp.zeros_like(bias_out)
        gain_out[...] = jnp.zeros_like(gain_out)
    for c in range(chunks):
        mixed, e = mixed_ref[tile_rows(c), :], grad_ref[tile_rows(c), :]
        g = z_ref[tile_rows(c), 2 * HK + HV:2 * HK + 2 * HV]
        r = lax.rsqrt(jnp.mean(mixed * mixed, axis=-1, keepdims=True) + group_epsilon)
        sig = sigmoid(g)
        unit = mixed * r
        out_ref[tile_rows(c), 2 * HK + HV:2 * HK + 2 * HV] = (e * unit * gain_ref[...] * (sig + g * sig * (1.0 - sig))).astype(bf)
        upstream = e * g * sig
        gain_out[...] += jnp.sum(upstream * unit, axis=0, keepdims=True)
        weighted = upstream * gain_ref[...]
        dm_ref[tile_rows(c), :] = (r * (weighted - unit * jnp.mean(unit * weighted, axis=-1, keepdims=True))).astype(bf)

    def score_grad(c, o):
        return nt(dm_ref[tile_rows(c), :], z_ref[tile_rows(o), 2 * HK:2 * HK + HV].astype(bf)) * SCALE

    for c in range(chunks):
        z = z_ref[tile_rows(c), :]
        q, k = z[:, :HK].astype(bf).astype(f32), z[:, HK:2 * HK].astype(bf).astype(f32)
        ld = log_sigmoid(logits_of(z, up_ref, bias_ref)) / 16.0
        levels, p, s, t = decay_sums(ld)
        pre[tile_rows(c), :], suf[tile_rows(c), :], tot[pl.ds(c * 8, 8), :] = p, s, t[:8]
        ds = score_grad(c, c)
        diagonal = jnp.sum(jnp.where(i == j, ds, 0.0), axis=-1, keepdims=True)
        ds = jnp.where(i > j, ds, 0.0)
        both = ds + ds.T
        dq, dk = diagonal * k, diagonal * q
        fl = jnp.zeros_like(dq)
        for h, upper, factor in levels:
            rows = (jnp.where(upper, q, k) * factor).astype(bf)
            near = jnp.where((apart >= h) & (apart < 2 * h), both, 0.0).astype(bf)
            back = nn(near, rows)
            part = back * factor
            dq, dk = dq + jnp.where(upper, part, 0.0), dk + jnp.where(upper, 0.0, part)
            moved = back * rows.astype(f32)
            fl = fl + jnp.where(upper, moved, -moved)
        dq_ref[tile_rows(c), :], dk_ref[tile_rows(c), :], flow[tile_rows(c), :] = dq, dk, fl
    for low_group, up_group in wide_levels(chunks):
        q_fac = [wide_factor(c, up_group, True, pre, suf, tot) for c in up_group]
        k_fac = [wide_factor(c, low_group, False, pre, suf, tot) for c in low_group]
        q_rows = [(z_ref[tile_rows(c), :HK].astype(bf).astype(f32) * f).astype(bf) for c, f in zip(up_group, q_fac)]
        k_rows = [(z_ref[tile_rows(c), HK:2 * HK].astype(bf).astype(f32) * f).astype(bf) for c, f in zip(low_group, k_fac)]
        grads = [[score_grad(c, o).astype(bf) for o in low_group] for c in up_group]
        for a, c in enumerate(up_group):
            back = sum(nn(grads[a][b], k_rows[b]) for b in range(len(low_group)))
            dq_ref[tile_rows(c), :] += back * q_fac[a]
            flow[tile_rows(c), :] += back * q_rows[a].astype(f32)
        for b, o in enumerate(low_group):
            back = sum(tn(grads[a][b], q_rows[a]) for a in range(len(up_group)))
            dk_ref[tile_rows(o), :] += back * k_fac[b]
            flow[tile_rows(o), :] -= back * k_rows[b].astype(f32)
    later = jnp.zeros((1, HK), f32)
    for c in reversed(range(chunks)):
        out_ref[tile_rows(c), :HK] = dq_ref[tile_rows(c), :].astype(bf)
        out_ref[tile_rows(c), HK:2 * HK] = dk_ref[tile_rows(c), :].astype(bf)
        out_ref[tile_rows(c), 2 * HK:2 * HK + HV] = tn(scores_ref[pl.ds(c * CH, (chunks - c) * CH), tile_rows(c)], dm_ref[pl.ds(c * CH, (chunks - c) * CH), :]).astype(bf)
        fl = flow[tile_rows(c), :]
        for h in steps_below(CH):
            fl = fl + jnp.where(rows_in < CH - h, pltpu.roll(fl, CH - h, 0), 0.0)
        fl = fl + later
        later = fl[:1]
        z = z_ref[tile_rows(c), :]
        logits = logits_of(z, up_ref, bias_ref)
        d_logit = fl * sigmoid(-logits) / 16.0
        bias_out[...] += jnp.sum(d_logit, axis=0, keepdims=True)
        d1, d2 = halves(d_logit)
        l1, l2 = halves(z[:, 2 * HK + 2 * HV:])
        up_out[...] += tn(l1, d1) + tn(l1, d2) + tn(l2, d1)
        out_ref[tile_rows(c), 2 * HK + 2 * HV:] = (nt(d1, up_ref[...]) + nt(d2, up_ref[...])).astype(bf)


norm_epsilon = 1e-06
MESH = pl.DeviceIdType.MESH
VMEM_SPEC = pl.BlockSpec(memory_space=pltpu.VMEM)
ANY_SPEC = pl.BlockSpec(memory_space=pl.ANY)
DMA = pltpu.SemaphoreType.DMA
RING = 8


def peer_of(index, bit):
    return jnp.where((index // bit) % 2 == 0, index + bit, index - bit)


def rms_unit(h):
    return lax.rsqrt(jnp.mean(h * h, axis=-1, keepdims=True) + norm_epsilon)


def remote(src, dst, send, recv, peer):
    return pltpu.make_async_remote_copy(
        src_ref=src, dst_ref=dst, send_sem=send, recv_sem=recv, device_id=peer, device_id_type=MESH
    )


def ring_place(n):
    index = lax.rem(lax.axis_index("dp"), n)
    return jnp.where(index % 2 == 0, index // 2, n - 1 - index // 2)


def ring_peer(ahead, n):
    place = lax.rem(ring_place(n) + ahead, n)
    index = lax.axis_index("dp")
    return {"dp": index - lax.rem(index, n) + jnp.where(place < n // 2, 2 * place, 2 * (n - 1 - place) + 1)}


def ring_cut(shape, n):
    rows, cols = shape
    if rows % (16 * n) == 0:
        return rows // (2 * n), cols, True
    if rows % (8 * n) == 0 and cols % 256 == 0:
        return rows // n, cols // 2, False
    return None


def tiles(total, size):
    return [(start, min(size, total - start)) for start in range(0, total, size)]


def raw_weights(l, proj, cat, decay_down, down_w, decay_up, up_w, heads, head_w):
    moves, at = [], 0
    for w in proj:
        size = w.shape[2]
        moves.append((w.at[l], cat.at[:, pl.ds(at, size)]))
        at += size
    rank = decay_down.shape[1]
    return moves + [(decay_down.at[l], down_w.at[pl.ds(0, rank)]), (decay_up.at[l], up_w.at[pl.ds(0, rank)]), (heads.at[l], head_w)]


def ffn_tile(here, cols, rows_in, grad, gate_w, up_w, down_w, inner, gate_low, up_low):
    gate_act, up_act = nt(rows_in[here, :], gate_w[cols, :]), nt(rows_in[here, :], up_w[cols, :])
    inner_grad = nt(grad[here, :], down_w[cols, :])
    sig = sigmoid(gate_act)
    swish = gate_act * sig
    inner[here, cols] = (swish * up_act).astype(bf)
    gate_low[here, cols] = (inner_grad * up_act * sig * (1.0 + gate_act * (1.0 - sig))).astype(bf)
    up_low[here, cols] = (inner_grad * swish).astype(bf)


class Forward:
    def __init__(self, depth, seqs, length, width, mix_cols, hidden_units):
        self.depth, self.seqs, self.length, self.width = depth, seqs, length, width
        self.mix_cols, self.z_cols, self.hidden_units = mix_cols, mix_cols + 128, hidden_units
        rows, quarter = seqs * length, seqs * length // 4
        self.saved = []
        for _ in range(depth):
            self.saved += [
                ((rows, width), bf), ((rows, self.z_cols), f32), ((rows, HV), bf), ((rows, HV), f32), ((rows, length), bf),
                ((quarter, width), f32), ((quarter, width), f32), ((rows, width), bf),
            ]
        self.saved += [((rows, width), bf)] + [((rows, hidden_units), bf)] * 3

    def call(self, collective, lengths, params, x, cotangent, proj, decay, heads, ffn_ws):
        depth, seqs, length, width = self.depth, self.seqs, self.length, self.width
        own = length // 4
        saved = [jax.ShapeDtypeStruct(shape, kind) for shape, kind in self.saved]
        scratch = [pltpu.VMEM(shape, kind) for shape, kind in self.saved]
        scratch += [pltpu.VMEM(x.shape, bf)]
        scratch += [pltpu.VMEM((width, self.mix_cols), bf), pltpu.VMEM((128, width), bf), pltpu.VMEM((128, HK), bf), pltpu.VMEM((HV, width), bf)] * depth
        scratch += [pltpu.VMEM((self.hidden_units, width), bf)] * 3
        scratch += [
            pltpu.VMEM((seqs, length, width), f32), pltpu.VMEM((seqs, 2 * own, width), f32), pltpu.VMEM((seqs, own, width), f32),
            pltpu.VMEM((seqs, length, width), f32),
            pltpu.VMEM((length, HK), f32), pltpu.VMEM((length, HK), f32), pltpu.VMEM((length // CH * 8, HK), f32),
            DMA((len(saved), seqs)), DMA((7 * depth + 8,)), DMA((5, seqs)), DMA((5, seqs)),
        ]
        smem = pl.BlockSpec(memory_space=pltpu.SMEM)
        arrays = (x, cotangent, *proj, *decay, heads, *ffn_ws)
        return pl.pallas_call(
            self.kernel, name="forward_blocks",
            in_specs=[smem] + [VMEM_SPEC] * len(params) + [ANY_SPEC] * len(arrays), out_specs=[ANY_SPEC] * len(saved), out_shape=saved,
            scratch_shapes=scratch,
            compiler_params=pltpu.CompilerParams(collective_id=collective, has_side_effects=True, vmem_limit_bytes=61 << 20),
            cost_estimate=pl.CostEstimate(flops=10**10, bytes_accessed=2 * 10**8, transcendentals=0),
        )(lengths, *params, *arrays)

    def kernel(self, *refs):
        depth, seqs, length = self.depth, self.seqs, self.length
        half, own = length // 2, length // 4
        kinds = 8
        refs = list(refs)

        def take(count):
            found = refs[:count]
            del refs[:count]
            return found

        lengths, gains, ffn_gains, bias, group = take(5)
        x_in, cotangent = take(2)
        proj, (decay_down, decay_up), heads, ffn_ws = take(4), take(2), take(1)[0], take(3)
        outs = take(len(self.saved))
        kept_for_later = take(len(self.saved))
        x = take(1)[0]
        mixer_w = [take(4) for _ in range(depth)]
        gate_w, up_w, down_w = take(3)
        partial, first, second, gathered, pre, suf, tot, store, load, send, recv = take(11)
        grad, inner, gate_low, up_low = kept_for_later[depth * kinds:]
        me = lax.axis_index("tensor")
        core, cross = me % 2, me // 2
        core_peer, cross_peer = {"tensor": peer_of(me, 1)}, {"tensor": peer_of(me, 2)}

        def local(src, dst, k):
            return pltpu.make_async_copy(src, dst, load.at[k])

        def of_seq(ref, s, height):
            return ref.at[pl.ds(s * height, height)]

        x_loads = [local(of_seq(x_in, s, length), of_seq(x, s, length), s) for s in range(seqs)]
        mixer_loads = []
        for l in range(depth):
            cat, low_w, up_map, head_w = mixer_w[l]
            moves = raw_weights(l, proj, cat, decay_down, low_w, decay_up, up_map, heads, head_w)
            mixer_loads.append([local(src, dst, 8 + 7 * l + k) for k, (src, dst) in enumerate(moves)])

        def ffn_loads(l):
            return [local(src.at[l], dst, 2 + k) for k, (src, dst) in enumerate(zip(ffn_ws, (gate_w, up_w, down_w)))]

        grad_load = local(cotangent, grad, 5)
        for l in range(depth):
            mixer_w[l][1][...] = jnp.zeros_like(mixer_w[l][1])
            mixer_w[l][2][...] = jnp.zeros_like(mixer_w[l][2])
        for step in x_loads[:1] + mixer_loads[0] + x_loads[1:] + ffn_loads(0) + [step for loads in mixer_loads[1:] for step in loads] + [grad_load]:
            step.start()
        barrier = pltpu.get_barrier_semaphore()
        for peer in (core_peer, cross_peer):
            pl.semaphore_signal(barrier, inc=1, device_id=peer, device_id_type=MESH)
        pl.semaphore_wait(barrier, 2)
        sent, stores = {}, []

        def copy(src, dst, stage, s, peer):
            step = remote(src, dst, send.at[stage, s], recv.at[stage, s], peer)
            step.start()
            sent[stage, s] = step

        def freed(s, stages):
            for stage in stages:
                if (stage, s) in sent:
                    sent.pop((stage, s)).wait_send()

        def piece(c, x_half, size):
            return pl.ds(pl.multiple_of(c * half + x_half * own, own), size)

        def keep_for_later(k, s):
            height = self.saved[k][0][0] // seqs
            step = pltpu.make_async_copy(of_seq(kept_for_later[k], s, height), of_seq(outs[k], s, height), store.at[k, s])
            step.start()
            stores.append(step)

        def scatter(s):
            copy(partial.at[s, piece(1 - core, 0, half)], first.at[s], 0, s, core_peer)
            sent[0, s].wait_recv()
            freed(s, (2, 3, 4))
            partial[s, piece(core, 1 - cross, own), :] += first[s, piece(0, 1 - cross, own), :]
            copy(partial.at[s, piece(core, 1 - cross, own)], second.at[s], 1, s, cross_peer)
            partial[s, piece(core, cross, own), :] += first[s, piece(0, cross, own), :]

        def settle(s, resid, new_resid, gain):
            sent[1, s].wait_recv()
            mine = pl.ds(s * own, own)
            new = resid[mine, :] + (partial[s, piece(core, cross, own), :] + second[s])
            new_resid[mine, :] = new
            gathered[s, piece(core, cross, own), :] = (new * rms_unit(new) * gain).astype(bf).astype(f32)
            block = gathered.at[s, piece(core, cross, own)]
            copy(block, block, 2, s, cross_peer)
            copy(block, block, 3, s, core_peer)

        def collect(s, dest):
            sent[2, s].wait_recv()
            block = gathered.at[s, piece(core, 1 - cross, own)]
            copy(block, block, 4, s, core_peer)
            dest[pl.ds(pl.multiple_of(s * length + core * half, half), half), :] = gathered[s, piece(core, 0, half), :].astype(bf)
            sent[3, s].wait_recv()
            sent[4, s].wait_recv()
            dest[pl.ds(pl.multiple_of(s * length + (1 - core) * half, half), half), :] = gathered[s, piece(1 - core, 0, half), :].astype(bf)

        def rows_of(s):
            return pl.ds(s * length, length)

        for l in range(depth):
            normed, z, gated, mixed, scores, entry, middle, normed_ffn = kept_for_later[l * kinds:(l + 1) * kinds]
            cat, low_w, up_map, head_w = mixer_w[l]
            for s in range(seqs):
                if l == 0:
                    x_loads[s].wait()
                    for part in range(4):
                        block = pl.ds(s * length + part * own, own)
                        h = x[block, :].astype(f32)
                        normed[block, :] = (h * rms_unit(h) * gains[l:l + 1, :]).astype(bf)
                    entry[pl.ds(s * own, own), :] = x[pl.ds(pl.multiple_of(s * length + core * half + cross * own, own), own), :].astype(f32)
                else:
                    collect(s, normed)
                if s == 0:
                    for step in mixer_loads[l]:
                        step.wait()
                keep_for_later(l * kinds, s)
                for start, size in tiles(self.mix_cols, 256):
                    cols = pl.ds(start, size)
                    z[rows_of(s), cols] = nn(normed[rows_of(s), :], cat[:, cols])
                z[rows_of(s), pl.ds(self.mix_cols, 128)] = nt(normed[rows_of(s), :], low_w[...])
                keep_for_later(l * kinds + 1, s)
                mixer_forward(
                    of_seq(z, s, length), up_map, bias.at[pl.ds(l, 1)], group.at[pl.ds(l, 1)], of_seq(gated, s, length),
                    of_seq(mixed, s, length), of_seq(scores, s, length), pre, suf, tot)
                for k in (2, 3, 4):
                    keep_for_later(l * kinds + k, s)
                freed(s, (0, 1))
                for start, size in tiles(self.width, 256):
                    cols = pl.ds(start, size)
                    partial[s, :, cols] = nn(gated[rows_of(s), :], head_w[:, cols])
                scatter(s)
            for s in range(seqs):
                settle(s, entry, middle, ffn_gains[l:l + 1, :])
                keep_for_later(l * kinds + 5, s)
                keep_for_later(l * kinds + 6, s)
            if l + 1 == depth:
                break
            for s in range(seqs):
                collect(s, normed_ffn)
                keep_for_later(l * kinds + 7, s)
                if s == 0:
                    for step in ffn_loads(l):
                        step.wait()
                for start, size in tiles(self.hidden_units, 256):
                    cols = pl.ds(start, size)
                    gate_act = nt(normed_ffn[rows_of(s), :], gate_w[cols, :])
                    up_act = nt(normed_ffn[rows_of(s), :], up_w[cols, :])
                    inner[rows_of(s), cols] = (gate_act * sigmoid(gate_act) * up_act).astype(bf)
                freed(s, (0, 1))
                for start, size in tiles(self.width, 256):
                    cols = pl.ds(start, size)
                    partial[s, :, cols] = nn(inner[rows_of(s), :], down_w[:, cols])
                if s + 1 == seqs:
                    for step in ffn_loads(l + 1):
                        step.start()
                scatter(s)
            for s in range(seqs):
                settle(s, middle, kept_for_later[(l + 1) * kinds + 5], gains[l + 1:l + 2, :])
        grad_load.wait()
        for s in range(seqs):
            kept = lax.broadcasted_iota(jnp.int32, (length, 1), 0) < lengths[s]
            grad[rows_of(s), :] = jnp.where(kept, grad[rows_of(s), :].astype(f32), 0.0).astype(bf)
            keep_for_later(depth * kinds, s)
        normed_ffn = kept_for_later[(depth - 1) * kinds + 7]
        for step in ffn_loads(depth - 1):
            step.wait()
        for s in range(seqs):
            collect(s, normed_ffn)
            keep_for_later((depth - 1) * kinds + 7, s)
            for start, size in tiles(self.hidden_units, 256):
                ffn_tile(rows_of(s), pl.ds(start, size), normed_ffn, grad, gate_w, up_w, down_w, inner, gate_low, up_low)
            for k in range(3):
                keep_for_later(depth * kinds + 1 + k, s)
        for s in range(seqs):
            freed(s, range(5))
        for step in stores:
            step.wait()


class RingJob:
    def __init__(self, n, shapes, reduce, gather):
        self.n, self.shapes, self.reduce, self.gather = n, shapes, reduce, gather
        self.cuts = [ring_cut(shape, n) for shape in shapes]
        self.pairs = [(a, way) for a in range(len(shapes)) for way in range(2)]

    def slots(self):
        return [pltpu.VMEM((2, self.n - 1, rows, cols), f32) for rows, cols, _ in self.cuts] if self.reduce else []

    def sems(self):
        each = DMA((self.n - 1, len(self.shapes), 2))
        return [each, each] * (self.reduce + self.gather) + ([DMA((len(self.shapes), 2))] if self.gather else [])

    def pieces(self):
        return [jax.ShapeDtypeStruct((2, rows, cols), f32) for rows, cols, _ in self.cuts]

    def full(self):
        return [jax.ShapeDtypeStruct(shape, f32) for shape in self.shapes]

    def segment(self, a, way, back):
        n = self.n
        place = ring_place(n)
        index = lax.rem((place if way == 0 else n - 1 - place) + (2 * n - back), n)
        rows, cols, by_rows = self.cuts[a]
        if by_rows:
            return (pl.ds(pl.multiple_of((index * 2 + way) * rows, rows), rows), pl.ds(0, cols))
        return (pl.ds(pl.multiple_of(index * rows, rows), rows), pl.ds(way * cols, cols))

    def hop(self, src, dst, sems, step, a, way):
        peer = ring_peer(1 if way == 0 else self.n - 1, self.n)
        return remote(src, dst, sems[0].at[step, a, way], sems[1].at[step, a, way], peer)

    def steps(self, own, slots, sems, pieces, outs):
        n = self.n
        if self.reduce:
            rs, sems = sems[:2], sems[2:]
            for a, way in self.pairs:
                self.hop(own[a].at[self.segment(a, way, 0)], slots[a].at[way, 0], rs, 0, a, way).start()
            for step in range(n - 1):
                yield
                for a, way in self.pairs:
                    slot = slots[a].at[way, step]
                    self.hop(slot, slot, rs, step, a, way).wait_recv()
                    self.add(a, way, slot, own[a], slot if self.gather or step < n - 2 else pieces[a].at[way], step + 1)
                    if step < n - 2:
                        self.hop(slot, slots[a].at[way, step + 1], rs, step + 1, a, way).start()
                    elif self.gather:
                        self.begin(a, way, slot, sems, outs)
        else:
            for a, way in self.pairs:
                self.begin(a, way, pieces[a].at[way], sems, outs)
        if self.gather:
            for step in range(n - 1):
                yield
                for a, way in self.pairs:
                    piece = outs[a].at[self.segment(a, way, step)]
                    self.hop(piece, piece, sems, step, a, way).wait_recv()
                    if step < n - 2:
                        self.hop(piece, piece, sems, step + 1, a, way).start()
            for a, way in self.pairs:
                end = slots[a].at[way, n - 2] if self.reduce else pieces[a].at[way]
                pltpu.make_async_copy(end, outs[a].at[self.segment(a, way, n - 1)], sems[2].at[a, way]).wait()
        for step in range(n - 1):
            for a, way in self.pairs:
                if self.reduce:
                    self.hop(slots[a].at[way, 0], slots[a].at[way, 0], rs, step, a, way).wait_send()
                if self.gather:
                    piece = outs[a].at[self.segment(a, way, 0)]
                    self.hop(piece, piece, sems, step, a, way).wait_send()

    def begin(self, a, way, piece, sems, outs):
        place = outs[a].at[self.segment(a, way, self.n - 1)]
        self.hop(piece, place, sems, 0, a, way).start()
        pltpu.make_async_copy(piece, place, sems[2].at[a, way]).start()

    def add(self, a, way, slot, own, out, back):
        row_ds, col_ds = self.segment(a, way, back)

        @pl.loop(0, self.cuts[a][0] // 8)
        def _(block):
            here = pl.ds(pl.multiple_of(block * 8, 8), 8)
            there = pl.ds(pl.multiple_of(row_ds.start + block * 8, 8), 8)
            out[here, :] = slot[here, :] + own[there, col_ds]


ROUNDS = 13
TREES = (
    (0, ((0, 5, 7), (1, 7, 6), (2, 3, 1), (3, 6, 4), (4, 4, 2), (5, 2, 0), (8, 1, 0))),
    (0, ((0, 7, 6), (1, 5, 3), (1, 6, 4), (2, 3, 2), (2, 4, 2), (3, 2, 0), (7, 1, 0))),
    (0, ((1, 5, 7), (2, 7, 6), (4, 6, 4), (5, 4, 2), (6, 2, 0), (7, 3, 1), (9, 1, 0))),
    (0, ((4, 4, 6), (6, 6, 7), (8, 7, 5), (9, 5, 3), (10, 3, 2), (11, 2, 0), (12, 1, 0))),
    (0, ((4, 7, 6), (5, 6, 4), (7, 4, 5), (8, 5, 3), (10, 3, 1), (11, 1, 0), (12, 2, 0))),
    (0, ((5, 6, 7), (6, 4, 2), (6, 7, 5), (7, 5, 3), (8, 3, 1), (9, 2, 0), (10, 1, 0))),
    (2, ((0, 7, 5), (2, 6, 4), (3, 1, 0), (3, 3, 5), (7, 0, 2), (8, 5, 4), (11, 4, 2))),
    (2, ((9, 7, 5), (10, 6, 4), (11, 1, 3), (11, 5, 4), (12, 0, 2), (12, 3, 2), (12, 4, 2))),
)

SHARDS = 4 * len(TREES)
WAYS = ("across", "up", "down")


def mirrored(place, image):
    return (place ^ 1 if image & 1 else place) ^ (6 if image & 2 else 0)


def way_of(src, dst):
    return 0 if dst == src ^ 1 else (1 if dst == src + 2 else 2)


def hop_tables():
    blank = lambda: [[[-1] * 8 for _ in WAYS] for _ in range(ROUNDS)]
    sends, arrives, slot_there, slot_here, back_sends, back_owned, back_arrives = (blank() for _ in range(7))
    owned, hops = [[] for _ in range(8)], []
    for t, (root, tree) in enumerate(TREES):
        for image in range(4):
            shard = 4 * t + image
            owner = mirrored(root, image)
            owned[owner].append(shard)
            for when, src, dst in tree:
                hops.append((when, mirrored(src, image), mirrored(dst, image), shard, owner))
    used = [0] * 8
    for when, src, dst, shard, owner in sorted(hops):
        way = way_of(src, dst)
        assert sends[when][way][src] < 0
        sends[when][way][src] = arrives[when][way][dst] = shard
        slot_there[when][way][src] = slot_here[when][way][dst] = used[dst]
        used[dst] += 1
        later, back = ROUNDS - 1 - when, way_of(dst, src)
        back_sends[later][back][dst] = back_arrives[later][back][src] = shard
        back_owned[later][back][dst] = int(dst == owner)
    return sends, arrives, slot_there, slot_here, back_sends, back_owned, back_arrives, owned, max(used)


SENDS, ARRIVES, SLOT_THERE, SLOT_HERE, BACK_SENDS, BACK_OWNED, BACK_ARRIVES, OWNED, SLOTS = hop_tables()
MOST_OWNED = max(len(shards_of) for shards_of in OWNED)


def block_place():
    return lax.rem(lax.axis_index("dp"), RING)


def look_up(row):
    place = block_place()
    found = jnp.int32(-1)
    for p, value in enumerate(row):
        if value != -1:
            found = jnp.where(place == p, jnp.int32(value), found)
    return found


def block_peer(way):
    place = block_place()
    step = (jnp.where(place % 2 == 0, 1, -1), 2, -2)[way]
    return {"dp": lax.axis_index("dp") + step}


def shard_cut(shape):
    rows, cols = shape
    if rows % (8 * SHARDS) == 0:
        return rows // SHARDS, cols, 1
    assert rows * 4 % (8 * SHARDS) == 0 and cols % 512 == 0
    return rows * 4 // SHARDS, cols // 4, 4


class BlockSum:
    def __init__(self, shapes, reduce, gather):
        self.shapes, self.reduce, self.gather = shapes, reduce, gather
        self.cuts = [shard_cut(shape) for shape in shapes]

    def slots(self):
        return [pltpu.VMEM((SLOTS, rows, cols), f32) for rows, cols, _ in self.cuts] if self.reduce else []

    def sems(self):
        each = DMA((ROUNDS, len(WAYS), len(self.shapes)))
        return [each, each] * (self.reduce + self.gather) + ([DMA((MOST_OWNED, len(self.shapes)))] if self.gather else [])

    def full(self):
        return [jax.ShapeDtypeStruct(shape, f32) for shape in self.shapes]

    def segment(self, a, shard):
        rows, cols, beside = self.cuts[a]
        if beside == 1:
            return (pl.ds(pl.multiple_of(shard * rows, rows), rows), pl.ds(0, cols))
        return (pl.ds(pl.multiple_of(shard // beside * rows, rows), rows), pl.ds(pl.multiple_of(shard % beside * cols, cols), cols))

    def hop(self, src, dst, sems, step, way, a):
        return remote(src, dst, sems[0].at[step, way, a], sems[1].at[step, way, a], block_peer(way))

    def arrays(self):
        return range(len(self.shapes))

    def steps(self, own, slots, sems, pieces, outs):
        rs = sems[:2] if self.reduce else None
        ag = sems[2 * self.reduce:] if self.gather else None
        if self.reduce:
            for a in self.arrays():
                self.send(own, slots, rs, 0, a)
            for step in range(ROUNDS):
                yield
                for a in self.arrays():
                    self.receive(own, slots, rs, step, a)
                    if step + 1 < ROUNDS:
                        self.send(own, slots, rs, step + 1, a)
        if self.gather:
            for k in range(MOST_OWNED):
                shard = look_up([shards_of[k] if k < len(shards_of) else -1 for shards_of in OWNED])

                @pl.when(shard >= 0)
                def _():
                    for a in self.arrays():
                        here = self.segment(a, shard)
                        pltpu.make_async_copy(own[a].at[here], outs[a].at[here], ag[2].at[k, a]).start()
            for a in self.arrays():
                self.send_back(own, outs, ag, 0, a)
            for step in range(ROUNDS):
                yield
                for a in self.arrays():
                    self.receive_back(outs, ag, step, a)
                    if step + 1 < ROUNDS:
                        self.send_back(own, outs, ag, step + 1, a)
            for k in range(MOST_OWNED):
                shard = look_up([shards_of[k] if k < len(shards_of) else -1 for shards_of in OWNED])

                @pl.when(shard >= 0)
                def _():
                    for a in self.arrays():
                        here = self.segment(a, shard)
                        pltpu.make_async_copy(own[a].at[here], outs[a].at[here], ag[2].at[k, a]).wait()
        for table, pair in ((SENDS, rs), (BACK_SENDS, ag)):
            for step in range(ROUNDS if pair else 0):
                for way in range(len(WAYS)):
                    shard = look_up(table[step][way])

                    @pl.when(shard >= 0)
                    def _():
                        for a in self.arrays():
                            piece = own[a].at[self.segment(a, shard)]
                            self.hop(piece, piece, pair, step, way, a).wait_send()

    def send(self, own, slots, sems, step, a):
        for way in range(len(WAYS)):
            shard, there = look_up(SENDS[step][way]), look_up(SLOT_THERE[step][way])

            @pl.when(shard >= 0)
            def _():
                self.hop(own[a].at[self.segment(a, shard)], slots[a].at[there], sems, step, way, a).start()

    def receive(self, own, slots, sems, step, a):
        for way in range(len(WAYS)):
            shard, here = look_up(ARRIVES[step][way]), look_up(SLOT_HERE[step][way])

            @pl.when(shard >= 0)
            def _():
                slot = slots[a].at[here]
                self.hop(slot, slot, sems, step, way, a).wait_recv()
                row_ds, col_ds = self.segment(a, shard)

                @pl.loop(0, self.cuts[a][0] // 8)
                def _(block):
                    rows = pl.ds(pl.multiple_of(row_ds.start + block * 8, 8), 8)
                    own[a][rows, col_ds] += slots[a][here, pl.ds(pl.multiple_of(block * 8, 8), 8), :]

    def send_back(self, own, outs, sems, step, a):
        for way in range(len(WAYS)):
            shard, mine = look_up(BACK_SENDS[step][way]), look_up(BACK_OWNED[step][way])
            for source, holds in ((own, 1), (outs, 0)):
                if any(entry == holds for entry in BACK_OWNED[step][way]):
                    @pl.when(jnp.logical_and(shard >= 0, mine == holds))
                    def _():
                        here = self.segment(a, shard)
                        self.hop(source[a].at[here], outs[a].at[here], sems, step, way, a).start()

    def receive_back(self, outs, sems, step, a):
        for way in range(len(WAYS)):
            shard = look_up(BACK_ARRIVES[step][way])

            @pl.when(shard >= 0)
            def _():
                piece = outs[a].at[self.segment(a, shard)]
                self.hop(piece, piece, sems, step, way, a).wait_recv()


class HalvingSum:
    def __init__(self, shapes):
        self.shapes = shapes

    def slots(self):
        return [pltpu.VMEM((shape[0] - shape[0] // 8, shape[1]), f32) for shape in self.shapes]

    def sems(self):
        each = DMA((6, len(self.shapes)))
        return [each, each, DMA((len(self.shapes),))]

    def full(self):
        return [jax.ShapeDtypeStruct(shape, f32) for shape in self.shapes]

    def block(self, a, level, other):
        place, start, size = block_place(), 0, self.shapes[a][0]
        for k in range(level):
            size //= 2
            bit = place // (1, 2, 4)[k] % 2
            start = start + (1 - bit if other and k == level - 1 else bit) * size
        return pl.ds(pl.multiple_of(start, size), size)

    def hop(self, src, dst, sems, step, a):
        bit = (1, 2, 4, 4, 2, 1)[step]
        place = block_place()
        peer = {"dp": lax.axis_index("dp") + jnp.where(place // bit % 2 == 0, bit, -bit)}
        return remote(src, dst, sems[0].at[step, a], sems[1].at[step, a], peer)

    def slot(self, a, slots, step):
        rows = self.shapes[a][0]
        start = sum(rows >> (k + 1) for k in range(step))
        return slots[a].at[pl.ds(start, rows >> (step + 1))]

    def steps(self, own, slots, sems, pieces, outs):
        arrays = range(len(self.shapes))
        for step in range(3):
            for a in arrays:
                self.hop(own[a].at[self.block(a, step + 1, True)], self.slot(a, slots, step), sems, step, a).start()
            yield
            for a in arrays:
                slot = self.slot(a, slots, step)
                self.hop(slot, slot, sems, step, a).wait_recv()
                own[a][self.block(a, step + 1, False), :] += slot[...]
        for a in arrays:
            mine = self.block(a, 3, False)
            pltpu.make_async_copy(own[a].at[mine], outs[a].at[mine], sems[2].at[a]).start()
        for step in range(3, 6):
            for a in arrays:
                mine = self.block(a, 6 - step, False)
                if step == 3:
                    pltpu.make_async_copy(own[a].at[mine], outs[a].at[mine], sems[2].at[a]).wait()
                self.hop(outs[a].at[mine], outs[a].at[mine], sems, step, a).start()
            yield
            for a in arrays:
                theirs = outs[a].at[self.block(a, 6 - step, True)]
                self.hop(theirs, theirs, sems, step, a).wait_recv()
        for step in range(6):
            for a in arrays:
                slot = self.slot(a, slots, step if step < 3 else 5 - step)
                self.hop(slot, slot, sems, step, a).wait_send()


def fill(dst, total, size, make):
    for start, extent in tiles(total, size):
        cols = pl.ds(start, extent)
        dst[:, cols] = make(cols)


class Backward:
    def __init__(self, top, l, n, tensor, seqs, length, width, mix_cols, hidden_units, rank):
        self.top, self.l, self.n, self.tensor, self.rank = top, l, n, tensor, rank
        self.seqs, self.length, self.width, self.mix_cols, self.hidden_units = seqs, length, width, mix_cols, hidden_units
        hidden = [(hidden_units, width)]
        self.ffn = [RingJob(n, hidden, True, True) if top else BlockSum(hidden, True, True) for _ in range(3)]
        mix_shapes = [(width, mix_cols), (HV, width)]
        self.mix = RingJob(n, mix_shapes, True, not top)
        self.above = RingJob(n, mix_shapes, False, True)
        self.small = HalvingSum([(8 * n, HK), (8 * n, width)])

    def small_outs(self):
        width = self.width
        return [jax.ShapeDtypeStruct(shape, f32) for shape in ((128, HK), (1, HK), (128, width), (1, width), (1, width), (1, HV))]

    def call(self, collective, lengths, params, arrays, extra):
        seqs, length, width = self.seqs, self.length, self.width
        rows, own = seqs * length, length // 4
        wide = jax.ShapeDtypeStruct((rows, width), bf)
        wide32, quarter = jax.ShapeDtypeStruct((rows, width), f32), jax.ShapeDtypeStruct((seqs * own, width), f32)
        smalls = self.small_outs()
        if self.top:
            outs = [wide32, wide, quarter] + [job.full()[0] for job in self.ffn]
            vmem_outs = self.mix.pieces() + smalls
            vmem_ins = 0
        else:
            outs = [wide32, wide] + [job.full()[0] for job in self.ffn] + self.mix.full() + self.above.full() + self.small.full()
            vmem_outs = []
            vmem_ins = len(extra) - 2
        scratch = [pltpu.VMEM(shape.shape, f32) for shape in [job.full()[0] for job in self.ffn] + self.mix.full()]
        scratch += [job.slots()[0] for job in self.ffn] + self.mix.slots() + [sem for job in self.ffn for sem in job.sems()] + self.mix.sems()
        if not self.top:
            scratch += self.above.sems() + [pltpu.VMEM(shape.shape, f32) for shape in self.small.full()] + self.small.slots() + self.small.sems()
            scratch += [pltpu.VMEM((self.tensor - 1, 8 * self.n, width), f32), DMA((self.tensor - 1,)), DMA((self.tensor - 1,))]
            scratch += [pltpu.VMEM(shape.shape, f32) for shape in smalls]
        scratch += [
            pltpu.VMEM((seqs, length, width), f32), pltpu.VMEM((seqs, 2 * own, width), f32), pltpu.VMEM((seqs, own, width), f32),
            pltpu.VMEM((seqs, length, width), f32), pltpu.VMEM((rows, width), bf), pltpu.VMEM((rows, width), bf),
            pltpu.VMEM(quarter.shape, f32), pltpu.VMEM(quarter.shape, f32), pltpu.VMEM(quarter.shape, f32),
            DMA((40,)), DMA((5, seqs)), DMA((5, seqs)),
        ]
        return pl.pallas_call(
            self.kernel, name="backward_top" if self.top else "backward_low",
            in_specs=[pl.BlockSpec(memory_space=pltpu.SMEM)] + [VMEM_SPEC] * len(params) + [ANY_SPEC] * len(arrays) + [VMEM_SPEC] * vmem_ins + [ANY_SPEC] * (len(extra) - vmem_ins),
            out_specs=[ANY_SPEC] * len(outs) + [VMEM_SPEC] * len(vmem_outs), out_shape=outs + vmem_outs, scratch_shapes=scratch,
            compiler_params=pltpu.CompilerParams(collective_id=collective, has_side_effects=True, vmem_limit_bytes=61 << 20),
            cost_estimate=pl.CostEstimate(flops=10**10, bytes_accessed=3 * 10**8, transcendentals=0),
        )(lengths, *params, *arrays, *extra)

    def kernel(self, *refs):
        top, l, seqs, length, width, rank = self.top, self.l, self.seqs, self.length, self.width, self.rank
        mix_cols, hidden_units = self.mix_cols, self.hidden_units
        half, own, rows = length // 2, length // 4, seqs * length
        refs = list(refs)

        def take(count):
            found = refs[:count]
            del refs[:count]
            return found

        lengths, gains, ffn_gains, bias, group = take(5)
        normed_ffn, ffn_grad, from_above, middle_in, entry_in, z_in, mixed_in, scores_in, gated_in, normed_in = take(10)
        proj, (decay_down, decay_up), heads_in, ffn_ws = take(4), take(2), take(1)[0], take(3)
        if top:
            acts = take(3)
            out_partial, out_grad, out_resid = take(3)
            ffn_outs, mix_outs = take(3), None
            mix_pieces, smalls = take(2), take(6)
        else:
            above_pieces, smalls_above = take(2), take(6)
            last_partial, last_middle = take(2)
            out_input, out_layer = take(2)
            ffn_outs, mix_outs, above_outs, small_outs = take(3), take(2), take(2), take(2)
            mix_pieces = None
        ffn_own, mix_own, ffn_slots, mix_slots = take(3), take(2), take(3), take(2)
        ffn_sems, mix_sems = [take(len(job.sems())) for job in self.ffn], take(len(self.mix.sems()))
        if not top:
            above_sems, small_own, small_slots, small_sems = take(len(self.above.sems())), take(2), take(2), take(len(self.small.sems()))
            shared, peer_send, peer_recv = take(3)
            smalls = take(6)
        up_sum, bias_sum, down_sum, attn_sum, ffn_sum, group_sum = smalls
        partial, first, second, gathered, rows_in, grad, resid, middle, entry, load, send, recv = take(12)
        pending = set()

        def ids():
            me = lax.axis_index("tensor")
            return me % 2, me // 2, {"tensor": peer_of(me, 1)}, {"tensor": peer_of(me, 2)}

        def piece(c, x_half, size):
            return pl.ds(pl.multiple_of(c * half + x_half * own, own), size)

        def of_seq(ref, s, height):
            return ref.at[pl.ds(s * height, height)]

        def plain(stage, s):
            src = (partial.at[s, pl.ds(0, half)], partial.at[s, pl.ds(0, own)])[stage] if stage < 2 else gathered.at[s, pl.ds(0, own)]
            dst = (first.at[s], second.at[s])[stage] if stage < 2 else src
            return remote(src, dst, send.at[stage, s], recv.at[stage, s], ids()[2 if stage in (0, 3, 4) else 3])

        def launch(src, dst, stage, s, peer):
            remote(src, dst, send.at[stage, s], recv.at[stage, s], peer).start()
            pending.add((stage, s))

        def freed(s, stages):
            for stage in stages:
                if (stage, s) in pending:
                    plain(stage, s).wait_send()
                    pending.discard((stage, s))

        def scatter(s):
            core, cross, core_peer, cross_peer = ids()
            launch(partial.at[s, piece(1 - core, 0, half)], first.at[s], 0, s, core_peer)
            plain(0, s).wait_recv()
            freed(s, (2, 3, 4))
            partial[s, piece(core, 1 - cross, own), :] += first[s, piece(0, 1 - cross, own), :]
            launch(partial.at[s, piece(core, 1 - cross, own)], second.at[s], 1, s, cross_peer)
            partial[s, piece(core, cross, own), :] += first[s, piece(0, cross, own), :]

        def arrived(s):
            core, cross, _, _ = ids()
            plain(1, s).wait_recv()
            return partial[s, piece(core, cross, own), :] + second[s]

        def publish(s, sent):
            core, cross, core_peer, cross_peer = ids()
            gathered[s, piece(core, cross, own), :] = sent
            block = gathered.at[s, piece(core, cross, own)]
            launch(block, block, 2, s, cross_peer)
            launch(block, block, 3, s, core_peer)

        def settle(s, h_ref, gain, gain_sum, rounded):
            total = arrived(s)
            mine = pl.ds(s * own, own)
            h = h_ref[mine, :]
            r = rms_unit(h)
            unit = h * r
            here = jnp.sum(total * unit, axis=0, keepdims=True)
            gain_sum[...] = here if s == 0 else gain_sum[...] + here
            weighted = total * gain
            new = resid[mine, :] + r * (weighted - unit * jnp.mean(unit * weighted, axis=-1, keepdims=True))
            resid[mine, :] = new
            publish(s, new.astype(bf).astype(f32) if rounded else new)

        def collect(s, dest):
            core, cross, core_peer, _ = ids()
            plain(2, s).wait_recv()
            block = gathered.at[s, piece(core, 1 - cross, own)]
            launch(block, block, 4, s, core_peer)
            if dest is not None:
                dest[pl.ds(pl.multiple_of(s * length + core * half, half), half), :] = gathered[s, piece(core, 0, half), :].astype(bf)
            plain(3, s).wait_recv()
            plain(4, s).wait_recv()
            if dest is not None:
                dest[pl.ds(pl.multiple_of(s * length + (1 - core) * half, half), half), :] = gathered[s, piece(1 - core, 0, half), :].astype(bf)

        jobs = []
        over = object()

        def pump(count=1):
            for _ in range(count):
                turns = max([times for _, times in jobs], default=0)
                for turn in range(turns):
                    for job in list(jobs):
                        if turn < job[1] and next(job[0], over) is over:
                            jobs.remove(job)

        def begin(job, times=1):
            next(job)
            jobs.append((job, times))

        def local(src, dst, k):
            return pltpu.make_async_copy(src, dst, load.at[k])

        def rows_of(s):
            return pl.ds(s * length, length)

        basics = [(normed_ffn, rows_in, 0), (ffn_grad, grad, 1), (middle_in, middle, 3), (entry_in, entry, 4)] + ([] if top else [(from_above, resid, 2)])
        for src, dst, k in basics:
            local(src, dst, k).start()
        barrier = pltpu.get_barrier_semaphore()
        level = block_place() // 2
        core_peer, cross_peer = ids()[2:]
        peers = [core_peer, cross_peer] if top else [{"tensor": lax.rem(lax.axis_index("tensor") + hop, self.tensor)} for hop in range(1, self.tensor)]
        if not top:
            peers.append({"dp": lax.axis_index("dp") + jnp.where(level // 2 == 0, 4, -4)})
        for peer in peers + [block_peer(0)]:
            pl.semaphore_signal(barrier, inc=1, device_id=peer, device_id_type=MESH)
        for way, there in ((1, level < RING // 2 - 1), (2, level > 0)):
            @pl.when(there)
            def _():
                pl.semaphore_signal(barrier, inc=1, device_id=block_peer(way), device_id_type=MESH)
        pl.semaphore_wait(barrier, len(peers) + jnp.where(jnp.logical_and(level > 0, level < RING // 2 - 1), 3, 2))
        if not top:
            begin(self.above.steps(None, None, above_sems, above_pieces, above_outs))

        def ffn_phase(gate_w, up_w, down_w, inner, gate_low, up_low):
            weights = [(src.at[l], dst, 5 + k) for k, (src, dst) in enumerate(zip(ffn_ws, (gate_w, up_w, down_w)))]
            if top:
                for k, (src, dst) in enumerate(zip(acts, (inner, gate_low, up_low))):
                    local(src, dst, 17 + k).start()
            for src, dst, k in weights:
                local(src, dst, k).start()
            for src, dst, k in basics[:2]:
                local(src, dst, k).wait()
            if top:
                local(acts[0], inner, 17).wait()
            else:
                for src, dst, k in weights:
                    local(src, dst, k).wait()
                for s in range(seqs):
                    for start, size in tiles(hidden_units, 256):
                        ffn_tile(rows_of(s), pl.ds(start, size), rows_in, grad, gate_w, up_w, down_w, inner, gate_low, up_low)
                    pump()
            fill(ffn_own[2], width, 512, lambda cols: tn(inner[...], grad[:, cols]))
            begin(self.ffn[2].steps(ffn_own[2:], ffn_slots[2:], ffn_sems[2], None, ffn_outs[2:]))
            if top:
                for k, (src, dst) in enumerate(zip(acts, (inner, gate_low, up_low))):
                    if k > 0:
                        local(src, dst, 17 + k).wait()
            for k, low_rows in ((0, gate_low), (1, up_low)):
                fill(ffn_own[k], width, 512, lambda cols: tn(low_rows[...], rows_in[:, cols]))
                begin(self.ffn[k].steps(ffn_own[k:k + 1], ffn_slots[k:k + 1], ffn_sems[k], None, ffn_outs[k:k + 1]))
            if top:
                for src, dst, k in weights:
                    local(src, dst, k).wait()
            for src, dst, k in basics[2:]:
                local(src, dst, k).wait()
            if top:
                core, cross, _, _ = ids()
                for s in range(seqs):
                    mine = pl.ds(pl.multiple_of(s * length + core * half + cross * own, own), own)
                    resid[pl.ds(s * own, own), :] = grad[mine, :].astype(f32)
            if top:
                for s in range(seqs):
                    fill(partial.at[s], width, 256, lambda cols: nn(inner[rows_of(s), :], down_w[:, cols]))
                    local(partial.at[s], of_seq(out_partial, s, length), 8 + s).start()
            for s in range(seqs):
                if top:
                    local(partial.at[s], of_seq(out_partial, s, length), 8 + s).wait()
                fill(partial.at[s], width, 256, lambda cols: nn(gate_low[rows_of(s), :], gate_w[:, cols]) + nn(up_low[rows_of(s), :], up_w[:, cols]))
                scatter(s)
                pump()

        hidden = (hidden_units, width)
        pl.run_scoped(ffn_phase, *[pltpu.VMEM(hidden, bf)] * 3, *[pltpu.VMEM((rows, hidden_units), bf)] * 3)

        def mixer_phase(cat, low_w, up_map, heads, z, mixed, scores, gated, low, ggrad, pre, suf, tot, dm, dq, dk, flow):
            low_w[...] = jnp.zeros_like(low_w)
            up_map[...] = jnp.zeros_like(up_map)
            moves = raw_weights(l, proj, cat, decay_down, low_w, decay_up, up_map, heads_in, heads) + [(gated_in, gated), (normed_in, rows_in)]
            once = [(src, dst, 24 + k) for k, (src, dst) in enumerate(moves)]
            each = [[(of_seq(src, s, length), dst, 14 + k) for k, (src, dst) in enumerate(((z_in, z), (mixed_in, mixed), (scores_in, scores)))] for s in range(seqs)]
            for src, dst, k in once + each[0]:
                local(src, dst, k).start()
            for s in range(seqs):
                settle(s, middle, ffn_gains[l:l + 1, :], ffn_sum, True)
                pump()
            for src, dst, k in once:
                local(src, dst, k).wait()
            for s in range(seqs):
                collect(s, grad)
                for src, dst, k in each[s]:
                    local(src, dst, k).wait()
                ggrad[...] = nt(grad[rows_of(s), :], heads[...])
                mixer_backward(
                    s == 0, z, up_map, bias.at[pl.ds(l, 1)], group.at[pl.ds(l, 1)], mixed, scores, ggrad, of_seq(low, s, length),
                    up_sum, bias_sum, group_sum, pre, suf, tot, dm, dq, dk, flow)
                pump()
                if s + 1 < seqs:
                    for src, dst, k in each[s + 1]:
                        local(src, dst, k).start()
                freed(s, (0, 1))
                fill(partial.at[s], width, 256, lambda cols: nt(low[rows_of(s), :mix_cols], cat[cols, :]) + nn(low[rows_of(s), mix_cols:], low_w[:, cols]))
                scatter(s)
                pump()
            fill(mix_own[0], mix_cols, 256, lambda cols: tn(rows_in[...], low[:, cols]))
            fill(mix_own[1], width, 512, lambda cols: tn(gated[...], grad[:, cols]))
            begin(self.mix.steps(mix_own, mix_slots, mix_sems, mix_pieces, mix_outs))
            down_sum[...] = tn(low[:, mix_cols:], rows_in[...])

        f32s = lambda count: [pltpu.VMEM((length, HK), f32)] * count
        pl.run_scoped(
            mixer_phase, pltpu.VMEM((width, mix_cols), bf), pltpu.VMEM((128, width), bf), pltpu.VMEM((128, HK), bf), pltpu.VMEM((HV, width), bf), pltpu.VMEM((length, mix_cols + 128), f32),
            pltpu.VMEM((length, HV), f32), pltpu.VMEM((length, length), bf), pltpu.VMEM((rows, HV), bf), pltpu.VMEM((rows, mix_cols + 128), bf),
            pltpu.VMEM((length, HV), f32), *f32s(2), pltpu.VMEM((length // CH * 8, HK), f32), pltpu.VMEM((length, HV), bf), *f32s(3))
        for s in range(seqs):
            pump()
            settle(s, entry, gains[l:l + 1, :], attn_sum, top)
        if top:
            local(resid, out_resid, 20).start()
            for s in range(seqs):
                pump()
                collect(s, grad)
                local(of_seq(grad, s, length), of_seq(out_grad, s, length), 21 + s).start()
            local(resid, out_resid, 20).wait()
            for s in range(seqs):
                local(of_seq(grad, s, length), of_seq(out_grad, s, length), 21 + s).wait()
        else:
            small_own[0][...] = jnp.zeros_like(small_own[0])
            small_own[1][...] = jnp.zeros_like(small_own[1])
            at0 = at1 = 0
            for terms in (smalls, smalls_above):
                small_own[0][at0:at0 + rank, :] = terms[0][:rank, :]
                small_own[0][at0 + rank:at0 + rank + 1, :] = terms[1][...]
                small_own[1][at1:at1 + rank, :] = terms[2][:rank, :]
                for k in (3, 4):
                    small_own[1][at1 + rank + k - 3:at1 + rank + k - 2, :] = terms[k][...]
                small_own[1][at1 + rank + 2:at1 + rank + 3, :HV] = terms[5][...]
                at0, at1 = at0 + rank + 8, at1 + rank + 8
            hops = range(self.tensor - 1)

            def to_peer(hop):
                peer = {"tensor": lax.rem(lax.axis_index("tensor") + hop + 1, self.tensor)}
                return remote(small_own[1], shared.at[hop], peer_send.at[hop], peer_recv.at[hop], peer)

            for hop in hops:
                to_peer(hop).start()
            local(last_middle, middle, 20).start()
            for s in range(seqs):
                freed(s, (0, 1))
                local(of_seq(last_partial, s, length), partial.at[s], 8 + s).start()
            pump()
            for hop in hops:
                to_peer(hop).wait()
            small_own[1][...] += sum(shared[hop] for hop in hops)
            begin(self.small.steps(small_own, small_slots, small_sems, None, small_outs))
            for s in range(seqs):
                collect(s, None)
                local(gathered.at[s], of_seq(out_input, s, length), 21 + s).start()
                pump()
            local(last_middle, middle, 20).wait()
            for s in range(seqs):
                local(gathered.at[s], of_seq(out_input, s, length), 21 + s).wait()
                local(of_seq(last_partial, s, length), partial.at[s], 8 + s).wait()
                scatter(s)
                pump()
            for s in range(seqs):
                total = arrived(s)
                mine = pl.ds(s * own, own)
                core, cross, _, _ = ids()
                row = lax.broadcasted_iota(jnp.int32, (own, 1), 0) + (core * half + cross * own)
                publish(s, jnp.where(row < lengths[s], middle[mine, :] + total, 0.0).astype(bf).astype(f32))
                pump()
            for s in range(seqs):
                collect(s, grad)
                local(of_seq(grad, s, length), of_seq(out_layer, s, length), 21 + s).start()
                pump()
            for s in range(seqs):
                local(of_seq(grad, s, length), of_seq(out_layer, s, length), 21 + s).wait()
        while jobs:
            pump()
        for s in range(seqs):
            freed(s, range(5))


class Finish:
    def __init__(self, rows, width, mix_cols, hidden_units, rank):
        self.rank, self.width = rank, width
        self.cols = ((0, HK), (HK, HK), (2 * HK, HV), (2 * HK + HV, HV))
        f = lambda *shape: jax.ShapeDtypeStruct(shape, f32)
        self.big = [f(2, hidden_units, width)] * 3 + [f(2, width, size) for _, size in self.cols] + [f(2, HV, width), f(rows, width)]
        self.big += [jax.ShapeDtypeStruct((rows, width), bf)]
        self.small = [f(2, rank, HK), f(2, HK), f(2, rank, width), f(2, width), f(2, width), f(2, HV)]

    def call(self, ffn, mix, rows_out, local, shared):
        arrays = list(ffn) + list(mix) + list(rows_out)
        return pl.pallas_call(
            self.kernel, name="finish", in_specs=[ANY_SPEC] * len(arrays) + [VMEM_SPEC] * 2,
            out_specs=[ANY_SPEC] * len(self.big) + [VMEM_SPEC] * len(self.small), out_shape=self.big + self.small,
            scratch_shapes=[pltpu.VMEM(a.shape, a.dtype) for a in arrays] + [DMA((len(arrays),)), DMA((24,))],
            compiler_params=pltpu.CompilerParams(vmem_limit_bytes=60 << 20),
            cost_estimate=pl.CostEstimate(flops=10**6, bytes_accessed=64 * 10**6, transcendentals=0),
        )(*arrays, local, shared)

    def kernel(self, *refs):
        rank, width = self.rank, self.width
        ins, (local, shared), outs, small = refs[:12], refs[12:14], refs[14:24], refs[24:30]
        load, store = refs[-2:]
        held = refs[30:42]
        loads = [pltpu.make_async_copy(src, dst, load.at[k]) for k, (src, dst) in enumerate(zip(ins, held))]
        for step in loads:
            step.start()
        stores = []

        def put(src, dst):
            step = pltpu.make_async_copy(src, dst, store.at[len(stores)])
            step.start()
            stores.append(step)

        for l in range(2):
            for k in range(3):
                loads[3 * l + k].wait()
                put(held[3 * l + k], outs[k].at[l])
        for l in range(2):
            loads[6 + 2 * l].wait()
            for k, (start, size) in enumerate(self.cols):
                put(held[6 + 2 * l].at[:, pl.ds(start, size)], outs[3 + k].at[l])
            loads[7 + 2 * l].wait()
            put(held[7 + 2 * l], outs[7].at[l])
        for k in range(2):
            loads[10 + k].wait()
            put(held[10 + k], outs[8 + k])
        up, bias, down, attn, ffn_gain, group = small
        for l in range(2):
            at = l * (rank + 8)
            up[l] = local[at:at + rank, :]
            bias[l:l + 1, :] = local[at + rank:at + rank + 1, :]
            down[l] = shared[at:at + rank, :]
            attn[l:l + 1, :] = shared[at + rank:at + rank + 1, :]
            ffn_gain[l:l + 1, :] = shared[at + rank + 1:at + rank + 2, :]
            group[l:l + 1, :] = shared[at + rank + 2:at + rank + 3, :HV]
        for step in stores:
            step.wait()


def shards(
    groups, tensor, layer_input, seq_lengths, attn_gain, query_proj, key_proj, value_proj, gate_proj,
    decay_down, decay_up, decay_bias, group_gain, output_proj, ffn_gain, ffn_gate, ffn_up, ffn_down, cotangent,
):
    seqs, length, width = layer_input.shape
    depth = attn_gain.shape[0]
    rank = decay_down.shape[2]
    rows = seqs * length
    mix_cols = 2 * HK + 2 * HV
    hidden_units = ffn_gate.shape[2]
    assert groups % RING == 0
    ring = RING
    proj = (query_proj, key_proj, value_proj, gate_proj)
    decay = (decay_down.transpose(0, 2, 1), decay_up)
    ffn_ws = (ffn_gate.transpose(0, 2, 1), ffn_up.transpose(0, 2, 1), ffn_down)
    params = (attn_gain, ffn_gain, decay_bias, group_gain)
    found = Forward(depth, seqs, length, width, mix_cols, hidden_units).call(
        0, seq_lengths, params, layer_input.reshape(rows, width), cotangent.reshape(rows, width), proj, decay, output_proj, ffn_ws)
    kinds = 8
    acts = found[depth * kinds:]

    def backward(top, l, ffn_grad, resid, extra):
        normed, z, gated, mixed, scores, entry, middle, normed_ffn = found[l * kinds:(l + 1) * kinds]
        arrays = (normed_ffn, ffn_grad, resid, middle, entry, z, mixed, scores, gated, normed, *proj, *decay, output_proj, *ffn_ws)
        return Backward(top, l, ring, tensor, seqs, length, width, mix_cols, hidden_units, rank).call(1 + l, seq_lengths, params, arrays, extra)

    ffn_sums, mix_sums = [None] * depth, [None] * depth
    last_partial, ffn_grad, resid, *found_top = backward(True, 1, acts[0], found[kinds + 6], acts[1:])
    ffn_sums[1] = found_top[:3]
    extra = (*found_top[3:], last_partial, found[kinds + 6])
    input_grad, layer_output, *sums = backward(False, 0, ffn_grad, resid, extra)
    if groups > ring:
        found_sums = lax.psum(tuple(part * (1.0 / ring) for part in (*sums, *ffn_sums[1])), "dp")
        sums, ffn_sums[1] = found_sums[:-3], found_sums[-3:]
    ffn_sums[0], mix_sums[0], mix_sums[1], (local, shared) = sums[:3], sums[3:5], sums[5:7], sums[7:]

    done = Finish(rows, width, mix_cols, hidden_units, rank).call(
        (*ffn_sums[0], *ffn_sums[1]), (*mix_sums[0], *mix_sums[1]), (input_grad, layer_output), local, shared)
    gate, up, down, query, key, value, out_gate, head, input_grad, layer_output, d_up, d_bias, d_down, attn, ffn, group = done
    return (
        layer_output.reshape(seqs, length, width),
        input_grad.reshape(seqs, length, width),
        attn,
        query,
        key,
        value,
        out_gate,
        d_down.transpose(0, 2, 1),
        d_up,
        d_bias,
        group,
        head,
        ffn,
        gate.transpose(0, 2, 1),
        up.transpose(0, 2, 1),
        down,
    )


def solution(mesh):
    over, across = P("dp", None, None), P(None, None, "tensor")
    deep = P(None, "tensor", None)
    return jax.shard_map(
        functools.partial(shards, mesh.shape["dp"], mesh.shape["tensor"]),
        mesh=mesh,
        in_specs=(over, P("dp"), P(), across, across, across, across, P(), across, P(None, "tensor"), P(), deep, P(), across, across, deep, over),
        out_specs=(over, over, P(), across, across, across, across, P(), across, P(None, "tensor"), P(), deep, P(), across, across, deep),
        check_vma=False,
    )
```
